32 devices in a mesh: dp: 8 (over z, x), tensor: 4 (over y, core).
Axes of the slice: x: 2, y: 2, z: 4, core: 2. Of those that a mesh axis runs over, the one named last changes fastest.
Arguments:
- x_in: bfloat16 [4096, 1536], P('dp'), may hold values from -6 to 6
- lengths: int32 [8], P('dp'), may hold values from 256 to 512, as said below
- routes: int32 [4096, 6], P('dp'), may hold values from 0 to 63, all different within a row; in each aligned block of 512 rows (0 to 511, 512 to 1023, ...) at most 64 rows name the same one
- route_w: float32 [4096, 6], P('dp'), may hold values from 0.08 to 0.32
- ln1_gain: float32 [1536], replicated, may hold values from 0.5 to 1.5
- w_zx: float32 [1536, 2, 3072], P('dp', None, 'tensor'), may hold values from -0.15625 to 0.15625
- w_bc: float32 [1536, 256], P('dp'), may hold values from -0.15625 to 0.15625
- w_dt: float32 [1536, 48], P('dp', 'tensor'), may hold values from -0.15625 to 0.15625
- conv_x: float32 [4, 3072], P(None, 'tensor'), may hold values from -3 to 3
- conv_x_bias: float32 [3072], P('tensor'), may hold values from -2 to 2
- conv_bc: float32 [4, 256], replicated, may hold values from -3 to 3
- conv_bc_bias: float32 [256], replicated, may hold values from -2 to 2
- dt_bias: float32 [48], P('tensor'), may hold values from -6 to -2
- a_log: float32 [48], P('tensor'), may hold values from 0 to 2.8
- d_skip: float32 [48], P('tensor'), may hold values from 0.5 to 1.5
- gnorm_gain: float32 [3072], P('tensor'), may hold values from 0.5 to 1.5
- w_out: float32 [1536, 3072], P('dp', 'tensor'), may hold values from -0.109375 to 0.109375
- ln2_gain: float32 [1536], replicated, may hold values from 0.5 to 1.5
- w_shared_gu: float32 [1536, 2, 1024], P('dp', None, 'tensor'), may hold values from -0.15625 to 0.15625
- w_shared_down: float32 [1536, 1024], P('dp', 'tensor'), may hold values from -0.1875 to 0.1875
- w_exp_gu: float32 [64, 1536, 2, 512], P('dp', None, None, 'tensor'), may hold values from -0.15625 to 0.15625
- w_exp_down: float32 [64, 512, 1536], P('dp', 'tensor'), may hold values from -0.25 to 0.25
- cotangent: bfloat16 [4096, 1536], P('dp'), may hold values from -6 to 6
Outputs:
- out: bfloat16 [4096, 1536], P('dp')
- grad_x: float32 [4096, 1536], P('dp')
- grad_ln1: float32 [1536], replicated
- grad_w_zx: float32 [1536, 2, 3072], P('dp', None, 'tensor')
- grad_w_bc: float32 [1536, 256], P('dp')
- grad_w_dt: float32 [1536, 48], P('dp', 'tensor')
- grad_conv_x: float32 [4, 3072], P(None, 'tensor')
- grad_conv_x_bias: float32 [3072], P('tensor')
- grad_conv_bc: float32 [4, 256], replicated
- grad_conv_bc_bias: float32 [256], replicated
- grad_dt_bias: float32 [48], P('tensor')
- grad_a_log: float32 [48], P('tensor')
- grad_d_skip: float32 [48], P('tensor')
- grad_gnorm: float32 [3072], P('tensor')
- grad_w_out: float32 [1536, 3072], P('dp', 'tensor')
- grad_ln2: float32 [1536], replicated
- grad_w_shared_gu: float32 [1536, 2, 1024], P('dp', None, 'tensor')
- grad_w_shared_down: float32 [1536, 1024], P('dp', 'tensor')
- grad_w_exp_gu: float32 [64, 1536, 2, 512], P('dp', None, None, 'tensor')
- grad_w_exp_down: float32 [64, 512, 1536], P('dp', 'tensor')
The draws below stay inside these ranges and needn't reach their ends.
Inputs may be any that keep to these rules, and one draw needn't show every extreme that they name: `routes`: in the 512 rows of one index of dp no expert is named by more than 64 rows; in some of these blocks an expert is named by exactly 64. `lengths`: the sequence of one index of dp fills all 512 slots.
All inputs are finite; a program needn't handle non-finite values.
Results may differ from the reference program's by a relative error of at most 0.025.
Values may be sent and summed in bfloat16 or wider, within the bound.
A program may use at most 320 MiB of HBM per device.

```python
import math
import jax
import jax.numpy as jnp
import numpy as np
from jax import lax

D = 1536
H = 48
P_SIZE = 64
STATE = 128
FE = 512
FS = 1024
TOP = 6
EXPERTS = 64
CONV = 4
BLOCK = 256
SLOTS = 512
DI = 3072
CAP = 64
TOKENS = 4096
N_DP = 8
N_TENSOR = 4


def draw_lengths(key, part):
    first_key, second_key = jax.random.split(key)
    values = jax.random.randint(first_key, (N_DP,), SLOTS // 2, SLOTS + 1)
    chosen = jax.random.randint(second_key, (), 0, N_DP)
    return jnp.where(jnp.arange(N_DP) == chosen, SLOTS, values).astype(jnp.int32)


def level_of(rng, dims, pieces, smallest, high):
    loudness = 1.0
    for dim, parts in pieces:
        steps = jax.random.uniform(jax.random.fold_in(jax.random.fold_in(rng, 6), dim), (parts,), jnp.float32, smallest / len(pieces), high / len(pieces))
        loudness = loudness * jnp.repeat(jnp.exp(steps), dims[dim] // parts).reshape((-1,) + (1,) * (len(dims) - 1 - dim))
    return loudness


def assign_block(stream_key, own, number, rows, number_of, top, most, lean):
    sequence = jax.random.permutation(stream_key, number_of)
    heavy_load, ordinary = portions_of(number_of, rows * top, most, lean, True), portions_of(number_of, rows * top, most, lean, False)
    places = jnp.arange(number_of)

    def named(tallies, offset_by):
        used = int((tallies > 0).sum())
        fixed = max(1, used // 4)
        shifted = fixed + (places - fixed + offset_by * (used - fixed)) % max(1, number_of - fixed)
        return jnp.zeros((number_of,), jnp.int32).at[sequence[jnp.where(places < fixed, places, shifted)]].set(jnp.asarray(tallies, jnp.int32))

    tallies = jnp.where(number % 4 == 0, named(heavy_load, number // 4), named(ordinary, number - number // 4 - 1))
    mixed = jax.random.permutation(jax.random.fold_in(own, 3), number_of)
    donor, receiver = mixed[0:number_of // 2 * 2:2], mixed[1:number_of // 2 * 2:2]
    room = jnp.minimum(tallies[donor] - 1, most - tallies[receiver]) // 2
    room = jnp.where((donor == sequence[0]) | (receiver == sequence[0]) | (tallies[receiver] == 0), 0, jnp.maximum(room, 0))
    shifted = jax.random.randint(jax.random.fold_in(own, 4), (number_of // 2,), 0, 1 << 20) % (room + 1)
    tallies = tallies.at[donor].add(-shifted).at[receiver].add(shifted)
    items = jnp.searchsorted(jnp.cumsum(tallies), jnp.arange(rows * top), side="right").astype(jnp.int32)
    listing = items.reshape(top, rows).T
    listing = listing[jax.random.permutation(jax.random.fold_in(own, 1), rows)]
    offset_by = jax.random.randint(jax.random.fold_in(own, 2), (rows, 1), 0, top)
    return jnp.take_along_axis(listing, (jnp.arange(top)[None, :] + offset_by) % top, axis=1)


def portions_of(count, total, most, skew, full):
    weights = [(1 << 20) // math.isqrt(grade ** skew) + 1 for grade in range(1, count + 1)]
    largest = most if full else min(most, max(-(-total // count), total * weights[0] // sum(weights)))
    least = 1 if total - largest >= count - 1 else 0
    counts, surplus = [largest] + [least] * (count - 1), total - largest - least * (count - 1)
    while surplus > 0:
        candidates = [i for i in range(1, count) if counts[i] < largest] or [i for i in range(1, count) if counts[i] < most]
        mass, budget = sum([weights[i] for i in candidates]), surplus
        for i in candidates:
            more = min(most - counts[i], max(1, budget * weights[i] // mass), surplus)
            counts[i] = counts[i] + more
            surplus = surplus - more
    return np.array(counts)


def scatter_about(key, shape, deviation, reach, pieces=(), kind=jnp.bfloat16):
    values = deviation * jax.random.normal(key, shape, jnp.float32)
    if pieces:
        values = values * level_of(key, shape, pieces, -0.22, 0.18)
    return jnp.clip(values, -reach, reach).astype(kind)


def setup_inputs(seed: int = 0) -> dict:
    splits = jax.random.split(jax.random.key(seed), 24)
    x_in = scatter_about(splits[0], (TOKENS, D), 1.0, 6.0, ((0, 8),))
    lengths = draw_lengths(jax.random.fold_in(splits[23], 71), 0)
    routes_keys = jax.random.split(jax.random.fold_in(splits[2], 1), TOKENS // SLOTS)
    routes_turns = jax.random.permutation(jax.random.fold_in(splits[2], 3), TOKENS // SLOTS)
    routes = jax.vmap(lambda own, number: assign_block(jax.random.fold_in(splits[2], 2), own, number, SLOTS, EXPERTS, TOP, CAP, 1))(routes_keys, routes_turns).reshape((TOKENS, TOP))
    route_w = jnp.clip(jnp.exp(math.log(0.32) - 1.3862944 * jax.random.uniform(splits[3], (TOKENS, TOP), jnp.float32) ** level_of(splits[3], (TOKENS, TOP), ((0, 8),), -0.2, 0.2)), 0.08, 0.32)
    ln1_gain = jnp.clip(1.0 + 0.1 * jax.random.normal(splits[4], (D,), jnp.float32), 0.5, 1.5)
    w_zx = scatter_about(splits[5], (D, 2, DI), D ** -0.5, 0.15625, ((0, 8), (2, 4)), jnp.float32)
    w_bc = scatter_about(splits[6], (D, 2 * STATE), D ** -0.5, 0.15625, ((0, 8),), jnp.float32)
    w_dt = scatter_about(splits[7], (D, H), D ** -0.5, 0.15625, ((0, 8), (1, 4)), jnp.float32)
    conv_x = scatter_about(splits[8], (CONV, DI), 0.5, 3.0, ((1, 4),), jnp.float32)
    conv_x_bias = scatter_about(splits[9], (DI,), 0.3, 2.0, ((0, 4),), jnp.float32)
    conv_bc = scatter_about(splits[10], (CONV, 2 * STATE), 0.5, 3.0, (), jnp.float32)
    conv_bc_bias = scatter_about(splits[11], (2 * STATE,), 0.3, 2.0, (), jnp.float32)
    dt_bias = jnp.clip(-6.0 + 4.0 * jax.random.uniform(splits[12], (H,), jnp.float32) ** level_of(splits[12], (H,), ((0, 4),), -0.2, 0.2), -6.0, -2.0)
    a_log = jnp.clip(2.8 * jax.random.uniform(splits[13], (H,), jnp.float32) ** level_of(splits[13], (H,), ((0, 4),), -0.2, 0.2), 0.0, 2.8)
    d_skip = jnp.clip(0.5 + 1.0 * jax.random.uniform(splits[14], (H,), jnp.float32) ** level_of(splits[14], (H,), ((0, 4),), -0.2, 0.2), 0.5, 1.5)
    gnorm_gain = jnp.clip(1.0 + 0.1 * jax.random.normal(splits[15], (DI,), jnp.float32), 0.5, 1.5)
    w_out = scatter_about(splits[16], (D, DI), DI ** -0.5, 0.109375, ((0, 8), (1, 4)), jnp.float32)
    ln2_gain = jnp.clip(1.0 + 0.1 * jax.random.normal(splits[17], (D,), jnp.float32), 0.5, 1.5)
    w_shared_gu = scatter_about(splits[18], (D, 2, FS), D ** -0.5, 0.15625, ((0, 8), (2, 4)), jnp.float32)
    w_shared_down = scatter_about(splits[19], (D, FS), FS ** -0.5, 0.1875, ((0, 8), (1, 4)), jnp.float32)
    w_exp_gu = scatter_about(splits[20], (EXPERTS, D, 2, FE), D ** -0.5, 0.15625, ((0, 8), (3, 4)), jnp.float32)
    w_exp_down = scatter_about(splits[21], (EXPERTS, FE, D), FE ** -0.5, 0.25, ((0, 8), (1, 4)), jnp.float32)
    cotangent = scatter_about(splits[22], (TOKENS, D), 1.0, 6.0, ((0, 8),))
    return dict(x_in=x_in, lengths=lengths, routes=routes, route_w=route_w, ln1_gain=ln1_gain, w_zx=w_zx, w_bc=w_bc, w_dt=w_dt, conv_x=conv_x, conv_x_bias=conv_x_bias, conv_bc=conv_bc, conv_bc_bias=conv_bc_bias, dt_bias=dt_bias, a_log=a_log, d_skip=d_skip, gnorm_gain=gnorm_gain, w_out=w_out, ln2_gain=ln2_gain, w_shared_gu=w_shared_gu, w_shared_down=w_shared_down, w_exp_gu=w_exp_gu, w_exp_down=w_exp_down, cotangent=cotangent)


EPSILON = 1e-05
HIGHEST = lax.Precision.HIGHEST

@jax.custom_vjp
def low(v):
    return lax.optimization_barrier(v.astype(jnp.bfloat16)).astype(jnp.float32)

@jax.custom_vjp
def low_back(v):
    return v

def low_keep(v):
    return (low(v), None)

def low_pass(kept, grad):
    return (grad,)

def back_keep(v):
    return (v, None)

def back_low(kept, grad):
    return (low(grad),)
low.defvjp(low_keep, low_pass)
low_back.defvjp(back_keep, back_low)

def rms_scale(values):
    return lax.rsqrt(lax.optimization_barrier(jnp.mean(values * values, axis=-1, keepdims=True)) + EPSILON)

def causal_conv(signal, kernel, offset):
    kernel_width = kernel.shape[0]
    seq_length = signal.shape[0]
    padded = jnp.concatenate([jnp.zeros((kernel_width - 1, signal.shape[1]), signal.dtype), signal], axis=0)
    summed = offset[None, :] + kernel[0][None, :] * padded[0:seq_length]
    for tap_index in range(1, kernel_width):
        summed = summed + kernel[tap_index][None, :] * padded[tap_index:tap_index + seq_length]
    return summed

def ssd_scan(head_values, step_sizes, log_rates, b_rows, c_rows, skip_gain, block_rows):
    seq_length, n_heads, head_size = head_values.shape
    n_state = b_rows.shape[1]
    n_blocks = seq_length // block_rows
    decay_rates = -jnp.exp(log_rates)[None, :] * step_sizes
    scaled = (head_values * step_sizes[:, :, None]).reshape(n_blocks, block_rows, n_heads, head_size)
    cumulative = jnp.cumsum(decay_rates.reshape(n_blocks, block_rows, n_heads), axis=1)
    b_block = b_rows.reshape(n_blocks, block_rows, n_state)
    c_block = c_rows.reshape(n_blocks, block_rows, n_state)
    positions = jnp.arange(block_rows)
    causal = (positions[:, None] >= positions[None, :])[None, :, :, None]
    differences = cumulative[:, :, None, :] - cumulative[:, None, :, :]
    decay_mask = jnp.where(causal, jnp.exp(jnp.where(causal, differences, 0.0)), 0.0)
    intersection = jnp.einsum('kin,kjn->kij', c_block, b_block, precision=HIGHEST)
    within = jnp.einsum('kij,kijh,kjhp->kihp', intersection, decay_mask, scaled, precision=HIGHEST)
    block_end = cumulative[:, -1, :]
    to_end = jnp.exp(block_end[:, None, :] - cumulative)
    states = jnp.einsum('kjn,kjh,kjhp->khnp', b_block, to_end, scaled, precision=HIGHEST)

    def carry_state(previous, inputs):
        block_decay, block_state = inputs
        return (block_decay[:, None, None] * previous + block_state, previous)
    final_state, entering = lax.scan(carry_state, jnp.zeros((n_heads, n_state, head_size), head_values.dtype), (jnp.exp(block_end), states))
    across = jnp.einsum('kin,khnp,kih->kihp', c_block, entering, jnp.exp(cumulative), precision=HIGHEST)
    return (within + across).reshape(seq_length, n_heads, head_size) + skip_gain[None, :, None] * head_values

def reference(x_in, lengths, routes, route_w, ln1_gain, w_zx, w_bc, w_dt, conv_x, conv_x_bias, conv_bc, conv_bc_bias, dt_bias, a_log, d_skip, gnorm_gain, w_out, ln2_gain, w_shared_gu, w_shared_down, w_exp_gu, w_exp_down, cotangent):
    token_count = N_DP * SLOTS
    pair_count = SLOTS * TOP
    expert_ids = routes.reshape(N_DP, pair_count).astype(jnp.int32)
    one_hot = (expert_ids[:, :, None] == jnp.arange(EXPERTS, dtype=jnp.int32)[None, None, :]).astype(jnp.int32)
    position = lax.optimization_barrier(jnp.sum(jnp.cumsum(one_hot, axis=1) * one_hot, axis=-1)) - 1
    block_ids = jnp.arange(N_DP, dtype=jnp.int32)[:, None]
    columns = (block_ids * CAP + position).astype(jnp.int32)
    tokens_of = (block_ids * SLOTS + jnp.arange(pair_count, dtype=jnp.int32)[None, :] // TOP).astype(jnp.int32)
    token_table = jnp.zeros((EXPERTS, N_DP * CAP), jnp.int32).at[expert_ids, columns].set(tokens_of)
    weight_table = jnp.zeros((EXPERTS, N_DP * CAP), route_w.dtype).at[expert_ids, columns].set(route_w.reshape(N_DP, pair_count))
    inside = jnp.arange(SLOTS, dtype=jnp.int32)
    live_mask = (inside[None, :] < lengths[:, None]).reshape(token_count).astype(jnp.float32)
    group_size = FE // N_TENSOR

    def forward(x_value, gain_one, proj_zx, proj_bc, proj_dt, kernel_x, offset_x, kernel_bc, offset_bc, dt_offset, log_rates, skip_gain, norm_gain, proj_out, gain_two, shared_gu, shared_down, expert_gu, expert_down):
        normed_one = low(x_value * rms_scale(x_value) * gain_one)
        zx_proj = low_back(jnp.einsum('td,dcf->tcf', normed_one, low(proj_zx), precision=HIGHEST))
        bc_proj = jnp.dot(normed_one, low(proj_bc), precision=HIGHEST)
        dt_proj = low_back(jnp.dot(normed_one, low(proj_dt), precision=HIGHEST))

        def mixer_block(inputs):
            x_part, bc_part, dt_part, z_part = inputs
            conv_values = jax.nn.silu(causal_conv(x_part, kernel_x, offset_x))
            conv_bc_values = jax.nn.silu(causal_conv(bc_part, kernel_bc, offset_bc))
            head_values = low(conv_values).reshape(SLOTS, H, P_SIZE)
            b_rows = low(conv_bc_values[:, :STATE])
            c_rows = low(conv_bc_values[:, STATE:])
            step_sizes = jax.nn.softplus(dt_part + dt_offset[None, :])
            output = ssd_scan(head_values, step_sizes, log_rates, b_rows, c_rows, skip_gain, BLOCK)
            return output.reshape(SLOTS, H * P_SIZE) * jax.nn.silu(z_part)
        gated_mix = lax.map(jax.checkpoint(mixer_block), (zx_proj[:, 1].reshape(N_DP, SLOTS, H * P_SIZE), bc_proj.reshape(N_DP, SLOTS, 2 * STATE), dt_proj.reshape(N_DP, SLOTS, H), zx_proj[:, 0].reshape(N_DP, SLOTS, H * P_SIZE))).reshape(token_count, H * P_SIZE)
        normed_mix = low(gated_mix * rms_scale(gated_mix) * norm_gain)
        mixer_out = low_back(jnp.dot(normed_mix, low(proj_out).T, precision=HIGHEST))
        hidden_one = x_value + mixer_out
        normed_two = low(hidden_one * rms_scale(hidden_one) * gain_two)
        shared_pre = low_back(jnp.einsum('td,dcf->tcf', normed_two, low(shared_gu), precision=HIGHEST))
        shared_act = low(jax.nn.silu(shared_pre[:, 0]) * shared_pre[:, 1])
        shared_out = low_back(jnp.dot(shared_act, low(shared_down).T, precision=HIGHEST))

        def expert_rows(inputs):
            gate_up, down_proj, token_ids, weights = inputs
            routed_rows = normed_two[token_ids]
            summed = jnp.zeros((token_ids.shape[0], D), routed_rows.dtype)
            for group_index in range(N_TENSOR):
                group_start = group_index * group_size
                part_rows = low_back(routed_rows)
                pre_act = low_back(jnp.einsum('rd,dcf->rcf', part_rows, gate_up[:, :, group_start:group_start + group_size], precision=HIGHEST))
                activated = low(jax.nn.silu(pre_act[:, 0]) * pre_act[:, 1])
                summed = summed + low_back(low(jnp.dot(activated, down_proj[group_start:group_start + group_size], precision=HIGHEST)))
            return summed * weights[:, None]

        def add_expert(total_moe, inputs):
            return (total_moe.at[inputs[2]].add(jax.checkpoint(expert_rows)(inputs)), None)
        moe_out, unused_out = lax.scan(add_expert, jnp.zeros_like(x_value), (low(expert_gu), low(expert_down), token_table, weight_table))
        return hidden_one + shared_out + moe_out
    out_value, pullback = jax.vjp(forward, x_in.astype(jnp.float32), ln1_gain.astype(jnp.float32), w_zx.astype(jnp.float32), w_bc.astype(jnp.float32), w_dt.astype(jnp.float32), conv_x.astype(jnp.float32), conv_x_bias.astype(jnp.float32), conv_bc.astype(jnp.float32), conv_bc_bias.astype(jnp.float32), dt_bias.astype(jnp.float32), a_log.astype(jnp.float32), d_skip.astype(jnp.float32), gnorm_gain.astype(jnp.float32), w_out.astype(jnp.float32), ln2_gain.astype(jnp.float32), w_shared_gu.astype(jnp.float32), w_shared_down.astype(jnp.float32), w_exp_gu.astype(jnp.float32), w_exp_down.astype(jnp.float32))
    gradients = pullback(cotangent.astype(jnp.float32) * live_mask[:, None])
    return (out_value.astype(jnp.bfloat16), gradients[0], gradients[1], gradients[2], gradients[3], gradients[4], gradients[5], gradients[6], gradients[7], gradients[8], gradients[9], gradients[10], gradients[11], gradients[12], gradients[13], gradients[14], gradients[15], gradients[16], gradients[17], gradients[18])
```

```python
import jax
import jax.numpy as jnp
from jax import lax
from jax.sharding import PartitionSpec as P

BLOCK = 256


EPSILON = 1e-05
HIGHEST = lax.Precision.HIGHEST
BF = jnp.bfloat16
F32 = jnp.float32


def rms_scale(values):
    return lax.rsqrt(jnp.mean(values * values, axis=-1, keepdims=True) + EPSILON)


def silu_parts(values):
    sigmoid_val = jax.nn.sigmoid(values)
    return (values * sigmoid_val, sigmoid_val * (1.0 + values * (1.0 - sigmoid_val)))


def round_keep(values):
    return lax.optimization_barrier(values.astype(BF)).astype(F32)


def dotf(spec, a, b):
    return jnp.einsum(spec, a, b, preferred_element_type=F32)


def causal_conv(signal, kernel, offset):
    kernel_width = kernel.shape[0]
    seq_length = signal.shape[0]
    padded = jnp.concatenate(
        [jnp.zeros((kernel_width - 1, signal.shape[1]), signal.dtype), signal], axis=0
    )
    summed = offset[None, :] + kernel[0][None, :] * padded[0:seq_length]
    for tap_index in range(1, kernel_width):
        summed = summed + kernel[tap_index][None, :] * padded[tap_index : tap_index + seq_length]
    return summed


def ssd_scan(head_values, step_sizes, log_rates, b_rows, c_rows, skip_gain, block_rows):
    seq_length, n_heads, head_size = head_values.shape
    n_state = b_rows.shape[1]
    n_blocks = seq_length // block_rows
    decay_rates = -jnp.exp(log_rates)[None, :] * step_sizes
    scaled = (head_values * step_sizes[:, :, None]).reshape(
        n_blocks, block_rows, n_heads, head_size
    )
    cumulative = jnp.cumsum(decay_rates.reshape(n_blocks, block_rows, n_heads), axis=1)
    b_block = b_rows.reshape(n_blocks, block_rows, n_state)
    c_block = c_rows.reshape(n_blocks, block_rows, n_state)
    positions = jnp.arange(block_rows)
    causal = (positions[:, None] >= positions[None, :])[None, :, :, None]
    differences = cumulative[:, :, None, :] - cumulative[:, None, :, :]
    decay_mask = jnp.where(causal, jnp.exp(jnp.where(causal, differences, 0.0)), 0.0)
    intersection = jnp.einsum("kin,kjn->kij", c_block, b_block, precision=HIGHEST)
    within = jnp.einsum("kij,kijh,kjhp->kihp", intersection, decay_mask, scaled, precision=HIGHEST)
    block_end = cumulative[:, -1, :]
    to_end = jnp.exp(block_end[:, None, :] - cumulative)
    states = jnp.einsum("kjn,kjh,kjhp->khnp", b_block, to_end, scaled, precision=HIGHEST)

    def carry_state(previous, inputs):
        block_decay, block_state = inputs
        return (block_decay[:, None, None] * previous + block_state, previous)

    final_state, entering = lax.scan(
        carry_state,
        jnp.zeros((n_heads, n_state, head_size), head_values.dtype),
        (jnp.exp(block_end), states),
    )
    across = jnp.einsum(
        "kin,khnp,kih->kihp", c_block, entering, jnp.exp(cumulative), precision=HIGHEST
    )
    return (within + across).reshape(seq_length, n_heads, head_size) + skip_gain[
        None, :, None
    ] * head_values


def mixer_forward(
    zx, bc_proj, dt_proj, conv_x, conv_x_bias, conv_bc, conv_bc_bias, dt_bias, a_log, d_skip
):
    slots = zx.shape[0]
    inner = conv_x.shape[1]
    heads = dt_bias.shape[0]
    state = conv_bc.shape[1] // 2

    def conv_block(x_part, bc_part, kernel_x, offset_x, kernel_bc, offset_bc):
        return (
            jax.nn.silu(causal_conv(x_part, kernel_x, offset_x)),
            jax.nn.silu(causal_conv(bc_part, kernel_bc, offset_bc)),
        )

    (conv_values, conv_bc_values), conv_back = jax.vjp(
        conv_block, zx[:, inner:], bc_proj, conv_x, conv_x_bias, conv_bc, conv_bc_bias
    )
    head_input = round_keep(conv_values)
    bc_input = round_keep(conv_bc_values)

    def scan_block(head_flat, b_rows, c_rows, dt_part, z_part, dt_offset, log_rates, skip_gain):
        step_sizes = jax.nn.softplus(dt_part + dt_offset[None, :])
        output = ssd_scan(
            head_flat.reshape(slots, heads, inner // heads),
            step_sizes,
            log_rates,
            b_rows,
            c_rows,
            skip_gain,
            BLOCK,
        )
        return output.reshape(slots, inner) * jax.nn.silu(z_part)

    gated_mix, scan_back = jax.vjp(
        scan_block,
        head_input,
        bc_input[:, :state],
        bc_input[:, state:],
        dt_proj,
        zx[:, :inner],
        dt_bias,
        a_log,
        d_skip,
    )

    def mixer_back(grad_gated):
        g_head, g_b, g_c, g_dt, g_z, g_dt_bias, g_a_log, g_d_skip = scan_back(grad_gated)
        g_xs, g_bc, g_cx, g_cxb, g_cbc, g_cbcb = conv_back(
            (g_head, jnp.concatenate([g_b, g_c], axis=1))
        )
        g_zx = jnp.concatenate([g_z, g_xs], axis=1).astype(BF)
        return (
            g_zx, g_bc, g_dt.astype(BF), g_cx, g_cxb, g_cbc, g_cbcb, g_dt_bias, g_a_log, g_d_skip
        )

    return gated_mix, mixer_back


def local(
    x_in,
    lengths,
    routes,
    route_w,
    ln1_gain,
    w_zx,
    w_bc,
    w_dt,
    conv_x,
    conv_x_bias,
    conv_bc,
    conv_bc_bias,
    dt_bias,
    a_log,
    d_skip,
    gnorm_gain,
    w_out,
    ln2_gain,
    w_shared_gu,
    w_shared_down,
    w_exp_gu,
    w_exp_down,
    cotangent,
):
    slots, width = x_in.shape
    n_dp = lax.axis_size("dp")
    n_t = lax.axis_size("tensor")
    my_t = lax.axis_index("tensor")
    my_dp = lax.axis_index("dp")
    piece = slots // n_t
    n_local = w_exp_gu.shape[0]
    n_experts = n_dp * n_local
    cap = slots * routes.shape[1] * 4 // (3 * n_experts)
    if cap > slots:
        cap = slots
    heads = dt_bias.shape[0]
    inner = conv_x.shape[1]
    head_size = inner // heads
    state = conv_bc.shape[1] // 2
    full_inner = inner * n_t
    rows = w_zx.shape[0]
    n_sh = w_shared_gu.shape[2]
    everyone = ("dp", "tensor")

    first = jnp.concatenate(
        [w_zx.reshape(rows, 2 * inner), w_bc, w_dt], axis=1
    ).astype(BF)
    second = jnp.concatenate(
        [w_out, w_shared_gu.reshape(rows, 2 * n_sh), w_shared_down], axis=1
    ).astype(BF)
    first = lax.all_gather(first, "dp", axis=0, tiled=True)
    second = lax.all_gather(second, "dp", axis=0, tiled=True)
    proj_zx = first[:, : 2 * inner]
    proj_bc = first[:, 2 * inner : 2 * inner + 2 * state]
    proj_dt = first[:, 2 * inner + 2 * state :]
    proj_out = second[:, :inner]
    shared_gu = second[:, inner : inner + 2 * n_sh]
    shared_down = second[:, inner + 2 * n_sh :]

    live = (jnp.arange(slots, dtype=jnp.int32) < lengths[0]).astype(F32)
    g2 = cotangent.astype(F32) * live[:, None]
    g2_low = g2.astype(BF)
    expert_range = jnp.arange(n_experts, dtype=jnp.int32)
    chosen = routes[:, :, None] == expert_range[None, None, :]
    weights = jnp.sum(jnp.where(chosen, route_w[:, :, None], 0.0), axis=1)
    weights = lax.all_gather(weights, "dp", axis=0, tiled=True)
    weights = lax.dynamic_slice_in_dim(weights, my_dp * n_local, n_local, axis=1)
    weights = weights.reshape(n_dp, slots, n_local)
    member = (weights > 0.0).astype(BF)
    before = (
        jnp.arange(slots)[:, None] > jnp.arange(slots)[None, :]
    ).astype(BF)
    position = dotf("ut,ste->sue", before, member).astype(jnp.int32)
    position = jnp.where(weights > 0.0, position, -1)
    pick = (
        position.transpose(0, 2, 1)[:, :, None, :]
        == jnp.arange(cap, dtype=jnp.int32)[None, None, :, None]
    )
    slot_weight = jnp.sum(
        jnp.where(pick, weights.transpose(0, 2, 1)[:, :, None, :], 0.0), axis=-1
    )
    pick = pick.astype(BF).reshape(n_dp, n_local * cap, slots)

    g2_piece = lax.dynamic_slice_in_dim(g2_low, my_t * piece, piece, axis=0)
    g2_all = lax.all_gather(g2_piece, everyone, axis=0, tiled=True).reshape(n_dp, slots, width)

    gate_w = w_exp_gu.astype(BF).reshape(n_local, width, -1)
    down_w = w_exp_down.astype(BF)

    x_float = x_in.astype(F32)
    scale_one = rms_scale(x_float)
    normed_one = (x_float * scale_one * ln1_gain).astype(BF)
    zx = dotf("td,df->tf", normed_one, proj_zx)
    bc_proj = dotf("td,df->tf", normed_one, proj_bc)
    dt_proj = dotf("td,df->tf", normed_one, proj_dt)

    gated_mix, mixer_back = mixer_forward(
        zx, bc_proj, dt_proj, conv_x, conv_x_bias, conv_bc, conv_bc_bias, dt_bias, a_log, d_skip
    )
    squares = lax.psum(jnp.sum(gated_mix * gated_mix, axis=-1), "tensor")
    scale_mix = lax.rsqrt(squares / full_inner + EPSILON)[:, None]
    normed_mix = (gated_mix * scale_mix * gnorm_gain).astype(BF)
    mixer_part = dotf("tc,dc->td", normed_mix, proj_out).astype(BF)
    mixer_out = lax.psum_scatter(
        mixer_part, "tensor", scatter_dimension=0, tiled=True
    ).astype(F32)
    x_piece = lax.dynamic_slice_in_dim(x_float, my_t * piece, piece, axis=0)
    hidden_one = x_piece + mixer_out
    scale_two = rms_scale(hidden_one)
    normed_two = (hidden_one * scale_two * ln2_gain).astype(BF)
    all_rows = lax.all_gather(normed_two, everyone, axis=0, tiled=True)
    mine = lax.dynamic_slice_in_dim(all_rows, my_dp * slots, slots, axis=0)
    all_rows = all_rows.reshape(n_dp, slots, width)

    shared_pre = dotf("td,df->tf", mine, shared_gu)
    s_gate, s_up = shared_pre[:, :n_sh], shared_pre[:, n_sh:]
    shared_silu, shared_slope = silu_parts(s_gate)
    shared_act = (shared_silu * s_up).astype(BF)
    grad_shared_act = dotf("td,df->tf", g2_low, shared_down)
    grad_shared_pre = jnp.concatenate(
        [grad_shared_act * s_up * shared_slope, grad_shared_act * shared_silu], axis=1
    ).astype(BF)
    grad_normed_shared = dotf("tf,df->td", grad_shared_pre, shared_gu)
    shared_part = dotf("tf,df->td", shared_act, shared_down)

    def by_expert(v):
        return v.reshape(n_dp, n_local, cap, v.shape[-1]).transpose(1, 0, 2, 3).reshape(
            n_local, n_dp * cap, v.shape[-1]
        )

    def by_source(v):
        return v.reshape(n_local, n_dp, cap, v.shape[-1]).transpose(1, 0, 2, 3).reshape(
            n_dp, n_local * cap, v.shape[-1]
        )

    sw = slot_weight.transpose(1, 0, 2).reshape(n_local, n_dp * cap, 1)
    q = by_expert(dotf("sct,std->scd", pick, g2_all))
    q = (q * sw).astype(BF)
    grad_act = dotf("erd,efd->erf", q, down_w)
    xr = by_expert(dotf("sct,std->scd", pick, all_rows).astype(BF))
    pre = dotf("erd,edf->erf", xr, gate_w)
    n_f = pre.shape[-1] // 2
    p_gate, p_up = pre[..., :n_f], pre[..., n_f:]
    act_silu, act_slope = silu_parts(p_gate)
    act = (act_silu * p_up).astype(BF)
    grad_pre = jnp.concatenate(
        [grad_act * p_up * act_slope, grad_act * act_silu], axis=-1
    ).astype(BF)
    back = by_source(dotf("erf,edf->erd", grad_pre, gate_w).astype(BF))
    dxn_part = dotf("sct,scd->std", pick, back)
    own = (jnp.arange(n_dp) == my_dp).astype(F32)[:, None, None]
    dxn_part = (dxn_part + own * grad_normed_shared[None]).astype(BF)
    grad_normed_two = lax.psum_scatter(
        dxn_part.reshape(n_dp * slots, width), everyone, scatter_dimension=0, tiled=True
    ).astype(F32)

    forth = by_source((dotf("erf,efd->erd", act, down_w) * sw).astype(BF))
    out_part = dotf("sct,scd->std", pick, forth)
    out_part = (out_part + own * shared_part[None]).astype(BF)
    ffn_out = lax.psum_scatter(
        out_part.reshape(n_dp * slots, width), everyone, scatter_dimension=0, tiled=True
    ).astype(F32)
    layer_out = lax.all_gather(
        (hidden_one + ffn_out).astype(BF), "tensor", axis=0, tiled=True
    )
    grad_exp_down = dotf("erf,erd->efd", act, q)
    grad_exp_gu = dotf("erd,erf->edf", xr, grad_pre).reshape(w_exp_gu.shape)
    grad_shared_down = dotf("td,tf->df", g2_low, shared_act)
    grad_shared_gu = dotf("td,tf->df", mine, grad_shared_pre)

    weighted_two = ln2_gain * grad_normed_two
    grad_ln2 = jnp.sum(grad_normed_two * hidden_one * scale_two, axis=0)
    g2_own = g2_piece.astype(F32)
    grad_one = (
        g2_own
        + scale_two * weighted_two
        - hidden_one * scale_two**3 * jnp.mean(weighted_two * hidden_one, axis=-1, keepdims=True)
    )
    dm = lax.all_gather(grad_one.astype(BF), "tensor", axis=0, tiled=True)
    grad_out_proj = dotf("td,tc->dc", dm, normed_mix)
    grad_normed_mix = dotf("td,dc->tc", dm, proj_out)
    weighted_mix = gnorm_gain * grad_normed_mix
    grad_gnorm = jnp.sum(grad_normed_mix * gated_mix * scale_mix, axis=0)
    product_sum = lax.psum(jnp.sum(weighted_mix * gated_mix, axis=-1), "tensor")[:, None]
    grad_gated = scale_mix * weighted_mix - gated_mix * scale_mix**3 * product_sum / full_inner
    (
        grad_zx,
        grad_bc,
        grad_dt_low,
        grad_conv_x,
        grad_conv_x_bias,
        grad_conv_bc,
        grad_conv_bc_bias,
        grad_dt_bias,
        grad_a_log,
        grad_d_skip,
    ) = mixer_back(grad_gated)
    bc_low = grad_bc.astype(BF)
    grad_first = jnp.concatenate([grad_zx, bc_low, grad_dt_low], axis=1)
    grad_input_part = dotf("tf,df->td", grad_first, first)
    grad_input_piece = lax.psum_scatter(
        grad_input_part.astype(BF), "tensor", scatter_dimension=0, tiled=True
    ).astype(F32)
    grad_first_w = dotf("td,tf->df", normed_one, grad_first).astype(BF)
    grad_second_w = jnp.concatenate(
        [grad_out_proj, grad_shared_gu, grad_shared_down], axis=1
    ).astype(BF)
    grad_second_w = lax.psum_scatter(grad_second_w, "dp", scatter_dimension=0, tiled=True)
    grad_first_w = lax.psum_scatter(grad_first_w, "dp", scatter_dimension=0, tiled=True)
    grad_bc_w = lax.psum(grad_first_w[:, 2 * inner : 2 * inner + 2 * state], "tensor")

    scale_piece = lax.dynamic_slice_in_dim(scale_one, my_t * piece, piece, axis=0)
    weighted_one = ln1_gain * grad_input_piece
    grad_ln1 = jnp.sum(grad_input_piece * x_piece * scale_piece, axis=0)
    grad_x = (
        grad_one
        + scale_piece * weighted_one
        - x_piece * scale_piece**3 * jnp.mean(weighted_one * x_piece, axis=-1, keepdims=True)
    )
    grad_x = lax.all_gather(grad_x.astype(BF), "tensor", axis=0, tiled=True).astype(F32)

    wide = jnp.concatenate(
        [grad_ln1, grad_ln2, grad_conv_bc.reshape(-1), grad_conv_bc_bias]
    )
    wide = lax.psum(wide, everyone)
    narrow = jnp.concatenate(
        [grad_conv_x.reshape(-1), grad_conv_x_bias, grad_gnorm, grad_dt_bias, grad_a_log, grad_d_skip]
    )
    narrow = lax.psum(narrow, "dp")
    taps = conv_x.shape[0]
    at = [0]

    def take(vector, *shape):
        size = 1
        for s in shape:
            size *= s
        part = lax.slice_in_dim(vector, at[0], at[0] + size).reshape(shape)
        at[0] += size
        return part

    o_ln1 = take(wide, width)
    o_ln2 = take(wide, width)
    o_conv_bc = take(wide, taps, 2 * state)
    o_conv_bc_bias = take(wide, 2 * state)
    at[0] = 0
    o_conv_x = take(narrow, taps, inner)
    o_conv_x_bias = take(narrow, inner)
    o_gnorm = take(narrow, inner)
    o_dt_bias = take(narrow, heads)
    o_a_log = take(narrow, heads)
    o_d_skip = take(narrow, heads)
    first_f = grad_first_w.astype(F32)
    second_f = grad_second_w.astype(F32)
    return (
        layer_out,
        grad_x,
        o_ln1,
        first_f[:, : 2 * inner].reshape(rows, 2, inner),
        grad_bc_w.astype(F32),
        first_f[:, 2 * inner + 2 * state :],
        o_conv_x,
        o_conv_x_bias,
        o_conv_bc,
        o_conv_bc_bias,
        o_dt_bias,
        o_a_log,
        o_d_skip,
        o_gnorm,
        second_f[:, :inner],
        o_ln2,
        second_f[:, inner : inner + 2 * n_sh].reshape(rows, 2, n_sh),
        second_f[:, inner + 2 * n_sh :],
        grad_exp_gu,
        grad_exp_down,
    )


def solution(mesh):
    return jax.shard_map(
        local,
        mesh=mesh,
        in_specs=(
            P("dp", None),
            P("dp"),
            P("dp", None),
            P("dp", None),
            P(),
            P("dp", None, "tensor"),
            P("dp", None),
            P("dp", "tensor"),
            P(None, "tensor"),
            P("tensor"),
            P(),
            P(),
            P("tensor"),
            P("tensor"),
            P("tensor"),
            P("tensor"),
            P("dp", "tensor"),
            P(),
            P("dp", None, "tensor"),
            P("dp", "tensor"),
            P("dp", None, None, "tensor"),
            P("dp", "tensor", None),
            P("dp", None),
        ),
        out_specs=(
            P("dp", None),
            P("dp", None),
            P(),
            P("dp", None, "tensor"),
            P("dp", None),
            P("dp", "tensor"),
            P(None, "tensor"),
            P("tensor"),
            P(),
            P(),
            P("tensor"),
            P("tensor"),
            P("tensor"),
            P("tensor"),
            P("dp", "tensor"),
            P(),
            P("dp", None, "tensor"),
            P("dp", "tensor"),
            P("dp", None, None, "tensor"),
            P("dp", "tensor", None),
        ),
        check_vma=False,
    )
```

```python
import functools

import jax
import jax.numpy as jnp
from jax import lax
from jax.experimental import pallas as pl
from jax.experimental.pallas import tpu as pltpu
from jax.sharding import PartitionSpec as P

BLOCK = 256


EPSILON = 1e-05
HIGHEST = lax.Precision.HIGHEST
BF = jnp.bfloat16
F32 = jnp.float32


def rms_scale(values):
    return lax.rsqrt(jnp.mean(values * values, axis=-1, keepdims=True) + EPSILON)


def silu_parts(values):
    sigmoid_val = jax.nn.sigmoid(values)
    return (values * sigmoid_val, sigmoid_val * (1.0 + values * (1.0 - sigmoid_val)))


def round_keep(values):
    return lax.optimization_barrier(values.astype(BF)).astype(F32)


def dotf(spec, a, b):
    return jnp.einsum(spec, a, b, preferred_element_type=F32)


def causal_conv(signal, kernel, offset):
    kernel_width = kernel.shape[0]
    seq_length = signal.shape[0]
    padded = jnp.concatenate(
        [jnp.zeros((kernel_width - 1, signal.shape[1]), signal.dtype), signal], axis=0
    )
    summed = offset[None, :] + kernel[0][None, :] * padded[0:seq_length]
    for tap_index in range(1, kernel_width):
        summed = summed + kernel[tap_index][None, :] * padded[tap_index : tap_index + seq_length]
    return summed


def ssd_scan(head_values, step_sizes, log_rates, b_rows, c_rows, skip_gain, block_rows):
    seq_length, n_heads, head_size = head_values.shape
    n_state = b_rows.shape[1]
    n_blocks = seq_length // block_rows
    decay_rates = -jnp.exp(log_rates)[None, :] * step_sizes
    scaled = (head_values * step_sizes[:, :, None]).reshape(
        n_blocks, block_rows, n_heads, head_size
    )
    cumulative = jnp.cumsum(decay_rates.reshape(n_blocks, block_rows, n_heads), axis=1)
    b_block = b_rows.reshape(n_blocks, block_rows, n_state)
    c_block = c_rows.reshape(n_blocks, block_rows, n_state)
    positions = jnp.arange(block_rows)
    causal = (positions[:, None] >= positions[None, :])[None, :, :, None]
    differences = cumulative[:, :, None, :] - cumulative[:, None, :, :]
    decay_mask = jnp.where(causal, jnp.exp(jnp.where(causal, differences, 0.0)), 0.0)
    intersection = jnp.einsum("kin,kjn->kij", c_block, b_block, precision=HIGHEST)
    within = jnp.einsum("kij,kijh,kjhp->kihp", intersection, decay_mask, scaled, precision=HIGHEST)
    block_end = cumulative[:, -1, :]
    to_end = jnp.exp(block_end[:, None, :] - cumulative)
    states = jnp.einsum("kjn,kjh,kjhp->khnp", b_block, to_end, scaled, precision=HIGHEST)

    def carry_state(previous, inputs):
        block_decay, block_state = inputs
        return (block_decay[:, None, None] * previous + block_state, previous)

    final_state, entering = lax.scan(
        carry_state,
        jnp.zeros((n_heads, n_state, head_size), head_values.dtype),
        (jnp.exp(block_end), states),
    )
    across = jnp.einsum(
        "kin,khnp,kih->kihp", c_block, entering, jnp.exp(cumulative), precision=HIGHEST
    )
    return (within + across).reshape(seq_length, n_heads, head_size) + skip_gain[
        None, :, None
    ] * head_values


def mixer_forward(
    zx, bc_proj, dt_proj, conv_x, conv_x_bias, conv_bc, conv_bc_bias, dt_bias, a_log, d_skip
):
    slots = zx.shape[0]
    inner = conv_x.shape[1]
    heads = dt_bias.shape[0]
    state = conv_bc.shape[1] // 2

    def conv_block(x_part, bc_part, kernel_x, offset_x, kernel_bc, offset_bc):
        return (
            jax.nn.silu(causal_conv(x_part, kernel_x, offset_x)),
            jax.nn.silu(causal_conv(bc_part, kernel_bc, offset_bc)),
        )

    (conv_values, conv_bc_values), conv_back = jax.vjp(
        conv_block, zx[:, inner:], bc_proj, conv_x, conv_x_bias, conv_bc, conv_bc_bias
    )
    head_input = round_keep(conv_values)
    bc_input = round_keep(conv_bc_values)

    def scan_block(head_flat, b_rows, c_rows, dt_part, z_part, dt_offset, log_rates, skip_gain):
        step_sizes = jax.nn.softplus(dt_part + dt_offset[None, :])
        output = ssd_scan(
            head_flat.reshape(slots, heads, inner // heads),
            step_sizes,
            log_rates,
            b_rows,
            c_rows,
            skip_gain,
            BLOCK,
        )
        return output.reshape(slots, inner) * jax.nn.silu(z_part)

    gated_mix, scan_back = jax.vjp(
        scan_block,
        head_input,
        bc_input[:, :state],
        bc_input[:, state:],
        dt_proj,
        zx[:, :inner],
        dt_bias,
        a_log,
        d_skip,
    )

    def mixer_back(grad_gated):
        g_head, g_b, g_c, g_dt, g_z, g_dt_bias, g_a_log, g_d_skip = scan_back(grad_gated)
        g_xs, g_bc, g_cx, g_cxb, g_cbc, g_cbcb = conv_back(
            (g_head, jnp.concatenate([g_b, g_c], axis=1))
        )
        g_zx = jnp.concatenate([g_z, g_xs], axis=1).astype(BF)
        return (
            g_zx, g_bc, g_dt.astype(BF), g_cx, g_cxb, g_cbc, g_cbcb, g_dt_bias, g_a_log, g_d_skip
        )

    return gated_mix, mixer_back


MESH = pl.DeviceIdType.MESH


def place():
    d = lax.axis_index("dp")
    t = lax.axis_index("tensor")
    return d // 2, d % 2, t // 2, t % 2


def device(hi, lo, th, tl):
    return (hi * 2 + lo, th * 2 + tl)


def greet(n_hi):
    hi, lo, th, tl = place()
    barrier = pltpu.get_barrier_semaphore()
    others = [device(lax.rem(hi + k, n_hi), lo, th, tl) for k in range(1, n_hi)]
    others += [device(hi, 1 - lo, th, tl), device(hi, lo, 1 - th, tl), device(hi, lo, th, 1 - tl)]
    for other in others:
        pl.semaphore_signal(barrier, inc=1, device_id=other, device_id_type=MESH)
    pl.semaphore_wait(barrier, len(others))


def gather_kernel(n_hi, x_ref, o_ref, own_sem, send_sem, recv_sem):
    hi, lo, th, tl = place()
    rows = x_ref.shape[0]
    half = rows // 2
    greet(n_hi)
    own_block = (hi * 2 + lo) * 4 + th * 2 + tl
    own = pltpu.make_async_copy(x_ref, o_ref.at[pl.ds(own_block * rows, rows)], own_sem)
    own.start()

    def slot(k, f, s, c):
        return ((c * 2 + s) * 2 + f) * n_hi + k

    def where(h, k, f, s, c):
        kk = lax.rem(hi + k, n_hi)
        l = 1 - lo if (f if h == 0 else s) else lo
        y = 1 - th if (s if h == 0 else f) else th
        z = 1 - tl if c else tl
        return ((kk * 2 + l) * 4 + y * 2 + z) * rows + h * half

    sends = []

    def push(h, k, f, s, c, step):
        at = where(h, k, f, s, c)
        if k == 0 and not (f or s or c):
            src = x_ref.at[pl.ds(h * half, half)]
        else:
            src = o_ref.at[pl.ds(at, half)]
        if step == "c":
            to, rk, rf, rs, rc = device(hi, lo, th, 1 - tl), k, f, s, 1
        elif step == "s":
            to = device(hi, lo, 1 - th, tl) if h == 0 else device(hi, 1 - lo, th, tl)
            rk, rf, rs, rc = k, f, 1, 0
        elif step == "f":
            to = device(hi, 1 - lo, th, tl) if h == 0 else device(hi, lo, 1 - th, tl)
            rk, rf, rs, rc = k, 1, 0, 0
        else:
            to = device(lax.rem(hi + step, n_hi), lo, th, tl)
            rk, rf, rs, rc = n_hi - step, 0, 0, 0
        r = slot(rk, rf, rs, rc)
        copy = pltpu.make_async_remote_copy(
            src_ref=src,
            dst_ref=o_ref.at[pl.ds(at, half)],
            send_sem=send_sem.at[h, r],
            recv_sem=recv_sem.at[h, r],
            device_id=to,
            device_id_type=MESH,
        )
        copy.start()
        sends.append(copy)

    def arrive(h, k, f, s, c):
        at = where(h, k, f, s, c)
        view = o_ref.at[pl.ds(at, half)]
        r = slot(k, f, s, c)
        pltpu.make_async_remote_copy(
            src_ref=view,
            dst_ref=view,
            send_sem=send_sem.at[h, r],
            recv_sem=recv_sem.at[h, r],
            device_id=device(hi, lo, th, 1 - tl),
            device_id_type=MESH,
        ).wait_recv()

    for k in range(1, n_hi):
        for h in range(2):
            push(h, 0, 0, 0, 0, k)
    for k in range(n_hi):
        for h in range(2):
            if k:
                arrive(h, k, 0, 0, 0)
            for step in ("f", "s", "c"):
                push(h, k, 0, 0, 0, step)
        for h in range(2):
            arrive(h, k, 1, 0, 0)
            for step in ("s", "c"):
                push(h, k, 1, 0, 0, step)
    for k in range(n_hi):
        for f in range(2):
            for h in range(2):
                arrive(h, k, f, 1, 0)
                push(h, k, f, 1, 0, "c")
    for k in range(n_hi):
        for f in range(2):
            for s in range(2):
                for h in range(2):
                    arrive(h, k, f, s, 1)
    own.wait()
    for copy in sends:
        copy.wait_send()


def gather_rows(x, n_dp, collective_id):
    rows, width = x.shape
    n_hi = n_dp // 2
    return pl.pallas_call(
        functools.partial(gather_kernel, n_hi),
        out_shape=jax.ShapeDtypeStruct((n_dp * 4 * rows, width), x.dtype),
        in_specs=[pl.BlockSpec(memory_space=pl.ANY)],
        out_specs=pl.BlockSpec(memory_space=pl.ANY),
        scratch_shapes=[
            pltpu.SemaphoreType.DMA,
            pltpu.SemaphoreType.DMA((2, 8 * n_hi)),
            pltpu.SemaphoreType.DMA((2, 8 * n_hi)),
        ],
        compiler_params=pltpu.CompilerParams(collective_id=collective_id, has_side_effects=True),
        name="gather_rows",
    )(x)


def scatter_kernel(
    n_hi, depth, p_ref, o_ref, stage, from_c, from_f, from_s, from_h,
    stage_sem, send_c, recv_c, send_f, recv_f, send_s, recv_s, send_h, recv_h,
):
    hi, lo, th, tl = place()
    rows = o_ref.shape[0]
    half = rows // 2
    greet(n_hi)

    def where(h, k, f, s, c):
        kk = lax.rem(hi + k, n_hi)
        l = 1 - lo if (f if h == 1 else s) else lo
        y = 1 - th if (s if h == 1 else f) else th
        z = 1 - tl if c else tl
        return ((kk * 2 + l) * 4 + y * 2 + z) * rows + h * half

    order = [(f, s, k, h) for f, s in ((1, 1), (1, 0), (0, 1), (0, 0)) for k in
             list(range(1, n_hi)) + [0] for h in range(2)]

    def slot(f, s, k):
        return (f * 2 + s) * n_hi + k

    def first(h):
        return device(hi, lo, 1 - th, tl) if h == 0 else device(hi, 1 - lo, th, tl)

    def second(h):
        return device(hi, 1 - lo, th, tl) if h == 0 else device(hi, lo, 1 - th, tl)

    sends = []

    def push(src, dst, ssem, rsem, to):
        copy = pltpu.make_async_remote_copy(
            src_ref=src, dst_ref=dst, send_sem=ssem, recv_sem=rsem,
            device_id=to, device_id_type=MESH,
        )
        copy.start()
        sends.append(copy)

    def arrive(dst, ssem, rsem):
        pltpu.make_async_remote_copy(
            src_ref=dst, dst_ref=dst, send_sem=ssem, recv_sem=rsem,
            device_id=device(hi, lo, th, 1 - tl), device_id_type=MESH,
        ).wait_recv()

    for f, s, k, h in order:
        n = slot(f, s, k)
        push(
            p_ref.at[pl.ds(where(h, k, f, s, 1), half)],
            from_c.at[h, n],
            send_c.at[h, n],
            recv_c.at[h, n],
            device(hi, lo, th, 1 - tl),
        )

    def load(i):
        f, s, k, h = order[i]
        return pltpu.make_async_copy(
            p_ref.at[pl.ds(where(h, k, f, s, 0), half)], stage.at[i % depth], stage_sem.at[i % depth]
        )

    for i in range(depth - 1):
        load(i).start()
    for i, (f, s, k, h) in enumerate(order):
        if i + depth - 1 < len(order):
            load(i + depth - 1).start()
        load(i).wait()
        n = slot(f, s, k)
        arrive(from_c.at[h, n], send_c.at[h, n], recv_c.at[h, n])
        total = stage[i % depth].astype(F32) + from_c[h, n].astype(F32)
        if f == 0:
            m = s * n_hi + k
            arrive(from_f.at[h, m], send_f.at[h, m], recv_f.at[h, m])
            total = total + from_f[h, m].astype(F32)
        if f == 0 and s == 0:
            arrive(from_s.at[h, k], send_s.at[h, k], recv_s.at[h, k])
            total = total + from_s[h, k].astype(F32)
        if f == 0 and s == 0 and k == 0:
            for j in range(1, n_hi):
                arrive(from_h.at[h, j - 1], send_h.at[h, j - 1], recv_h.at[h, j - 1])
                total = total + from_h[h, j - 1].astype(F32)
            o_ref[pl.ds(h * half, half), :] = total.astype(o_ref.dtype)
            continue
        from_c[h, n] = total.astype(from_c.dtype)
        src = from_c.at[h, n]
        if f == 1:
            m = s * n_hi + k
            push(src, from_f.at[h, m], send_f.at[h, m], recv_f.at[h, m], first(h))
        elif s == 1:
            push(src, from_s.at[h, k], send_s.at[h, k], recv_s.at[h, k], second(h))
        else:
            j = n_hi - k
            push(
                src, from_h.at[h, j - 1], send_h.at[h, j - 1], recv_h.at[h, j - 1],
                device(lax.rem(hi + k, n_hi), lo, th, tl),
            )
    for copy in sends:
        copy.wait_send()


def scatter_rows(p, n_dp, collective_id):
    width = p.shape[1]
    rows = p.shape[0] // (n_dp * 4)
    half = rows // 2
    n_hi = n_dp // 2
    depth = 4
    dma = pltpu.SemaphoreType.DMA
    return pl.pallas_call(
        functools.partial(scatter_kernel, n_hi, depth),
        out_shape=jax.ShapeDtypeStruct((rows, width), F32),
        in_specs=[pl.BlockSpec(memory_space=pl.ANY)],
        out_specs=pl.BlockSpec(memory_space=pltpu.VMEM),
        scratch_shapes=[
            pltpu.VMEM((depth, half, width), p.dtype),
            pltpu.VMEM((2, 4 * n_hi, half, width), p.dtype),
            pltpu.VMEM((2, 2 * n_hi, half, width), p.dtype),
            pltpu.VMEM((2, n_hi, half, width), p.dtype),
            pltpu.VMEM((2, n_hi - 1, half, width), p.dtype),
            dma((depth,)),
            dma((2, 4 * n_hi)),
            dma((2, 4 * n_hi)),
            dma((2, 2 * n_hi)),
            dma((2, 2 * n_hi)),
            dma((2, n_hi)),
            dma((2, n_hi)),
            dma((2, n_hi - 1)),
            dma((2, n_hi - 1)),
        ],
        compiler_params=pltpu.CompilerParams(
            collective_id=collective_id, has_side_effects=True, vmem_limit_bytes=60 << 20
        ),
        name="scatter_rows",
    )(p)


def small_kernel(n_hi, wide, x_ref, o_ref, got_f, got_h, got_t, send_sem, recv_sem, send_h, recv_h):
    hi, lo, th, tl = place()
    greet(n_hi)

    def trade(src, dst, i, to):
        copy = pltpu.make_async_remote_copy(
            src_ref=src, dst_ref=dst, send_sem=send_sem.at[i], recv_sem=recv_sem.at[i],
            device_id=to, device_id_type=MESH,
        )
        copy.start()
        copy.wait()

    trade(x_ref, got_f, 0, device(hi, 1 - lo, th, tl))
    got_h[hi] = x_ref[...] + got_f[...]
    copies = []
    for k in range(1, n_hi):
        copy = pltpu.make_async_remote_copy(
            src_ref=got_h.at[hi], dst_ref=got_h.at[hi],
            send_sem=send_h.at[k - 1], recv_sem=recv_h.at[k - 1],
            device_id=device(lax.rem(hi + k, n_hi), lo, th, tl), device_id_type=MESH,
        )
        copy.start()
        copies.append(copy)
    for copy in copies:
        copy.wait()
    total = got_h[0]
    for k in range(1, n_hi):
        total = total + got_h[k]
    o_ref[...] = total
    for i, to in enumerate((device(hi, lo, th, 1 - tl), device(hi, lo, 1 - th, tl))):
        trade(o_ref.at[pl.ds(0, wide)], got_t.at[i], i + 1, to)
        o_ref[pl.ds(0, wide), :] = o_ref[pl.ds(0, wide), :] + got_t[i]


def sum_small(x, wide, n_dp, collective_id):
    n_hi = n_dp // 2
    dma = pltpu.SemaphoreType.DMA
    vmem = pl.BlockSpec(memory_space=pltpu.VMEM)
    return pl.pallas_call(
        functools.partial(small_kernel, n_hi, wide),
        out_shape=jax.ShapeDtypeStruct(x.shape, F32),
        in_specs=[vmem],
        out_specs=vmem,
        scratch_shapes=[
            pltpu.VMEM(x.shape, F32),
            pltpu.VMEM((n_hi,) + x.shape, F32),
            pltpu.VMEM((2, wide, x.shape[1]), F32),
            dma((3,)),
            dma((3,)),
            dma((n_hi - 1,)),
            dma((n_hi - 1,)),
        ],
        compiler_params=pltpu.CompilerParams(collective_id=collective_id, has_side_effects=True),
        name="sum_small",
    )(x)


def local(
    x_in,
    lengths,
    routes,
    route_w,
    ln1_gain,
    w_zx,
    w_bc,
    w_dt,
    conv_x,
    conv_x_bias,
    conv_bc,
    conv_bc_bias,
    dt_bias,
    a_log,
    d_skip,
    gnorm_gain,
    w_out,
    ln2_gain,
    w_shared_gu,
    w_shared_down,
    w_exp_gu,
    w_exp_down,
    cotangent,
):
    slots, width = x_in.shape
    n_dp = lax.axis_size("dp")
    n_t = lax.axis_size("tensor")
    my_t = lax.axis_index("tensor")
    my_dp = lax.axis_index("dp")
    piece = slots // n_t
    n_local = w_exp_gu.shape[0]
    n_experts = n_dp * n_local
    cap = slots * routes.shape[1] * 4 // (3 * n_experts)
    if cap > slots:
        cap = slots
    heads = dt_bias.shape[0]
    inner = conv_x.shape[1]
    head_size = inner // heads
    state = conv_bc.shape[1] // 2
    full_inner = inner * n_t
    rows = w_zx.shape[0]
    n_sh = w_shared_gu.shape[2]

    first = jnp.concatenate(
        [w_zx.reshape(rows, 2 * inner), w_bc, w_dt], axis=1
    ).astype(BF)
    second = jnp.concatenate(
        [w_out, w_shared_gu.reshape(rows, 2 * n_sh), w_shared_down], axis=1
    ).astype(BF)
    first = lax.all_gather(first, "dp", axis=0, tiled=True)
    second = lax.all_gather(second, "dp", axis=0, tiled=True)
    proj_zx = first[:, : 2 * inner]
    proj_bc = first[:, 2 * inner : 2 * inner + 2 * state]
    proj_dt = first[:, 2 * inner + 2 * state :]
    proj_out = second[:, :inner]
    shared_gu = second[:, inner : inner + 2 * n_sh]
    shared_down = second[:, inner + 2 * n_sh :]

    live = (jnp.arange(slots, dtype=jnp.int32) < lengths[0]).astype(F32)
    g2 = cotangent.astype(F32) * live[:, None]
    g2_low = g2.astype(BF)
    expert_range = jnp.arange(n_experts, dtype=jnp.int32)
    chosen = routes[:, :, None] == expert_range[None, None, :]
    weights = jnp.sum(jnp.where(chosen, route_w[:, :, None], 0.0), axis=1)
    weights = lax.all_gather(weights, "dp", axis=0, tiled=True)
    weights = lax.dynamic_slice_in_dim(weights, my_dp * n_local, n_local, axis=1)
    weights = weights.reshape(n_dp, slots, n_local)
    member = (weights > 0.0).astype(BF)
    before = (
        jnp.arange(slots)[:, None] > jnp.arange(slots)[None, :]
    ).astype(BF)
    position = dotf("ut,ste->sue", before, member).astype(jnp.int32)
    position = jnp.where(weights > 0.0, position, -1)
    pick = (
        position.transpose(0, 2, 1)[:, :, None, :]
        == jnp.arange(cap, dtype=jnp.int32)[None, None, :, None]
    )
    slot_weight = jnp.sum(
        jnp.where(pick, weights.transpose(0, 2, 1)[:, :, None, :], 0.0), axis=-1
    )
    pick = pick.astype(BF).reshape(n_dp, n_local * cap, slots)

    g2_piece = lax.dynamic_slice_in_dim(g2_low, my_t * piece, piece, axis=0)
    g2_all = gather_rows(g2_piece, n_dp, 1).reshape(n_dp, slots, width)

    gate_w = w_exp_gu.astype(BF).reshape(n_local, width, -1)
    down_w = w_exp_down.astype(BF)

    x_float = x_in.astype(F32)
    scale_one = rms_scale(x_float)
    normed_one = (x_float * scale_one * ln1_gain).astype(BF)
    zx = dotf("td,df->tf", normed_one, proj_zx)
    bc_proj = dotf("td,df->tf", normed_one, proj_bc)
    dt_proj = dotf("td,df->tf", normed_one, proj_dt)

    gated_mix, mixer_back = mixer_forward(
        zx, bc_proj, dt_proj, conv_x, conv_x_bias, conv_bc, conv_bc_bias, dt_bias, a_log, d_skip
    )
    squares = lax.psum(jnp.sum(gated_mix * gated_mix, axis=-1), "tensor")
    scale_mix = lax.rsqrt(squares / full_inner + EPSILON)[:, None]
    normed_mix = (gated_mix * scale_mix * gnorm_gain).astype(BF)
    mixer_part = dotf("tc,dc->td", normed_mix, proj_out).astype(BF)
    mixer_out = lax.psum_scatter(
        mixer_part, "tensor", scatter_dimension=0, tiled=True
    ).astype(F32)
    x_piece = lax.dynamic_slice_in_dim(x_float, my_t * piece, piece, axis=0)
    hidden_one = x_piece + mixer_out
    scale_two = rms_scale(hidden_one)
    normed_two = (hidden_one * scale_two * ln2_gain).astype(BF)
    all_rows = gather_rows(normed_two, n_dp, 2)
    mine = lax.dynamic_slice_in_dim(all_rows, my_dp * slots, slots, axis=0)
    all_rows = all_rows.reshape(n_dp, slots, width)

    shared_pre = dotf("td,df->tf", mine, shared_gu)
    s_gate, s_up = shared_pre[:, :n_sh], shared_pre[:, n_sh:]
    shared_silu, shared_slope = silu_parts(s_gate)
    shared_act = (shared_silu * s_up).astype(BF)
    grad_shared_act = dotf("td,df->tf", g2_low, shared_down)
    grad_shared_pre = jnp.concatenate(
        [grad_shared_act * s_up * shared_slope, grad_shared_act * shared_silu], axis=1
    ).astype(BF)
    grad_normed_shared = dotf("tf,df->td", grad_shared_pre, shared_gu)
    shared_part = dotf("tf,df->td", shared_act, shared_down)

    def by_expert(v):
        return v.reshape(n_dp, n_local, cap, v.shape[-1]).transpose(1, 0, 2, 3).reshape(
            n_local, n_dp * cap, v.shape[-1]
        )

    def by_source(v):
        return v.reshape(n_local, n_dp, cap, v.shape[-1]).transpose(1, 0, 2, 3).reshape(
            n_dp, n_local * cap, v.shape[-1]
        )

    sw = slot_weight.transpose(1, 0, 2).reshape(n_local, n_dp * cap, 1)
    q = by_expert(dotf("sct,std->scd", pick, g2_all))
    q = (q * sw).astype(BF)
    grad_act = dotf("erd,efd->erf", q, down_w)
    xr = by_expert(dotf("sct,std->scd", pick, all_rows).astype(BF))
    pre = dotf("erd,edf->erf", xr, gate_w)
    n_f = pre.shape[-1] // 2
    p_gate, p_up = pre[..., :n_f], pre[..., n_f:]
    act_silu, act_slope = silu_parts(p_gate)
    act = (act_silu * p_up).astype(BF)
    grad_pre = jnp.concatenate(
        [grad_act * p_up * act_slope, grad_act * act_silu], axis=-1
    ).astype(BF)
    back = by_source(dotf("erf,edf->erd", grad_pre, gate_w).astype(BF))
    dxn_part = dotf("sct,scd->std", pick, back)
    own = (jnp.arange(n_dp) == my_dp).astype(F32)[:, None, None]
    dxn_part = (dxn_part + own * grad_normed_shared[None]).astype(BF)
    grad_normed_two = scatter_rows(dxn_part.reshape(n_dp * slots, width), n_dp, 3)

    forth = by_source((dotf("erf,efd->erd", act, down_w) * sw).astype(BF))
    out_part = dotf("sct,scd->std", pick, forth)
    out_part = (out_part + own * shared_part[None]).astype(BF)
    ffn_out = scatter_rows(out_part.reshape(n_dp * slots, width), n_dp, 4)
    layer_out = lax.all_gather(
        (hidden_one + ffn_out).astype(BF), "tensor", axis=0, tiled=True
    )
    grad_exp_down = dotf("erf,erd->efd", act, q)
    grad_exp_gu = dotf("erd,erf->edf", xr, grad_pre).reshape(w_exp_gu.shape)
    grad_shared_down = dotf("td,tf->df", g2_low, shared_act)
    grad_shared_gu = dotf("td,tf->df", mine, grad_shared_pre)

    weighted_two = ln2_gain * grad_normed_two
    grad_ln2 = jnp.sum(grad_normed_two * hidden_one * scale_two, axis=0)
    g2_own = g2_piece.astype(F32)
    grad_one = (
        g2_own
        + scale_two * weighted_two
        - hidden_one * scale_two**3 * jnp.mean(weighted_two * hidden_one, axis=-1, keepdims=True)
    )
    dm = lax.all_gather(grad_one.astype(BF), "tensor", axis=0, tiled=True)
    grad_out_proj = dotf("td,tc->dc", dm, normed_mix)
    grad_normed_mix = dotf("td,dc->tc", dm, proj_out)
    weighted_mix = gnorm_gain * grad_normed_mix
    grad_gnorm = jnp.sum(grad_normed_mix * gated_mix * scale_mix, axis=0)
    product_sum = lax.psum(jnp.sum(weighted_mix * gated_mix, axis=-1), "tensor")[:, None]
    grad_gated = scale_mix * weighted_mix - gated_mix * scale_mix**3 * product_sum / full_inner
    (
        grad_zx,
        grad_bc,
        grad_dt_low,
        grad_conv_x,
        grad_conv_x_bias,
        grad_conv_bc,
        grad_conv_bc_bias,
        grad_dt_bias,
        grad_a_log,
        grad_d_skip,
    ) = mixer_back(grad_gated)
    bc_low = grad_bc.astype(BF)
    grad_first = jnp.concatenate([grad_zx, bc_low, grad_dt_low], axis=1)
    grad_input_part = dotf("tf,df->td", grad_first, first)
    grad_input_piece = lax.psum_scatter(
        grad_input_part.astype(BF), "tensor", scatter_dimension=0, tiled=True
    ).astype(F32)
    grad_first_w = dotf("td,tf->df", normed_one, grad_first).astype(BF)
    grad_second_w = jnp.concatenate(
        [grad_out_proj, grad_shared_gu, grad_shared_down], axis=1
    ).astype(BF)
    grad_second_w = lax.psum_scatter(grad_second_w, "dp", scatter_dimension=0, tiled=True)
    grad_first_w = lax.psum_scatter(grad_first_w, "dp", scatter_dimension=0, tiled=True)
    grad_bc_w = lax.psum(grad_first_w[:, 2 * inner : 2 * inner + 2 * state], "tensor")

    scale_piece = lax.dynamic_slice_in_dim(scale_one, my_t * piece, piece, axis=0)
    weighted_one = ln1_gain * grad_input_piece
    grad_ln1 = jnp.sum(grad_input_piece * x_piece * scale_piece, axis=0)
    grad_x = (
        grad_one
        + scale_piece * weighted_one
        - x_piece * scale_piece**3 * jnp.mean(weighted_one * x_piece, axis=-1, keepdims=True)
    )
    grad_x = lax.all_gather(grad_x.astype(BF), "tensor", axis=0, tiled=True).astype(F32)

    wide = jnp.concatenate(
        [grad_ln1, grad_ln2, grad_conv_bc.reshape(-1), grad_conv_bc_bias]
    )
    narrow = jnp.concatenate(
        [grad_conv_x.reshape(-1), grad_conv_x_bias, grad_gnorm, grad_dt_bias, grad_a_log, grad_d_skip]
    )

    def lanes(vector):
        return jnp.pad(vector, (0, -vector.shape[0] % 1024)).reshape(-1, 128)

    wide = lanes(wide)
    n_wide = wide.shape[0]
    sums = sum_small(jnp.concatenate([wide, lanes(narrow)], axis=0), n_wide, n_dp, 5)
    wide, narrow = sums[:n_wide].reshape(-1), sums[n_wide:].reshape(-1)
    taps = conv_x.shape[0]
    at = [0]

    def take(vector, *shape):
        size = 1
        for s in shape:
            size *= s
        part = lax.slice_in_dim(vector, at[0], at[0] + size).reshape(shape)
        at[0] += size
        return part

    o_ln1 = take(wide, width)
    o_ln2 = take(wide, width)
    o_conv_bc = take(wide, taps, 2 * state)
    o_conv_bc_bias = take(wide, 2 * state)
    at[0] = 0
    o_conv_x = take(narrow, taps, inner)
    o_conv_x_bias = take(narrow, inner)
    o_gnorm = take(narrow, inner)
    o_dt_bias = take(narrow, heads)
    o_a_log = take(narrow, heads)
    o_d_skip = take(narrow, heads)
    first_f = grad_first_w.astype(F32)
    second_f = grad_second_w.astype(F32)
    return (
        layer_out,
        grad_x,
        o_ln1,
        first_f[:, : 2 * inner].reshape(rows, 2, inner),
        grad_bc_w.astype(F32),
        first_f[:, 2 * inner + 2 * state :],
        o_conv_x,
        o_conv_x_bias,
        o_conv_bc,
        o_conv_bc_bias,
        o_dt_bias,
        o_a_log,
        o_d_skip,
        o_gnorm,
        second_f[:, :inner],
        o_ln2,
        second_f[:, inner : inner + 2 * n_sh].reshape(rows, 2, n_sh),
        second_f[:, inner + 2 * n_sh :],
        grad_exp_gu,
        grad_exp_down,
    )


def solution(mesh):
    return jax.shard_map(
        local,
        mesh=mesh,
        in_specs=(
            P("dp", None),
            P("dp"),
            P("dp", None),
            P("dp", None),
            P(),
            P("dp", None, "tensor"),
            P("dp", None),
            P("dp", "tensor"),
            P(None, "tensor"),
            P("tensor"),
            P(),
            P(),
            P("tensor"),
            P("tensor"),
            P("tensor"),
            P("tensor"),
            P("dp", "tensor"),
            P(),
            P("dp", None, "tensor"),
            P("dp", "tensor"),
            P("dp", None, None, "tensor"),
            P("dp", "tensor", None),
            P("dp", None),
        ),
        out_specs=(
            P("dp", None),
            P("dp", None),
            P(),
            P("dp", None, "tensor"),
            P("dp", None),
            P("dp", "tensor"),
            P(None, "tensor"),
            P("tensor"),
            P(),
            P(),
            P("tensor"),
            P("tensor"),
            P("tensor"),
            P("tensor"),
            P("dp", "tensor"),
            P(),
            P("dp", None, "tensor"),
            P("dp", "tensor"),
            P("dp", None, None, "tensor"),
            P("dp", "tensor", None),
        ),
        check_vma=False,
    )
```

```python
import functools

import jax
import jax.numpy as jnp
from jax import lax
from jax.experimental import pallas as pl
from jax.experimental.pallas import tpu as pltpu
from jax.sharding import PartitionSpec as P

BLOCK = 256


EPSILON = 1e-05
HIGHEST = lax.Precision.HIGHEST
BF = jnp.bfloat16
F32 = jnp.float32


def rms_scale(values):
    return lax.rsqrt(jnp.mean(values * values, axis=-1, keepdims=True) + EPSILON)


def silu_parts(values):
    sigmoid_val = jax.nn.sigmoid(values)
    return (values * sigmoid_val, sigmoid_val * (1.0 + values * (1.0 - sigmoid_val)))


def round_keep(values):
    return lax.optimization_barrier(values.astype(BF)).astype(F32)


def dotf(spec, a, b):
    return jnp.einsum(spec, a, b, preferred_element_type=F32)


def causal_conv(signal, kernel, offset):
    kernel_width = kernel.shape[0]
    seq_length = signal.shape[0]
    padded = jnp.concatenate(
        [jnp.zeros((kernel_width - 1, signal.shape[1]), signal.dtype), signal], axis=0
    )
    summed = offset[None, :] + kernel[0][None, :] * padded[0:seq_length]
    for tap_index in range(1, kernel_width):
        summed = summed + kernel[tap_index][None, :] * padded[tap_index : tap_index + seq_length]
    return summed


def ssd_scan(head_values, step_sizes, log_rates, b_rows, c_rows, skip_gain, block_rows):
    seq_length, n_heads, head_size = head_values.shape
    n_state = b_rows.shape[1]
    n_blocks = seq_length // block_rows
    decay_rates = -jnp.exp(log_rates)[None, :] * step_sizes
    scaled = (head_values * step_sizes[:, :, None]).reshape(
        n_blocks, block_rows, n_heads, head_size
    )
    cumulative = jnp.cumsum(decay_rates.reshape(n_blocks, block_rows, n_heads), axis=1)
    b_block = b_rows.reshape(n_blocks, block_rows, n_state)
    c_block = c_rows.reshape(n_blocks, block_rows, n_state)
    positions = jnp.arange(block_rows)
    causal = (positions[:, None] >= positions[None, :])[None, :, :, None]
    differences = cumulative[:, :, None, :] - cumulative[:, None, :, :]
    decay_mask = jnp.where(causal, jnp.exp(jnp.where(causal, differences, 0.0)), 0.0)
    intersection = jnp.einsum("kin,kjn->kij", c_block, b_block, precision=HIGHEST)
    within = jnp.einsum("kij,kijh,kjhp->kihp", intersection, decay_mask, scaled, precision=HIGHEST)
    block_end = cumulative[:, -1, :]
    to_end = jnp.exp(block_end[:, None, :] - cumulative)
    states = jnp.einsum("kjn,kjh,kjhp->khnp", b_block, to_end, scaled, precision=HIGHEST)

    def carry_state(previous, inputs):
        block_decay, block_state = inputs
        return (block_decay[:, None, None] * previous + block_state, previous)

    final_state, entering = lax.scan(
        carry_state,
        jnp.zeros((n_heads, n_state, head_size), head_values.dtype),
        (jnp.exp(block_end), states),
    )
    across = jnp.einsum(
        "kin,khnp,kih->kihp", c_block, entering, jnp.exp(cumulative), precision=HIGHEST
    )
    return (within + across).reshape(seq_length, n_heads, head_size) + skip_gain[
        None, :, None
    ] * head_values


def mixer_forward(
    zx, bc_proj, dt_proj, conv_x, conv_x_bias, conv_bc, conv_bc_bias, dt_bias, a_log, d_skip
):
    slots = zx.shape[0]
    inner = conv_x.shape[1]
    heads = dt_bias.shape[0]
    state = conv_bc.shape[1] // 2

    def conv_block(x_part, bc_part, kernel_x, offset_x, kernel_bc, offset_bc):
        return (
            jax.nn.silu(causal_conv(x_part, kernel_x, offset_x)),
            jax.nn.silu(causal_conv(bc_part, kernel_bc, offset_bc)),
        )

    (conv_values, conv_bc_values), conv_back = jax.vjp(
        conv_block, zx[:, inner:], bc_proj, conv_x, conv_x_bias, conv_bc, conv_bc_bias
    )
    head_input = round_keep(conv_values)
    bc_input = round_keep(conv_bc_values)

    def scan_block(head_flat, b_rows, c_rows, dt_part, z_part, dt_offset, log_rates, skip_gain):
        step_sizes = jax.nn.softplus(dt_part + dt_offset[None, :])
        output = ssd_scan(
            head_flat.reshape(slots, heads, inner // heads),
            step_sizes,
            log_rates,
            b_rows,
            c_rows,
            skip_gain,
            BLOCK,
        )
        return output.reshape(slots, inner) * jax.nn.silu(z_part)

    gated_mix, scan_back = jax.vjp(
        scan_block,
        head_input,
        bc_input[:, :state],
        bc_input[:, state:],
        dt_proj,
        zx[:, :inner],
        dt_bias,
        a_log,
        d_skip,
    )

    def mixer_back(grad_gated):
        g_head, g_b, g_c, g_dt, g_z, g_dt_bias, g_a_log, g_d_skip = scan_back(grad_gated)
        g_xs, g_bc, g_cx, g_cxb, g_cbc, g_cbcb = conv_back(
            (g_head, jnp.concatenate([g_b, g_c], axis=1))
        )
        g_zx = jnp.concatenate([g_z, g_xs], axis=1).astype(BF)
        return (
            g_zx, g_bc, g_dt.astype(BF), g_cx, g_cxb, g_cbc, g_cbcb, g_dt_bias, g_a_log, g_d_skip
        )

    return gated_mix, mixer_back


MESH = pl.DeviceIdType.MESH
DMA = pltpu.SemaphoreType.DMA
VMEM_SPEC = pl.BlockSpec(memory_space=pltpu.VMEM)
ANY_SPEC = pl.BlockSpec(memory_space=pl.ANY)


def place():
    d = lax.axis_index("dp")
    t = lax.axis_index("tensor")
    return d // 2, d % 2, t // 2, t % 2


def device(hi, lo, th, tl):
    return (hi * 2 + lo, th * 2 + tl)


def greet(n_hi):
    hi, lo, th, tl = place()
    barrier = pltpu.get_barrier_semaphore()
    others = [device(lax.rem(hi + k, n_hi), lo, th, tl) for k in range(1, n_hi)]
    others += [device(hi, 1 - lo, th, tl), device(hi, lo, 1 - th, tl), device(hi, lo, th, 1 - tl)]
    for other in others:
        pl.semaphore_signal(barrier, inc=1, device_id=other, device_id_type=MESH)
    pl.semaphore_wait(barrier, len(others))


def remote(src, dst, ssem, rsem, to):
    return pltpu.make_async_remote_copy(
        src_ref=src, dst_ref=dst, send_sem=ssem, recv_sem=rsem, device_id=to, device_id_type=MESH
    )


class Sends:
    def __init__(self):
        self.copies = []

    def push(self, src, dst, ssem, rsem, to):
        copy = remote(src, dst, ssem, rsem, to)
        copy.start()
        self.copies.append(copy)

    def finish(self):
        for copy in self.copies:
            copy.wait_send()


def arrive(dst, ssem, rsem, to):
    remote(dst, dst, ssem, rsem, to).wait_recv()


TENSOR_SUM_SCRATCH = lambda rows, width, dtype: [
    pltpu.VMEM((2, rows, width), dtype),
    pltpu.VMEM((rows, width), dtype),
    DMA((3,)),
    DMA((3,)),
]


def tensor_sum_start(sends, part_ref, got_c, ssem, rsem):
    hi, lo, th, tl = place()
    to_c = device(hi, lo, th, 1 - tl)
    for j, y in enumerate((1 - th, th)):
        sends.push(part_ref.at[y * 2 + 1 - tl], got_c.at[j], ssem.at[j], rsem.at[j], to_c)


def tensor_sum_middle(sends, part_ref, got_c, got_y, ssem, rsem):
    hi, lo, th, tl = place()
    arrive(got_c.at[0], ssem.at[0], rsem.at[0], device(hi, lo, th, 1 - tl))
    total = part_ref[(1 - th) * 2 + tl].astype(F32) + got_c[0].astype(F32)
    got_c[0] = total.astype(got_c.dtype)
    sends.push(got_c.at[0], got_y, ssem.at[2], rsem.at[2], device(hi, lo, 1 - th, tl))


def tensor_sum_end(part_ref, got_c, got_y, ssem, rsem):
    hi, lo, th, tl = place()
    arrive(got_c.at[1], ssem.at[1], rsem.at[1], device(hi, lo, th, 1 - tl))
    total = part_ref[th * 2 + tl].astype(F32) + got_c[1].astype(F32)
    arrive(got_y, ssem.at[2], rsem.at[2], device(hi, lo, 1 - th, tl))
    return total + got_y[...].astype(F32)


def tensor_spread_start(sends, o_ref, ssem, rsem):
    hi, lo, th, tl = place()
    own = o_ref.at[th * 2 + tl]
    sends.push(own, own, ssem.at[0], rsem.at[0], device(hi, lo, 1 - th, tl))
    sends.push(own, own, ssem.at[1], rsem.at[1], device(hi, lo, th, 1 - tl))


def tensor_spread_end(sends, o_ref, ssem, rsem):
    hi, lo, th, tl = place()
    other = o_ref.at[(1 - th) * 2 + tl]
    to_c = device(hi, lo, th, 1 - tl)
    arrive(other, ssem.at[0], rsem.at[0], device(hi, lo, 1 - th, tl))
    sends.push(other, other, ssem.at[2], rsem.at[2], to_c)
    arrive(o_ref.at[th * 2 + 1 - tl], ssem.at[1], rsem.at[1], to_c)
    arrive(o_ref.at[(1 - th) * 2 + 1 - tl], ssem.at[2], rsem.at[2], to_c)


def gather_steps(n_hi, x_ref, o_ref, own_sem, send_sem, recv_sem):
    hi, lo, th, tl = place()
    rows = x_ref.shape[0]
    half = rows // 2
    own_block = (hi * 2 + lo) * 4 + th * 2 + tl
    own = pltpu.make_async_copy(x_ref, o_ref.at[pl.ds(own_block * rows, rows)], own_sem)
    own.start()
    sends = Sends()

    def slot(k, f, s, c):
        return ((c * 2 + s) * 2 + f) * n_hi + k

    def where(h, k, f, s, c):
        kk = lax.rem(hi + k, n_hi)
        l = 1 - lo if (f if h == 0 else s) else lo
        y = 1 - th if (s if h == 0 else f) else th
        z = 1 - tl if c else tl
        return ((kk * 2 + l) * 4 + y * 2 + z) * rows + h * half

    def push(h, k, f, s, c, step):
        at = where(h, k, f, s, c)
        if k == 0 and not (f or s or c):
            src = x_ref.at[pl.ds(h * half, half)]
        else:
            src = o_ref.at[pl.ds(at, half)]
        if step == "c":
            to, r = device(hi, lo, th, 1 - tl), slot(k, f, s, 1)
        elif step == "s":
            to = device(hi, lo, 1 - th, tl) if h == 0 else device(hi, 1 - lo, th, tl)
            r = slot(k, f, 1, 0)
        elif step == "f":
            to = device(hi, 1 - lo, th, tl) if h == 0 else device(hi, lo, 1 - th, tl)
            r = slot(k, 1, 0, 0)
        else:
            to, r = device(lax.rem(hi + step, n_hi), lo, th, tl), slot(n_hi - step, 0, 0, 0)
        sends.push(src, o_ref.at[pl.ds(at, half)], send_sem.at[h, r], recv_sem.at[h, r], to)

    def got(h, k, f, s, c):
        r = slot(k, f, s, c)
        arrive(
            o_ref.at[pl.ds(where(h, k, f, s, c), half)],
            send_sem.at[h, r], recv_sem.at[h, r], device(hi, lo, th, 1 - tl),
        )

    for k in range(1, n_hi):
        for h in range(2):
            push(h, 0, 0, 0, 0, k)
    for k in range(n_hi):
        for h in range(2):
            if k:
                got(h, k, 0, 0, 0)
            for step in ("f", "s", "c"):
                push(h, k, 0, 0, 0, step)
        for h in range(2):
            got(h, k, 1, 0, 0)
            for step in ("s", "c"):
                push(h, k, 1, 0, 0, step)
    for k in range(n_hi):
        for f in range(2):
            for h in range(2):
                got(h, k, f, 1, 0)
                push(h, k, f, 1, 0, "c")
    for k in range(n_hi):
        for f in range(2):
            for s in range(2):
                for h in range(2):
                    got(h, k, f, s, 1)
    own.wait()
    sends.finish()


def gather_kernel(n_hi, x_ref, o_ref, own_sem, send_sem, recv_sem):
    greet(n_hi)
    gather_steps(n_hi, x_ref, o_ref, own_sem, send_sem, recv_sem)


def gather_rows(x, n_dp, collective_id):
    rows, width = x.shape
    n_hi = n_dp // 2
    return pl.pallas_call(
        functools.partial(gather_kernel, n_hi),
        out_shape=jax.ShapeDtypeStruct((n_dp * 4 * rows, width), x.dtype),
        in_specs=[ANY_SPEC],
        out_specs=ANY_SPEC,
        scratch_shapes=[DMA, DMA((2, 8 * n_hi)), DMA((2, 8 * n_hi))],
        compiler_params=pltpu.CompilerParams(collective_id=collective_id, has_side_effects=True),
        name="gather_rows",
    )(x)


def middle_kernel(
    n_hi, part_ref, x_ref, gain_ref, o_ref, hidden_ref, normed, got_c, got_y, t_send, t_recv,
    own_sem, send_sem, recv_sem,
):
    greet(n_hi)
    sends = Sends()
    tensor_sum_start(sends, part_ref, got_c, t_send, t_recv)
    tensor_sum_middle(sends, part_ref, got_c, got_y, t_send, t_recv)
    hidden = x_ref[...].astype(F32) + tensor_sum_end(part_ref, got_c, got_y, t_send, t_recv)
    hidden_ref[...] = hidden
    normed[...] = (hidden * rms_scale(hidden) * gain_ref[...]).astype(normed.dtype)
    gather_steps(n_hi, normed, o_ref, own_sem, send_sem, recv_sem)
    sends.finish()


def middle(part, x_piece, gain, n_dp, collective_id):
    rows, width = x_piece.shape
    n_hi = n_dp // 2
    return pl.pallas_call(
        functools.partial(middle_kernel, n_hi),
        out_shape=(
            jax.ShapeDtypeStruct((n_dp * 4 * rows, width), part.dtype),
            jax.ShapeDtypeStruct((rows, width), F32),
        ),
        in_specs=[VMEM_SPEC] * 3,
        out_specs=(ANY_SPEC, VMEM_SPEC),
        scratch_shapes=[pltpu.VMEM((rows, width), part.dtype)]
        + TENSOR_SUM_SCRATCH(rows, width, part.dtype)
        + [DMA, DMA((2, 8 * n_hi)), DMA((2, 8 * n_hi))],
        compiler_params=pltpu.CompilerParams(collective_id=collective_id, has_side_effects=True),
        name="middle",
    )(part.reshape(4, rows, width), x_piece, gain.reshape(1, width))


def scatter_steps(n_hi, sends, p_ref, o_ref, bufs):
    (stage, from_c, from_f, from_s, from_h,
     stage_sem, send_c, recv_c, send_f, recv_f, send_s, recv_s, send_h, recv_h) = bufs
    depth = stage.shape[0]
    hi, lo, th, tl = place()
    to_c = device(hi, lo, th, 1 - tl)
    rows = o_ref.shape[0]
    half = rows // 2

    def where(h, k, f, s, c):
        kk = lax.rem(hi + k, n_hi)
        l = 1 - lo if (f if h == 1 else s) else lo
        y = 1 - th if (s if h == 1 else f) else th
        z = 1 - tl if c else tl
        return ((kk * 2 + l) * 4 + y * 2 + z) * rows + h * half

    order = [(f, s, k, h) for f, s in ((1, 1), (1, 0), (0, 1), (0, 0)) for k in
             list(range(1, n_hi)) + [0] for h in range(2)]

    def slot(f, s, k):
        return (f * 2 + s) * n_hi + k

    def first(h):
        return device(hi, lo, 1 - th, tl) if h == 0 else device(hi, 1 - lo, th, tl)

    def second(h):
        return device(hi, 1 - lo, th, tl) if h == 0 else device(hi, lo, 1 - th, tl)

    for f, s, k, h in order:
        n = slot(f, s, k)
        sends.push(
            p_ref.at[pl.ds(where(h, k, f, s, 1), half)], from_c.at[h, n], send_c.at[h, n],
            recv_c.at[h, n], to_c,
        )

    def load(i):
        f, s, k, h = order[i]
        return pltpu.make_async_copy(
            p_ref.at[pl.ds(where(h, k, f, s, 0), half)], stage.at[i % depth], stage_sem.at[i % depth]
        )

    for i in range(depth - 1):
        load(i).start()
    for i, (f, s, k, h) in enumerate(order):
        if i + depth - 1 < len(order):
            load(i + depth - 1).start()
        load(i).wait()
        n = slot(f, s, k)
        arrive(from_c.at[h, n], send_c.at[h, n], recv_c.at[h, n], to_c)
        total = stage[i % depth].astype(F32) + from_c[h, n].astype(F32)
        if f == 0:
            m = s * n_hi + k
            arrive(from_f.at[h, m], send_f.at[h, m], recv_f.at[h, m], to_c)
            total = total + from_f[h, m].astype(F32)
        if f == 0 and s == 0:
            arrive(from_s.at[h, k], send_s.at[h, k], recv_s.at[h, k], to_c)
            total = total + from_s[h, k].astype(F32)
        if f == 0 and s == 0 and k == 0:
            for j in range(n_hi - 1):
                arrive(from_h.at[h, j], send_h.at[h, j], recv_h.at[h, j], to_c)
                total = total + from_h[h, j].astype(F32)
            o_ref[pl.ds(h * half, half), :] = total
            continue
        from_c[h, n] = total.astype(from_c.dtype)
        src = from_c.at[h, n]
        if f == 1:
            m = s * n_hi + k
            sends.push(src, from_f.at[h, m], send_f.at[h, m], recv_f.at[h, m], first(h))
        elif s == 1:
            sends.push(src, from_s.at[h, k], send_s.at[h, k], recv_s.at[h, k], second(h))
        else:
            j = n_hi - k - 1
            sends.push(
                src, from_h.at[h, j], send_h.at[h, j], recv_h.at[h, j],
                device(lax.rem(hi + k, n_hi), lo, th, tl),
            )


def scatter_scratch(n_hi, half, width, dtype, depth=4):
    return [
        pltpu.VMEM((depth, half, width), dtype),
        pltpu.VMEM((2, 4 * n_hi, half, width), dtype),
        pltpu.VMEM((2, 2 * n_hi, half, width), dtype),
        pltpu.VMEM((2, n_hi, half, width), dtype),
        pltpu.VMEM((2, n_hi - 1, half, width), dtype),
        DMA((depth,)),
        DMA((2, 4 * n_hi)), DMA((2, 4 * n_hi)),
        DMA((2, 2 * n_hi)), DMA((2, 2 * n_hi)),
        DMA((2, n_hi)), DMA((2, n_hi)),
        DMA((2, n_hi - 1)), DMA((2, n_hi - 1)),
    ]


def scatter_kernel(n_hi, p_ref, o_ref, *bufs):
    greet(n_hi)
    sends = Sends()
    scatter_steps(n_hi, sends, p_ref, o_ref, bufs)
    sends.finish()


def scatter_rows(p, n_dp, collective_id):
    width = p.shape[1]
    rows = p.shape[0] // (n_dp * 4)
    n_hi = n_dp // 2
    return pl.pallas_call(
        functools.partial(scatter_kernel, n_hi),
        out_shape=jax.ShapeDtypeStruct((rows, width), F32),
        in_specs=[ANY_SPEC],
        out_specs=VMEM_SPEC,
        scratch_shapes=scatter_scratch(n_hi, rows // 2, width, p.dtype),
        compiler_params=pltpu.CompilerParams(
            collective_id=collective_id, has_side_effects=True, vmem_limit_bytes=60 << 20
        ),
        name="scatter_rows",
    )(p)


def turn_kernel(
    n_hi, p_ref, hidden_ref, g2_ref, gain_ref, grad_ref, sum_ref, dm_ref, total_ref, sp_send, sp_recv, *bufs
):
    hi, lo, th, tl = place()
    greet(n_hi)
    sends = Sends()
    scatter_steps(n_hi, sends, p_ref, total_ref, bufs)
    grad = total_ref[...]
    hidden = hidden_ref[...]
    scale = rms_scale(hidden)
    weighted = gain_ref[...] * grad
    sum_ref[...] = jnp.sum(grad * hidden * scale, axis=0, keepdims=True)
    mean = jnp.mean(weighted * hidden, axis=-1, keepdims=True)
    grad = g2_ref[...].astype(F32) + scale * weighted - hidden * (scale * scale * scale) * mean
    grad_ref[...] = grad
    dm_ref[th * 2 + tl] = grad.astype(dm_ref.dtype)
    tensor_spread_start(sends, dm_ref, sp_send, sp_recv)
    tensor_spread_end(sends, dm_ref, sp_send, sp_recv)
    sends.finish()


def turn(p, hidden, g2_piece, gain, n_dp, collective_id):
    rows, width = hidden.shape
    n_hi = n_dp // 2
    return pl.pallas_call(
        functools.partial(turn_kernel, n_hi),
        out_shape=(
            jax.ShapeDtypeStruct((rows, width), F32),
            jax.ShapeDtypeStruct((1, width), F32),
            jax.ShapeDtypeStruct((4, rows, width), p.dtype),
        ),
        in_specs=[ANY_SPEC] + [VMEM_SPEC] * 3,
        out_specs=(VMEM_SPEC,) * 3,
        scratch_shapes=[pltpu.VMEM((rows, width), F32), DMA((3,)), DMA((3,))]
        + scatter_scratch(n_hi, rows // 2, width, p.dtype),
        compiler_params=pltpu.CompilerParams(
            collective_id=collective_id, has_side_effects=True, vmem_limit_bytes=60 << 20
        ),
        name="turn",
    )(p, hidden, g2_piece, gain.reshape(1, width))


def tail_kernel(
    n_hi, wide, bc_at, w_ref, part_ref, grad_ref, x_ref, gain_ref, small_ref,
    ow_ref, ox_ref, os_ref,
    stage, from_f, from_h, stage_sem, send_f, recv_f, send_h, recv_h,
    got_c, got_y, t_send, t_recv, sp_send, sp_recv,
    small, small_f, small_h, small_t, sm_send, sm_recv, smh_send, smh_recv,
    bc_own, bc_got, bc_send, bc_recv,
):
    hi, lo, th, tl = place()
    to_f, to_y, to_c = device(hi, 1 - lo, th, tl), device(hi, lo, 1 - th, tl), device(hi, lo, th, 1 - tl)
    half = w_ref.shape[2]
    greet(n_hi)
    sends = Sends()
    order = [(k, h) for k in list(range(1, n_hi)) + [0] for h in range(2)]

    def owner(k, l):
        return lax.rem(hi + k, n_hi) * 2 + l

    for k, h in order:
        sends.push(w_ref.at[owner(k, 1 - lo), h], from_f.at[h, k], send_f.at[h, k], recv_f.at[h, k], to_f)
    loads = [
        pltpu.make_async_copy(w_ref.at[owner(k, lo), h], stage.at[h, k], stage_sem.at[h, k])
        for k, h in order
    ]
    for copy in loads:
        copy.start()
    tensor_sum_start(sends, part_ref, got_c, t_send, t_recv)
    tensor_sum_middle(sends, part_ref, got_c, got_y, t_send, t_recv)
    grad = tensor_sum_end(part_ref, got_c, got_y, t_send, t_recv)
    x = x_ref[...].astype(F32)
    scale = rms_scale(x)
    weighted = gain_ref[...] * grad
    mean = jnp.mean(weighted * x, axis=-1, keepdims=True)
    ox_ref[th * 2 + tl] = (
        grad_ref[...] + scale * weighted - x * (scale * scale * scale) * mean
    ).astype(ox_ref.dtype)
    tensor_spread_start(sends, ox_ref, sp_send, sp_recv)
    small[...] = small_ref[...]
    small[0:1, :] = jnp.sum(grad * x * scale, axis=0, keepdims=True)
    sends.push(small, small_f, sm_send.at[0], sm_recv.at[0], to_f)

    finals = []
    for i, (k, h) in enumerate(order):
        loads[i].wait()
        arrive(from_f.at[h, k], send_f.at[h, k], recv_f.at[h, k], to_c)
        if k == 0:
            continue
        from_f[h, k] = (stage[h, k].astype(F32) + from_f[h, k].astype(F32)).astype(from_f.dtype)
        j = n_hi - k - 1
        sends.push(
            from_f.at[h, k], from_h.at[h, j], send_h.at[h, j], recv_h.at[h, j],
            device(lax.rem(hi + k, n_hi), lo, th, tl),
        )
        if i == 0:
            tensor_spread_end(sends, ox_ref, sp_send, sp_recv)
        if i == 1:
            arrive(small_f, sm_send.at[0], sm_recv.at[0], to_c)
            small_h[hi] = small[...] + small_f[...]
            for q in range(1, n_hi):
                sends.push(
                    small_h.at[hi], small_h.at[hi], smh_send.at[q - 1], smh_recv.at[q - 1],
                    device(lax.rem(hi + q, n_hi), lo, th, tl),
                )
    for q in range(1, n_hi):
        arrive(small_h.at[lax.rem(hi - q + n_hi, n_hi)], smh_send.at[q - 1], smh_recv.at[q - 1], to_c)
    total = small_h[0]
    for q in range(1, n_hi):
        total = total + small_h[q]
    os_ref[...] = total
    sends.push(os_ref.at[pl.ds(0, wide)], small_t.at[0], sm_send.at[1], sm_recv.at[1], to_c)
    for h in range(2):
        total = stage[h, 0].astype(F32) + from_f[h, 0].astype(F32)
        for j in range(n_hi - 1):
            arrive(from_h.at[h, j], send_h.at[h, j], recv_h.at[h, j], to_c)
            total = total + from_h[h, j].astype(F32)
        ow_ref[h] = total
        bc_own[0, h] = total[:, bc_at : bc_at + bc_own.shape[3]].astype(bc_own.dtype)
    sends.push(bc_own.at[0], bc_got.at[0], bc_send.at[0], bc_recv.at[0], to_c)
    arrive(small_t.at[0], sm_send.at[1], sm_recv.at[1], to_c)
    small_t[2] = os_ref[pl.ds(0, wide), :] + small_t[0]
    sends.push(small_t.at[2], small_t.at[1], sm_send.at[2], sm_recv.at[2], to_y)
    arrive(bc_got.at[0], bc_send.at[0], bc_recv.at[0], to_c)
    bc_own[1] = (bc_own[0].astype(F32) + bc_got[0].astype(F32)).astype(bc_own.dtype)
    sends.push(bc_own.at[1], bc_got.at[1], bc_send.at[1], bc_recv.at[1], to_y)
    arrive(small_t.at[1], sm_send.at[2], sm_recv.at[2], to_c)
    arrive(bc_got.at[1], bc_send.at[1], bc_recv.at[1], to_c)
    for h in range(2):
        ow_ref[h, :, bc_at : bc_at + bc_own.shape[3]] = bc_own[1, h].astype(F32) + bc_got[1, h].astype(F32)
    sends.finish()
    os_ref[pl.ds(0, wide), :] = small_t[2] + small_t[1]


def tail(w, part, grad_one, x_piece, gain, small, wide, bc_at, bc_width, n_dp, collective_id):
    rows, width = x_piece.shape
    n_hi = n_dp // 2
    half = w.shape[0] // (2 * n_dp)
    w_width = w.shape[1]
    dt = w.dtype
    return pl.pallas_call(
        functools.partial(tail_kernel, n_hi, wide, bc_at),
        out_shape=(
            jax.ShapeDtypeStruct((2, half, w_width), F32),
            jax.ShapeDtypeStruct((4, rows, width), dt),
            jax.ShapeDtypeStruct(small.shape, F32),
        ),
        in_specs=[ANY_SPEC] + [VMEM_SPEC] * 5,
        out_specs=(VMEM_SPEC,) * 3,
        scratch_shapes=[
            pltpu.VMEM((2, n_hi, half, w_width), dt),
            pltpu.VMEM((2, n_hi, half, w_width), dt),
            pltpu.VMEM((2, n_hi - 1, half, w_width), dt),
            DMA((2, n_hi)),
            DMA((2, n_hi)), DMA((2, n_hi)),
            DMA((2, n_hi - 1)), DMA((2, n_hi - 1)),
        ]
        + TENSOR_SUM_SCRATCH(rows, width, part.dtype)
        + [
            DMA((3,)), DMA((3,)),
            pltpu.VMEM(small.shape, F32),
            pltpu.VMEM(small.shape, F32),
            pltpu.VMEM((n_hi,) + small.shape, F32),
            pltpu.VMEM((3, wide, small.shape[1]), F32),
            DMA((3,)), DMA((3,)),
            DMA((n_hi - 1,)), DMA((n_hi - 1,)),
            pltpu.VMEM((2, 2, half, bc_width), dt),
            pltpu.VMEM((2, 2, half, bc_width), dt),
            DMA((2,)), DMA((2,)),
        ],
        compiler_params=pltpu.CompilerParams(
            collective_id=collective_id, has_side_effects=True, vmem_limit_bytes=60 << 20
        ),
        name="tail",
    )(
        w.reshape(n_dp, 2, half, w_width), part.reshape(4, rows, width), grad_one, x_piece,
        gain.reshape(1, width), small,
    )


def local(
    x_in,
    lengths,
    routes,
    route_w,
    ln1_gain,
    w_zx,
    w_bc,
    w_dt,
    conv_x,
    conv_x_bias,
    conv_bc,
    conv_bc_bias,
    dt_bias,
    a_log,
    d_skip,
    gnorm_gain,
    w_out,
    ln2_gain,
    w_shared_gu,
    w_shared_down,
    w_exp_gu,
    w_exp_down,
    cotangent,
):
    slots, width = x_in.shape
    n_dp = lax.axis_size("dp")
    n_t = lax.axis_size("tensor")
    my_t = lax.axis_index("tensor")
    my_dp = lax.axis_index("dp")
    piece = slots // n_t
    n_local = w_exp_gu.shape[0]
    n_experts = n_dp * n_local
    cap = slots * routes.shape[1] * 4 // (3 * n_experts)
    if cap > slots:
        cap = slots
    heads = dt_bias.shape[0]
    inner = conv_x.shape[1]
    head_size = inner // heads
    state = conv_bc.shape[1] // 2
    full_inner = inner * n_t
    rows = w_zx.shape[0]
    n_sh = w_shared_gu.shape[2]

    dt_at = 2 * inner + 2 * state
    first_width = dt_at + heads + -(dt_at + heads) % 128
    first = jnp.concatenate(
        [
            w_zx.reshape(rows, 2 * inner),
            w_bc,
            w_dt,
            jnp.zeros((rows, first_width - dt_at - heads), F32),
        ],
        axis=1,
    ).astype(BF)
    first = lax.all_gather(first, "dp", axis=0, tiled=True)
    proj_out = lax.all_gather(w_out.astype(BF), "dp", axis=0, tiled=True)
    shared = jnp.concatenate([w_shared_gu.reshape(rows, 2 * n_sh), w_shared_down], axis=1)
    shared = lax.all_gather(shared.astype(BF), "dp", axis=0, tiled=True)
    shared_gu = shared[:, : 2 * n_sh]
    shared_down = shared[:, 2 * n_sh :]

    live = (jnp.arange(slots, dtype=jnp.int32) < lengths[0]).astype(F32)
    g2 = cotangent.astype(F32) * live[:, None]
    g2_low = g2.astype(BF)
    expert_range = jnp.arange(n_experts, dtype=jnp.int32)
    chosen = routes[:, :, None] == expert_range[None, None, :]
    weights = jnp.sum(jnp.where(chosen, route_w[:, :, None], 0.0), axis=1)
    high = weights.astype(BF)
    low = (weights - high.astype(F32)).astype(BF)
    table = jnp.concatenate([g2_low, high, low], axis=1)
    table = lax.dynamic_slice_in_dim(table, my_t * piece, piece, axis=0)
    table = gather_rows(table, n_dp, 1)
    g2_all = table[:, :width].reshape(n_dp, slots, width)
    g2_piece = lax.dynamic_slice_in_dim(g2_low, my_t * piece, piece, axis=0)
    high = lax.dynamic_slice_in_dim(table, width + my_dp * n_local, n_local, axis=1)
    low = lax.dynamic_slice_in_dim(table, width + n_experts + my_dp * n_local, n_local, axis=1)
    weights = (high.astype(F32) + low.astype(F32)).reshape(n_dp, slots, n_local)
    member = (weights > 0.0).astype(BF)
    before = (
        jnp.arange(slots)[:, None] > jnp.arange(slots)[None, :]
    ).astype(BF)
    position = dotf("ut,ste->sue", before, member).astype(jnp.int32)
    position = jnp.where(weights > 0.0, position, -1)
    pick = (
        position.transpose(0, 2, 1)[:, :, None, :]
        == jnp.arange(cap, dtype=jnp.int32)[None, None, :, None]
    )
    slot_weight = jnp.sum(
        jnp.where(pick, weights.transpose(0, 2, 1)[:, :, None, :], 0.0), axis=-1
    )
    pick = pick.astype(BF).reshape(n_dp, n_local * cap, slots)

    gate_w = w_exp_gu.astype(BF).reshape(n_local, width, -1)
    down_w = w_exp_down.astype(BF)

    x_float = x_in.astype(F32)
    scale_one = rms_scale(x_float)
    normed_one = (x_float * scale_one * ln1_gain).astype(BF)
    firsts = dotf("td,df->tf", normed_one, first)
    zx = firsts[:, : 2 * inner]
    bc_proj = firsts[:, 2 * inner : dt_at]
    dt_proj = firsts[:, dt_at : dt_at + heads]

    gated_mix, mixer_back = mixer_forward(
        zx, bc_proj, dt_proj, conv_x, conv_x_bias, conv_bc, conv_bc_bias, dt_bias, a_log, d_skip
    )
    squares = lax.psum(jnp.sum(gated_mix * gated_mix, axis=-1), "tensor")
    scale_mix = lax.rsqrt(squares / full_inner + EPSILON)[:, None]
    normed_mix = (gated_mix * scale_mix * gnorm_gain).astype(BF)
    mixer_part = dotf("tc,dc->td", normed_mix, proj_out).astype(BF)
    x_piece = lax.dynamic_slice_in_dim(x_in, my_t * piece, piece, axis=0)
    all_rows, hidden_one = middle(mixer_part, x_piece, ln2_gain, n_dp, 2)
    mine = lax.dynamic_slice_in_dim(all_rows, my_dp * slots, slots, axis=0)
    all_rows = all_rows.reshape(n_dp, slots, width)

    shared_pre = dotf("td,df->tf", mine, shared_gu)
    s_gate, s_up = shared_pre[:, :n_sh], shared_pre[:, n_sh:]
    shared_silu, shared_slope = silu_parts(s_gate)
    shared_act = (shared_silu * s_up).astype(BF)
    grad_shared_act = dotf("td,df->tf", g2_low, shared_down)
    grad_shared_pre = jnp.concatenate(
        [grad_shared_act * s_up * shared_slope, grad_shared_act * shared_silu], axis=1
    ).astype(BF)
    grad_normed_shared = dotf("tf,df->td", grad_shared_pre, shared_gu)
    shared_part = dotf("tf,df->td", shared_act, shared_down)

    def by_expert(v):
        return v.reshape(n_dp, n_local, cap, v.shape[-1]).transpose(1, 0, 2, 3).reshape(
            n_local, n_dp * cap, v.shape[-1]
        )

    def by_source(v):
        return v.reshape(n_local, n_dp, cap, v.shape[-1]).transpose(1, 0, 2, 3).reshape(
            n_dp, n_local * cap, v.shape[-1]
        )

    sw = slot_weight.transpose(1, 0, 2).reshape(n_local, n_dp * cap, 1)
    q = by_expert(dotf("sct,std->scd", pick, g2_all))
    q = (q * sw).astype(BF)
    grad_act = dotf("erd,efd->erf", q, down_w)
    xr = by_expert(dotf("sct,std->scd", pick, all_rows).astype(BF))
    pre = dotf("erd,edf->erf", xr, gate_w)
    n_f = pre.shape[-1] // 2
    p_gate, p_up = pre[..., :n_f], pre[..., n_f:]
    act_silu, act_slope = silu_parts(p_gate)
    act = (act_silu * p_up).astype(BF)
    grad_pre = jnp.concatenate(
        [grad_act * p_up * act_slope, grad_act * act_silu], axis=-1
    ).astype(BF)
    back = by_source(dotf("erf,edf->erd", grad_pre, gate_w).astype(BF))
    dxn_part = dotf("sct,scd->std", pick, back)
    own = (jnp.arange(n_dp) == my_dp).astype(F32)[:, None, None]
    dxn_part = (dxn_part + own * grad_normed_shared[None]).astype(BF)
    grad_one, sum_ln2, dm = turn(
        dxn_part.reshape(n_dp * slots, width), hidden_one, g2_piece, ln2_gain, n_dp, 3
    )
    dm = dm.reshape(slots, width)

    forth = by_source((dotf("erf,efd->erd", act, down_w) * sw).astype(BF))
    out_part = dotf("sct,scd->std", pick, forth)
    out_part = (out_part + own * shared_part[None]).astype(BF)
    ffn_out = scatter_rows(out_part.reshape(n_dp * slots, width), n_dp, 4)
    layer_out = lax.all_gather(
        (hidden_one + ffn_out).astype(BF), "tensor", axis=0, tiled=True
    )
    grad_exp_down = dotf("erf,erd->efd", act, q)
    grad_exp_gu = dotf("erd,erf->edf", xr, grad_pre).reshape(w_exp_gu.shape)
    grad_shared_down = dotf("td,tf->df", g2_low, shared_act)
    grad_shared_gu = dotf("td,tf->df", mine, grad_shared_pre)

    grad_out_proj = dotf("td,tc->dc", dm, normed_mix)
    grad_normed_mix = dotf("td,dc->tc", dm, proj_out)
    weighted_mix = gnorm_gain * grad_normed_mix
    grad_gnorm = jnp.sum(grad_normed_mix * gated_mix * scale_mix, axis=0)
    product_sum = lax.psum(jnp.sum(weighted_mix * gated_mix, axis=-1), "tensor")[:, None]
    grad_gated = scale_mix * weighted_mix - gated_mix * scale_mix**3 * product_sum / full_inner
    (
        grad_zx,
        grad_bc,
        grad_dt_low,
        grad_conv_x,
        grad_conv_x_bias,
        grad_conv_bc,
        grad_conv_bc_bias,
        grad_dt_bias,
        grad_a_log,
        grad_d_skip,
    ) = mixer_back(grad_gated)
    grad_first = jnp.concatenate(
        [
            grad_zx,
            grad_bc.astype(BF),
            grad_dt_low,
            jnp.zeros((slots, first_width - dt_at - heads), BF),
        ],
        axis=1,
    )
    grad_input_part = dotf("tf,df->td", grad_first, first).astype(BF)
    grad_first_w = dotf("td,tf->df", normed_one, grad_first).astype(BF)
    grad_shared_w = jnp.concatenate([grad_shared_gu, grad_shared_down], axis=1).astype(BF)
    grad_shared_w = lax.psum_scatter(grad_shared_w, "dp", scatter_dimension=0, tiled=True)
    grad_out_w = lax.psum_scatter(
        grad_out_proj.astype(BF), "dp", scatter_dimension=0, tiled=True
    )

    def lanes(*vectors):
        vector = jnp.concatenate([v.reshape(-1) for v in vectors])
        return jnp.pad(vector, (0, -vector.shape[0] % (8 * width))).reshape(-1, width)

    taps = conv_x.shape[0]
    wide = lanes(jnp.zeros((width,), F32), sum_ln2, grad_conv_bc, grad_conv_bc_bias)
    n_wide = wide.shape[0]
    narrow = lanes(
        grad_conv_x, grad_conv_x_bias, grad_gnorm, grad_dt_bias, grad_a_log, grad_d_skip
    )
    first_f, grad_x, sums = tail(
        grad_first_w,
        grad_input_part,
        grad_one,
        x_piece,
        ln1_gain,
        jnp.concatenate([wide, narrow], axis=0),
        n_wide,
        2 * inner,
        2 * state,
        n_dp,
        5,
    )
    first_f = first_f.reshape(rows, first_width)
    grad_x = grad_x.reshape(slots, width).astype(F32)
    wide, narrow = sums[:n_wide].reshape(-1), sums[n_wide:].reshape(-1)
    at = [0]

    def take(vector, *shape):
        size = 1
        for s in shape:
            size *= s
        part = lax.slice_in_dim(vector, at[0], at[0] + size).reshape(shape)
        at[0] += size
        return part

    o_ln1 = take(wide, width)
    o_ln2 = take(wide, width)
    o_conv_bc = take(wide, taps, 2 * state)
    o_conv_bc_bias = take(wide, 2 * state)
    at[0] = 0
    o_conv_x = take(narrow, taps, inner)
    o_conv_x_bias = take(narrow, inner)
    o_gnorm = take(narrow, inner)
    o_dt_bias = take(narrow, heads)
    o_a_log = take(narrow, heads)
    o_d_skip = take(narrow, heads)
    shared_f = grad_shared_w.astype(F32)
    return (
        layer_out,
        grad_x,
        o_ln1,
        first_f[:, : 2 * inner].reshape(rows, 2, inner),
        first_f[:, 2 * inner : dt_at],
        first_f[:, dt_at : dt_at + heads],
        o_conv_x,
        o_conv_x_bias,
        o_conv_bc,
        o_conv_bc_bias,
        o_dt_bias,
        o_a_log,
        o_d_skip,
        o_gnorm,
        grad_out_w.astype(F32),
        o_ln2,
        shared_f[:, : 2 * n_sh].reshape(rows, 2, n_sh),
        shared_f[:, 2 * n_sh :],
        grad_exp_gu,
        grad_exp_down,
    )


def solution(mesh):
    return jax.shard_map(
        local,
        mesh=mesh,
        in_specs=(
            P("dp", None),
            P("dp"),
            P("dp", None),
            P("dp", None),
            P(),
            P("dp", None, "tensor"),
            P("dp", None),
            P("dp", "tensor"),
            P(None, "tensor"),
            P("tensor"),
            P(),
            P(),
            P("tensor"),
            P("tensor"),
            P("tensor"),
            P("tensor"),
            P("dp", "tensor"),
            P(),
            P("dp", None, "tensor"),
            P("dp", "tensor"),
            P("dp", None, None, "tensor"),
            P("dp", "tensor", None),
            P("dp", None),
        ),
        out_specs=(
            P("dp", None),
            P("dp", None),
            P(),
            P("dp", None, "tensor"),
            P("dp", None),
            P("dp", "tensor"),
            P(None, "tensor"),
            P("tensor"),
            P(),
            P(),
            P("tensor"),
            P("tensor"),
            P("tensor"),
            P("tensor"),
            P("dp", "tensor"),
            P(),
            P("dp", None, "tensor"),
            P("dp", "tensor"),
            P("dp", None, None, "tensor"),
            P("dp", "tensor", None),
        ),
        check_vma=False,
    )
```

```python
import functools

import jax
import jax.numpy as jnp
from jax import lax
from jax.experimental import pallas as pl
from jax.experimental.pallas import tpu as pltpu
from jax.sharding import PartitionSpec as P

BLOCK = 256


EPSILON = 1e-05
HIGHEST = lax.Precision.HIGHEST
BF = jnp.bfloat16
F32 = jnp.float32


def rms_scale(values):
    return lax.rsqrt(jnp.mean(values * values, axis=-1, keepdims=True) + EPSILON)


def silu_parts(values):
    sigmoid_val = jax.nn.sigmoid(values)
    return (values * sigmoid_val, sigmoid_val * (1.0 + values * (1.0 - sigmoid_val)))


def round_keep(values):
    return lax.optimization_barrier(values.astype(BF)).astype(F32)


def dotf(spec, a, b):
    return jnp.einsum(spec, a, b, preferred_element_type=F32)


def causal_conv(signal, kernel, offset):
    kernel_width = kernel.shape[0]
    seq_length = signal.shape[0]
    padded = jnp.concatenate(
        [jnp.zeros((kernel_width - 1, signal.shape[1]), signal.dtype), signal], axis=0
    )
    summed = offset[None, :] + kernel[0][None, :] * padded[0:seq_length]
    for tap_index in range(1, kernel_width):
        summed = summed + kernel[tap_index][None, :] * padded[tap_index : tap_index + seq_length]
    return summed


def ssd_scan(head_values, step_sizes, log_rates, b_rows, c_rows, skip_gain, block_rows):
    seq_length, n_heads, head_size = head_values.shape
    n_state = b_rows.shape[1]
    n_blocks = seq_length // block_rows
    decay_rates = -jnp.exp(log_rates)[None, :] * step_sizes
    scaled = (head_values * step_sizes[:, :, None]).reshape(
        n_blocks, block_rows, n_heads, head_size
    )
    cumulative = jnp.cumsum(decay_rates.reshape(n_blocks, block_rows, n_heads), axis=1)
    b_block = b_rows.reshape(n_blocks, block_rows, n_state)
    c_block = c_rows.reshape(n_blocks, block_rows, n_state)
    positions = jnp.arange(block_rows)
    causal = (positions[:, None] >= positions[None, :])[None, :, :, None]
    differences = cumulative[:, :, None, :] - cumulative[:, None, :, :]
    decay_mask = jnp.where(causal, jnp.exp(jnp.where(causal, differences, 0.0)), 0.0)
    intersection = jnp.einsum("kin,kjn->kij", c_block, b_block, precision=HIGHEST)
    within = jnp.einsum("kij,kijh,kjhp->kihp", intersection, decay_mask, scaled, precision=HIGHEST)
    block_end = cumulative[:, -1, :]
    to_end = jnp.exp(block_end[:, None, :] - cumulative)
    states = jnp.einsum("kjn,kjh,kjhp->khnp", b_block, to_end, scaled, precision=HIGHEST)

    def carry_state(previous, inputs):
        block_decay, block_state = inputs
        return (block_decay[:, None, None] * previous + block_state, previous)

    final_state, entering = lax.scan(
        carry_state,
        jnp.zeros((n_heads, n_state, head_size), head_values.dtype),
        (jnp.exp(block_end), states),
    )
    across = jnp.einsum(
        "kin,khnp,kih->kihp", c_block, entering, jnp.exp(cumulative), precision=HIGHEST
    )
    return (within + across).reshape(seq_length, n_heads, head_size) + skip_gain[
        None, :, None
    ] * head_values


def mixer_forward(
    zx, bc_proj, dt_proj, conv_x, conv_x_bias, conv_bc, conv_bc_bias, dt_bias, a_log, d_skip
):
    slots = zx.shape[0]
    inner = conv_x.shape[1]
    heads = dt_bias.shape[0]
    state = conv_bc.shape[1] // 2

    def conv_block(x_part, bc_part, kernel_x, offset_x, kernel_bc, offset_bc):
        return (
            jax.nn.silu(causal_conv(x_part, kernel_x, offset_x)),
            jax.nn.silu(causal_conv(bc_part, kernel_bc, offset_bc)),
        )

    (conv_values, conv_bc_values), conv_back = jax.vjp(
        conv_block, zx[:, inner:], bc_proj, conv_x, conv_x_bias, conv_bc, conv_bc_bias
    )
    head_input = round_keep(conv_values)
    bc_input = round_keep(conv_bc_values)

    def scan_block(head_flat, b_rows, c_rows, dt_part, z_part, dt_offset, log_rates, skip_gain):
        step_sizes = jax.nn.softplus(dt_part + dt_offset[None, :])
        output = ssd_scan(
            head_flat.reshape(slots, heads, inner // heads),
            step_sizes,
            log_rates,
            b_rows,
            c_rows,
            skip_gain,
            BLOCK,
        )
        return output.reshape(slots, inner) * jax.nn.silu(z_part)

    gated_mix, scan_back = jax.vjp(
        scan_block,
        head_input,
        bc_input[:, :state],
        bc_input[:, state:],
        dt_proj,
        zx[:, :inner],
        dt_bias,
        a_log,
        d_skip,
    )

    def mixer_back(grad_gated):
        g_head, g_b, g_c, g_dt, g_z, g_dt_bias, g_a_log, g_d_skip = scan_back(grad_gated)
        g_xs, g_bc, g_cx, g_cxb, g_cbc, g_cbcb = conv_back(
            (g_head, jnp.concatenate([g_b, g_c], axis=1))
        )
        g_zx = jnp.concatenate([g_z, g_xs], axis=1).astype(BF)
        return (
            g_zx, g_bc, g_dt.astype(BF), g_cx, g_cxb, g_cbc, g_cbcb, g_dt_bias, g_a_log, g_d_skip
        )

    return gated_mix, mixer_back


MESH = pl.DeviceIdType.MESH
DMA = pltpu.SemaphoreType.DMA
VMEM_SPEC = pl.BlockSpec(memory_space=pltpu.VMEM)
ANY_SPEC = pl.BlockSpec(memory_space=pl.ANY)


def place():
    d = lax.axis_index("dp")
    t = lax.axis_index("tensor")
    return d // 2, d % 2, t // 2, t % 2


def device(hi, lo, th, tl):
    return (hi * 2 + lo, th * 2 + tl)


def greet(n_hi):
    hi, lo, th, tl = place()
    barrier = pltpu.get_barrier_semaphore()
    others = [device(lax.rem(hi + k, n_hi), lo, th, tl) for k in range(1, n_hi)]
    others += [device(hi, 1 - lo, th, tl), device(hi, lo, 1 - th, tl), device(hi, lo, th, 1 - tl)]
    for other in others:
        pl.semaphore_signal(barrier, inc=1, device_id=other, device_id_type=MESH)
    pl.semaphore_wait(barrier, len(others))


def remote(src, dst, ssem, rsem, to):
    return pltpu.make_async_remote_copy(
        src_ref=src, dst_ref=dst, send_sem=ssem, recv_sem=rsem, device_id=to, device_id_type=MESH
    )


class Sends:
    def __init__(self):
        self.copies = []

    def push(self, src, dst, ssem, rsem, to):
        copy = remote(src, dst, ssem, rsem, to)
        copy.start()
        self.copies.append(copy)

    def finish(self):
        for copy in self.copies:
            copy.wait_send()


def arrive(dst, ssem, rsem, to):
    remote(dst, dst, ssem, rsem, to).wait_recv()


TENSOR_SUM_SCRATCH = lambda rows, width, dtype: [
    pltpu.VMEM((2, rows, width), dtype),
    pltpu.VMEM((rows, width), dtype),
    DMA((3,)),
    DMA((3,)),
]


def tensor_sum_start(sends, part_ref, got_c, ssem, rsem):
    hi, lo, th, tl = place()
    to_c = device(hi, lo, th, 1 - tl)
    for j, y in enumerate((1 - th, th)):
        sends.push(part_ref.at[y * 2 + 1 - tl], got_c.at[j], ssem.at[j], rsem.at[j], to_c)


def tensor_sum_middle(sends, part_ref, got_c, got_y, ssem, rsem):
    hi, lo, th, tl = place()
    arrive(got_c.at[0], ssem.at[0], rsem.at[0], device(hi, lo, th, 1 - tl))
    total = part_ref[(1 - th) * 2 + tl].astype(F32) + got_c[0].astype(F32)
    got_c[0] = total.astype(got_c.dtype)
    sends.push(got_c.at[0], got_y, ssem.at[2], rsem.at[2], device(hi, lo, 1 - th, tl))


def tensor_sum_end(part_ref, got_c, got_y, ssem, rsem):
    hi, lo, th, tl = place()
    arrive(got_c.at[1], ssem.at[1], rsem.at[1], device(hi, lo, th, 1 - tl))
    total = part_ref[th * 2 + tl].astype(F32) + got_c[1].astype(F32)
    arrive(got_y, ssem.at[2], rsem.at[2], device(hi, lo, 1 - th, tl))
    return total + got_y[...].astype(F32)


def tensor_spread_start(sends, o_ref, ssem, rsem):
    hi, lo, th, tl = place()
    own = o_ref.at[th * 2 + tl]
    sends.push(own, own, ssem.at[0], rsem.at[0], device(hi, lo, 1 - th, tl))
    sends.push(own, own, ssem.at[1], rsem.at[1], device(hi, lo, th, 1 - tl))


def tensor_spread_end(sends, o_ref, ssem, rsem):
    hi, lo, th, tl = place()
    other = o_ref.at[(1 - th) * 2 + tl]
    to_c = device(hi, lo, th, 1 - tl)
    arrive(other, ssem.at[0], rsem.at[0], device(hi, lo, 1 - th, tl))
    sends.push(other, other, ssem.at[2], rsem.at[2], to_c)
    arrive(o_ref.at[th * 2 + 1 - tl], ssem.at[1], rsem.at[1], to_c)
    arrive(o_ref.at[(1 - th) * 2 + 1 - tl], ssem.at[2], rsem.at[2], to_c)


def gather_steps(n_hi, x_ref, o_ref, own_sem, send_sem, recv_sem):
    hi, lo, th, tl = place()
    rows = x_ref.shape[0]
    half = rows // 2
    own_block = (hi * 2 + lo) * 4 + th * 2 + tl
    own = pltpu.make_async_copy(x_ref, o_ref.at[pl.ds(own_block * rows, rows)], own_sem)
    own.start()
    sends = Sends()

    def slot(k, f, s, c):
        return ((c * 2 + s) * 2 + f) * n_hi + k

    def where(h, k, f, s, c):
        kk = lax.rem(hi + k, n_hi)
        l = 1 - lo if (f if h == 0 else s) else lo
        y = 1 - th if (s if h == 0 else f) else th
        z = 1 - tl if c else tl
        return ((kk * 2 + l) * 4 + y * 2 + z) * rows + h * half

    def push(h, k, f, s, c, step):
        at = where(h, k, f, s, c)
        if k == 0 and not (f or s or c):
            src = x_ref.at[pl.ds(h * half, half)]
        else:
            src = o_ref.at[pl.ds(at, half)]
        if step == "c":
            to, r = device(hi, lo, th, 1 - tl), slot(k, f, s, 1)
        elif step == "s":
            to = device(hi, lo, 1 - th, tl) if h == 0 else device(hi, 1 - lo, th, tl)
            r = slot(k, f, 1, 0)
        elif step == "f":
            to = device(hi, 1 - lo, th, tl) if h == 0 else device(hi, lo, 1 - th, tl)
            r = slot(k, 1, 0, 0)
        else:
            to, r = device(lax.rem(hi + step, n_hi), lo, th, tl), slot(n_hi - step, 0, 0, 0)
        sends.push(src, o_ref.at[pl.ds(at, half)], send_sem.at[h, r], recv_sem.at[h, r], to)

    def got(h, k, f, s, c):
        r = slot(k, f, s, c)
        arrive(
            o_ref.at[pl.ds(where(h, k, f, s, c), half)],
            send_sem.at[h, r], recv_sem.at[h, r], device(hi, lo, th, 1 - tl),
        )

    for k in range(1, n_hi):
        for h in range(2):
            push(h, 0, 0, 0, 0, k)
    for k in range(n_hi):
        for h in range(2):
            if k:
                got(h, k, 0, 0, 0)
            for step in ("f", "s", "c"):
                push(h, k, 0, 0, 0, step)
        for h in range(2):
            got(h, k, 1, 0, 0)
            for step in ("s", "c"):
                push(h, k, 1, 0, 0, step)
    for k in range(n_hi):
        for f in range(2):
            for h in range(2):
                got(h, k, f, 1, 0)
                push(h, k, f, 1, 0, "c")
    for k in range(n_hi):
        for f in range(2):
            for s in range(2):
                for h in range(2):
                    got(h, k, f, s, 1)
    own.wait()
    sends.finish()


def gather_kernel(n_hi, x_ref, o_ref, own_sem, send_sem, recv_sem):
    greet(n_hi)
    gather_steps(n_hi, x_ref, o_ref, own_sem, send_sem, recv_sem)


def gather_rows(x, n_dp, collective_id):
    rows, width = x.shape
    n_hi = n_dp // 2
    return pl.pallas_call(
        functools.partial(gather_kernel, n_hi),
        out_shape=jax.ShapeDtypeStruct((n_dp * 4 * rows, width), x.dtype),
        in_specs=[ANY_SPEC],
        out_specs=ANY_SPEC,
        scratch_shapes=[DMA, DMA((2, 8 * n_hi)), DMA((2, 8 * n_hi))],
        compiler_params=pltpu.CompilerParams(collective_id=collective_id, has_side_effects=True),
        name="gather_rows",
    )(x)


def middle_kernel(
    n_hi, part_ref, x_ref, gain_ref, o_ref, hidden_ref, normed, got_c, got_y, t_send, t_recv,
    own_sem, send_sem, recv_sem,
):
    greet(n_hi)
    sends = Sends()
    tensor_sum_start(sends, part_ref, got_c, t_send, t_recv)
    tensor_sum_middle(sends, part_ref, got_c, got_y, t_send, t_recv)
    hidden = x_ref[...].astype(F32) + tensor_sum_end(part_ref, got_c, got_y, t_send, t_recv)
    hidden_ref[...] = hidden
    normed[...] = (hidden * rms_scale(hidden) * gain_ref[...]).astype(normed.dtype)
    gather_steps(n_hi, normed, o_ref, own_sem, send_sem, recv_sem)
    sends.finish()


def middle(part, x_piece, gain, n_dp, collective_id):
    rows, width = x_piece.shape
    n_hi = n_dp // 2
    return pl.pallas_call(
        functools.partial(middle_kernel, n_hi),
        out_shape=(
            jax.ShapeDtypeStruct((n_dp * 4 * rows, width), part.dtype),
            jax.ShapeDtypeStruct((rows, width), F32),
        ),
        in_specs=[VMEM_SPEC] * 3,
        out_specs=(ANY_SPEC, VMEM_SPEC),
        scratch_shapes=[pltpu.VMEM((rows, width), part.dtype)]
        + TENSOR_SUM_SCRATCH(rows, width, part.dtype)
        + [DMA, DMA((2, 8 * n_hi)), DMA((2, 8 * n_hi))],
        compiler_params=pltpu.CompilerParams(collective_id=collective_id, has_side_effects=True),
        name="middle",
    )(part.reshape(4, rows, width), x_piece, gain.reshape(1, width))


def scatter_steps(n_hi, sends, p_ref, o_ref, bufs):
    (stage, from_c, from_f, from_s, from_h,
     stage_sem, send_c, recv_c, send_f, recv_f, send_s, recv_s, send_h, recv_h) = bufs
    depth = stage.shape[0]
    hi, lo, th, tl = place()
    to_c = device(hi, lo, th, 1 - tl)
    rows = o_ref.shape[0]
    half = rows // 2

    def where(h, k, f, s, c):
        kk = lax.rem(hi + k, n_hi)
        l = 1 - lo if (f if h == 1 else s) else lo
        y = 1 - th if (s if h == 1 else f) else th
        z = 1 - tl if c else tl
        return ((kk * 2 + l) * 4 + y * 2 + z) * rows + h * half

    order = [(f, s, k, h) for f, s in ((1, 1), (1, 0), (0, 1), (0, 0)) for k in
             list(range(1, n_hi)) + [0] for h in range(2)]

    def slot(f, s, k):
        return (f * 2 + s) * n_hi + k

    def first(h):
        return device(hi, lo, 1 - th, tl) if h == 0 else device(hi, 1 - lo, th, tl)

    def second(h):
        return device(hi, 1 - lo, th, tl) if h == 0 else device(hi, lo, 1 - th, tl)

    for f, s, k, h in order:
        n = slot(f, s, k)
        sends.push(
            p_ref.at[pl.ds(where(h, k, f, s, 1), half)], from_c.at[h, n], send_c.at[h, n],
            recv_c.at[h, n], to_c,
        )

    def load(i):
        f, s, k, h = order[i]
        return pltpu.make_async_copy(
            p_ref.at[pl.ds(where(h, k, f, s, 0), half)], stage.at[i % depth], stage_sem.at[i % depth]
        )

    for i in range(depth - 1):
        load(i).start()
    for i, (f, s, k, h) in enumerate(order):
        if i + depth - 1 < len(order):
            load(i + depth - 1).start()
        load(i).wait()
        n = slot(f, s, k)
        arrive(from_c.at[h, n], send_c.at[h, n], recv_c.at[h, n], to_c)
        total = stage[i % depth].astype(F32) + from_c[h, n].astype(F32)
        if f == 0:
            m = s * n_hi + k
            arrive(from_f.at[h, m], send_f.at[h, m], recv_f.at[h, m], to_c)
            total = total + from_f[h, m].astype(F32)
        if f == 0 and s == 0:
            arrive(from_s.at[h, k], send_s.at[h, k], recv_s.at[h, k], to_c)
            total = total + from_s[h, k].astype(F32)
        if f == 0 and s == 0 and k == 0:
            for j in range(n_hi - 1):
                arrive(from_h.at[h, j], send_h.at[h, j], recv_h.at[h, j], to_c)
                total = total + from_h[h, j].astype(F32)
            o_ref[pl.ds(h * half, half), :] = total
            continue
        from_c[h, n] = total.astype(from_c.dtype)
        src = from_c.at[h, n]
        if f == 1:
            m = s * n_hi + k
            sends.push(src, from_f.at[h, m], send_f.at[h, m], recv_f.at[h, m], first(h))
        elif s == 1:
            sends.push(src, from_s.at[h, k], send_s.at[h, k], recv_s.at[h, k], second(h))
        else:
            j = n_hi - k - 1
            sends.push(
                src, from_h.at[h, j], send_h.at[h, j], recv_h.at[h, j],
                device(lax.rem(hi + k, n_hi), lo, th, tl),
            )


def scatter_scratch(n_hi, half, width, dtype, depth=4):
    return [
        pltpu.VMEM((depth, half, width), dtype),
        pltpu.VMEM((2, 4 * n_hi, half, width), dtype),
        pltpu.VMEM((2, 2 * n_hi, half, width), dtype),
        pltpu.VMEM((2, n_hi, half, width), dtype),
        pltpu.VMEM((2, n_hi - 1, half, width), dtype),
        DMA((depth,)),
        DMA((2, 4 * n_hi)), DMA((2, 4 * n_hi)),
        DMA((2, 2 * n_hi)), DMA((2, 2 * n_hi)),
        DMA((2, n_hi)), DMA((2, n_hi)),
        DMA((2, n_hi - 1)), DMA((2, n_hi - 1)),
    ]


def scatter_kernel(n_hi, p_ref, o_ref, *bufs):
    greet(n_hi)
    sends = Sends()
    scatter_steps(n_hi, sends, p_ref, o_ref, bufs)
    sends.finish()


def scatter_rows(p, n_dp, collective_id):
    width = p.shape[1]
    rows = p.shape[0] // (n_dp * 4)
    n_hi = n_dp // 2
    return pl.pallas_call(
        functools.partial(scatter_kernel, n_hi),
        out_shape=jax.ShapeDtypeStruct((rows, width), F32),
        in_specs=[ANY_SPEC],
        out_specs=VMEM_SPEC,
        scratch_shapes=scatter_scratch(n_hi, rows // 2, width, p.dtype),
        compiler_params=pltpu.CompilerParams(
            collective_id=collective_id, has_side_effects=True, vmem_limit_bytes=60 << 20
        ),
        name="scatter_rows",
    )(p)


def turn_kernel(
    n_hi, p_ref, hidden_ref, g2_ref, gain_ref, grad_ref, sum_ref, dm_ref, total_ref, sp_send, sp_recv, *bufs
):
    hi, lo, th, tl = place()
    greet(n_hi)
    sends = Sends()
    scatter_steps(n_hi, sends, p_ref, total_ref, bufs)
    grad = total_ref[...]
    hidden = hidden_ref[...]
    scale = rms_scale(hidden)
    weighted = gain_ref[...] * grad
    sum_ref[...] = jnp.sum(grad * hidden * scale, axis=0, keepdims=True)
    mean = jnp.mean(weighted * hidden, axis=-1, keepdims=True)
    grad = g2_ref[...].astype(F32) + scale * weighted - hidden * (scale * scale * scale) * mean
    grad_ref[...] = grad
    dm_ref[th * 2 + tl] = grad.astype(dm_ref.dtype)
    tensor_spread_start(sends, dm_ref, sp_send, sp_recv)
    tensor_spread_end(sends, dm_ref, sp_send, sp_recv)
    sends.finish()


def turn(p, hidden, g2_piece, gain, n_dp, collective_id):
    rows, width = hidden.shape
    n_hi = n_dp // 2
    return pl.pallas_call(
        functools.partial(turn_kernel, n_hi),
        out_shape=(
            jax.ShapeDtypeStruct((rows, width), F32),
            jax.ShapeDtypeStruct((1, width), F32),
            jax.ShapeDtypeStruct((4, rows, width), p.dtype),
        ),
        in_specs=[ANY_SPEC] + [VMEM_SPEC] * 3,
        out_specs=(VMEM_SPEC,) * 3,
        scratch_shapes=[pltpu.VMEM((rows, width), F32), DMA((3,)), DMA((3,))]
        + scatter_scratch(n_hi, rows // 2, width, p.dtype),
        compiler_params=pltpu.CompilerParams(
            collective_id=collective_id, has_side_effects=True, vmem_limit_bytes=60 << 20
        ),
        name="turn",
    )(p, hidden, g2_piece, gain.reshape(1, width))


def tail_kernel(
    n_hi, wide, bc_at, w_ref, part_ref, grad_ref, x_ref, gain_ref, small_ref,
    ow_ref, ox_ref, os_ref,
    stage, from_f, from_h, stage_sem, send_f, recv_f, send_h, recv_h,
    got_c, got_y, t_send, t_recv, sp_send, sp_recv,
    small, small_f, small_h, small_t, sm_send, sm_recv, smh_send, smh_recv,
    bc_own, bc_got, bc_send, bc_recv,
):
    hi, lo, th, tl = place()
    to_f, to_y, to_c = device(hi, 1 - lo, th, tl), device(hi, lo, 1 - th, tl), device(hi, lo, th, 1 - tl)
    half = w_ref.shape[2]
    greet(n_hi)
    sends = Sends()
    order = [(k, h) for k in list(range(1, n_hi)) + [0] for h in range(2)]

    def owner(k, l):
        return lax.rem(hi + k, n_hi) * 2 + l

    for k, h in order:
        sends.push(w_ref.at[owner(k, 1 - lo), h], from_f.at[h, k], send_f.at[h, k], recv_f.at[h, k], to_f)
    loads = [
        pltpu.make_async_copy(w_ref.at[owner(k, lo), h], stage.at[h, k], stage_sem.at[h, k])
        for k, h in order
    ]
    for copy in loads:
        copy.start()
    tensor_sum_start(sends, part_ref, got_c, t_send, t_recv)
    tensor_sum_middle(sends, part_ref, got_c, got_y, t_send, t_recv)
    grad = tensor_sum_end(part_ref, got_c, got_y, t_send, t_recv)
    x = x_ref[...].astype(F32)
    scale = rms_scale(x)
    weighted = gain_ref[...] * grad
    mean = jnp.mean(weighted * x, axis=-1, keepdims=True)
    ox_ref[th * 2 + tl] = (
        grad_ref[...] + scale * weighted - x * (scale * scale * scale) * mean
    ).astype(ox_ref.dtype)
    tensor_spread_start(sends, ox_ref, sp_send, sp_recv)
    small[...] = small_ref[...]
    small[0:1, :] = jnp.sum(grad * x * scale, axis=0, keepdims=True)
    sends.push(small, small_f, sm_send.at[0], sm_recv.at[0], to_f)

    finals = []
    for i, (k, h) in enumerate(order):
        loads[i].wait()
        arrive(from_f.at[h, k], send_f.at[h, k], recv_f.at[h, k], to_c)
        if k == 0:
            continue
        from_f[h, k] = (stage[h, k].astype(F32) + from_f[h, k].astype(F32)).astype(from_f.dtype)
        j = n_hi - k - 1
        sends.push(
            from_f.at[h, k], from_h.at[h, j], send_h.at[h, j], recv_h.at[h, j],
            device(lax.rem(hi + k, n_hi), lo, th, tl),
        )
        if i == 0:
            tensor_spread_end(sends, ox_ref, sp_send, sp_recv)
        if i == 1:
            arrive(small_f, sm_send.at[0], sm_recv.at[0], to_c)
            small_h[hi] = small[...] + small_f[...]
            for q in range(1, n_hi):
                sends.push(
                    small_h.at[hi], small_h.at[hi], smh_send.at[q - 1], smh_recv.at[q - 1],
                    device(lax.rem(hi + q, n_hi), lo, th, tl),
                )
    for q in range(1, n_hi):
        arrive(small_h.at[lax.rem(hi - q + n_hi, n_hi)], smh_send.at[q - 1], smh_recv.at[q - 1], to_c)
    total = small_h[0]
    for q in range(1, n_hi):
        total = total + small_h[q]
    os_ref[...] = total
    sends.push(os_ref.at[pl.ds(0, wide)], small_t.at[0], sm_send.at[1], sm_recv.at[1], to_c)
    for h in range(2):
        total = stage[h, 0].astype(F32) + from_f[h, 0].astype(F32)
        for j in range(n_hi - 1):
            arrive(from_h.at[h, j], send_h.at[h, j], recv_h.at[h, j], to_c)
            total = total + from_h[h, j].astype(F32)
        ow_ref[h] = total
        bc_own[0, h] = total[:, bc_at : bc_at + bc_own.shape[3]].astype(bc_own.dtype)
    sends.push(bc_own.at[0], bc_got.at[0], bc_send.at[0], bc_recv.at[0], to_c)
    arrive(small_t.at[0], sm_send.at[1], sm_recv.at[1], to_c)
    small_t[2] = os_ref[pl.ds(0, wide), :] + small_t[0]
    sends.push(small_t.at[2], small_t.at[1], sm_send.at[2], sm_recv.at[2], to_y)
    arrive(bc_got.at[0], bc_send.at[0], bc_recv.at[0], to_c)
    bc_own[1] = (bc_own[0].astype(F32) + bc_got[0].astype(F32)).astype(bc_own.dtype)
    sends.push(bc_own.at[1], bc_got.at[1], bc_send.at[1], bc_recv.at[1], to_y)
    arrive(small_t.at[1], sm_send.at[2], sm_recv.at[2], to_c)
    arrive(bc_got.at[1], bc_send.at[1], bc_recv.at[1], to_c)
    for h in range(2):
        ow_ref[h, :, bc_at : bc_at + bc_own.shape[3]] = bc_own[1, h].astype(F32) + bc_got[1, h].astype(F32)
    sends.finish()
    os_ref[pl.ds(0, wide), :] = small_t[2] + small_t[1]


def tail(w, part, grad_one, x_piece, gain, small, wide, bc_at, bc_width, n_dp, collective_id):
    rows, width = x_piece.shape
    n_hi = n_dp // 2
    half = w.shape[0] // (2 * n_dp)
    w_width = w.shape[1]
    dt = w.dtype
    return pl.pallas_call(
        functools.partial(tail_kernel, n_hi, wide, bc_at),
        out_shape=(
            jax.ShapeDtypeStruct((2, half, w_width), F32),
            jax.ShapeDtypeStruct((4, rows, width), dt),
            jax.ShapeDtypeStruct(small.shape, F32),
        ),
        in_specs=[ANY_SPEC] + [VMEM_SPEC] * 5,
        out_specs=(VMEM_SPEC,) * 3,
        scratch_shapes=[
            pltpu.VMEM((2, n_hi, half, w_width), dt),
            pltpu.VMEM((2, n_hi, half, w_width), dt),
            pltpu.VMEM((2, n_hi - 1, half, w_width), dt),
            DMA((2, n_hi)),
            DMA((2, n_hi)), DMA((2, n_hi)),
            DMA((2, n_hi - 1)), DMA((2, n_hi - 1)),
        ]
        + TENSOR_SUM_SCRATCH(rows, width, part.dtype)
        + [
            DMA((3,)), DMA((3,)),
            pltpu.VMEM(small.shape, F32),
            pltpu.VMEM(small.shape, F32),
            pltpu.VMEM((n_hi,) + small.shape, F32),
            pltpu.VMEM((3, wide, small.shape[1]), F32),
            DMA((3,)), DMA((3,)),
            DMA((n_hi - 1,)), DMA((n_hi - 1,)),
            pltpu.VMEM((2, 2, half, bc_width), dt),
            pltpu.VMEM((2, 2, half, bc_width), dt),
            DMA((2,)), DMA((2,)),
        ],
        compiler_params=pltpu.CompilerParams(
            collective_id=collective_id, has_side_effects=True, vmem_limit_bytes=60 << 20
        ),
        name="tail",
    )(
        w.reshape(n_dp, 2, half, w_width), part.reshape(4, rows, width), grad_one, x_piece,
        gain.reshape(1, width), small,
    )


def dot_mm(a, b):
    return lax.dot_general(a, b, (((1,), (0,)), ((), ())), preferred_element_type=F32)


def dot_nt(a, b):
    return lax.dot_general(a, b, (((1,), (1,)), ((), ())), preferred_element_type=F32)


def dot_tn(a, b):
    return lax.dot_general(a, b, (((0,), (0,)), ((), ())), preferred_element_type=F32)


def experts_kernel(
    n_dp, n_local, cap, chunk, pos_ref, wt_ref, x_ref, g_ref, gu_ref, dn_ref,
    dxn_ref, out_ref, ggu_ref, gdn_ref, pick, xr, q, sw, gu,
):
    step = pl.program_id(0)
    width = x_ref.shape[1]
    hidden = dn_ref.shape[1]
    slots = x_ref.shape[0]
    columns = [pl.ds(c, chunk) for c in range(0, width, chunk)]

    @pl.when(step < n_dp)
    def _():
        s = step
        lane = lax.broadcasted_iota(jnp.int32, (cap, slots), 0)
        for e in range(n_local):
            hit = lane == pos_ref[0, e : e + 1, :]
            pick[s, e * cap : (e + 1) * cap, :] = jnp.where(hit, 1.0, 0.0).astype(BF)
            sw[e, s] = jnp.sum(jnp.where(hit, wt_ref[0, e : e + 1, :], 0.0), axis=1, keepdims=True)
        chosen = pick[s]
        for c in columns:
            rows = dot_mm(chosen, x_ref[:, c]).astype(BF)
            grads = dot_mm(chosen, g_ref[:, c])
            for e in range(n_local):
                xr[e, s, :, c] = rows[e * cap : (e + 1) * cap]
                q[e, s, :, c] = (grads[e * cap : (e + 1) * cap] * sw[e, s]).astype(BF)

    @pl.when(jnp.logical_and(step >= n_dp, step < n_dp + n_local))
    def _():
        e = step - n_dp
        gu[:, :hidden] = gu_ref[pl.ds(0, width, stride=2), :].astype(BF)
        gu[:, hidden:] = gu_ref[pl.ds(1, width, stride=2), :].astype(BF)
        down = dn_ref[0].astype(BF)
        x = xr[e].reshape(n_dp * cap, width)
        qe = q[e].reshape(n_dp * cap, width)
        pre = dot_mm(x, gu[...])
        grad_act = dot_nt(qe, down)
        gate, up = pre[:, :hidden], pre[:, hidden:]
        sig = 1.0 / (1.0 + jnp.exp(-gate))
        act_silu = gate * sig
        slope = sig * (1.0 + gate * (1.0 - sig))
        value = act_silu * up
        act = value.astype(BF)
        scaled = (value * sw[e].reshape(n_dp * cap, 1)).astype(BF)
        grad_pre = jnp.concatenate([grad_act * up * slope, grad_act * act_silu], axis=1).astype(BF)
        ggu = dot_tn(x, grad_pre)
        ggu_ref[pl.ds(0, width, stride=2), :] = ggu[:, :hidden]
        ggu_ref[pl.ds(1, width, stride=2), :] = ggu[:, hidden:]
        gdn_ref[0] = dot_tn(act, qe)
        for c in columns:
            xr[e, :, :, c] = dot_nt(grad_pre, gu[c, :]).astype(BF).reshape(n_dp, cap, chunk)
            q[e, :, :, c] = dot_mm(scaled, down[:, c.start : c.start + chunk]).astype(BF).reshape(n_dp, cap, chunk)

    @pl.when(step >= n_dp + n_local)
    def _():
        s = step - n_dp - n_local
        chosen = pick[s]
        for c in columns:
            dxn_ref[:, c] = dot_tn(chosen, xr[:, s, :, c].reshape(n_local * cap, chunk)).astype(BF)
            out_ref[:, c] = dot_tn(chosen, q[:, s, :, c].reshape(n_local * cap, chunk)).astype(BF)


def experts(position, weights, rows, table, w_gu, w_down, cap):
    n_dp, n_local, slots = position.shape
    width = rows.shape[1]
    hidden = w_down.shape[1]
    chunk = width // 3 if width % 384 == 0 else width
    by_source = lambda i: (jnp.clip(i, 0, n_dp - 1), 0, 0)
    rows_in = lambda i: (jnp.clip(i, 0, n_dp - 1), 0)
    rows_out = lambda i: (jnp.clip(i - n_dp - n_local, 0, n_dp - 1), 0)
    flat = lambda i: (jnp.clip(i - n_dp, 0, n_local - 1), 0)
    deep = lambda i: (jnp.clip(i - n_dp, 0, n_local - 1), 0, 0)
    total = n_dp * n_local * cap
    return pl.pallas_call(
        functools.partial(experts_kernel, n_dp, n_local, cap, chunk),
        grid=(2 * n_dp + n_local,),
        out_shape=(
            jax.ShapeDtypeStruct((n_dp * slots, width), BF),
            jax.ShapeDtypeStruct((n_dp * slots, width), BF),
            jax.ShapeDtypeStruct((n_local * width * 2, hidden), F32),
            jax.ShapeDtypeStruct((n_local, hidden, width), F32),
        ),
        in_specs=[
            pl.BlockSpec((1, n_local, slots), by_source),
            pl.BlockSpec((1, n_local, slots), by_source),
            pl.BlockSpec((slots, width), rows_in),
            pl.BlockSpec((slots, width), rows_in),
            pl.BlockSpec((width * 2, hidden), flat),
            pl.BlockSpec((1, hidden, width), deep),
        ],
        out_specs=(
            pl.BlockSpec((slots, width), rows_out),
            pl.BlockSpec((slots, width), rows_out),
            pl.BlockSpec((width * 2, hidden), flat),
            pl.BlockSpec((1, hidden, width), deep),
        ),
        scratch_shapes=[
            pltpu.VMEM((n_dp, n_local * cap, slots), BF),
            pltpu.VMEM((n_local, n_dp, cap, width), BF),
            pltpu.VMEM((n_local, n_dp, cap, width), BF),
            pltpu.VMEM((n_local, n_dp, cap, 1), F32),
            pltpu.VMEM((width, 2 * hidden), BF),
        ],
        compiler_params=pltpu.CompilerParams(
            dimension_semantics=("arbitrary",), vmem_limit_bytes=60 << 20
        ),
        cost_estimate=pl.CostEstimate(
            flops=8 * total * slots * width + 18 * total * width * hidden,
            bytes_accessed=8 * n_dp * slots * width + 24 * n_local * width * hidden,
            transcendentals=total * hidden,
        ),
        name="experts",
    )(
        position,
        weights,
        rows,
        table,
        w_gu.reshape(n_local * width * 2, hidden),
        w_down,
    )


def local(
    x_in,
    lengths,
    routes,
    route_w,
    ln1_gain,
    w_zx,
    w_bc,
    w_dt,
    conv_x,
    conv_x_bias,
    conv_bc,
    conv_bc_bias,
    dt_bias,
    a_log,
    d_skip,
    gnorm_gain,
    w_out,
    ln2_gain,
    w_shared_gu,
    w_shared_down,
    w_exp_gu,
    w_exp_down,
    cotangent,
):
    slots, width = x_in.shape
    n_dp = lax.axis_size("dp")
    n_t = lax.axis_size("tensor")
    my_t = lax.axis_index("tensor")
    my_dp = lax.axis_index("dp")
    piece = slots // n_t
    n_local = w_exp_gu.shape[0]
    n_experts = n_dp * n_local
    cap = slots * routes.shape[1] * 4 // (3 * n_experts)
    if cap > slots:
        cap = slots
    heads = dt_bias.shape[0]
    inner = conv_x.shape[1]
    head_size = inner // heads
    state = conv_bc.shape[1] // 2
    full_inner = inner * n_t
    rows = w_zx.shape[0]
    n_sh = w_shared_gu.shape[2]

    dt_at = 2 * inner + 2 * state
    first_width = dt_at + heads + -(dt_at + heads) % 128
    first = jnp.concatenate(
        [
            w_zx.reshape(rows, 2 * inner),
            w_bc,
            w_dt,
            jnp.zeros((rows, first_width - dt_at - heads), F32),
        ],
        axis=1,
    ).astype(BF)
    first = lax.all_gather(first, "dp", axis=0, tiled=True)
    proj_out = lax.all_gather(w_out.astype(BF), "dp", axis=0, tiled=True)
    shared = jnp.concatenate([w_shared_gu.reshape(rows, 2 * n_sh), w_shared_down], axis=1)
    shared = lax.all_gather(shared.astype(BF), "dp", axis=0, tiled=True)
    shared_gu = shared[:, : 2 * n_sh]
    shared_down = shared[:, 2 * n_sh :]

    live = (jnp.arange(slots, dtype=jnp.int32) < lengths[0]).astype(F32)
    g2 = cotangent.astype(F32) * live[:, None]
    g2_low = g2.astype(BF)
    expert_range = jnp.arange(n_experts, dtype=jnp.int32)
    chosen = routes[:, :, None] == expert_range[None, None, :]
    weights = jnp.sum(jnp.where(chosen, route_w[:, :, None], 0.0), axis=1)
    high = weights.astype(BF)
    low = (weights - high.astype(F32)).astype(BF)
    table = jnp.concatenate([g2_low, high, low], axis=1)
    table = lax.dynamic_slice_in_dim(table, my_t * piece, piece, axis=0)
    table = gather_rows(table, n_dp, 1)
    g2_piece = lax.dynamic_slice_in_dim(g2_low, my_t * piece, piece, axis=0)
    high = lax.dynamic_slice_in_dim(table, width + my_dp * n_local, n_local, axis=1)
    low = lax.dynamic_slice_in_dim(table, width + n_experts + my_dp * n_local, n_local, axis=1)
    weights = (high.astype(F32) + low.astype(F32)).reshape(n_dp, slots, n_local)
    member = (weights > 0.0).astype(BF)
    before = (
        jnp.arange(slots)[:, None] > jnp.arange(slots)[None, :]
    ).astype(BF)
    position = dotf("ut,ste->seu", before, member).astype(jnp.int32)
    weights = weights.transpose(0, 2, 1)
    position = jnp.where(weights > 0.0, position, -1)

    x_float = x_in.astype(F32)
    scale_one = rms_scale(x_float)
    normed_one = (x_float * scale_one * ln1_gain).astype(BF)
    firsts = dotf("td,df->tf", normed_one, first)
    zx = firsts[:, : 2 * inner]
    bc_proj = firsts[:, 2 * inner : dt_at]
    dt_proj = firsts[:, dt_at : dt_at + heads]

    gated_mix, mixer_back = mixer_forward(
        zx, bc_proj, dt_proj, conv_x, conv_x_bias, conv_bc, conv_bc_bias, dt_bias, a_log, d_skip
    )
    squares = lax.psum(jnp.sum(gated_mix * gated_mix, axis=-1), "tensor")
    scale_mix = lax.rsqrt(squares / full_inner + EPSILON)[:, None]
    normed_mix = (gated_mix * scale_mix * gnorm_gain).astype(BF)
    mixer_part = dotf("tc,dc->td", normed_mix, proj_out).astype(BF)
    x_piece = lax.dynamic_slice_in_dim(x_in, my_t * piece, piece, axis=0)
    all_rows, hidden_one = middle(mixer_part, x_piece, ln2_gain, n_dp, 2)
    mine = lax.dynamic_slice_in_dim(all_rows, my_dp * slots, slots, axis=0)

    shared_pre = dotf("td,df->tf", mine, shared_gu)
    s_gate, s_up = shared_pre[:, :n_sh], shared_pre[:, n_sh:]
    shared_silu, shared_slope = silu_parts(s_gate)
    shared_act = (shared_silu * s_up).astype(BF)
    grad_shared_act = dotf("td,df->tf", g2_low, shared_down)
    grad_shared_pre = jnp.concatenate(
        [grad_shared_act * s_up * shared_slope, grad_shared_act * shared_silu], axis=1
    ).astype(BF)
    grad_normed_shared = dotf("tf,df->td", grad_shared_pre, shared_gu)
    shared_part = dotf("tf,df->td", shared_act, shared_down)

    dxn_part, out_part, grad_exp_gu, grad_exp_down = experts(
        position, weights, all_rows, table, w_exp_gu, w_exp_down, cap
    )
    grad_exp_gu = grad_exp_gu.reshape(w_exp_gu.shape)

    def add_own(total, own):
        at = my_dp * slots
        own = own + lax.dynamic_slice_in_dim(total, at, slots, axis=0).astype(F32)
        return lax.dynamic_update_slice_in_dim(total, own.astype(BF), at, axis=0)

    dxn_part = add_own(dxn_part, grad_normed_shared)
    out_part = add_own(out_part, shared_part)
    grad_one, sum_ln2, dm = turn(
        dxn_part, hidden_one, g2_piece, ln2_gain, n_dp, 3
    )
    dm = dm.reshape(slots, width)

    ffn_out = scatter_rows(out_part, n_dp, 4)
    layer_out = lax.all_gather(
        (hidden_one + ffn_out).astype(BF), "tensor", axis=0, tiled=True
    )
    grad_shared_down = dotf("td,tf->df", g2_low, shared_act)
    grad_shared_gu = dotf("td,tf->df", mine, grad_shared_pre)

    grad_out_proj = dotf("td,tc->dc", dm, normed_mix)
    grad_normed_mix = dotf("td,dc->tc", dm, proj_out)
    weighted_mix = gnorm_gain * grad_normed_mix
    grad_gnorm = jnp.sum(grad_normed_mix * gated_mix * scale_mix, axis=0)
    product_sum = lax.psum(jnp.sum(weighted_mix * gated_mix, axis=-1), "tensor")[:, None]
    grad_gated = scale_mix * weighted_mix - gated_mix * scale_mix**3 * product_sum / full_inner
    (
        grad_zx,
        grad_bc,
        grad_dt_low,
        grad_conv_x,
        grad_conv_x_bias,
        grad_conv_bc,
        grad_conv_bc_bias,
        grad_dt_bias,
        grad_a_log,
        grad_d_skip,
    ) = mixer_back(grad_gated)
    grad_first = jnp.concatenate(
        [
            grad_zx,
            grad_bc.astype(BF),
            grad_dt_low,
            jnp.zeros((slots, first_width - dt_at - heads), BF),
        ],
        axis=1,
    )
    grad_input_part = dotf("tf,df->td", grad_first, first).astype(BF)
    grad_first_w = dotf("td,tf->df", normed_one, grad_first).astype(BF)
    grad_shared_w = jnp.concatenate([grad_shared_gu, grad_shared_down], axis=1).astype(BF)
    grad_shared_w = lax.psum_scatter(grad_shared_w, "dp", scatter_dimension=0, tiled=True)
    grad_out_w = lax.psum_scatter(
        grad_out_proj.astype(BF), "dp", scatter_dimension=0, tiled=True
    )

    def lanes(*vectors):
        vector = jnp.concatenate([v.reshape(-1) for v in vectors])
        return jnp.pad(vector, (0, -vector.shape[0] % (8 * width))).reshape(-1, width)

    taps = conv_x.shape[0]
    wide = lanes(jnp.zeros((width,), F32), sum_ln2, grad_conv_bc, grad_conv_bc_bias)
    n_wide = wide.shape[0]
    narrow = lanes(
        grad_conv_x, grad_conv_x_bias, grad_gnorm, grad_dt_bias, grad_a_log, grad_d_skip
    )
    first_f, grad_x, sums = tail(
        grad_first_w,
        grad_input_part,
        grad_one,
        x_piece,
        ln1_gain,
        jnp.concatenate([wide, narrow], axis=0),
        n_wide,
        2 * inner,
        2 * state,
        n_dp,
        5,
    )
    first_f = first_f.reshape(rows, first_width)
    grad_x = grad_x.reshape(slots, width).astype(F32)
    wide, narrow = sums[:n_wide].reshape(-1), sums[n_wide:].reshape(-1)
    at = [0]

    def take(vector, *shape):
        size = 1
        for s in shape:
            size *= s
        part = lax.slice_in_dim(vector, at[0], at[0] + size).reshape(shape)
        at[0] += size
        return part

    o_ln1 = take(wide, width)
    o_ln2 = take(wide, width)
    o_conv_bc = take(wide, taps, 2 * state)
    o_conv_bc_bias = take(wide, 2 * state)
    at[0] = 0
    o_conv_x = take(narrow, taps, inner)
    o_conv_x_bias = take(narrow, inner)
    o_gnorm = take(narrow, inner)
    o_dt_bias = take(narrow, heads)
    o_a_log = take(narrow, heads)
    o_d_skip = take(narrow, heads)
    shared_f = grad_shared_w.astype(F32)
    return (
        layer_out,
        grad_x,
        o_ln1,
        first_f[:, : 2 * inner].reshape(rows, 2, inner),
        first_f[:, 2 * inner : dt_at],
        first_f[:, dt_at : dt_at + heads],
        o_conv_x,
        o_conv_x_bias,
        o_conv_bc,
        o_conv_bc_bias,
        o_dt_bias,
        o_a_log,
        o_d_skip,
        o_gnorm,
        grad_out_w.astype(F32),
        o_ln2,
        shared_f[:, : 2 * n_sh].reshape(rows, 2, n_sh),
        shared_f[:, 2 * n_sh :],
        grad_exp_gu,
        grad_exp_down,
    )


def solution(mesh):
    return jax.shard_map(
        local,
        mesh=mesh,
        in_specs=(
            P("dp", None),
            P("dp"),
            P("dp", None),
            P("dp", None),
            P(),
            P("dp", None, "tensor"),
            P("dp", None),
            P("dp", "tensor"),
            P(None, "tensor"),
            P("tensor"),
            P(),
            P(),
            P("tensor"),
            P("tensor"),
            P("tensor"),
            P("tensor"),
            P("dp", "tensor"),
            P(),
            P("dp", None, "tensor"),
            P("dp", "tensor"),
            P("dp", None, None, "tensor"),
            P("dp", "tensor", None),
            P("dp", None),
        ),
        out_specs=(
            P("dp", None),
            P("dp", None),
            P(),
            P("dp", None, "tensor"),
            P("dp", None),
            P("dp", "tensor"),
            P(None, "tensor"),
            P("tensor"),
            P(),
            P(),
            P("tensor"),
            P("tensor"),
            P("tensor"),
            P("tensor"),
            P("dp", "tensor"),
            P(),
            P("dp", None, "tensor"),
            P("dp", "tensor"),
            P("dp", None, None, "tensor"),
            P("dp", "tensor", None),
        ),
        check_vma=False,
    )
```

```python
import functools

import jax
import jax.numpy as jnp
from jax import lax
from jax.experimental import pallas as pl
from jax.experimental.pallas import tpu as pltpu
from jax.sharding import PartitionSpec as P

BLOCK = 256


EPSILON = 1e-05
HIGHEST = lax.Precision.HIGHEST
BF = jnp.bfloat16
F32 = jnp.float32


def rms_scale(values):
    return lax.rsqrt(jnp.mean(values * values, axis=-1, keepdims=True) + EPSILON)


def silu_parts(values):
    sigmoid_val = jax.nn.sigmoid(values)
    return (values * sigmoid_val, sigmoid_val * (1.0 + values * (1.0 - sigmoid_val)))


def round_keep(values):
    return lax.optimization_barrier(values.astype(BF)).astype(F32)


def dotf(spec, a, b):
    return jnp.einsum(spec, a, b, preferred_element_type=F32)


def causal_conv(signal, kernel, offset):
    kernel_width = kernel.shape[0]
    seq_length = signal.shape[0]
    padded = jnp.concatenate(
        [jnp.zeros((kernel_width - 1, signal.shape[1]), signal.dtype), signal], axis=0
    )
    summed = offset[None, :] + kernel[0][None, :] * padded[0:seq_length]
    for tap_index in range(1, kernel_width):
        summed = summed + kernel[tap_index][None, :] * padded[tap_index : tap_index + seq_length]
    return summed


def ssd_scan(head_values, step_sizes, log_rates, b_rows, c_rows, skip_gain, block_rows):
    seq_length, n_heads, head_size = head_values.shape
    n_state = b_rows.shape[1]
    n_blocks = seq_length // block_rows
    decay_rates = -jnp.exp(log_rates)[None, :] * step_sizes
    scaled = (head_values * step_sizes[:, :, None]).reshape(
        n_blocks, block_rows, n_heads, head_size
    )
    cumulative = jnp.cumsum(decay_rates.reshape(n_blocks, block_rows, n_heads), axis=1)
    b_block = b_rows.reshape(n_blocks, block_rows, n_state)
    c_block = c_rows.reshape(n_blocks, block_rows, n_state)
    positions = jnp.arange(block_rows)
    causal = (positions[:, None] >= positions[None, :])[None, :, :, None]
    differences = cumulative[:, :, None, :] - cumulative[:, None, :, :]
    decay_mask = jnp.where(causal, jnp.exp(jnp.where(causal, differences, 0.0)), 0.0)
    intersection = jnp.einsum("kin,kjn->kij", c_block, b_block, precision=HIGHEST)
    within = jnp.einsum("kij,kijh,kjhp->kihp", intersection, decay_mask, scaled, precision=HIGHEST)
    block_end = cumulative[:, -1, :]
    to_end = jnp.exp(block_end[:, None, :] - cumulative)
    states = jnp.einsum("kjn,kjh,kjhp->khnp", b_block, to_end, scaled, precision=HIGHEST)

    def carry_state(previous, inputs):
        block_decay, block_state = inputs
        return (block_decay[:, None, None] * previous + block_state, previous)

    final_state, entering = lax.scan(
        carry_state,
        jnp.zeros((n_heads, n_state, head_size), head_values.dtype),
        (jnp.exp(block_end), states),
    )
    across = jnp.einsum(
        "kin,khnp,kih->kihp", c_block, entering, jnp.exp(cumulative), precision=HIGHEST
    )
    return (within + across).reshape(seq_length, n_heads, head_size) + skip_gain[
        None, :, None
    ] * head_values


def mixer_forward(
    zx, bc_proj, dt_proj, conv_x, conv_x_bias, conv_bc, conv_bc_bias, dt_bias, a_log, d_skip
):
    slots = zx.shape[0]
    inner = conv_x.shape[1]
    heads = dt_bias.shape[0]
    state = conv_bc.shape[1] // 2

    def conv_block(x_part, bc_part, kernel_x, offset_x, kernel_bc, offset_bc):
        return (
            jax.nn.silu(causal_conv(x_part, kernel_x, offset_x)),
            jax.nn.silu(causal_conv(bc_part, kernel_bc, offset_bc)),
        )

    (conv_values, conv_bc_values), conv_back = jax.vjp(
        conv_block, zx[:, inner:], bc_proj, conv_x, conv_x_bias, conv_bc, conv_bc_bias
    )
    head_input = round_keep(conv_values)
    bc_input = round_keep(conv_bc_values)

    def scan_block(head_flat, b_rows, c_rows, dt_part, z_part, dt_offset, log_rates, skip_gain):
        step_sizes = jax.nn.softplus(dt_part + dt_offset[None, :])
        output = ssd_scan(
            head_flat.reshape(slots, heads, inner // heads),
            step_sizes,
            log_rates,
            b_rows,
            c_rows,
            skip_gain,
            BLOCK,
        )
        return output.reshape(slots, inner) * jax.nn.silu(z_part)

    gated_mix, scan_back = jax.vjp(
        scan_block,
        head_input,
        bc_input[:, :state],
        bc_input[:, state:],
        dt_proj,
        zx[:, :inner],
        dt_bias,
        a_log,
        d_skip,
    )

    def mixer_back(grad_gated):
        g_head, g_b, g_c, g_dt, g_z, g_dt_bias, g_a_log, g_d_skip = scan_back(grad_gated)
        g_xs, g_bc, g_cx, g_cxb, g_cbc, g_cbcb = conv_back(
            (g_head, jnp.concatenate([g_b, g_c], axis=1))
        )
        g_zx = jnp.concatenate([g_z, g_xs], axis=1).astype(BF)
        return (
            g_zx, g_bc, g_dt.astype(BF), g_cx, g_cxb, g_cbc, g_cbcb, g_dt_bias, g_a_log, g_d_skip
        )

    return gated_mix, mixer_back


MESH = pl.DeviceIdType.MESH
DMA = pltpu.SemaphoreType.DMA
VMEM_SPEC = pl.BlockSpec(memory_space=pltpu.VMEM)
ANY_SPEC = pl.BlockSpec(memory_space=pl.ANY)


def place():
    d = lax.axis_index("dp")
    t = lax.axis_index("tensor")
    return d // 2, d % 2, t // 2, t % 2


def device(hi, lo, th, tl):
    return (hi * 2 + lo, th * 2 + tl)


def greet(n_hi, tensor=True):
    hi, lo, th, tl = place()
    barrier = pltpu.get_barrier_semaphore()
    others = [device(lax.rem(hi + k, n_hi), lo, th, tl) for k in range(1, n_hi)]
    others += [device(hi, 1 - lo, th, tl)]
    if tensor:
        others += [device(hi, lo, 1 - th, tl), device(hi, lo, th, 1 - tl)]
    for other in others:
        pl.semaphore_signal(barrier, inc=1, device_id=other, device_id_type=MESH)
    pl.semaphore_wait(barrier, len(others))


def remote(src, dst, ssem, rsem, to):
    return pltpu.make_async_remote_copy(
        src_ref=src, dst_ref=dst, send_sem=ssem, recv_sem=rsem, device_id=to, device_id_type=MESH
    )


class Sends:
    def __init__(self):
        self.copies = []

    def push(self, src, dst, ssem, rsem, to):
        copy = remote(src, dst, ssem, rsem, to)
        copy.start()
        self.copies.append(copy)

    def finish(self):
        for copy in self.copies:
            copy.wait_send()


def arrive(dst, ssem, rsem, to):
    remote(dst, dst, ssem, rsem, to).wait_recv()


TENSOR_SUM_SCRATCH = lambda rows, width, dtype: [
    pltpu.VMEM((2, rows, width), dtype),
    pltpu.VMEM((rows, width), dtype),
    DMA((3,)),
    DMA((3,)),
]


def tensor_sum_start(sends, part_ref, got_c, ssem, rsem):
    hi, lo, th, tl = place()
    to_c = device(hi, lo, th, 1 - tl)
    for j, y in enumerate((1 - th, th)):
        sends.push(part_ref.at[y * 2 + 1 - tl], got_c.at[j], ssem.at[j], rsem.at[j], to_c)


def tensor_sum_middle(sends, part_ref, got_c, got_y, ssem, rsem):
    hi, lo, th, tl = place()
    arrive(got_c.at[0], ssem.at[0], rsem.at[0], device(hi, lo, th, 1 - tl))
    total = part_ref[(1 - th) * 2 + tl].astype(F32) + got_c[0].astype(F32)
    got_c[0] = total.astype(got_c.dtype)
    sends.push(got_c.at[0], got_y, ssem.at[2], rsem.at[2], device(hi, lo, 1 - th, tl))


def tensor_sum_end(part_ref, got_c, got_y, ssem, rsem):
    hi, lo, th, tl = place()
    arrive(got_c.at[1], ssem.at[1], rsem.at[1], device(hi, lo, th, 1 - tl))
    total = part_ref[th * 2 + tl].astype(F32) + got_c[1].astype(F32)
    arrive(got_y, ssem.at[2], rsem.at[2], device(hi, lo, 1 - th, tl))
    return total + got_y[...].astype(F32)


def tensor_spread_start(sends, o_ref, ssem, rsem):
    hi, lo, th, tl = place()
    own = o_ref.at[th * 2 + tl]
    sends.push(own, own, ssem.at[0], rsem.at[0], device(hi, lo, 1 - th, tl))
    sends.push(own, own, ssem.at[1], rsem.at[1], device(hi, lo, th, 1 - tl))


def tensor_spread_end(sends, o_ref, ssem, rsem):
    hi, lo, th, tl = place()
    other = o_ref.at[(1 - th) * 2 + tl]
    to_c = device(hi, lo, th, 1 - tl)
    arrive(other, ssem.at[0], rsem.at[0], device(hi, lo, 1 - th, tl))
    sends.push(other, other, ssem.at[2], rsem.at[2], to_c)
    arrive(o_ref.at[th * 2 + 1 - tl], ssem.at[1], rsem.at[1], to_c)
    arrive(o_ref.at[(1 - th) * 2 + 1 - tl], ssem.at[2], rsem.at[2], to_c)


def gather_steps(n_hi, x_ref, o_ref, own_sem, send_sem, recv_sem):
    hi, lo, th, tl = place()
    rows = x_ref.shape[0]
    half = rows // 2
    own_block = (hi * 2 + lo) * 4 + th * 2 + tl
    own = pltpu.make_async_copy(x_ref, o_ref.at[pl.ds(own_block * rows, rows)], own_sem)
    own.start()
    sends = Sends()

    def slot(k, f, s, c):
        return ((c * 2 + s) * 2 + f) * n_hi + k

    def where(h, k, f, s, c):
        kk = lax.rem(hi + k, n_hi)
        l = 1 - lo if (f if h == 0 else s) else lo
        y = 1 - th if (s if h == 0 else f) else th
        z = 1 - tl if c else tl
        return ((kk * 2 + l) * 4 + y * 2 + z) * rows + h * half

    def push(h, k, f, s, c, step):
        at = where(h, k, f, s, c)
        if k == 0 and not (f or s or c):
            src = x_ref.at[pl.ds(h * half, half)]
        else:
            src = o_ref.at[pl.ds(at, half)]
        if step == "c":
            to, r = device(hi, lo, th, 1 - tl), slot(k, f, s, 1)
        elif step == "s":
            to = device(hi, lo, 1 - th, tl) if h == 0 else device(hi, 1 - lo, th, tl)
            r = slot(k, f, 1, 0)
        elif step == "f":
            to = device(hi, 1 - lo, th, tl) if h == 0 else device(hi, lo, 1 - th, tl)
            r = slot(k, 1, 0, 0)
        else:
            to, r = device(lax.rem(hi + step, n_hi), lo, th, tl), slot(n_hi - step, 0, 0, 0)
        sends.push(src, o_ref.at[pl.ds(at, half)], send_sem.at[h, r], recv_sem.at[h, r], to)

    def got(h, k, f, s, c):
        r = slot(k, f, s, c)
        arrive(
            o_ref.at[pl.ds(where(h, k, f, s, c), half)],
            send_sem.at[h, r], recv_sem.at[h, r], device(hi, lo, th, 1 - tl),
        )

    for k in range(1, n_hi):
        for h in range(2):
            push(h, 0, 0, 0, 0, k)
    for k in range(n_hi):
        for h in range(2):
            if k:
                got(h, k, 0, 0, 0)
            for step in ("f", "s", "c"):
                push(h, k, 0, 0, 0, step)
        yield
        for h in range(2):
            got(h, k, 1, 0, 0)
            for step in ("s", "c"):
                push(h, k, 1, 0, 0, step)
        yield
    for k in range(n_hi):
        for f in range(2):
            for h in range(2):
                got(h, k, f, 1, 0)
                push(h, k, f, 1, 0, "c")
        yield
    for k in range(n_hi):
        for f in range(2):
            for s in range(2):
                for h in range(2):
                    got(h, k, f, s, 1)
    own.wait()
    sends.finish()


def in_turns(*streams):
    live = list(streams)
    while live:
        for stream in list(live):
            if next(stream, True) is True:
                live.remove(stream)


def middle_kernel(
    n_hi, part_ref, x_ref, gain_ref, table_ref, o_ref, all_table_ref, hidden_ref,
    normed, got_c, got_y, t_send, t_recv, *sems,
):
    greet(n_hi)
    sends = Sends()
    tensor_sum_start(sends, part_ref, got_c, t_send, t_recv)
    tables = gather_steps(n_hi, table_ref, all_table_ref, *sems[:3])
    next(tables)
    tensor_sum_middle(sends, part_ref, got_c, got_y, t_send, t_recv)
    hidden = x_ref[...].astype(F32) + tensor_sum_end(part_ref, got_c, got_y, t_send, t_recv)
    hidden_ref[...] = hidden
    normed[...] = (hidden * rms_scale(hidden) * gain_ref[...]).astype(normed.dtype)
    in_turns(gather_steps(n_hi, normed, o_ref, *sems[3:]), tables)
    sends.finish()


def middle(part, x_piece, gain, table, n_dp, collective_id):
    rows, width = x_piece.shape
    n_hi = n_dp // 2
    gather_sems = [DMA, DMA((2, 8 * n_hi)), DMA((2, 8 * n_hi))]
    return pl.pallas_call(
        functools.partial(middle_kernel, n_hi),
        out_shape=(
            jax.ShapeDtypeStruct((n_dp * 4 * rows, width), part.dtype),
            jax.ShapeDtypeStruct((n_dp * 4 * rows, table.shape[1]), table.dtype),
            jax.ShapeDtypeStruct((rows, width), F32),
        ),
        in_specs=[VMEM_SPEC] * 3 + [ANY_SPEC],
        out_specs=(ANY_SPEC, ANY_SPEC, VMEM_SPEC),
        scratch_shapes=[pltpu.VMEM((rows, width), part.dtype)]
        + TENSOR_SUM_SCRATCH(rows, width, part.dtype)
        + gather_sems
        + gather_sems,
        compiler_params=pltpu.CompilerParams(collective_id=collective_id, has_side_effects=True),
        name="middle",
    )(part.reshape(4, rows, width), x_piece, gain.reshape(1, width), table)


def start_kernel(n_hi, n, *refs):
    ins, outs, sems = refs[:n], refs[n : 2 * n], refs[2 * n :]
    hi, lo, th, tl = place()
    to_f = device(hi, 1 - lo, th, tl)
    greet(n_hi, tensor=False)
    sends = Sends()
    own = []

    def at(k, l):
        return lax.rem(hi + k, n_hi) * 2 + l

    for w_ref, o_ref, (own_sem, send_h, recv_h, send_f, recv_f) in zip(
        ins, outs, [sems[5 * i : 5 * i + 5] for i in range(n)]
    ):
        for h in range(2):
            for k in range(1, n_hi):
                sends.push(
                    w_ref.at[h], o_ref.at[at(0, lo), h], send_h.at[h, k - 1], recv_h.at[h, n_hi - k - 1],
                    device(lax.rem(hi + k, n_hi), lo, th, tl),
                )
            sends.push(w_ref.at[h], o_ref.at[at(0, lo), h], send_f.at[h, 0], recv_f.at[h, 0], to_f)
        copy = pltpu.make_async_copy(w_ref, o_ref.at[at(0, lo)], own_sem)
        copy.start()
        own.append(copy)
    for o_ref, (own_sem, send_h, recv_h, send_f, recv_f) in zip(
        outs, [sems[5 * i : 5 * i + 5] for i in range(n)]
    ):
        for k in range(1, n_hi):
            for h in range(2):
                view = o_ref.at[at(k, lo), h]
                arrive(view, send_h.at[h, k - 1], recv_h.at[h, k - 1], to_f)
                sends.push(view, view, send_f.at[h, k], recv_f.at[h, k], to_f)
    for o_ref, (own_sem, send_h, recv_h, send_f, recv_f) in zip(
        outs, [sems[5 * i : 5 * i + 5] for i in range(n)]
    ):
        for k in range(n_hi):
            for h in range(2):
                arrive(o_ref.at[at(k, 1 - lo), h], send_f.at[h, k], recv_f.at[h, k], to_f)
    for copy in own:
        copy.wait()
    sends.finish()


def start(weights, n_dp, collective_id):
    n_hi = n_dp // 2
    n = len(weights)
    half = weights[0].shape[0] // 2
    outs = pl.pallas_call(
        functools.partial(start_kernel, n_hi, n),
        out_shape=[jax.ShapeDtypeStruct((n_dp, 2, half, w.shape[1]), w.dtype) for w in weights],
        in_specs=[ANY_SPEC] * n,
        out_specs=[ANY_SPEC] * n,
        scratch_shapes=[
            DMA,
            DMA((2, n_hi - 1)), DMA((2, n_hi - 1)),
            DMA((2, n_hi)), DMA((2, n_hi)),
        ] * n,
        compiler_params=pltpu.CompilerParams(collective_id=collective_id, has_side_effects=True),
        name="start",
    )(*[w.reshape(2, half, w.shape[1]) for w in weights])
    return [o.reshape(n_dp * 2 * half, o.shape[3]) for o in outs]


def scatter_steps(n_hi, sends, p_ref, o_ref, bufs):
    (stage, from_c, from_f, from_s, from_h,
     stage_sem, send_c, recv_c, send_f, recv_f, send_s, recv_s, send_h, recv_h) = bufs
    depth = stage.shape[0]
    hi, lo, th, tl = place()
    to_c = device(hi, lo, th, 1 - tl)
    rows = o_ref.shape[0]
    half = rows // 2

    def where(h, k, f, s, c):
        kk = lax.rem(hi + k, n_hi)
        l = 1 - lo if (f if h == 1 else s) else lo
        y = 1 - th if (s if h == 1 else f) else th
        z = 1 - tl if c else tl
        return ((kk * 2 + l) * 4 + y * 2 + z) * rows + h * half

    ks = list(range(1, n_hi)) + [0]
    order = []
    for i in range(n_hi + 2):
        for lag, groups in ((0, ((1, 1), (1, 0))), (1, ((0, 1),)), (2, ((0, 0),))):
            if 0 <= i - lag < n_hi:
                order += [(f, s, ks[i - lag], h) for f, s in groups for h in range(2)]

    def slot(f, s, k):
        return (f * 2 + s) * n_hi + k

    def first(h):
        return device(hi, lo, 1 - th, tl) if h == 0 else device(hi, 1 - lo, th, tl)

    def second(h):
        return device(hi, 1 - lo, th, tl) if h == 0 else device(hi, lo, 1 - th, tl)

    for f, s, k, h in order:
        n = slot(f, s, k)
        sends.push(
            p_ref.at[pl.ds(where(h, k, f, s, 1), half)], from_c.at[h, n], send_c.at[h, n],
            recv_c.at[h, n], to_c,
        )

    def load(i):
        f, s, k, h = order[i]
        return pltpu.make_async_copy(
            p_ref.at[pl.ds(where(h, k, f, s, 0), half)], stage.at[i % depth], stage_sem.at[i % depth]
        )

    for i in range(depth - 1):
        load(i).start()
    for i, (f, s, k, h) in enumerate(order):
        if i + depth - 1 < len(order):
            load(i + depth - 1).start()
        load(i).wait()
        n = slot(f, s, k)
        arrive(from_c.at[h, n], send_c.at[h, n], recv_c.at[h, n], to_c)
        total = stage[i % depth].astype(F32) + from_c[h, n].astype(F32)
        if f == 0:
            m = s * n_hi + k
            arrive(from_f.at[h, m], send_f.at[h, m], recv_f.at[h, m], to_c)
            total = total + from_f[h, m].astype(F32)
        if f == 0 and s == 0:
            arrive(from_s.at[h, k], send_s.at[h, k], recv_s.at[h, k], to_c)
            total = total + from_s[h, k].astype(F32)
        if f == 0 and s == 0 and k == 0:
            for j in range(n_hi - 1):
                arrive(from_h.at[h, j], send_h.at[h, j], recv_h.at[h, j], to_c)
                total = total + from_h[h, j].astype(F32)
            o_ref[pl.ds(h * half, half), :] = total
            continue
        from_c[h, n] = total.astype(from_c.dtype)
        src = from_c.at[h, n]
        if f == 1:
            m = s * n_hi + k
            sends.push(src, from_f.at[h, m], send_f.at[h, m], recv_f.at[h, m], first(h))
        elif s == 1:
            sends.push(src, from_s.at[h, k], send_s.at[h, k], recv_s.at[h, k], second(h))
        else:
            j = n_hi - k - 1
            sends.push(
                src, from_h.at[h, j], send_h.at[h, j], recv_h.at[h, j],
                device(lax.rem(hi + k, n_hi), lo, th, tl),
            )


def scatter_scratch(n_hi, half, width, dtype, depth=4):
    return [
        pltpu.VMEM((depth, half, width), dtype),
        pltpu.VMEM((2, 4 * n_hi, half, width), dtype),
        pltpu.VMEM((2, 2 * n_hi, half, width), dtype),
        pltpu.VMEM((2, n_hi, half, width), dtype),
        pltpu.VMEM((2, n_hi - 1, half, width), dtype),
        DMA((depth,)),
        DMA((2, 4 * n_hi)), DMA((2, 4 * n_hi)),
        DMA((2, 2 * n_hi)), DMA((2, 2 * n_hi)),
        DMA((2, n_hi)), DMA((2, n_hi)),
        DMA((2, n_hi - 1)), DMA((2, n_hi - 1)),
    ]


def scatter_kernel(n_hi, p_ref, o_ref, *bufs):
    greet(n_hi)
    sends = Sends()
    scatter_steps(n_hi, sends, p_ref, o_ref, bufs)
    sends.finish()


def scatter_rows(p, n_dp, collective_id):
    width = p.shape[1]
    rows = p.shape[0] // (n_dp * 4)
    n_hi = n_dp // 2
    return pl.pallas_call(
        functools.partial(scatter_kernel, n_hi),
        out_shape=jax.ShapeDtypeStruct((rows, width), F32),
        in_specs=[ANY_SPEC],
        out_specs=VMEM_SPEC,
        scratch_shapes=scatter_scratch(n_hi, rows // 2, width, p.dtype),
        compiler_params=pltpu.CompilerParams(
            collective_id=collective_id, has_side_effects=True, vmem_limit_bytes=60 << 20
        ),
        name="scatter_rows",
    )(p)


def turn_kernel(
    n_hi, p_ref, hidden_ref, g2_ref, gain_ref, grad_ref, sum_ref, dm_ref, total_ref, sp_send, sp_recv, *bufs
):
    hi, lo, th, tl = place()
    greet(n_hi)
    sends = Sends()
    scatter_steps(n_hi, sends, p_ref, total_ref, bufs)
    grad = total_ref[...]
    hidden = hidden_ref[...]
    scale = rms_scale(hidden)
    weighted = gain_ref[...] * grad
    sum_ref[...] = jnp.sum(grad * hidden * scale, axis=0, keepdims=True)
    mean = jnp.mean(weighted * hidden, axis=-1, keepdims=True)
    grad = g2_ref[...].astype(F32) + scale * weighted - hidden * (scale * scale * scale) * mean
    grad_ref[...] = grad
    dm_ref[th * 2 + tl] = grad.astype(dm_ref.dtype)
    tensor_spread_start(sends, dm_ref, sp_send, sp_recv)
    tensor_spread_end(sends, dm_ref, sp_send, sp_recv)
    sends.finish()


def turn(p, hidden, g2_piece, gain, n_dp, collective_id):
    rows, width = hidden.shape
    n_hi = n_dp // 2
    return pl.pallas_call(
        functools.partial(turn_kernel, n_hi),
        out_shape=(
            jax.ShapeDtypeStruct((rows, width), F32),
            jax.ShapeDtypeStruct((1, width), F32),
            jax.ShapeDtypeStruct((4, rows, width), p.dtype),
        ),
        in_specs=[ANY_SPEC] + [VMEM_SPEC] * 3,
        out_specs=(VMEM_SPEC,) * 3,
        scratch_shapes=[pltpu.VMEM((rows, width), F32), DMA((3,)), DMA((3,))]
        + scatter_scratch(n_hi, rows // 2, width, p.dtype),
        compiler_params=pltpu.CompilerParams(
            collective_id=collective_id, has_side_effects=True, vmem_limit_bytes=60 << 20
        ),
        name="turn",
    )(p, hidden, g2_piece, gain.reshape(1, width))


def tail_kernel(n_hi, wide, bc_at, n, *refs):
    part_ref, grad_ref, x_ref, gain_ref, small_ref = refs[:5]
    w_refs = refs[5 : 5 + n]
    ox_ref, os_ref = refs[5 + n : 7 + n]
    ow_refs = refs[7 + n : 7 + 2 * n]
    (got_c, got_y, t_send, t_recv, sp_send, sp_recv,
     small, small_f, small_h, small_t, sm_send, sm_recv, smh_send, smh_recv,
     bc_own, bc_got, bc_send, bc_recv) = refs[7 + 2 * n : 25 + 2 * n]
    rest = refs[25 + 2 * n :]
    bufs = [rest[8 * i : 8 * i + 8] for i in range(n)]
    hi, lo, th, tl = place()
    to_f, to_y, to_c = device(hi, 1 - lo, th, tl), device(hi, lo, 1 - th, tl), device(hi, lo, th, 1 - tl)
    greet(n_hi)
    sends = Sends()
    order = [(k, h) for k in list(range(1, n_hi)) + [0] for h in range(2)]

    def owner(k, l):
        return lax.rem(hi + k, n_hi) * 2 + l

    for w_ref, (stage, from_f, from_h, stage_sem, send_f, recv_f, send_h, recv_h) in zip(w_refs, bufs):
        for k, h in order:
            sends.push(
                w_ref.at[owner(k, 1 - lo), h], from_f.at[h, k], send_f.at[h, k], recv_f.at[h, k], to_f
            )
    loads = []
    for w_ref, (stage, from_f, from_h, stage_sem, send_f, recv_f, send_h, recv_h) in zip(w_refs, bufs):
        for k, h in order:
            copy = pltpu.make_async_copy(w_ref.at[owner(k, lo), h], stage.at[h, k], stage_sem.at[h, k])
            copy.start()
            loads.append(copy)
    tensor_sum_start(sends, part_ref, got_c, t_send, t_recv)
    tensor_sum_middle(sends, part_ref, got_c, got_y, t_send, t_recv)
    grad = tensor_sum_end(part_ref, got_c, got_y, t_send, t_recv)
    x = x_ref[...].astype(F32)
    scale = rms_scale(x)
    weighted = gain_ref[...] * grad
    mean = jnp.mean(weighted * x, axis=-1, keepdims=True)
    ox_ref[th * 2 + tl] = (
        grad_ref[...] + scale * weighted - x * (scale * scale * scale) * mean
    ).astype(ox_ref.dtype)
    tensor_spread_start(sends, ox_ref, sp_send, sp_recv)
    small[...] = small_ref[...]
    small[0:1, :] = jnp.sum(grad * x * scale, axis=0, keepdims=True)
    sends.push(small, small_f, sm_send.at[0], sm_recv.at[0], to_f)

    events = [(w, k, h) for w in range(n) for k, h in order]
    for i, (w, k, h) in enumerate(events):
        if k == 0:
            continue
        stage, from_f, from_h, stage_sem, send_f, recv_f, send_h, recv_h = bufs[w]
        loads[i].wait()
        arrive(from_f.at[h, k], send_f.at[h, k], recv_f.at[h, k], to_c)
        from_f[h, k] = (stage[h, k].astype(F32) + from_f[h, k].astype(F32)).astype(from_f.dtype)
        j = n_hi - k - 1
        sends.push(
            from_f.at[h, k], from_h.at[h, j], send_h.at[h, j], recv_h.at[h, j],
            device(lax.rem(hi + k, n_hi), lo, th, tl),
        )
        if i == 0:
            tensor_spread_end(sends, ox_ref, sp_send, sp_recv)
        if i == 1:
            arrive(small_f, sm_send.at[0], sm_recv.at[0], to_c)
            small_h[hi] = small[...] + small_f[...]
            for q in range(1, n_hi):
                sends.push(
                    small_h.at[hi], small_h.at[hi], smh_send.at[q - 1], smh_recv.at[q - 1],
                    device(lax.rem(hi + q, n_hi), lo, th, tl),
                )
    for q in range(1, n_hi):
        arrive(small_h.at[lax.rem(hi - q + n_hi, n_hi)], smh_send.at[q - 1], smh_recv.at[q - 1], to_c)
    total = small_h[0]
    for q in range(1, n_hi):
        total = total + small_h[q]
    os_ref[...] = total
    sends.push(os_ref.at[pl.ds(0, wide)], small_t.at[0], sm_send.at[1], sm_recv.at[1], to_c)
    for i, (w, k, h) in enumerate(events):
        if k:
            continue
        stage, from_f, from_h, stage_sem, send_f, recv_f, send_h, recv_h = bufs[w]
        loads[i].wait()
        arrive(from_f.at[h, 0], send_f.at[h, 0], recv_f.at[h, 0], to_c)
        total = stage[h, 0].astype(F32) + from_f[h, 0].astype(F32)
        for j in range(n_hi - 1):
            arrive(from_h.at[h, j], send_h.at[h, j], recv_h.at[h, j], to_c)
            total = total + from_h[h, j].astype(F32)
        ow_refs[w][h] = total
        if w == 0:
            bc_own[0, h] = total[:, bc_at : bc_at + bc_own.shape[3]].astype(bc_own.dtype)
            if h == 1:
                sends.push(bc_own.at[0], bc_got.at[0], bc_send.at[0], bc_recv.at[0], to_c)
                arrive(small_t.at[0], sm_send.at[1], sm_recv.at[1], to_c)
                small_t[2] = os_ref[pl.ds(0, wide), :] + small_t[0]
                sends.push(small_t.at[2], small_t.at[1], sm_send.at[2], sm_recv.at[2], to_y)
                arrive(bc_got.at[0], bc_send.at[0], bc_recv.at[0], to_c)
                bc_own[1] = (bc_own[0].astype(F32) + bc_got[0].astype(F32)).astype(bc_own.dtype)
                sends.push(bc_own.at[1], bc_got.at[1], bc_send.at[1], bc_recv.at[1], to_y)
    arrive(small_t.at[1], sm_send.at[2], sm_recv.at[2], to_c)
    arrive(bc_got.at[1], bc_send.at[1], bc_recv.at[1], to_c)
    for h in range(2):
        ow_refs[0][h, :, bc_at : bc_at + bc_own.shape[3]] = (
            bc_own[1, h].astype(F32) + bc_got[1, h].astype(F32)
        )
    sends.finish()
    os_ref[pl.ds(0, wide), :] = small_t[2] + small_t[1]


def tail(weights, part, grad_one, x_piece, gain, small, wide, bc_at, bc_width, n_dp, collective_id):
    rows, width = x_piece.shape
    n_hi = n_dp // 2
    n = len(weights)
    half = weights[0].shape[0] // (2 * n_dp)
    dt = weights[0].dtype
    scratch = TENSOR_SUM_SCRATCH(rows, width, part.dtype) + [
        DMA((3,)), DMA((3,)),
        pltpu.VMEM(small.shape, F32),
        pltpu.VMEM(small.shape, F32),
        pltpu.VMEM((n_hi,) + small.shape, F32),
        pltpu.VMEM((3, wide, small.shape[1]), F32),
        DMA((3,)), DMA((3,)),
        DMA((n_hi - 1,)), DMA((n_hi - 1,)),
        pltpu.VMEM((2, 2, half, bc_width), dt),
        pltpu.VMEM((2, 2, half, bc_width), dt),
        DMA((2,)), DMA((2,)),
    ]
    for w in weights:
        scratch += [
            pltpu.VMEM((2, n_hi, half, w.shape[1]), dt),
            pltpu.VMEM((2, n_hi, half, w.shape[1]), dt),
            pltpu.VMEM((2, n_hi - 1, half, w.shape[1]), dt),
            DMA((2, n_hi)),
            DMA((2, n_hi)), DMA((2, n_hi)),
            DMA((2, n_hi - 1)), DMA((2, n_hi - 1)),
        ]
    outs = pl.pallas_call(
        functools.partial(tail_kernel, n_hi, wide, bc_at, n),
        out_shape=[
            jax.ShapeDtypeStruct((4, rows, width), dt),
            jax.ShapeDtypeStruct(small.shape, F32),
        ] + [jax.ShapeDtypeStruct((2, half, w.shape[1]), F32) for w in weights],
        in_specs=[VMEM_SPEC] * 5 + [ANY_SPEC] * n,
        out_specs=[VMEM_SPEC] * (2 + n),
        scratch_shapes=scratch,
        compiler_params=pltpu.CompilerParams(
            collective_id=collective_id, has_side_effects=True, vmem_limit_bytes=60 << 20
        ),
        name="tail",
    )(
        part.reshape(4, rows, width), grad_one, x_piece, gain.reshape(1, width), small,
        *[w.reshape(n_dp, 2, half, w.shape[1]) for w in weights],
    )
    return outs[0], outs[1], [o.reshape(2 * half, o.shape[2]) for o in outs[2:]]


def dot_mm(a, b):
    return lax.dot_general(a, b, (((1,), (0,)), ((), ())), preferred_element_type=F32)


def dot_nt(a, b):
    return lax.dot_general(a, b, (((1,), (1,)), ((), ())), preferred_element_type=F32)


def dot_tn(a, b):
    return lax.dot_general(a, b, (((0,), (0,)), ((), ())), preferred_element_type=F32)


def experts_kernel(
    n_dp, n_local, cap, chunk, pos_ref, wt_ref, x_ref, g_ref, gu_ref, dn_ref,
    dxn_ref, out_ref, ggu_ref, gdn_ref, pick, xr, q, sw, gu,
):
    step = pl.program_id(0)
    width = x_ref.shape[1]
    hidden = dn_ref.shape[1]
    slots = x_ref.shape[0]
    columns = [pl.ds(c, chunk) for c in range(0, width, chunk)]

    @pl.when(step < n_dp)
    def _():
        s = step
        lane = lax.broadcasted_iota(jnp.int32, (cap, slots), 0)
        for e in range(n_local):
            hit = lane == pos_ref[0, e : e + 1, :]
            pick[s, e * cap : (e + 1) * cap, :] = jnp.where(hit, 1.0, 0.0).astype(BF)
            sw[e, s] = jnp.sum(jnp.where(hit, wt_ref[0, e : e + 1, :], 0.0), axis=1, keepdims=True)
        chosen = pick[s]
        for c in columns:
            rows = dot_mm(chosen, x_ref[:, c]).astype(BF)
            grads = dot_mm(chosen, g_ref[:, c])
            for e in range(n_local):
                xr[e, s, :, c] = rows[e * cap : (e + 1) * cap]
                q[e, s, :, c] = (grads[e * cap : (e + 1) * cap] * sw[e, s]).astype(BF)

    @pl.when(jnp.logical_and(step >= n_dp, step < n_dp + n_local))
    def _():
        e = step - n_dp
        gu[:, :hidden] = gu_ref[pl.ds(0, width, stride=2), :].astype(BF)
        gu[:, hidden:] = gu_ref[pl.ds(1, width, stride=2), :].astype(BF)
        down = dn_ref[0].astype(BF)
        x = xr[e].reshape(n_dp * cap, width)
        qe = q[e].reshape(n_dp * cap, width)
        pre = dot_mm(x, gu[...])
        grad_act = dot_nt(qe, down)
        gate, up = pre[:, :hidden], pre[:, hidden:]
        sig = 1.0 / (1.0 + jnp.exp(-gate))
        act_silu = gate * sig
        slope = sig * (1.0 + gate * (1.0 - sig))
        value = act_silu * up
        act = value.astype(BF)
        scaled = (value * sw[e].reshape(n_dp * cap, 1)).astype(BF)
        grad_pre = jnp.concatenate([grad_act * up * slope, grad_act * act_silu], axis=1).astype(BF)
        ggu = dot_tn(x, grad_pre)
        ggu_ref[pl.ds(0, width, stride=2), :] = ggu[:, :hidden]
        ggu_ref[pl.ds(1, width, stride=2), :] = ggu[:, hidden:]
        gdn_ref[0] = dot_tn(act, qe)
        for c in columns:
            xr[e, :, :, c] = dot_nt(grad_pre, gu[c, :]).astype(BF).reshape(n_dp, cap, chunk)
            q[e, :, :, c] = dot_mm(scaled, down[:, c.start : c.start + chunk]).astype(BF).reshape(n_dp, cap, chunk)

    @pl.when(step >= n_dp + n_local)
    def _():
        s = step - n_dp - n_local
        chosen = pick[s]
        for c in columns:
            dxn_ref[:, c] = dot_tn(chosen, xr[:, s, :, c].reshape(n_local * cap, chunk)).astype(BF)
            out_ref[:, c] = dot_tn(chosen, q[:, s, :, c].reshape(n_local * cap, chunk)).astype(BF)


def experts(position, weights, rows, table, w_gu, w_down, cap):
    n_dp, n_local, slots = position.shape
    width = rows.shape[1]
    hidden = w_down.shape[1]
    chunk = width // 3 if width % 384 == 0 else width
    by_source = lambda i: (jnp.clip(i, 0, n_dp - 1), 0, 0)
    rows_in = lambda i: (jnp.clip(i, 0, n_dp - 1), 0)
    rows_out = lambda i: (jnp.clip(i - n_dp - n_local, 0, n_dp - 1), 0)
    flat = lambda i: (jnp.clip(i - n_dp, 0, n_local - 1), 0)
    deep = lambda i: (jnp.clip(i - n_dp, 0, n_local - 1), 0, 0)
    total = n_dp * n_local * cap
    return pl.pallas_call(
        functools.partial(experts_kernel, n_dp, n_local, cap, chunk),
        grid=(2 * n_dp + n_local,),
        out_shape=(
            jax.ShapeDtypeStruct((n_dp * slots, width), BF),
            jax.ShapeDtypeStruct((n_dp * slots, width), BF),
            jax.ShapeDtypeStruct((n_local * width * 2, hidden), F32),
            jax.ShapeDtypeStruct((n_local, hidden, width), F32),
        ),
        in_specs=[
            pl.BlockSpec((1, n_local, slots), by_source),
            pl.BlockSpec((1, n_local, slots), by_source),
            pl.BlockSpec((slots, width), rows_in),
            pl.BlockSpec((slots, width), rows_in),
            pl.BlockSpec((width * 2, hidden), flat),
            pl.BlockSpec((1, hidden, width), deep),
        ],
        out_specs=(
            pl.BlockSpec((slots, width), rows_out),
            pl.BlockSpec((slots, width), rows_out),
            pl.BlockSpec((width * 2, hidden), flat),
            pl.BlockSpec((1, hidden, width), deep),
        ),
        scratch_shapes=[
            pltpu.VMEM((n_dp, n_local * cap, slots), BF),
            pltpu.VMEM((n_local, n_dp, cap, width), BF),
            pltpu.VMEM((n_local, n_dp, cap, width), BF),
            pltpu.VMEM((n_local, n_dp, cap, 1), F32),
            pltpu.VMEM((width, 2 * hidden), BF),
        ],
        compiler_params=pltpu.CompilerParams(
            dimension_semantics=("arbitrary",), vmem_limit_bytes=60 << 20
        ),
        cost_estimate=pl.CostEstimate(
            flops=8 * total * slots * width + 18 * total * width * hidden,
            bytes_accessed=8 * n_dp * slots * width + 24 * n_local * width * hidden,
            transcendentals=total * hidden,
        ),
        name="experts",
    )(
        position,
        weights,
        rows,
        table,
        w_gu.reshape(n_local * width * 2, hidden),
        w_down,
    )


def local(
    x_in,
    lengths,
    routes,
    route_w,
    ln1_gain,
    w_zx,
    w_bc,
    w_dt,
    conv_x,
    conv_x_bias,
    conv_bc,
    conv_bc_bias,
    dt_bias,
    a_log,
    d_skip,
    gnorm_gain,
    w_out,
    ln2_gain,
    w_shared_gu,
    w_shared_down,
    w_exp_gu,
    w_exp_down,
    cotangent,
):
    slots, width = x_in.shape
    n_dp = lax.axis_size("dp")
    n_t = lax.axis_size("tensor")
    my_t = lax.axis_index("tensor")
    my_dp = lax.axis_index("dp")
    piece = slots // n_t
    n_local = w_exp_gu.shape[0]
    n_experts = n_dp * n_local
    cap = slots * routes.shape[1] * 4 // (3 * n_experts)
    if cap > slots:
        cap = slots
    heads = dt_bias.shape[0]
    inner = conv_x.shape[1]
    head_size = inner // heads
    state = conv_bc.shape[1] // 2
    full_inner = inner * n_t
    rows = w_zx.shape[0]
    n_sh = w_shared_gu.shape[2]

    dt_at = 2 * inner + 2 * state
    first_width = dt_at + heads + -(dt_at + heads) % 128
    first = jnp.concatenate(
        [
            w_zx.reshape(rows, 2 * inner),
            w_bc,
            w_dt,
            jnp.zeros((rows, first_width - dt_at - heads), F32),
        ],
        axis=1,
    ).astype(BF)
    first, proj_out = start([first, w_out.astype(BF)], n_dp, 1)
    shared = jnp.concatenate([w_shared_gu.reshape(rows, 2 * n_sh), w_shared_down], axis=1)
    shared, first = lax.optimization_barrier((shared.astype(BF), first))
    shared = lax.all_gather(shared, "dp", axis=0, tiled=True)
    shared_gu = shared[:, : 2 * n_sh]
    shared_down = shared[:, 2 * n_sh :]

    live = (jnp.arange(slots, dtype=jnp.int32) < lengths[0]).astype(F32)
    g2 = cotangent.astype(F32) * live[:, None]
    g2_low = g2.astype(BF)
    expert_range = jnp.arange(n_experts, dtype=jnp.int32)
    chosen = routes[:, :, None] == expert_range[None, None, :]
    weights = jnp.sum(jnp.where(chosen, route_w[:, :, None], 0.0), axis=1)
    high = weights.astype(BF)
    low = (weights - high.astype(F32)).astype(BF)
    table = jnp.concatenate([g2_low, high, low], axis=1)
    table = lax.dynamic_slice_in_dim(table, my_t * piece, piece, axis=0)
    g2_piece = lax.dynamic_slice_in_dim(g2_low, my_t * piece, piece, axis=0)

    x_float = x_in.astype(F32)
    scale_one = rms_scale(x_float)
    normed_one = (x_float * scale_one * ln1_gain).astype(BF)
    firsts = dotf("td,df->tf", normed_one, first)
    zx = firsts[:, : 2 * inner]
    bc_proj = firsts[:, 2 * inner : dt_at]
    dt_proj = firsts[:, dt_at : dt_at + heads]

    gated_mix, mixer_back = mixer_forward(
        zx, bc_proj, dt_proj, conv_x, conv_x_bias, conv_bc, conv_bc_bias, dt_bias, a_log, d_skip
    )
    squares = lax.psum(jnp.sum(gated_mix * gated_mix, axis=-1), "tensor")
    scale_mix = lax.rsqrt(squares / full_inner + EPSILON)[:, None]
    normed_mix = (gated_mix * scale_mix * gnorm_gain).astype(BF)
    mixer_part = dotf("tc,dc->td", normed_mix, proj_out).astype(BF)
    x_piece = lax.dynamic_slice_in_dim(x_in, my_t * piece, piece, axis=0)
    all_rows, table, hidden_one = middle(mixer_part, x_piece, ln2_gain, table, n_dp, 2)
    mine = lax.dynamic_slice_in_dim(all_rows, my_dp * slots, slots, axis=0)

    shared_pre = dotf("td,df->tf", mine, shared_gu)
    s_gate, s_up = shared_pre[:, :n_sh], shared_pre[:, n_sh:]
    shared_silu, shared_slope = silu_parts(s_gate)
    shared_act = (shared_silu * s_up).astype(BF)
    grad_shared_act = dotf("td,df->tf", g2_low, shared_down)
    grad_shared_pre = jnp.concatenate(
        [grad_shared_act * s_up * shared_slope, grad_shared_act * shared_silu], axis=1
    ).astype(BF)
    grad_normed_shared = dotf("tf,df->td", grad_shared_pre, shared_gu)
    shared_part = dotf("tf,df->td", shared_act, shared_down)

    high = lax.dynamic_slice_in_dim(table, width + my_dp * n_local, n_local, axis=1)
    low = lax.dynamic_slice_in_dim(table, width + n_experts + my_dp * n_local, n_local, axis=1)
    weights = (high.astype(F32) + low.astype(F32)).reshape(n_dp, slots, n_local)
    member = (weights > 0.0).astype(BF)
    before = (
        jnp.arange(slots)[:, None] > jnp.arange(slots)[None, :]
    ).astype(BF)
    position = dotf("ut,ste->seu", before, member).astype(jnp.int32)
    weights = weights.transpose(0, 2, 1)
    position = jnp.where(weights > 0.0, position, -1)

    dxn_part, out_part, grad_exp_gu, grad_exp_down = experts(
        position, weights, all_rows, table, w_exp_gu, w_exp_down, cap
    )
    grad_exp_gu = grad_exp_gu.reshape(w_exp_gu.shape)

    def add_own(total, own):
        at = my_dp * slots
        own = own + lax.dynamic_slice_in_dim(total, at, slots, axis=0).astype(F32)
        return lax.dynamic_update_slice_in_dim(total, own.astype(BF), at, axis=0)

    dxn_part = add_own(dxn_part, grad_normed_shared)
    out_part = add_own(out_part, shared_part)
    ffn_out = scatter_rows(out_part, n_dp, 4)
    dxn_part, ffn_out = lax.optimization_barrier((dxn_part, ffn_out))
    grad_one, sum_ln2, dm = turn(
        dxn_part, hidden_one, g2_piece, ln2_gain, n_dp, 3
    )
    dm = dm.reshape(slots, width)

    layer_out = lax.all_gather(
        (hidden_one + ffn_out).astype(BF), "tensor", axis=0, tiled=True
    )
    grad_shared_down = dotf("td,tf->df", g2_low, shared_act)
    grad_shared_gu = dotf("td,tf->df", mine, grad_shared_pre)

    grad_shared_w = jnp.concatenate([grad_shared_gu, grad_shared_down], axis=1).astype(BF)
    grad_shared_w, dm = lax.optimization_barrier((grad_shared_w, dm))
    grad_shared_w = lax.psum_scatter(grad_shared_w, "dp", scatter_dimension=0, tiled=True)
    grad_out_proj = dotf("td,tc->dc", dm, normed_mix)
    grad_normed_mix = dotf("td,dc->tc", dm, proj_out)
    weighted_mix = gnorm_gain * grad_normed_mix
    grad_gnorm = jnp.sum(grad_normed_mix * gated_mix * scale_mix, axis=0)
    product_sum = lax.psum(jnp.sum(weighted_mix * gated_mix, axis=-1), "tensor")[:, None]
    grad_gated = scale_mix * weighted_mix - gated_mix * scale_mix**3 * product_sum / full_inner
    (
        grad_zx,
        grad_bc,
        grad_dt_low,
        grad_conv_x,
        grad_conv_x_bias,
        grad_conv_bc,
        grad_conv_bc_bias,
        grad_dt_bias,
        grad_a_log,
        grad_d_skip,
    ) = mixer_back(grad_gated)
    grad_first = jnp.concatenate(
        [
            grad_zx,
            grad_bc.astype(BF),
            grad_dt_low,
            jnp.zeros((slots, first_width - dt_at - heads), BF),
        ],
        axis=1,
    )
    grad_input_part = dotf("tf,df->td", grad_first, first).astype(BF)
    grad_first_w = dotf("td,tf->df", normed_one, grad_first).astype(BF)
    def lanes(*vectors):
        vector = jnp.concatenate([v.reshape(-1) for v in vectors])
        return jnp.pad(vector, (0, -vector.shape[0] % (8 * width))).reshape(-1, width)

    taps = conv_x.shape[0]
    wide = lanes(jnp.zeros((width,), F32), sum_ln2, grad_conv_bc, grad_conv_bc_bias)
    n_wide = wide.shape[0]
    narrow = lanes(
        grad_conv_x, grad_conv_x_bias, grad_gnorm, grad_dt_bias, grad_a_log, grad_d_skip
    )
    grad_x, sums, (first_f, grad_out_w) = tail(
        [grad_first_w, grad_out_proj.astype(BF)],
        grad_input_part,
        grad_one,
        x_piece,
        ln1_gain,
        jnp.concatenate([wide, narrow], axis=0),
        n_wide,
        2 * inner,
        2 * state,
        n_dp,
        5,
    )
    grad_x = grad_x.reshape(slots, width).astype(F32)
    wide, narrow = sums[:n_wide].reshape(-1), sums[n_wide:].reshape(-1)
    at = [0]

    def take(vector, *shape):
        size = 1
        for s in shape:
            size *= s
        part = lax.slice_in_dim(vector, at[0], at[0] + size).reshape(shape)
        at[0] += size
        return part

    o_ln1 = take(wide, width)
    o_ln2 = take(wide, width)
    o_conv_bc = take(wide, taps, 2 * state)
    o_conv_bc_bias = take(wide, 2 * state)
    at[0] = 0
    o_conv_x = take(narrow, taps, inner)
    o_conv_x_bias = take(narrow, inner)
    o_gnorm = take(narrow, inner)
    o_dt_bias = take(narrow, heads)
    o_a_log = take(narrow, heads)
    o_d_skip = take(narrow, heads)
    shared_f = grad_shared_w.astype(F32)
    return (
        layer_out,
        grad_x,
        o_ln1,
        first_f[:, : 2 * inner].reshape(rows, 2, inner),
        first_f[:, 2 * inner : dt_at],
        first_f[:, dt_at : dt_at + heads],
        o_conv_x,
        o_conv_x_bias,
        o_conv_bc,
        o_conv_bc_bias,
        o_dt_bias,
        o_a_log,
        o_d_skip,
        o_gnorm,
        grad_out_w,
        o_ln2,
        shared_f[:, : 2 * n_sh].reshape(rows, 2, n_sh),
        shared_f[:, 2 * n_sh :],
        grad_exp_gu,
        grad_exp_down,
    )


def solution(mesh):
    return jax.shard_map(
        local,
        mesh=mesh,
        in_specs=(
            P("dp", None),
            P("dp"),
            P("dp", None),
            P("dp", None),
            P(),
            P("dp", None, "tensor"),
            P("dp", None),
            P("dp", "tensor"),
            P(None, "tensor"),
            P("tensor"),
            P(),
            P(),
            P("tensor"),
            P("tensor"),
            P("tensor"),
            P("tensor"),
            P("dp", "tensor"),
            P(),
            P("dp", None, "tensor"),
            P("dp", "tensor"),
            P("dp", None, None, "tensor"),
            P("dp", "tensor", None),
            P("dp", None),
        ),
        out_specs=(
            P("dp", None),
            P("dp", None),
            P(),
            P("dp", None, "tensor"),
            P("dp", None),
            P("dp", "tensor"),
            P(None, "tensor"),
            P("tensor"),
            P(),
            P(),
            P("tensor"),
            P("tensor"),
            P("tensor"),
            P("tensor"),
            P("dp", "tensor"),
            P(),
            P("dp", None, "tensor"),
            P("dp", "tensor"),
            P("dp", None, None, "tensor"),
            P("dp", "tensor", None),
        ),
        check_vma=False,
    )
```

```python
import functools

import jax
import jax.numpy as jnp
from jax import lax
from jax.experimental import pallas as pl
from jax.experimental.pallas import tpu as pltpu
from jax.sharding import PartitionSpec as P

BLOCK = 256


EPSILON = 1e-05
HIGHEST = lax.Precision.HIGHEST
BF = jnp.bfloat16
F32 = jnp.float32


def rms_scale(values):
    return lax.rsqrt(jnp.mean(values * values, axis=-1, keepdims=True) + EPSILON)


def silu_parts(values):
    sigmoid_val = jax.nn.sigmoid(values)
    return (values * sigmoid_val, sigmoid_val * (1.0 + values * (1.0 - sigmoid_val)))


def round_keep(values):
    return lax.optimization_barrier(values.astype(BF)).astype(F32)


def dotf(spec, a, b):
    return jnp.einsum(spec, a, b, preferred_element_type=F32)


def causal_conv(signal, kernel, offset):
    kernel_width = kernel.shape[0]
    seq_length = signal.shape[0]
    padded = jnp.concatenate(
        [jnp.zeros((kernel_width - 1, signal.shape[1]), signal.dtype), signal], axis=0
    )
    summed = offset[None, :] + kernel[0][None, :] * padded[0:seq_length]
    for tap_index in range(1, kernel_width):
        summed = summed + kernel[tap_index][None, :] * padded[tap_index : tap_index + seq_length]
    return summed


def ssd_scan(head_values, step_sizes, log_rates, b_rows, c_rows, skip_gain, block_rows):
    seq_length, n_heads, head_size = head_values.shape
    n_state = b_rows.shape[1]
    n_blocks = seq_length // block_rows
    decay_rates = -jnp.exp(log_rates)[None, :] * step_sizes
    scaled = (head_values * step_sizes[:, :, None]).reshape(
        n_blocks, block_rows, n_heads, head_size
    )
    cumulative = jnp.cumsum(decay_rates.reshape(n_blocks, block_rows, n_heads), axis=1)
    b_block = b_rows.reshape(n_blocks, block_rows, n_state)
    c_block = c_rows.reshape(n_blocks, block_rows, n_state)
    positions = jnp.arange(block_rows)
    causal = (positions[:, None] >= positions[None, :])[None, :, :, None]
    differences = cumulative[:, :, None, :] - cumulative[:, None, :, :]
    decay_mask = jnp.where(causal, jnp.exp(jnp.where(causal, differences, 0.0)), 0.0)
    intersection = jnp.einsum("kin,kjn->kij", c_block, b_block, precision=HIGHEST)
    within = jnp.einsum("kij,kijh,kjhp->kihp", intersection, decay_mask, scaled, precision=HIGHEST)
    block_end = cumulative[:, -1, :]
    to_end = jnp.exp(block_end[:, None, :] - cumulative)
    states = jnp.einsum("kjn,kjh,kjhp->khnp", b_block, to_end, scaled, precision=HIGHEST)

    def carry_state(previous, inputs):
        block_decay, block_state = inputs
        return (block_decay[:, None, None] * previous + block_state, previous)

    final_state, entering = lax.scan(
        carry_state,
        jnp.zeros((n_heads, n_state, head_size), head_values.dtype),
        (jnp.exp(block_end), states),
    )
    across = jnp.einsum(
        "kin,khnp,kih->kihp", c_block, entering, jnp.exp(cumulative), precision=HIGHEST
    )
    return (within + across).reshape(seq_length, n_heads, head_size) + skip_gain[
        None, :, None
    ] * head_values


def mixer_forward(
    zx, bc_proj, dt_proj, conv_x, conv_x_bias, conv_bc, conv_bc_bias, dt_bias, a_log, d_skip
):
    slots = zx.shape[0]
    inner = conv_x.shape[1]
    heads = dt_bias.shape[0]
    state = conv_bc.shape[1] // 2

    def conv_block(x_part, bc_part, kernel_x, offset_x, kernel_bc, offset_bc):
        return (
            jax.nn.silu(causal_conv(x_part, kernel_x, offset_x)),
            jax.nn.silu(causal_conv(bc_part, kernel_bc, offset_bc)),
        )

    (conv_values, conv_bc_values), conv_back = jax.vjp(
        conv_block, zx[:, inner:], bc_proj, conv_x, conv_x_bias, conv_bc, conv_bc_bias
    )
    head_input = round_keep(conv_values)
    bc_input = round_keep(conv_bc_values)

    def scan_block(head_flat, b_rows, c_rows, dt_part, z_part, dt_offset, log_rates, skip_gain):
        step_sizes = jax.nn.softplus(dt_part + dt_offset[None, :])
        output = ssd_scan(
            head_flat.reshape(slots, heads, inner // heads),
            step_sizes,
            log_rates,
            b_rows,
            c_rows,
            skip_gain,
            BLOCK,
        )
        return output.reshape(slots, inner) * jax.nn.silu(z_part)

    gated_mix, scan_back = jax.vjp(
        scan_block,
        head_input,
        bc_input[:, :state],
        bc_input[:, state:],
        dt_proj,
        zx[:, :inner],
        dt_bias,
        a_log,
        d_skip,
    )

    def mixer_back(grad_gated):
        g_head, g_b, g_c, g_dt, g_z, g_dt_bias, g_a_log, g_d_skip = scan_back(grad_gated)
        g_xs, g_bc, g_cx, g_cxb, g_cbc, g_cbcb = conv_back(
            (g_head, jnp.concatenate([g_b, g_c], axis=1))
        )
        g_zx = jnp.concatenate([g_z, g_xs], axis=1).astype(BF)
        return (
            g_zx, g_bc, g_dt.astype(BF), g_cx, g_cxb, g_cbc, g_cbcb, g_dt_bias, g_a_log, g_d_skip
        )

    return gated_mix, mixer_back


MESH = pl.DeviceIdType.MESH
DMA = pltpu.SemaphoreType.DMA
VMEM_SPEC = pl.BlockSpec(memory_space=pltpu.VMEM)
ANY_SPEC = pl.BlockSpec(memory_space=pl.ANY)


def place():
    d = lax.axis_index("dp")
    t = lax.axis_index("tensor")
    return d // 2, d % 2, t // 2, t % 2


def device(hi, lo, th, tl):
    return (hi * 2 + lo, th * 2 + tl)


def peer(hi, k, n_hi):
    if n_hi & (n_hi - 1):
        return lax.rem(hi + k, n_hi)
    other, bit = hi, 1
    while bit <= k:
        if k & bit:
            other = other + bit * (1 - 2 * lax.rem(hi // bit, 2))
        bit *= 2
    return other


def back(k, n_hi):
    return n_hi - k if n_hi & (n_hi - 1) else k


def greet(n_hi, tensor=True):
    hi, lo, th, tl = place()
    barrier = pltpu.get_barrier_semaphore()
    others = [device(peer(hi, k, n_hi), lo, th, tl) for k in range(1, n_hi)]
    others += [device(hi, 1 - lo, th, tl)]
    if tensor:
        others += [device(hi, lo, 1 - th, tl), device(hi, lo, th, 1 - tl)]
    for other in others:
        pl.semaphore_signal(barrier, inc=1, device_id=other, device_id_type=MESH)
    pl.semaphore_wait(barrier, len(others))


def remote(src, dst, ssem, rsem, to):
    return pltpu.make_async_remote_copy(
        src_ref=src, dst_ref=dst, send_sem=ssem, recv_sem=rsem, device_id=to, device_id_type=MESH
    )


class Sends:
    def __init__(self):
        self.copies = []

    def push(self, src, dst, ssem, rsem, to):
        copy = remote(src, dst, ssem, rsem, to)
        copy.start()
        self.copies.append(copy)

    def finish(self):
        for copy in self.copies:
            copy.wait_send()


def arrive(dst, ssem, rsem, to):
    remote(dst, dst, ssem, rsem, to).wait_recv()


TENSOR_SUM_SCRATCH = lambda rows, width, dtype: [
    pltpu.VMEM((2, rows, width), dtype),
    pltpu.VMEM((rows, width), dtype),
    DMA((3,)),
    DMA((3,)),
]


def tensor_sum_start(sends, part_ref, got_c, ssem, rsem):
    hi, lo, th, tl = place()
    to_c = device(hi, lo, th, 1 - tl)
    for j, y in enumerate((1 - th, th)):
        sends.push(part_ref.at[y * 2 + 1 - tl], got_c.at[j], ssem.at[j], rsem.at[j], to_c)


def tensor_sum_middle(sends, part_ref, got_c, got_y, ssem, rsem):
    hi, lo, th, tl = place()
    arrive(got_c.at[0], ssem.at[0], rsem.at[0], device(hi, lo, th, 1 - tl))
    total = part_ref[(1 - th) * 2 + tl].astype(F32) + got_c[0].astype(F32)
    got_c[0] = total.astype(got_c.dtype)
    sends.push(got_c.at[0], got_y, ssem.at[2], rsem.at[2], device(hi, lo, 1 - th, tl))


def tensor_sum_end(part_ref, got_c, got_y, ssem, rsem):
    hi, lo, th, tl = place()
    arrive(got_c.at[1], ssem.at[1], rsem.at[1], device(hi, lo, th, 1 - tl))
    total = part_ref[th * 2 + tl].astype(F32) + got_c[1].astype(F32)
    arrive(got_y, ssem.at[2], rsem.at[2], device(hi, lo, 1 - th, tl))
    return total + got_y[...].astype(F32)


def tensor_spread_start(sends, o_ref, ssem, rsem):
    hi, lo, th, tl = place()
    own = o_ref.at[th * 2 + tl]
    sends.push(own, own, ssem.at[0], rsem.at[0], device(hi, lo, 1 - th, tl))
    sends.push(own, own, ssem.at[1], rsem.at[1], device(hi, lo, th, 1 - tl))


def tensor_spread_end(sends, o_ref, ssem, rsem):
    hi, lo, th, tl = place()
    other = o_ref.at[(1 - th) * 2 + tl]
    to_c = device(hi, lo, th, 1 - tl)
    arrive(other, ssem.at[0], rsem.at[0], device(hi, lo, 1 - th, tl))
    sends.push(other, other, ssem.at[2], rsem.at[2], to_c)
    arrive(o_ref.at[th * 2 + 1 - tl], ssem.at[1], rsem.at[1], to_c)
    arrive(o_ref.at[(1 - th) * 2 + 1 - tl], ssem.at[2], rsem.at[2], to_c)


def gather_steps(n_hi, x_ref, o_ref, own_sem, send_sem, recv_sem, lo_first=(True, False)):
    hi, lo, th, tl = place()
    rows = x_ref.shape[0]
    half = rows // 2
    own_block = (hi * 2 + lo) * 4 + th * 2 + tl
    own = pltpu.make_async_copy(x_ref, o_ref.at[pl.ds(own_block * rows, rows)], own_sem)
    own.start()
    sends = Sends()

    def slot(k, f, s, c):
        return ((c * 2 + s) * 2 + f) * n_hi + k

    def where(h, k, f, s, c):
        kk = peer(hi, k, n_hi)
        l = 1 - lo if (f if lo_first[h] else s) else lo
        y = 1 - th if (s if lo_first[h] else f) else th
        z = 1 - tl if c else tl
        return ((kk * 2 + l) * 4 + y * 2 + z) * rows + h * half

    def push(h, k, f, s, c, step):
        at = where(h, k, f, s, c)
        if k == 0 and not (f or s or c):
            src = x_ref.at[pl.ds(h * half, half)]
        else:
            src = o_ref.at[pl.ds(at, half)]
        if step == "c":
            to, r = device(hi, lo, th, 1 - tl), slot(k, f, s, 1)
        elif step == "s":
            to = device(hi, lo, 1 - th, tl) if lo_first[h] else device(hi, 1 - lo, th, tl)
            r = slot(k, f, 1, 0)
        elif step == "f":
            to = device(hi, 1 - lo, th, tl) if lo_first[h] else device(hi, lo, 1 - th, tl)
            r = slot(k, 1, 0, 0)
        else:
            to, r = device(peer(hi, step, n_hi), lo, th, tl), slot(back(step, n_hi), 0, 0, 0)
        sends.push(src, o_ref.at[pl.ds(at, half)], send_sem.at[h, r], recv_sem.at[h, r], to)

    def got(h, k, f, s, c):
        r = slot(k, f, s, c)
        arrive(
            o_ref.at[pl.ds(where(h, k, f, s, c), half)],
            send_sem.at[h, r], recv_sem.at[h, r], device(hi, lo, th, 1 - tl),
        )

    for k in range(1, n_hi):
        for h in range(2):
            push(h, 0, 0, 0, 0, k)
    for k in range(n_hi):
        for h in range(2):
            if k:
                got(h, k, 0, 0, 0)
            for step in ("f", "s", "c"):
                push(h, k, 0, 0, 0, step)
        yield
        for h in range(2):
            got(h, k, 1, 0, 0)
            for step in ("s", "c"):
                push(h, k, 1, 0, 0, step)
        yield
    for k in range(n_hi):
        for f in range(2):
            for h in range(2):
                got(h, k, f, 1, 0)
                push(h, k, f, 1, 0, "c")
        yield
    for k in range(n_hi):
        for f in range(2):
            for s in range(2):
                for h in range(2):
                    got(h, k, f, s, 1)
    own.wait()
    sends.finish()


def in_turns(*streams):
    live = list(streams)
    while live:
        for stream in list(live):
            if next(stream, True) is True:
                live.remove(stream)


def middle_kernel(
    n_hi, part_ref, x_ref, gain_ref, o_ref, hidden_ref,
    normed, got_c, got_y, t_send, t_recv, *sems,
):
    greet(n_hi)
    sends = Sends()
    tensor_sum_start(sends, part_ref, got_c, t_send, t_recv)
    tensor_sum_middle(sends, part_ref, got_c, got_y, t_send, t_recv)
    hidden = x_ref[...].astype(F32) + tensor_sum_end(part_ref, got_c, got_y, t_send, t_recv)
    hidden_ref[...] = hidden
    normed[...] = (hidden * rms_scale(hidden) * gain_ref[...]).astype(normed.dtype)
    in_turns(gather_steps(n_hi, normed, o_ref, *sems))
    sends.finish()


def middle(part, x_piece, gain, n_dp, collective_id):
    rows, width = x_piece.shape
    n_hi = n_dp // 2
    return pl.pallas_call(
        functools.partial(middle_kernel, n_hi),
        out_shape=(
            jax.ShapeDtypeStruct((n_dp * 4 * rows, width), part.dtype),
            jax.ShapeDtypeStruct((rows, width), F32),
        ),
        in_specs=[VMEM_SPEC] * 3,
        out_specs=(ANY_SPEC, VMEM_SPEC),
        scratch_shapes=[pltpu.VMEM((rows, width), part.dtype)]
        + TENSOR_SUM_SCRATCH(rows, width, part.dtype)
        + [DMA, DMA((2, 8 * n_hi)), DMA((2, 8 * n_hi))],
        compiler_params=pltpu.CompilerParams(collective_id=collective_id, has_side_effects=True),
        name="middle",
    )(part.reshape(4, rows, width), x_piece, gain.reshape(1, width))


def weight_steps(n_hi, w_ref, o_ref, own_sem, send_h, recv_h, send_f, recv_f):
    hi, lo, th, tl = place()
    to_f = device(hi, 1 - lo, th, tl)
    sends = Sends()

    def at(k, l):
        return peer(hi, k, n_hi) * 2 + l

    for h in range(2):
        for k in range(1, n_hi):
            sends.push(
                w_ref.at[h], o_ref.at[at(0, lo), h], send_h.at[h, k - 1], recv_h.at[h, back(k, n_hi) - 1],
                device(peer(hi, k, n_hi), lo, th, tl),
            )
        sends.push(w_ref.at[h], o_ref.at[at(0, lo), h], send_f.at[h, 0], recv_f.at[h, 0], to_f)
    own = pltpu.make_async_copy(w_ref, o_ref.at[at(0, lo)], own_sem)
    own.start()
    yield
    for k in range(1, n_hi):
        for h in range(2):
            view = o_ref.at[at(k, lo), h]
            arrive(view, send_h.at[h, k - 1], recv_h.at[h, k - 1], to_f)
            sends.push(view, view, send_f.at[h, k], recv_f.at[h, k], to_f)
        yield
    for k in range(n_hi):
        for h in range(2):
            arrive(o_ref.at[at(k, 1 - lo), h], send_f.at[h, k], recv_f.at[h, k], to_f)
    own.wait()
    sends.finish()


def start_kernel(n_hi, n, *refs):
    ins, outs, sems = refs[: n + 1], refs[n + 1 : 2 * n + 2], refs[2 * n + 2 :]
    greet(n_hi)
    streams = [
        weight_steps(n_hi, ins[i], outs[i], *sems[5 * i : 5 * i + 5]) for i in range(n)
    ] + [gather_steps(n_hi, ins[n], outs[n], *sems[5 * n :], lo_first=(True, True))]
    in_turns(*streams)


def start(weights, table, n_dp, collective_id):
    n_hi = n_dp // 2
    n = len(weights)
    half = weights[0].shape[0] // 2
    outs = pl.pallas_call(
        functools.partial(start_kernel, n_hi, n),
        out_shape=[jax.ShapeDtypeStruct((n_dp, 2, half, w.shape[1]), w.dtype) for w in weights]
        + [jax.ShapeDtypeStruct((n_dp * 4 * table.shape[0], table.shape[1]), table.dtype)],
        in_specs=[ANY_SPEC] * (n + 1),
        out_specs=[ANY_SPEC] * (n + 1),
        scratch_shapes=[
            DMA,
            DMA((2, n_hi - 1)), DMA((2, n_hi - 1)),
            DMA((2, n_hi)), DMA((2, n_hi)),
        ] * n + [DMA, DMA((2, 8 * n_hi)), DMA((2, 8 * n_hi))],
        compiler_params=pltpu.CompilerParams(collective_id=collective_id, has_side_effects=True),
        name="start",
    )(*[w.reshape(2, half, w.shape[1]) for w in weights], table)
    return [o.reshape(n_dp * 2 * half, o.shape[3]) for o in outs[:n]] + [outs[n]]


def scatter_steps(n_hi, sends, p_ref, o_ref, bufs):
    (stage, from_c, from_f, from_s, from_h,
     stage_sem, send_c, recv_c, send_f, recv_f, send_s, recv_s, send_h, recv_h) = bufs
    depth = stage.shape[0]
    hi, lo, th, tl = place()
    to_c = device(hi, lo, th, 1 - tl)
    rows = o_ref.shape[0]
    half = rows // 2

    def where(h, k, f, s, c):
        kk = peer(hi, k, n_hi)
        l = 1 - lo if (f if h == 1 else s) else lo
        y = 1 - th if (s if h == 1 else f) else th
        z = 1 - tl if c else tl
        return ((kk * 2 + l) * 4 + y * 2 + z) * rows + h * half

    ks = list(range(1, n_hi)) + [0]
    order = []
    for i in range(n_hi + 2):
        for lag, groups in ((0, ((1, 1), (1, 0))), (1, ((0, 1),)), (2, ((0, 0),))):
            if 0 <= i - lag < n_hi:
                order += [(f, s, ks[i - lag], h) for f, s in groups for h in range(2)]

    def slot(f, s, k):
        return (f * 2 + s) * n_hi + k

    def first(h):
        return device(hi, lo, 1 - th, tl) if h == 0 else device(hi, 1 - lo, th, tl)

    def second(h):
        return device(hi, 1 - lo, th, tl) if h == 0 else device(hi, lo, 1 - th, tl)

    for f, s, k, h in order:
        n = slot(f, s, k)
        sends.push(
            p_ref.at[pl.ds(where(h, k, f, s, 1), half)], from_c.at[h, n], send_c.at[h, n],
            recv_c.at[h, n], to_c,
        )

    def load(i):
        f, s, k, h = order[i]
        return pltpu.make_async_copy(
            p_ref.at[pl.ds(where(h, k, f, s, 0), half)], stage.at[i % depth], stage_sem.at[i % depth]
        )

    for i in range(depth - 1):
        load(i).start()
    for i, (f, s, k, h) in enumerate(order):
        if i + depth - 1 < len(order):
            load(i + depth - 1).start()
        load(i).wait()
        n = slot(f, s, k)
        arrive(from_c.at[h, n], send_c.at[h, n], recv_c.at[h, n], to_c)
        total = stage[i % depth].astype(F32) + from_c[h, n].astype(F32)
        if f == 0:
            m = s * n_hi + k
            arrive(from_f.at[h, m], send_f.at[h, m], recv_f.at[h, m], to_c)
            total = total + from_f[h, m].astype(F32)
        if f == 0 and s == 0:
            arrive(from_s.at[h, k], send_s.at[h, k], recv_s.at[h, k], to_c)
            total = total + from_s[h, k].astype(F32)
        if f == 0 and s == 0 and k == 0:
            for j in range(n_hi - 1):
                arrive(from_h.at[h, j], send_h.at[h, j], recv_h.at[h, j], to_c)
                total = total + from_h[h, j].astype(F32)
            o_ref[pl.ds(h * half, half), :] = total
            continue
        from_c[h, n] = total.astype(from_c.dtype)
        src = from_c.at[h, n]
        if f == 1:
            m = s * n_hi + k
            sends.push(src, from_f.at[h, m], send_f.at[h, m], recv_f.at[h, m], first(h))
        elif s == 1:
            sends.push(src, from_s.at[h, k], send_s.at[h, k], recv_s.at[h, k], second(h))
        else:
            j = back(k, n_hi) - 1
            sends.push(
                src, from_h.at[h, j], send_h.at[h, j], recv_h.at[h, j],
                device(peer(hi, k, n_hi), lo, th, tl),
            )


def scatter_scratch(n_hi, half, width, dtype, depth=4):
    return [
        pltpu.VMEM((depth, half, width), dtype),
        pltpu.VMEM((2, 4 * n_hi, half, width), dtype),
        pltpu.VMEM((2, 2 * n_hi, half, width), dtype),
        pltpu.VMEM((2, n_hi, half, width), dtype),
        pltpu.VMEM((2, n_hi - 1, half, width), dtype),
        DMA((depth,)),
        DMA((2, 4 * n_hi)), DMA((2, 4 * n_hi)),
        DMA((2, 2 * n_hi)), DMA((2, 2 * n_hi)),
        DMA((2, n_hi)), DMA((2, n_hi)),
        DMA((2, n_hi - 1)), DMA((2, n_hi - 1)),
    ]


def scatter_kernel(n_hi, p_ref, o_ref, *bufs):
    greet(n_hi)
    sends = Sends()
    scatter_steps(n_hi, sends, p_ref, o_ref, bufs)
    sends.finish()


def scatter_rows(p, n_dp, collective_id):
    width = p.shape[1]
    rows = p.shape[0] // (n_dp * 4)
    n_hi = n_dp // 2
    return pl.pallas_call(
        functools.partial(scatter_kernel, n_hi),
        out_shape=jax.ShapeDtypeStruct((rows, width), F32),
        in_specs=[ANY_SPEC],
        out_specs=VMEM_SPEC,
        scratch_shapes=scatter_scratch(n_hi, rows // 2, width, p.dtype),
        compiler_params=pltpu.CompilerParams(
            collective_id=collective_id, has_side_effects=True, vmem_limit_bytes=60 << 20
        ),
        name="scatter_rows",
    )(p)


def turn_kernel(
    n_hi, p_ref, hidden_ref, g2_ref, gain_ref, grad_ref, sum_ref, dm_ref, total_ref, sp_send, sp_recv, *bufs
):
    hi, lo, th, tl = place()
    greet(n_hi)
    sends = Sends()
    scatter_steps(n_hi, sends, p_ref, total_ref, bufs)
    grad = total_ref[...]
    hidden = hidden_ref[...]
    scale = rms_scale(hidden)
    weighted = gain_ref[...] * grad
    sum_ref[...] = jnp.sum(grad * hidden * scale, axis=0, keepdims=True)
    mean = jnp.mean(weighted * hidden, axis=-1, keepdims=True)
    grad = g2_ref[...].astype(F32) + scale * weighted - hidden * (scale * scale * scale) * mean
    grad_ref[...] = grad
    dm_ref[th * 2 + tl] = grad.astype(dm_ref.dtype)
    tensor_spread_start(sends, dm_ref, sp_send, sp_recv)
    tensor_spread_end(sends, dm_ref, sp_send, sp_recv)
    sends.finish()


def turn(p, hidden, g2_piece, gain, n_dp, collective_id):
    rows, width = hidden.shape
    n_hi = n_dp // 2
    return pl.pallas_call(
        functools.partial(turn_kernel, n_hi),
        out_shape=(
            jax.ShapeDtypeStruct((rows, width), F32),
            jax.ShapeDtypeStruct((1, width), F32),
            jax.ShapeDtypeStruct((4, rows, width), p.dtype),
        ),
        in_specs=[ANY_SPEC] + [VMEM_SPEC] * 3,
        out_specs=(VMEM_SPEC,) * 3,
        scratch_shapes=[pltpu.VMEM((rows, width), F32), DMA((3,)), DMA((3,))]
        + scatter_scratch(n_hi, rows // 2, width, p.dtype),
        compiler_params=pltpu.CompilerParams(
            collective_id=collective_id, has_side_effects=True, vmem_limit_bytes=60 << 20
        ),
        name="turn",
    )(p, hidden, g2_piece, gain.reshape(1, width))


def tail_kernel(n_hi, wide, bc_at, n, *refs):
    part_ref, grad_ref, x_ref, gain_ref, small_ref = refs[:5]
    w_refs = refs[5 : 5 + n]
    ox_ref, os_ref = refs[5 + n : 7 + n]
    ow_refs = refs[7 + n : 7 + 2 * n]
    (got_c, got_y, t_send, t_recv, sp_send, sp_recv,
     small, small_f, small_h, small_t, sm_send, sm_recv, smh_send, smh_recv,
     bc_own, bc_got, bc_send, bc_recv) = refs[7 + 2 * n : 25 + 2 * n]
    rest = refs[25 + 2 * n :]
    bufs = [rest[8 * i : 8 * i + 8] for i in range(n)]
    hi, lo, th, tl = place()
    to_f, to_y, to_c = device(hi, 1 - lo, th, tl), device(hi, lo, 1 - th, tl), device(hi, lo, th, 1 - tl)
    greet(n_hi)
    sends = Sends()
    order = [(k, h) for k in list(range(1, n_hi)) + [0] for h in range(2)]

    def owner(k, l):
        return peer(hi, k, n_hi) * 2 + l

    for w_ref, (stage, from_f, from_h, stage_sem, send_f, recv_f, send_h, recv_h) in zip(w_refs, bufs):
        for k, h in order:
            sends.push(
                w_ref.at[owner(k, 1 - lo), h], from_f.at[h, k], send_f.at[h, k], recv_f.at[h, k], to_f
            )
    loads = []
    for w_ref, (stage, from_f, from_h, stage_sem, send_f, recv_f, send_h, recv_h) in zip(w_refs, bufs):
        for k, h in order:
            copy = pltpu.make_async_copy(w_ref.at[owner(k, lo), h], stage.at[h, k], stage_sem.at[h, k])
            copy.start()
            loads.append(copy)
    tensor_sum_start(sends, part_ref, got_c, t_send, t_recv)
    tensor_sum_middle(sends, part_ref, got_c, got_y, t_send, t_recv)
    grad = tensor_sum_end(part_ref, got_c, got_y, t_send, t_recv)
    x = x_ref[...].astype(F32)
    scale = rms_scale(x)
    weighted = gain_ref[...] * grad
    mean = jnp.mean(weighted * x, axis=-1, keepdims=True)
    ox_ref[th * 2 + tl] = (
        grad_ref[...] + scale * weighted - x * (scale * scale * scale) * mean
    ).astype(ox_ref.dtype)
    tensor_spread_start(sends, ox_ref, sp_send, sp_recv)
    small[...] = small_ref[...]
    small[0:1, :] = jnp.sum(grad * x * scale, axis=0, keepdims=True)
    sends.push(small, small_f, sm_send.at[0], sm_recv.at[0], to_f)

    events = [(w, k, h) for w in range(n) for k, h in order]
    for i, (w, k, h) in enumerate(events):
        if k == 0:
            continue
        stage, from_f, from_h, stage_sem, send_f, recv_f, send_h, recv_h = bufs[w]
        loads[i].wait()
        arrive(from_f.at[h, k], send_f.at[h, k], recv_f.at[h, k], to_c)
        from_f[h, k] = (stage[h, k].astype(F32) + from_f[h, k].astype(F32)).astype(from_f.dtype)
        j = back(k, n_hi) - 1
        sends.push(
            from_f.at[h, k], from_h.at[h, j], send_h.at[h, j], recv_h.at[h, j],
            device(peer(hi, k, n_hi), lo, th, tl),
        )
        if i == 0:
            tensor_spread_end(sends, ox_ref, sp_send, sp_recv)
        if i == 1:
            arrive(small_f, sm_send.at[0], sm_recv.at[0], to_c)
            small_h[hi] = small[...] + small_f[...]
            for q in range(1, n_hi):
                sends.push(
                    small_h.at[hi], small_h.at[hi], smh_send.at[q - 1], smh_recv.at[back(q, n_hi) - 1],
                    device(peer(hi, q, n_hi), lo, th, tl),
                )
    for q in range(1, n_hi):
        arrive(small_h.at[peer(hi, q, n_hi)], smh_send.at[q - 1], smh_recv.at[q - 1], to_c)
    total = small_h[0]
    for q in range(1, n_hi):
        total = total + small_h[q]
    os_ref[...] = total
    sends.push(os_ref.at[pl.ds(0, wide)], small_t.at[0], sm_send.at[1], sm_recv.at[1], to_c)
    for i, (w, k, h) in enumerate(events):
        if k:
            continue
        stage, from_f, from_h, stage_sem, send_f, recv_f, send_h, recv_h = bufs[w]
        loads[i].wait()
        arrive(from_f.at[h, 0], send_f.at[h, 0], recv_f.at[h, 0], to_c)
        total = stage[h, 0].astype(F32) + from_f[h, 0].astype(F32)
        for j in range(n_hi - 1):
            arrive(from_h.at[h, j], send_h.at[h, j], recv_h.at[h, j], to_c)
            total = total + from_h[h, j].astype(F32)
        ow_refs[w][h] = total
        if w == 0:
            bc_own[0, h] = total[:, bc_at : bc_at + bc_own.shape[3]].astype(bc_own.dtype)
            if h == 1:
                sends.push(bc_own.at[0], bc_got.at[0], bc_send.at[0], bc_recv.at[0], to_c)
                arrive(small_t.at[0], sm_send.at[1], sm_recv.at[1], to_c)
                small_t[2] = os_ref[pl.ds(0, wide), :] + small_t[0]
                sends.push(small_t.at[2], small_t.at[1], sm_send.at[2], sm_recv.at[2], to_y)
                arrive(bc_got.at[0], bc_send.at[0], bc_recv.at[0], to_c)
                bc_own[1] = (bc_own[0].astype(F32) + bc_got[0].astype(F32)).astype(bc_own.dtype)
                sends.push(bc_own.at[1], bc_got.at[1], bc_send.at[1], bc_recv.at[1], to_y)
    arrive(small_t.at[1], sm_send.at[2], sm_recv.at[2], to_c)
    arrive(bc_got.at[1], bc_send.at[1], bc_recv.at[1], to_c)
    for h in range(2):
        ow_refs[0][h, :, bc_at : bc_at + bc_own.shape[3]] = (
            bc_own[1, h].astype(F32) + bc_got[1, h].astype(F32)
        )
    sends.finish()
    os_ref[pl.ds(0, wide), :] = small_t[2] + small_t[1]


def tail(weights, part, grad_one, x_piece, gain, small, wide, bc_at, bc_width, n_dp, collective_id):
    rows, width = x_piece.shape
    n_hi = n_dp // 2
    n = len(weights)
    half = weights[0].shape[0] // (2 * n_dp)
    dt = weights[0].dtype
    scratch = TENSOR_SUM_SCRATCH(rows, width, part.dtype) + [
        DMA((3,)), DMA((3,)),
        pltpu.VMEM(small.shape, F32),
        pltpu.VMEM(small.shape, F32),
        pltpu.VMEM((n_hi,) + small.shape, F32),
        pltpu.VMEM((3, wide, small.shape[1]), F32),
        DMA((3,)), DMA((3,)),
        DMA((n_hi - 1,)), DMA((n_hi - 1,)),
        pltpu.VMEM((2, 2, half, bc_width), dt),
        pltpu.VMEM((2, 2, half, bc_width), dt),
        DMA((2,)), DMA((2,)),
    ]
    for w in weights:
        scratch += [
            pltpu.VMEM((2, n_hi, half, w.shape[1]), dt),
            pltpu.VMEM((2, n_hi, half, w.shape[1]), dt),
            pltpu.VMEM((2, n_hi - 1, half, w.shape[1]), dt),
            DMA((2, n_hi)),
            DMA((2, n_hi)), DMA((2, n_hi)),
            DMA((2, n_hi - 1)), DMA((2, n_hi - 1)),
        ]
    outs = pl.pallas_call(
        functools.partial(tail_kernel, n_hi, wide, bc_at, n),
        out_shape=[
            jax.ShapeDtypeStruct((4, rows, width), dt),
            jax.ShapeDtypeStruct(small.shape, F32),
        ] + [jax.ShapeDtypeStruct((2, half, w.shape[1]), F32) for w in weights],
        in_specs=[VMEM_SPEC] * 5 + [ANY_SPEC] * n,
        out_specs=[VMEM_SPEC] * (2 + n),
        scratch_shapes=scratch,
        compiler_params=pltpu.CompilerParams(
            collective_id=collective_id, has_side_effects=True, vmem_limit_bytes=60 << 20
        ),
        name="tail",
    )(
        part.reshape(4, rows, width), grad_one, x_piece, gain.reshape(1, width), small,
        *[w.reshape(n_dp, 2, half, w.shape[1]) for w in weights],
    )
    return outs[0], outs[1], [o.reshape(2 * half, o.shape[2]) for o in outs[2:]]


def dot_mm(a, b):
    return lax.dot_general(a, b, (((1,), (0,)), ((), ())), preferred_element_type=F32)


def dot_nt(a, b):
    return lax.dot_general(a, b, (((1,), (1,)), ((), ())), preferred_element_type=F32)


def dot_tn(a, b):
    return lax.dot_general(a, b, (((0,), (0,)), ((), ())), preferred_element_type=F32)


def experts_kernel(
    n_dp, n_local, cap, chunk, pos_ref, wt_ref, x_ref, g_ref, gu_ref, dn_ref,
    dxn_ref, out_ref, ggu_ref, gdn_ref, pick, xr, q, sw, gu,
):
    step = pl.program_id(0)
    width = x_ref.shape[1]
    hidden = dn_ref.shape[1]
    slots = x_ref.shape[0]
    columns = [pl.ds(c, chunk) for c in range(0, width, chunk)]

    @pl.when(step < n_dp)
    def _():
        s = step
        lane = lax.broadcasted_iota(jnp.int32, (cap, slots), 0)
        for e in range(n_local):
            hit = lane == pos_ref[0, e : e + 1, :]
            pick[s, e * cap : (e + 1) * cap, :] = jnp.where(hit, 1.0, 0.0).astype(BF)
            sw[e, s] = jnp.sum(jnp.where(hit, wt_ref[0, e : e + 1, :], 0.0), axis=1, keepdims=True)
        chosen = pick[s]
        for c in columns:
            rows = dot_mm(chosen, x_ref[:, c]).astype(BF)
            grads = dot_mm(chosen, g_ref[:, c])
            for e in range(n_local):
                xr[e, s, :, c] = rows[e * cap : (e + 1) * cap]
                q[e, s, :, c] = (grads[e * cap : (e + 1) * cap] * sw[e, s]).astype(BF)

    @pl.when(jnp.logical_and(step >= n_dp, step < n_dp + n_local))
    def _():
        e = step - n_dp
        gu[:, :hidden] = gu_ref[pl.ds(0, width, stride=2), :].astype(BF)
        gu[:, hidden:] = gu_ref[pl.ds(1, width, stride=2), :].astype(BF)
        down = dn_ref[0].astype(BF)
        x = xr[e].reshape(n_dp * cap, width)
        qe = q[e].reshape(n_dp * cap, width)
        pre = dot_mm(x, gu[...])
        grad_act = dot_nt(qe, down)
        gate, up = pre[:, :hidden], pre[:, hidden:]
        sig = 1.0 / (1.0 + jnp.exp(-gate))
        act_silu = gate * sig
        slope = sig * (1.0 + gate * (1.0 - sig))
        value = act_silu * up
        act = value.astype(BF)
        scaled = (value * sw[e].reshape(n_dp * cap, 1)).astype(BF)
        grad_pre = jnp.concatenate([grad_act * up * slope, grad_act * act_silu], axis=1).astype(BF)
        ggu = dot_tn(x, grad_pre)
        ggu_ref[pl.ds(0, width, stride=2), :] = ggu[:, :hidden]
        ggu_ref[pl.ds(1, width, stride=2), :] = ggu[:, hidden:]
        gdn_ref[0] = dot_tn(act, qe)
        for c in columns:
            xr[e, :, :, c] = dot_nt(grad_pre, gu[c, :]).astype(BF).reshape(n_dp, cap, chunk)
            q[e, :, :, c] = dot_mm(scaled, down[:, c.start : c.start + chunk]).astype(BF).reshape(n_dp, cap, chunk)

    @pl.when(step >= n_dp + n_local)
    def _():
        s = step - n_dp - n_local
        chosen = pick[s]
        for c in columns:
            dxn_ref[:, c] = dot_tn(chosen, xr[:, s, :, c].reshape(n_local * cap, chunk)).astype(BF)
            out_ref[:, c] = dot_tn(chosen, q[:, s, :, c].reshape(n_local * cap, chunk)).astype(BF)


def experts(position, weights, rows, table, w_gu, w_down, cap):
    n_dp, n_local, slots = position.shape
    width = rows.shape[1]
    hidden = w_down.shape[1]
    chunk = width // 3 if width % 384 == 0 else width
    by_source = lambda i: (jnp.clip(i, 0, n_dp - 1), 0, 0)
    rows_in = lambda i: (jnp.clip(i, 0, n_dp - 1), 0)
    rows_out = lambda i: (jnp.clip(i - n_dp - n_local, 0, n_dp - 1), 0)
    flat = lambda i: (jnp.clip(i - n_dp, 0, n_local - 1), 0)
    deep = lambda i: (jnp.clip(i - n_dp, 0, n_local - 1), 0, 0)
    total = n_dp * n_local * cap
    return pl.pallas_call(
        functools.partial(experts_kernel, n_dp, n_local, cap, chunk),
        grid=(2 * n_dp + n_local,),
        out_shape=(
            jax.ShapeDtypeStruct((n_dp * slots, width), BF),
            jax.ShapeDtypeStruct((n_dp * slots, width), BF),
            jax.ShapeDtypeStruct((n_local * width * 2, hidden), F32),
            jax.ShapeDtypeStruct((n_local, hidden, width), F32),
        ),
        in_specs=[
            pl.BlockSpec((1, n_local, slots), by_source),
            pl.BlockSpec((1, n_local, slots), by_source),
            pl.BlockSpec((slots, width), rows_in),
            pl.BlockSpec((slots, width), rows_in),
            pl.BlockSpec((width * 2, hidden), flat),
            pl.BlockSpec((1, hidden, width), deep),
        ],
        out_specs=(
            pl.BlockSpec((slots, width), rows_out),
            pl.BlockSpec((slots, width), rows_out),
            pl.BlockSpec((width * 2, hidden), flat),
            pl.BlockSpec((1, hidden, width), deep),
        ),
        scratch_shapes=[
            pltpu.VMEM((n_dp, n_local * cap, slots), BF),
            pltpu.VMEM((n_local, n_dp, cap, width), BF),
            pltpu.VMEM((n_local, n_dp, cap, width), BF),
            pltpu.VMEM((n_local, n_dp, cap, 1), F32),
            pltpu.VMEM((width, 2 * hidden), BF),
        ],
        compiler_params=pltpu.CompilerParams(
            dimension_semantics=("arbitrary",), vmem_limit_bytes=60 << 20
        ),
        cost_estimate=pl.CostEstimate(
            flops=8 * total * slots * width + 18 * total * width * hidden,
            bytes_accessed=8 * n_dp * slots * width + 24 * n_local * width * hidden,
            transcendentals=total * hidden,
        ),
        name="experts",
    )(
        position,
        weights,
        rows,
        table,
        w_gu.reshape(n_local * width * 2, hidden),
        w_down,
    )


def local(
    x_in,
    lengths,
    routes,
    route_w,
    ln1_gain,
    w_zx,
    w_bc,
    w_dt,
    conv_x,
    conv_x_bias,
    conv_bc,
    conv_bc_bias,
    dt_bias,
    a_log,
    d_skip,
    gnorm_gain,
    w_out,
    ln2_gain,
    w_shared_gu,
    w_shared_down,
    w_exp_gu,
    w_exp_down,
    cotangent,
):
    slots, width = x_in.shape
    n_dp = lax.axis_size("dp")
    n_t = lax.axis_size("tensor")
    my_t = lax.axis_index("tensor")
    my_dp = lax.axis_index("dp")
    piece = slots // n_t
    n_local = w_exp_gu.shape[0]
    n_experts = n_dp * n_local
    cap = slots * routes.shape[1] * 4 // (3 * n_experts)
    if cap > slots:
        cap = slots
    heads = dt_bias.shape[0]
    inner = conv_x.shape[1]
    head_size = inner // heads
    state = conv_bc.shape[1] // 2
    full_inner = inner * n_t
    rows = w_zx.shape[0]
    n_sh = w_shared_gu.shape[2]

    dt_at = 2 * inner + 2 * state
    first_width = dt_at + heads + -(dt_at + heads) % 128
    first = jnp.concatenate(
        [
            w_zx.reshape(rows, 2 * inner),
            w_bc,
            w_dt,
            jnp.zeros((rows, first_width - dt_at - heads), F32),
        ],
        axis=1,
    ).astype(BF)
    shared = jnp.concatenate([w_shared_gu.reshape(rows, 2 * n_sh), w_shared_down], axis=1)

    live = (jnp.arange(slots, dtype=jnp.int32) < lengths[0]).astype(F32)
    g2 = cotangent.astype(F32) * live[:, None]
    g2_low = g2.astype(BF)
    expert_range = jnp.arange(n_experts, dtype=jnp.int32)
    chosen = routes[:, :, None] == expert_range[None, None, :]
    weights = jnp.sum(jnp.where(chosen, route_w[:, :, None], 0.0), axis=1)
    high = weights.astype(BF)
    low = (weights - high.astype(F32)).astype(BF)
    table = jnp.concatenate([g2_low, high, low], axis=1)
    table = lax.dynamic_slice_in_dim(table, my_t * piece, piece, axis=0)
    g2_piece = lax.dynamic_slice_in_dim(g2_low, my_t * piece, piece, axis=0)

    first, proj_out, table = start([first, w_out.astype(BF)], table, n_dp, 1)
    shared, first = lax.optimization_barrier((shared.astype(BF), first))
    shared = lax.all_gather(shared, "dp", axis=0, tiled=True)
    shared_gu = shared[:, : 2 * n_sh]
    shared_down = shared[:, 2 * n_sh :]

    x_float = x_in.astype(F32)
    scale_one = rms_scale(x_float)
    normed_one = (x_float * scale_one * ln1_gain).astype(BF)
    firsts = dotf("td,df->tf", normed_one, first)
    zx = firsts[:, : 2 * inner]
    bc_proj = firsts[:, 2 * inner : dt_at]
    dt_proj = firsts[:, dt_at : dt_at + heads]

    gated_mix, mixer_back = mixer_forward(
        zx, bc_proj, dt_proj, conv_x, conv_x_bias, conv_bc, conv_bc_bias, dt_bias, a_log, d_skip
    )
    squares = lax.psum(jnp.sum(gated_mix * gated_mix, axis=-1), "tensor")
    scale_mix = lax.rsqrt(squares / full_inner + EPSILON)[:, None]
    normed_mix = (gated_mix * scale_mix * gnorm_gain).astype(BF)
    mixer_part = dotf("tc,dc->td", normed_mix, proj_out).astype(BF)
    x_piece = lax.dynamic_slice_in_dim(x_in, my_t * piece, piece, axis=0)
    all_rows, hidden_one = middle(mixer_part, x_piece, ln2_gain, n_dp, 2)
    mine = lax.dynamic_slice_in_dim(all_rows, my_dp * slots, slots, axis=0)

    shared_pre = dotf("td,df->tf", mine, shared_gu)
    s_gate, s_up = shared_pre[:, :n_sh], shared_pre[:, n_sh:]
    shared_silu, shared_slope = silu_parts(s_gate)
    shared_act = (shared_silu * s_up).astype(BF)
    grad_shared_act = dotf("td,df->tf", g2_low, shared_down)
    grad_shared_pre = jnp.concatenate(
        [grad_shared_act * s_up * shared_slope, grad_shared_act * shared_silu], axis=1
    ).astype(BF)
    grad_normed_shared = dotf("tf,df->td", grad_shared_pre, shared_gu)
    shared_part = dotf("tf,df->td", shared_act, shared_down)

    high = lax.dynamic_slice_in_dim(table, width + my_dp * n_local, n_local, axis=1)
    low = lax.dynamic_slice_in_dim(table, width + n_experts + my_dp * n_local, n_local, axis=1)
    weights = (high.astype(F32) + low.astype(F32)).reshape(n_dp, slots, n_local)
    member = (weights > 0.0).astype(BF)
    before = (
        jnp.arange(slots)[:, None] > jnp.arange(slots)[None, :]
    ).astype(BF)
    position = dotf("ut,ste->seu", before, member).astype(jnp.int32)
    weights = weights.transpose(0, 2, 1)
    position = jnp.where(weights > 0.0, position, -1)

    dxn_part, out_part, grad_exp_gu, grad_exp_down = experts(
        position, weights, all_rows, table, w_exp_gu, w_exp_down, cap
    )
    grad_exp_gu = grad_exp_gu.reshape(w_exp_gu.shape)

    def add_own(total, own):
        at = my_dp * slots
        own = own + lax.dynamic_slice_in_dim(total, at, slots, axis=0).astype(F32)
        return lax.dynamic_update_slice_in_dim(total, own.astype(BF), at, axis=0)

    dxn_part = add_own(dxn_part, grad_normed_shared)
    out_part = add_own(out_part, shared_part)
    ffn_out = scatter_rows(out_part, n_dp, 4)
    dxn_part, ffn_out = lax.optimization_barrier((dxn_part, ffn_out))
    grad_one, sum_ln2, dm = turn(
        dxn_part, hidden_one, g2_piece, ln2_gain, n_dp, 3
    )
    dm = dm.reshape(slots, width)

    layer_out = lax.all_gather(
        (hidden_one + ffn_out).astype(BF), "tensor", axis=0, tiled=True
    )
    grad_shared_down = dotf("td,tf->df", g2_low, shared_act)
    grad_shared_gu = dotf("td,tf->df", mine, grad_shared_pre)

    grad_shared_w = jnp.concatenate([grad_shared_gu, grad_shared_down], axis=1).astype(BF)
    grad_shared_w = lax.psum_scatter(grad_shared_w, "dp", scatter_dimension=0, tiled=True)
    grad_out_w = dotf("td,tc->dc", dm, normed_mix).astype(BF)
    grad_out_w = lax.psum_scatter(grad_out_w, "dp", scatter_dimension=0, tiled=True)
    grad_normed_mix = dotf("td,dc->tc", dm, proj_out)
    weighted_mix = gnorm_gain * grad_normed_mix
    grad_gnorm = jnp.sum(grad_normed_mix * gated_mix * scale_mix, axis=0)
    product_sum = lax.psum(jnp.sum(weighted_mix * gated_mix, axis=-1), "tensor")[:, None]
    grad_gated = scale_mix * weighted_mix - gated_mix * scale_mix**3 * product_sum / full_inner
    (
        grad_zx,
        grad_bc,
        grad_dt_low,
        grad_conv_x,
        grad_conv_x_bias,
        grad_conv_bc,
        grad_conv_bc_bias,
        grad_dt_bias,
        grad_a_log,
        grad_d_skip,
    ) = mixer_back(grad_gated)
    grad_first = jnp.concatenate(
        [
            grad_zx,
            grad_bc.astype(BF),
            grad_dt_low,
            jnp.zeros((slots, first_width - dt_at - heads), BF),
        ],
        axis=1,
    )
    grad_input_part = dotf("tf,df->td", grad_first, first).astype(BF)
    grad_first_w = dotf("td,tf->df", normed_one, grad_first).astype(BF)
    def lanes(*vectors):
        vector = jnp.concatenate([v.reshape(-1) for v in vectors])
        return jnp.pad(vector, (0, -vector.shape[0] % (8 * width))).reshape(-1, width)

    taps = conv_x.shape[0]
    wide = lanes(jnp.zeros((width,), F32), sum_ln2, grad_conv_bc, grad_conv_bc_bias)
    n_wide = wide.shape[0]
    narrow = lanes(
        grad_conv_x, grad_conv_x_bias, grad_gnorm, grad_dt_bias, grad_a_log, grad_d_skip
    )
    grad_first_w, grad_out_w, grad_shared_w = lax.optimization_barrier(
        (grad_first_w, grad_out_w, grad_shared_w)
    )
    grad_x, sums, (first_f,) = tail(
        [grad_first_w],
        grad_input_part,
        grad_one,
        x_piece,
        ln1_gain,
        jnp.concatenate([wide, narrow], axis=0),
        n_wide,
        2 * inner,
        2 * state,
        n_dp,
        5,
    )
    grad_x = grad_x.reshape(slots, width).astype(F32)
    wide, narrow = sums[:n_wide].reshape(-1), sums[n_wide:].reshape(-1)
    at = [0]

    def take(vector, *shape):
        size = 1
        for s in shape:
            size *= s
        part = lax.slice_in_dim(vector, at[0], at[0] + size).reshape(shape)
        at[0] += size
        return part

    o_ln1 = take(wide, width)
    o_ln2 = take(wide, width)
    o_conv_bc = take(wide, taps, 2 * state)
    o_conv_bc_bias = take(wide, 2 * state)
    at[0] = 0
    o_conv_x = take(narrow, taps, inner)
    o_conv_x_bias = take(narrow, inner)
    o_gnorm = take(narrow, inner)
    o_dt_bias = take(narrow, heads)
    o_a_log = take(narrow, heads)
    o_d_skip = take(narrow, heads)
    shared_f = grad_shared_w.astype(F32)
    return (
        layer_out,
        grad_x,
        o_ln1,
        first_f[:, : 2 * inner].reshape(rows, 2, inner),
        first_f[:, 2 * inner : dt_at],
        first_f[:, dt_at : dt_at + heads],
        o_conv_x,
        o_conv_x_bias,
        o_conv_bc,
        o_conv_bc_bias,
        o_dt_bias,
        o_a_log,
        o_d_skip,
        o_gnorm,
        grad_out_w.astype(F32),
        o_ln2,
        shared_f[:, : 2 * n_sh].reshape(rows, 2, n_sh),
        shared_f[:, 2 * n_sh :],
        grad_exp_gu,
        grad_exp_down,
    )


def solution(mesh):
    return jax.shard_map(
        local,
        mesh=mesh,
        in_specs=(
            P("dp", None),
            P("dp"),
            P("dp", None),
            P("dp", None),
            P(),
            P("dp", None, "tensor"),
            P("dp", None),
            P("dp", "tensor"),
            P(None, "tensor"),
            P("tensor"),
            P(),
            P(),
            P("tensor"),
            P("tensor"),
            P("tensor"),
            P("tensor"),
            P("dp", "tensor"),
            P(),
            P("dp", None, "tensor"),
            P("dp", "tensor"),
            P("dp", None, None, "tensor"),
            P("dp", "tensor", None),
            P("dp", None),
        ),
        out_specs=(
            P("dp", None),
            P("dp", None),
            P(),
            P("dp", None, "tensor"),
            P("dp", None),
            P("dp", "tensor"),
            P(None, "tensor"),
            P("tensor"),
            P(),
            P(),
            P("tensor"),
            P("tensor"),
            P("tensor"),
            P("tensor"),
            P("dp", "tensor"),
            P(),
            P("dp", None, "tensor"),
            P("dp", "tensor"),
            P("dp", None, None, "tensor"),
            P("dp", "tensor", None),
        ),
        check_vma=False,
    )
```

```python
import functools

import jax
import jax.numpy as jnp
from jax import lax
from jax.experimental import pallas as pl
from jax.experimental.pallas import tpu as pltpu
from jax.sharding import PartitionSpec as P

BLOCK = 256


EPSILON = 1e-05
HIGHEST = lax.Precision.HIGHEST
BF = jnp.bfloat16
F32 = jnp.float32


def rms_scale(values):
    return lax.rsqrt(jnp.mean(values * values, axis=-1, keepdims=True) + EPSILON)


def silu_parts(values):
    sigmoid_val = jax.nn.sigmoid(values)
    return (values * sigmoid_val, sigmoid_val * (1.0 + values * (1.0 - sigmoid_val)))


def round_keep(values):
    return lax.optimization_barrier(values.astype(BF)).astype(F32)


def dotf(spec, a, b):
    return jnp.einsum(spec, a, b, preferred_element_type=F32)


def causal_conv(signal, kernel, offset):
    kernel_width = kernel.shape[0]
    seq_length = signal.shape[0]
    padded = jnp.concatenate(
        [jnp.zeros((kernel_width - 1, signal.shape[1]), signal.dtype), signal], axis=0
    )
    summed = offset[None, :] + kernel[0][None, :] * padded[0:seq_length]
    for tap_index in range(1, kernel_width):
        summed = summed + kernel[tap_index][None, :] * padded[tap_index : tap_index + seq_length]
    return summed


def ssd_scan(head_values, step_sizes, log_rates, b_rows, c_rows, skip_gain, block_rows):
    seq_length, n_heads, head_size = head_values.shape
    n_state = b_rows.shape[1]
    n_blocks = seq_length // block_rows
    decay_rates = -jnp.exp(log_rates)[None, :] * step_sizes
    scaled = (head_values * step_sizes[:, :, None]).reshape(
        n_blocks, block_rows, n_heads, head_size
    )
    cumulative = jnp.cumsum(decay_rates.reshape(n_blocks, block_rows, n_heads), axis=1)
    b_block = b_rows.reshape(n_blocks, block_rows, n_state)
    c_block = c_rows.reshape(n_blocks, block_rows, n_state)
    positions = jnp.arange(block_rows)
    causal = (positions[:, None] >= positions[None, :])[None, :, :, None]
    differences = cumulative[:, :, None, :] - cumulative[:, None, :, :]
    decay_mask = jnp.where(causal, jnp.exp(jnp.where(causal, differences, 0.0)), 0.0)
    intersection = jnp.einsum("kin,kjn->kij", c_block, b_block, precision=HIGHEST)
    within = jnp.einsum("kij,kijh,kjhp->kihp", intersection, decay_mask, scaled, precision=HIGHEST)
    block_end = cumulative[:, -1, :]
    to_end = jnp.exp(block_end[:, None, :] - cumulative)
    states = jnp.einsum("kjn,kjh,kjhp->khnp", b_block, to_end, scaled, precision=HIGHEST)

    def carry_state(previous, inputs):
        block_decay, block_state = inputs
        return (block_decay[:, None, None] * previous + block_state, previous)

    final_state, entering = lax.scan(
        carry_state,
        jnp.zeros((n_heads, n_state, head_size), head_values.dtype),
        (jnp.exp(block_end), states),
    )
    across = jnp.einsum(
        "kin,khnp,kih->kihp", c_block, entering, jnp.exp(cumulative), precision=HIGHEST
    )
    return (within + across).reshape(seq_length, n_heads, head_size) + skip_gain[
        None, :, None
    ] * head_values


def mixer_forward(
    zx, bc_proj, dt_proj, conv_x, conv_x_bias, conv_bc, conv_bc_bias, dt_bias, a_log, d_skip
):
    slots = zx.shape[0]
    inner = conv_x.shape[1]
    heads = dt_bias.shape[0]
    state = conv_bc.shape[1] // 2

    def conv_block(x_part, bc_part, kernel_x, offset_x, kernel_bc, offset_bc):
        return (
            jax.nn.silu(causal_conv(x_part, kernel_x, offset_x)),
            jax.nn.silu(causal_conv(bc_part, kernel_bc, offset_bc)),
        )

    (conv_values, conv_bc_values), conv_back = jax.vjp(
        conv_block, zx[:, inner:], bc_proj, conv_x, conv_x_bias, conv_bc, conv_bc_bias
    )
    head_input = round_keep(conv_values)
    bc_input = round_keep(conv_bc_values)

    def scan_block(head_flat, b_rows, c_rows, dt_part, z_part, dt_offset, log_rates, skip_gain):
        step_sizes = jax.nn.softplus(dt_part + dt_offset[None, :])
        output = ssd_scan(
            head_flat.reshape(slots, heads, inner // heads),
            step_sizes,
            log_rates,
            b_rows,
            c_rows,
            skip_gain,
            BLOCK,
        )
        return output.reshape(slots, inner) * jax.nn.silu(z_part)

    gated_mix, scan_back = jax.vjp(
        scan_block,
        head_input,
        bc_input[:, :state],
        bc_input[:, state:],
        dt_proj,
        zx[:, :inner],
        dt_bias,
        a_log,
        d_skip,
    )

    def mixer_back(grad_gated):
        g_head, g_b, g_c, g_dt, g_z, g_dt_bias, g_a_log, g_d_skip = scan_back(grad_gated)
        g_xs, g_bc, g_cx, g_cxb, g_cbc, g_cbcb = conv_back(
            (g_head, jnp.concatenate([g_b, g_c], axis=1))
        )
        g_zx = jnp.concatenate([g_z, g_xs], axis=1).astype(BF)
        return (
            g_zx, g_bc, g_dt.astype(BF), g_cx, g_cxb, g_cbc, g_cbcb, g_dt_bias, g_a_log, g_d_skip
        )

    return gated_mix, mixer_back


MESH = pl.DeviceIdType.MESH
DMA = pltpu.SemaphoreType.DMA
VMEM_SPEC = pl.BlockSpec(memory_space=pltpu.VMEM)
ANY_SPEC = pl.BlockSpec(memory_space=pl.ANY)


def place():
    d = lax.axis_index("dp")
    t = lax.axis_index("tensor")
    return d // 2, d % 2, t // 2, t % 2


def device(hi, lo, th, tl):
    return (hi * 2 + lo, th * 2 + tl)


def peer(hi, k, n_hi):
    if n_hi & (n_hi - 1):
        return lax.rem(hi + k, n_hi)
    other, bit = hi, 1
    while bit <= k:
        if k & bit:
            other = other + bit * (1 - 2 * lax.rem(hi // bit, 2))
        bit *= 2
    return other


def back(k, n_hi):
    return n_hi - k if n_hi & (n_hi - 1) else k


def greet(n_hi, tensor=True):
    hi, lo, th, tl = place()
    barrier = pltpu.get_barrier_semaphore()
    others = [device(peer(hi, k, n_hi), lo, th, tl) for k in range(1, n_hi)]
    others += [device(hi, 1 - lo, th, tl)]
    if tensor:
        others += [device(hi, lo, 1 - th, tl), device(hi, lo, th, 1 - tl)]
    for other in others:
        pl.semaphore_signal(barrier, inc=1, device_id=other, device_id_type=MESH)
    pl.semaphore_wait(barrier, len(others))


def remote(src, dst, ssem, rsem, to):
    return pltpu.make_async_remote_copy(
        src_ref=src, dst_ref=dst, send_sem=ssem, recv_sem=rsem, device_id=to, device_id_type=MESH
    )


class Sends:
    def __init__(self):
        self.copies = []

    def push(self, src, dst, ssem, rsem, to):
        copy = remote(src, dst, ssem, rsem, to)
        copy.start()
        self.copies.append(copy)

    def finish(self):
        for copy in self.copies:
            copy.wait_send()


def arrive(dst, ssem, rsem, to):
    remote(dst, dst, ssem, rsem, to).wait_recv()


TENSOR_SUM_SCRATCH = lambda rows, width, dtype: [
    pltpu.VMEM((2, rows, width), dtype),
    pltpu.VMEM((rows, width), dtype),
    DMA((3,)),
    DMA((3,)),
]


def tensor_sum_start(sends, part_ref, got_c, ssem, rsem):
    hi, lo, th, tl = place()
    to_c = device(hi, lo, th, 1 - tl)
    for j, y in enumerate((1 - th, th)):
        sends.push(part_ref.at[y * 2 + 1 - tl], got_c.at[j], ssem.at[j], rsem.at[j], to_c)


def tensor_sum_middle(sends, part_ref, got_c, got_y, ssem, rsem):
    hi, lo, th, tl = place()
    arrive(got_c.at[0], ssem.at[0], rsem.at[0], device(hi, lo, th, 1 - tl))
    total = part_ref[(1 - th) * 2 + tl].astype(F32) + got_c[0].astype(F32)
    got_c[0] = total.astype(got_c.dtype)
    sends.push(got_c.at[0], got_y, ssem.at[2], rsem.at[2], device(hi, lo, 1 - th, tl))


def tensor_sum_end(part_ref, got_c, got_y, ssem, rsem):
    hi, lo, th, tl = place()
    arrive(got_c.at[1], ssem.at[1], rsem.at[1], device(hi, lo, th, 1 - tl))
    total = part_ref[th * 2 + tl].astype(F32) + got_c[1].astype(F32)
    arrive(got_y, ssem.at[2], rsem.at[2], device(hi, lo, 1 - th, tl))
    return total + got_y[...].astype(F32)


def tensor_spread_start(sends, o_ref, ssem, rsem):
    hi, lo, th, tl = place()
    own = o_ref.at[th * 2 + tl]
    sends.push(own, own, ssem.at[0], rsem.at[0], device(hi, lo, 1 - th, tl))
    sends.push(own, own, ssem.at[1], rsem.at[1], device(hi, lo, th, 1 - tl))


def tensor_spread_end(sends, o_ref, ssem, rsem):
    hi, lo, th, tl = place()
    other = o_ref.at[(1 - th) * 2 + tl]
    to_c = device(hi, lo, th, 1 - tl)
    arrive(other, ssem.at[0], rsem.at[0], device(hi, lo, 1 - th, tl))
    sends.push(other, other, ssem.at[2], rsem.at[2], to_c)
    arrive(o_ref.at[th * 2 + 1 - tl], ssem.at[1], rsem.at[1], to_c)
    arrive(o_ref.at[(1 - th) * 2 + 1 - tl], ssem.at[2], rsem.at[2], to_c)


def gather_steps(n_hi, x_ref, o_ref, own_sem, send_sem, recv_sem, lo_first=(True, False)):
    hi, lo, th, tl = place()
    rows = x_ref.shape[0]
    half = rows // 2
    own_block = (hi * 2 + lo) * 4 + th * 2 + tl
    own = pltpu.make_async_copy(x_ref, o_ref.at[pl.ds(own_block * rows, rows)], own_sem)
    own.start()
    sends = Sends()

    def slot(k, f, s, c):
        return ((c * 2 + s) * 2 + f) * n_hi + k

    def where(h, k, f, s, c):
        kk = peer(hi, k, n_hi)
        l = 1 - lo if (f if lo_first[h] else s) else lo
        y = 1 - th if (s if lo_first[h] else f) else th
        z = 1 - tl if c else tl
        return ((kk * 2 + l) * 4 + y * 2 + z) * rows + h * half

    def push(h, k, f, s, c, step):
        at = where(h, k, f, s, c)
        if k == 0 and not (f or s or c):
            src = x_ref.at[pl.ds(h * half, half)]
        else:
            src = o_ref.at[pl.ds(at, half)]
        if step == "c":
            to, r = device(hi, lo, th, 1 - tl), slot(k, f, s, 1)
        elif step == "s":
            to = device(hi, lo, 1 - th, tl) if lo_first[h] else device(hi, 1 - lo, th, tl)
            r = slot(k, f, 1, 0)
        elif step == "f":
            to = device(hi, 1 - lo, th, tl) if lo_first[h] else device(hi, lo, 1 - th, tl)
            r = slot(k, 1, 0, 0)
        else:
            to, r = device(peer(hi, step, n_hi), lo, th, tl), slot(back(step, n_hi), 0, 0, 0)
        sends.push(src, o_ref.at[pl.ds(at, half)], send_sem.at[h, r], recv_sem.at[h, r], to)

    def got(h, k, f, s, c):
        r = slot(k, f, s, c)
        arrive(
            o_ref.at[pl.ds(where(h, k, f, s, c), half)],
            send_sem.at[h, r], recv_sem.at[h, r], device(hi, lo, th, 1 - tl),
        )

    for k in range(n_hi):
        for h in range(2):
            if k:
                got(h, k, 0, 0, 0)
            if k < n_hi - 1:
                push(h, 0, 0, 0, 0, k + 1)
            for step in ("f", "s", "c"):
                push(h, k, 0, 0, 0, step)
        yield
        for h in range(2):
            got(h, k, 1, 0, 0)
            for step in ("s", "c"):
                push(h, k, 1, 0, 0, step)
        yield
    for k in range(n_hi):
        for f in range(2):
            for h in range(2):
                got(h, k, f, 1, 0)
                push(h, k, f, 1, 0, "c")
        yield
    for k in range(n_hi):
        for f in range(2):
            for s in range(2):
                for h in range(2):
                    got(h, k, f, s, 1)
    own.wait()
    sends.finish()


def in_turns(*streams):
    live = list(streams)
    while live:
        for stream in list(live):
            if next(stream, True) is True:
                live.remove(stream)


def middle_kernel(
    n_hi, part_ref, x_ref, gain_ref, o_ref, hidden_ref,
    normed, got_c, got_y, t_send, t_recv, *sems,
):
    greet(n_hi)
    sends = Sends()
    tensor_sum_start(sends, part_ref, got_c, t_send, t_recv)
    tensor_sum_middle(sends, part_ref, got_c, got_y, t_send, t_recv)
    hidden = x_ref[...].astype(F32) + tensor_sum_end(part_ref, got_c, got_y, t_send, t_recv)
    hidden_ref[...] = hidden
    normed[...] = (hidden * rms_scale(hidden) * gain_ref[...]).astype(normed.dtype)
    in_turns(gather_steps(n_hi, normed, o_ref, *sems))
    sends.finish()


def middle(part, x_piece, gain, n_dp, collective_id):
    rows, width = x_piece.shape
    n_hi = n_dp // 2
    return pl.pallas_call(
        functools.partial(middle_kernel, n_hi),
        out_shape=(
            jax.ShapeDtypeStruct((n_dp * 4 * rows, width), part.dtype),
            jax.ShapeDtypeStruct((rows, width), F32),
        ),
        in_specs=[VMEM_SPEC] * 3,
        out_specs=(ANY_SPEC, VMEM_SPEC),
        scratch_shapes=[pltpu.VMEM((rows, width), part.dtype)]
        + TENSOR_SUM_SCRATCH(rows, width, part.dtype)
        + [DMA, DMA((2, 8 * n_hi)), DMA((2, 8 * n_hi))],
        compiler_params=pltpu.CompilerParams(collective_id=collective_id, has_side_effects=True),
        name="middle",
    )(part.reshape(4, rows, width), x_piece, gain.reshape(1, width))


def weight_steps(n_hi, w_ref, o_ref, own_sem, send_b, recv_b, send_a, recv_a, send_f, recv_f):
    hi, lo, th, tl = place()
    to_f = device(hi, 1 - lo, th, tl)
    above = device(lax.rem(hi + 1, n_hi), lo, th, tl)
    below = device(lax.rem(hi + n_hi - 1, n_hi), lo, th, tl)
    sends = []

    def push(cond, src, at, h, ssem, rsem, to):
        copy = remote(src, o_ref.at[at, h], ssem, rsem, to)
        sends.append((cond, copy))
        if cond is None:
            copy.start()
        else:
            pl.when(cond)(copy.start)

    def block(j, l):
        return lax.rem(hi + j + n_hi, n_hi) * 2 + l

    for h in range(2):
        at = block(0, lo)
        push(hi < n_hi - 1, w_ref.at[h], at, h, send_b.at[h, 0], recv_b.at[h, 0], above)
        push(hi > 0, w_ref.at[h], at, h, send_a.at[h, 0], recv_a.at[h, 0], below)
        push(None, w_ref.at[h], at, h, send_f.at[h, 0], recv_f.at[h, 0], to_f)
    own = pltpu.make_async_copy(w_ref, o_ref.at[block(0, lo)], own_sem)
    own.start()
    yield
    for j in range(1, n_hi):
        for h in range(2):
            for down in (0, 1):
                valid = hi + j < n_hi if down else hi - j >= 0
                at = block(j if down else -j, lo)
                view = o_ref.at[at, h]
                sem = (send_a if down else send_b).at[h, j - 1], (recv_a if down else recv_b).at[h, j - 1]
                pl.when(valid)(remote(view, view, *sem, to_f).wait_recv)
                if j < n_hi - 1:
                    on = jnp.logical_and(valid, hi > 0 if down else hi < n_hi - 1)
                    push(
                        on, view, at, h, (send_a if down else send_b).at[h, j],
                        (recv_a if down else recv_b).at[h, j], below if down else above,
                    )
                f = 1 + down * (n_hi - 1) + j - 1
                push(valid, view, at, h, send_f.at[h, f], recv_f.at[h, f], to_f)
        yield
    for h in range(2):
        view = o_ref.at[block(0, 1 - lo), h]
        arrive(view, send_f.at[h, 0], recv_f.at[h, 0], to_f)
    for j in range(1, n_hi):
        for h in range(2):
            for down in (0, 1):
                valid = hi + j < n_hi if down else hi - j >= 0
                view = o_ref.at[block(j if down else -j, 1 - lo), h]
                f = 1 + down * (n_hi - 1) + j - 1
                pl.when(valid)(remote(view, view, send_f.at[h, f], recv_f.at[h, f], to_f).wait_recv)
    own.wait()
    for cond, copy in sends:
        if cond is None:
            copy.wait_send()
        else:
            pl.when(cond)(copy.wait_send)


def start_kernel(n_hi, n, *refs):
    ins, outs, sems = refs[: n + 1], refs[n + 1 : 2 * n + 2], refs[2 * n + 2 :]
    greet(n_hi)
    streams = [
        weight_steps(n_hi, ins[i], outs[i], *sems[7 * i : 7 * i + 7]) for i in range(n)
    ] + [gather_steps(n_hi, ins[n], outs[n], *sems[7 * n :], lo_first=(True, True))]
    in_turns(*streams)


def start(weights, table, n_dp, collective_id):
    n_hi = n_dp // 2
    n = len(weights)
    half = weights[0].shape[0] // 2
    outs = pl.pallas_call(
        functools.partial(start_kernel, n_hi, n),
        out_shape=[jax.ShapeDtypeStruct((n_dp, 2, half, w.shape[1]), w.dtype) for w in weights]
        + [jax.ShapeDtypeStruct((n_dp * 4 * table.shape[0], table.shape[1]), table.dtype)],
        in_specs=[ANY_SPEC] * (n + 1),
        out_specs=[ANY_SPEC] * (n + 1),
        scratch_shapes=[
            DMA,
            DMA((2, n_hi - 1)), DMA((2, n_hi - 1)),
            DMA((2, n_hi - 1)), DMA((2, n_hi - 1)),
            DMA((2, 2 * n_hi - 1)), DMA((2, 2 * n_hi - 1)),
        ] * n + [DMA, DMA((2, 8 * n_hi)), DMA((2, 8 * n_hi))],
        compiler_params=pltpu.CompilerParams(collective_id=collective_id, has_side_effects=True),
        name="start",
    )(*[w.reshape(2, half, w.shape[1]) for w in weights], table)
    return [o.reshape(n_dp * 2 * half, o.shape[3]) for o in outs[:n]] + [outs[n]]


def scatter_steps(n_hi, sends, p_ref, o_ref, bufs):
    (stage, from_c, from_f, from_s, from_h,
     stage_sem, send_c, recv_c, send_f, recv_f, send_s, recv_s, send_h, recv_h) = bufs
    depth = stage.shape[0]
    hi, lo, th, tl = place()
    to_c = device(hi, lo, th, 1 - tl)
    rows = o_ref.shape[0]
    half = rows // 2

    def where(h, k, f, s, c):
        kk = peer(hi, k, n_hi)
        l = 1 - lo if (f if h == 1 else s) else lo
        y = 1 - th if (s if h == 1 else f) else th
        z = 1 - tl if c else tl
        return ((kk * 2 + l) * 4 + y * 2 + z) * rows + h * half

    ks = list(range(1, n_hi)) + [0]
    order = []
    for i in range(n_hi + 2):
        for lag, groups in ((0, ((1, 1), (1, 0))), (1, ((0, 1),)), (2, ((0, 0),))):
            if 0 <= i - lag < n_hi:
                order += [(f, s, ks[i - lag], h) for f, s in groups for h in range(2)]

    def slot(f, s, k):
        return (f * 2 + s) * n_hi + k

    def first(h):
        return device(hi, lo, 1 - th, tl) if h == 0 else device(hi, 1 - lo, th, tl)

    def second(h):
        return device(hi, 1 - lo, th, tl) if h == 0 else device(hi, lo, 1 - th, tl)

    for f, s, k, h in order:
        n = slot(f, s, k)
        sends.push(
            p_ref.at[pl.ds(where(h, k, f, s, 1), half)], from_c.at[h, n], send_c.at[h, n],
            recv_c.at[h, n], to_c,
        )

    def load(i):
        f, s, k, h = order[i]
        return pltpu.make_async_copy(
            p_ref.at[pl.ds(where(h, k, f, s, 0), half)], stage.at[i % depth], stage_sem.at[i % depth]
        )

    for i in range(depth - 1):
        load(i).start()
    for i, (f, s, k, h) in enumerate(order):
        if i + depth - 1 < len(order):
            load(i + depth - 1).start()
        load(i).wait()
        n = slot(f, s, k)
        arrive(from_c.at[h, n], send_c.at[h, n], recv_c.at[h, n], to_c)
        total = stage[i % depth].astype(F32) + from_c[h, n].astype(F32)
        if f == 0:
            m = s * n_hi + k
            arrive(from_f.at[h, m], send_f.at[h, m], recv_f.at[h, m], to_c)
            total = total + from_f[h, m].astype(F32)
        if f == 0 and s == 0:
            arrive(from_s.at[h, k], send_s.at[h, k], recv_s.at[h, k], to_c)
            total = total + from_s[h, k].astype(F32)
        if f == 0 and s == 0 and k == 0:
            for j in range(n_hi - 1):
                arrive(from_h.at[h, j], send_h.at[h, j], recv_h.at[h, j], to_c)
                total = total + from_h[h, j].astype(F32)
            o_ref[pl.ds(h * half, half), :] = total
            continue
        from_c[h, n] = total.astype(from_c.dtype)
        src = from_c.at[h, n]
        if f == 1:
            m = s * n_hi + k
            sends.push(src, from_f.at[h, m], send_f.at[h, m], recv_f.at[h, m], first(h))
        elif s == 1:
            sends.push(src, from_s.at[h, k], send_s.at[h, k], recv_s.at[h, k], second(h))
        else:
            j = back(k, n_hi) - 1
            sends.push(
                src, from_h.at[h, j], send_h.at[h, j], recv_h.at[h, j],
                device(peer(hi, k, n_hi), lo, th, tl),
            )


def scatter_scratch(n_hi, half, width, dtype, depth=4):
    return [
        pltpu.VMEM((depth, half, width), dtype),
        pltpu.VMEM((2, 4 * n_hi, half, width), dtype),
        pltpu.VMEM((2, 2 * n_hi, half, width), dtype),
        pltpu.VMEM((2, n_hi, half, width), dtype),
        pltpu.VMEM((2, n_hi - 1, half, width), dtype),
        DMA((depth,)),
        DMA((2, 4 * n_hi)), DMA((2, 4 * n_hi)),
        DMA((2, 2 * n_hi)), DMA((2, 2 * n_hi)),
        DMA((2, n_hi)), DMA((2, n_hi)),
        DMA((2, n_hi - 1)), DMA((2, n_hi - 1)),
    ]


def scatter_kernel(n_hi, p_ref, o_ref, *bufs):
    greet(n_hi)
    sends = Sends()
    scatter_steps(n_hi, sends, p_ref, o_ref, bufs)
    sends.finish()


def scatter_rows(p, n_dp, collective_id):
    width = p.shape[1]
    rows = p.shape[0] // (n_dp * 4)
    n_hi = n_dp // 2
    return pl.pallas_call(
        functools.partial(scatter_kernel, n_hi),
        out_shape=jax.ShapeDtypeStruct((rows, width), F32),
        in_specs=[ANY_SPEC],
        out_specs=VMEM_SPEC,
        scratch_shapes=scatter_scratch(n_hi, rows // 2, width, p.dtype),
        compiler_params=pltpu.CompilerParams(
            collective_id=collective_id, has_side_effects=True, vmem_limit_bytes=60 << 20
        ),
        name="scatter_rows",
    )(p)


def turn_kernel(
    n_hi, p_ref, hidden_ref, g2_ref, gain_ref, grad_ref, sum_ref, dm_ref, total_ref, sp_send, sp_recv, *bufs
):
    hi, lo, th, tl = place()
    greet(n_hi)
    sends = Sends()
    scatter_steps(n_hi, sends, p_ref, total_ref, bufs)
    grad = total_ref[...]
    hidden = hidden_ref[...]
    scale = rms_scale(hidden)
    weighted = gain_ref[...] * grad
    sum_ref[...] = jnp.sum(grad * hidden * scale, axis=0, keepdims=True)
    mean = jnp.mean(weighted * hidden, axis=-1, keepdims=True)
    grad = g2_ref[...].astype(F32) + scale * weighted - hidden * (scale * scale * scale) * mean
    grad_ref[...] = grad
    dm_ref[th * 2 + tl] = grad.astype(dm_ref.dtype)
    tensor_spread_start(sends, dm_ref, sp_send, sp_recv)
    tensor_spread_end(sends, dm_ref, sp_send, sp_recv)
    sends.finish()


def turn(p, hidden, g2_piece, gain, n_dp, collective_id):
    rows, width = hidden.shape
    n_hi = n_dp // 2
    return pl.pallas_call(
        functools.partial(turn_kernel, n_hi),
        out_shape=(
            jax.ShapeDtypeStruct((rows, width), F32),
            jax.ShapeDtypeStruct((1, width), F32),
            jax.ShapeDtypeStruct((4, rows, width), p.dtype),
        ),
        in_specs=[ANY_SPEC] + [VMEM_SPEC] * 3,
        out_specs=(VMEM_SPEC,) * 3,
        scratch_shapes=[pltpu.VMEM((rows, width), F32), DMA((3,)), DMA((3,))]
        + scatter_scratch(n_hi, rows // 2, width, p.dtype),
        compiler_params=pltpu.CompilerParams(
            collective_id=collective_id, has_side_effects=True, vmem_limit_bytes=60 << 20
        ),
        name="turn",
    )(p, hidden, g2_piece, gain.reshape(1, width))


def tail_kernel(n_hi, wide, bc_at, n, *refs):
    part_ref, grad_ref, x_ref, gain_ref, small_ref = refs[:5]
    w_refs = refs[5 : 5 + n]
    ox_ref, os_ref = refs[5 + n : 7 + n]
    ow_refs = refs[7 + n : 7 + 2 * n]
    (got_c, got_y, t_send, t_recv, sp_send, sp_recv,
     small, small_f, small_h, small_t, sm_send, sm_recv, smh_send, smh_recv,
     bc_own, bc_got, bc_send, bc_recv) = refs[7 + 2 * n : 25 + 2 * n]
    rest = refs[25 + 2 * n :]
    bufs = [rest[8 * i : 8 * i + 8] for i in range(n)]
    hi, lo, th, tl = place()
    to_f, to_y, to_c = device(hi, 1 - lo, th, tl), device(hi, lo, 1 - th, tl), device(hi, lo, th, 1 - tl)
    greet(n_hi)
    sends = Sends()
    order = [(k, h) for k in reversed(range(n_hi)) for h in range(2)]
    events = [(w, k, h) for w in range(n) for k, h in order]
    events = [e for e in events if e[1]] + [e for e in events if not e[1]]

    def owner(k, l):
        return peer(hi, k, n_hi) * 2 + l

    def forward(i):
        if i < len(events):
            w, k, h = events[i]
            stage, from_f, from_h, stage_sem, send_f, recv_f, send_h, recv_h = bufs[w]
            sends.push(
                w_refs[w].at[owner(k, 1 - lo), h], from_f.at[h, k], send_f.at[h, k], recv_f.at[h, k], to_f
            )

    window = 4
    for i in range(window):
        forward(i)
    loads = []
    for w, k, h in events:
        copy = pltpu.make_async_copy(
            w_refs[w].at[owner(k, lo), h], bufs[w][0].at[h, k], bufs[w][3].at[h, k]
        )
        copy.start()
        loads.append(copy)
    tensor_sum_start(sends, part_ref, got_c, t_send, t_recv)
    tensor_sum_middle(sends, part_ref, got_c, got_y, t_send, t_recv)
    grad = tensor_sum_end(part_ref, got_c, got_y, t_send, t_recv)
    x = x_ref[...].astype(F32)
    scale = rms_scale(x)
    weighted = gain_ref[...] * grad
    mean = jnp.mean(weighted * x, axis=-1, keepdims=True)
    ox_ref[th * 2 + tl] = (
        grad_ref[...] + scale * weighted - x * (scale * scale * scale) * mean
    ).astype(ox_ref.dtype)
    tensor_spread_start(sends, ox_ref, sp_send, sp_recv)
    small[...] = small_ref[...]
    small[0:1, :] = jnp.sum(grad * x * scale, axis=0, keepdims=True)
    sends.push(small, small_f, sm_send.at[0], sm_recv.at[0], to_f)

    for i, (w, k, h) in enumerate(events):
        if k == 0:
            break
        stage, from_f, from_h, stage_sem, send_f, recv_f, send_h, recv_h = bufs[w]
        loads[i].wait()
        arrive(from_f.at[h, k], send_f.at[h, k], recv_f.at[h, k], to_c)
        forward(i + window)
        from_f[h, k] = (stage[h, k].astype(F32) + from_f[h, k].astype(F32)).astype(from_f.dtype)
        j = back(k, n_hi) - 1
        sends.push(
            from_f.at[h, k], from_h.at[h, j], send_h.at[h, j], recv_h.at[h, j],
            device(peer(hi, k, n_hi), lo, th, tl),
        )
        if i == 0:
            tensor_spread_end(sends, ox_ref, sp_send, sp_recv)
        if i == 1:
            arrive(small_f, sm_send.at[0], sm_recv.at[0], to_c)
            small_h[hi] = small[...] + small_f[...]
            for q in range(1, n_hi):
                sends.push(
                    small_h.at[hi], small_h.at[hi], smh_send.at[q - 1], smh_recv.at[back(q, n_hi) - 1],
                    device(peer(hi, q, n_hi), lo, th, tl),
                )
    for q in range(1, n_hi):
        arrive(small_h.at[peer(hi, q, n_hi)], smh_send.at[q - 1], smh_recv.at[q - 1], to_c)
    total = small_h[0]
    for q in range(1, n_hi):
        total = total + small_h[q]
    os_ref[...] = total
    sends.push(os_ref.at[pl.ds(0, wide)], small_t.at[0], sm_send.at[1], sm_recv.at[1], to_c)
    for i, (w, k, h) in enumerate(events):
        if k:
            continue
        forward(i + window)
        stage, from_f, from_h, stage_sem, send_f, recv_f, send_h, recv_h = bufs[w]
        loads[i].wait()
        arrive(from_f.at[h, 0], send_f.at[h, 0], recv_f.at[h, 0], to_c)
        total = stage[h, 0].astype(F32) + from_f[h, 0].astype(F32)
        for j in range(n_hi - 1):
            arrive(from_h.at[h, j], send_h.at[h, j], recv_h.at[h, j], to_c)
            total = total + from_h[h, j].astype(F32)
        ow_refs[w][h] = total
        if w == 0:
            bc_own[0, h] = total[:, bc_at : bc_at + bc_own.shape[3]].astype(bc_own.dtype)
            if h == 1:
                sends.push(bc_own.at[0], bc_got.at[0], bc_send.at[0], bc_recv.at[0], to_c)
                arrive(small_t.at[0], sm_send.at[1], sm_recv.at[1], to_c)
                small_t[2] = os_ref[pl.ds(0, wide), :] + small_t[0]
                sends.push(small_t.at[2], small_t.at[1], sm_send.at[2], sm_recv.at[2], to_y)
                arrive(bc_got.at[0], bc_send.at[0], bc_recv.at[0], to_c)
                bc_own[1] = (bc_own[0].astype(F32) + bc_got[0].astype(F32)).astype(bc_own.dtype)
                sends.push(bc_own.at[1], bc_got.at[1], bc_send.at[1], bc_recv.at[1], to_y)
    arrive(small_t.at[1], sm_send.at[2], sm_recv.at[2], to_c)
    arrive(bc_got.at[1], bc_send.at[1], bc_recv.at[1], to_c)
    for h in range(2):
        ow_refs[0][h, :, bc_at : bc_at + bc_own.shape[3]] = (
            bc_own[1, h].astype(F32) + bc_got[1, h].astype(F32)
        )
    sends.finish()
    os_ref[pl.ds(0, wide), :] = small_t[2] + small_t[1]


def tail(weights, part, grad_one, x_piece, gain, small, wide, bc_at, bc_width, n_dp, collective_id):
    rows, width = x_piece.shape
    n_hi = n_dp // 2
    n = len(weights)
    half = weights[0].shape[0] // (2 * n_dp)
    dt = weights[0].dtype
    scratch = TENSOR_SUM_SCRATCH(rows, width, part.dtype) + [
        DMA((3,)), DMA((3,)),
        pltpu.VMEM(small.shape, F32),
        pltpu.VMEM(small.shape, F32),
        pltpu.VMEM((n_hi,) + small.shape, F32),
        pltpu.VMEM((3, wide, small.shape[1]), F32),
        DMA((3,)), DMA((3,)),
        DMA((n_hi - 1,)), DMA((n_hi - 1,)),
        pltpu.VMEM((2, 2, half, bc_width), dt),
        pltpu.VMEM((2, 2, half, bc_width), dt),
        DMA((2,)), DMA((2,)),
    ]
    for w in weights:
        scratch += [
            pltpu.VMEM((2, n_hi, half, w.shape[1]), dt),
            pltpu.VMEM((2, n_hi, half, w.shape[1]), dt),
            pltpu.VMEM((2, n_hi - 1, half, w.shape[1]), dt),
            DMA((2, n_hi)),
            DMA((2, n_hi)), DMA((2, n_hi)),
            DMA((2, n_hi - 1)), DMA((2, n_hi - 1)),
        ]
    outs = pl.pallas_call(
        functools.partial(tail_kernel, n_hi, wide, bc_at, n),
        out_shape=[
            jax.ShapeDtypeStruct((4, rows, width), dt),
            jax.ShapeDtypeStruct(small.shape, F32),
        ] + [jax.ShapeDtypeStruct((2, half, w.shape[1]), F32) for w in weights],
        in_specs=[VMEM_SPEC] * 5 + [ANY_SPEC] * n,
        out_specs=[VMEM_SPEC] * (2 + n),
        scratch_shapes=scratch,
        compiler_params=pltpu.CompilerParams(
            collective_id=collective_id, has_side_effects=True, vmem_limit_bytes=60 << 20
        ),
        name="tail",
    )(
        part.reshape(4, rows, width), grad_one, x_piece, gain.reshape(1, width), small,
        *[w.reshape(n_dp, 2, half, w.shape[1]) for w in weights],
    )
    return outs[0], outs[1], [o.reshape(2 * half, o.shape[2]) for o in outs[2:]]


def dot_mm(a, b):
    return lax.dot_general(a, b, (((1,), (0,)), ((), ())), preferred_element_type=F32)


def dot_nt(a, b):
    return lax.dot_general(a, b, (((1,), (1,)), ((), ())), preferred_element_type=F32)


def dot_tn(a, b):
    return lax.dot_general(a, b, (((0,), (0,)), ((), ())), preferred_element_type=F32)


def experts_kernel(
    n_dp, n_local, cap, chunk, pos_ref, wt_ref, x_ref, g_ref, gu_ref, dn_ref,
    dxn_ref, out_ref, ggu_ref, gdn_ref, pick, xr, q, sw, gu,
):
    step = pl.program_id(0)
    width = x_ref.shape[1]
    hidden = dn_ref.shape[1]
    slots = x_ref.shape[0]
    columns = [pl.ds(c, chunk) for c in range(0, width, chunk)]

    @pl.when(step < n_dp)
    def _():
        s = step
        lane = lax.broadcasted_iota(jnp.int32, (cap, slots), 0)
        for e in range(n_local):
            hit = lane == pos_ref[0, e : e + 1, :]
            pick[s, e * cap : (e + 1) * cap, :] = jnp.where(hit, 1.0, 0.0).astype(BF)
            sw[e, s] = jnp.sum(jnp.where(hit, wt_ref[0, e : e + 1, :], 0.0), axis=1, keepdims=True)
        chosen = pick[s]
        for c in columns:
            rows = dot_mm(chosen, x_ref[:, c]).astype(BF)
            grads = dot_mm(chosen, g_ref[:, c])
            for e in range(n_local):
                xr[e, s, :, c] = rows[e * cap : (e + 1) * cap]
                q[e, s, :, c] = (grads[e * cap : (e + 1) * cap] * sw[e, s]).astype(BF)

    @pl.when(jnp.logical_and(step >= n_dp, step < n_dp + n_local))
    def _():
        e = step - n_dp
        gu[:, :hidden] = gu_ref[pl.ds(0, width, stride=2), :].astype(BF)
        gu[:, hidden:] = gu_ref[pl.ds(1, width, stride=2), :].astype(BF)
        down = dn_ref[0].astype(BF)
        x = xr[e].reshape(n_dp * cap, width)
        qe = q[e].reshape(n_dp * cap, width)
        pre = dot_mm(x, gu[...])
        grad_act = dot_nt(qe, down)
        gate, up = pre[:, :hidden], pre[:, hidden:]
        sig = 1.0 / (1.0 + jnp.exp(-gate))
        act_silu = gate * sig
        slope = sig * (1.0 + gate * (1.0 - sig))
        value = act_silu * up
        act = value.astype(BF)
        scaled = (value * sw[e].reshape(n_dp * cap, 1)).astype(BF)
        grad_pre = jnp.concatenate([grad_act * up * slope, grad_act * act_silu], axis=1).astype(BF)
        ggu = dot_tn(x, grad_pre)
        ggu_ref[pl.ds(0, width, stride=2), :] = ggu[:, :hidden]
        ggu_ref[pl.ds(1, width, stride=2), :] = ggu[:, hidden:]
        gdn_ref[0] = dot_tn(act, qe)
        for c in columns:
            xr[e, :, :, c] = dot_nt(grad_pre, gu[c, :]).astype(BF).reshape(n_dp, cap, chunk)
            q[e, :, :, c] = dot_mm(scaled, down[:, c.start : c.start + chunk]).astype(BF).reshape(n_dp, cap, chunk)

    @pl.when(step >= n_dp + n_local)
    def _():
        s = step - n_dp - n_local
        chosen = pick[s]
        for c in columns:
            dxn_ref[:, c] = dot_tn(chosen, xr[:, s, :, c].reshape(n_local * cap, chunk)).astype(BF)
            out_ref[:, c] = dot_tn(chosen, q[:, s, :, c].reshape(n_local * cap, chunk)).astype(BF)


def experts(position, weights, rows, table, w_gu, w_down, cap):
    n_dp, n_local, slots = position.shape
    width = rows.shape[1]
    hidden = w_down.shape[1]
    chunk = width // 3 if width % 384 == 0 else width
    by_source = lambda i: (jnp.clip(i, 0, n_dp - 1), 0, 0)
    rows_in = lambda i: (jnp.clip(i, 0, n_dp - 1), 0)
    rows_out = lambda i: (jnp.clip(i - n_dp - n_local, 0, n_dp - 1), 0)
    flat = lambda i: (jnp.clip(i - n_dp, 0, n_local - 1), 0)
    deep = lambda i: (jnp.clip(i - n_dp, 0, n_local - 1), 0, 0)
    total = n_dp * n_local * cap
    return pl.pallas_call(
        functools.partial(experts_kernel, n_dp, n_local, cap, chunk),
        grid=(2 * n_dp + n_local,),
        out_shape=(
            jax.ShapeDtypeStruct((n_dp * slots, width), BF),
            jax.ShapeDtypeStruct((n_dp * slots, width), BF),
            jax.ShapeDtypeStruct((n_local * width * 2, hidden), F32),
            jax.ShapeDtypeStruct((n_local, hidden, width), F32),
        ),
        in_specs=[
            pl.BlockSpec((1, n_local, slots), by_source),
            pl.BlockSpec((1, n_local, slots), by_source),
            pl.BlockSpec((slots, width), rows_in),
            pl.BlockSpec((slots, width), rows_in),
            pl.BlockSpec((width * 2, hidden), flat),
            pl.BlockSpec((1, hidden, width), deep),
        ],
        out_specs=(
            pl.BlockSpec((slots, width), rows_out),
            pl.BlockSpec((slots, width), rows_out),
            pl.BlockSpec((width * 2, hidden), flat),
            pl.BlockSpec((1, hidden, width), deep),
        ),
        scratch_shapes=[
            pltpu.VMEM((n_dp, n_local * cap, slots), BF),
            pltpu.VMEM((n_local, n_dp, cap, width), BF),
            pltpu.VMEM((n_local, n_dp, cap, width), BF),
            pltpu.VMEM((n_local, n_dp, cap, 1), F32),
            pltpu.VMEM((width, 2 * hidden), BF),
        ],
        compiler_params=pltpu.CompilerParams(
            dimension_semantics=("arbitrary",), vmem_limit_bytes=60 << 20
        ),
        cost_estimate=pl.CostEstimate(
            flops=8 * total * slots * width + 18 * total * width * hidden,
            bytes_accessed=8 * n_dp * slots * width + 24 * n_local * width * hidden,
            transcendentals=total * hidden,
        ),
        name="experts",
    )(
        position,
        weights,
        rows,
        table,
        w_gu.reshape(n_local * width * 2, hidden),
        w_down,
    )


def local(
    x_in,
    lengths,
    routes,
    route_w,
    ln1_gain,
    w_zx,
    w_bc,
    w_dt,
    conv_x,
    conv_x_bias,
    conv_bc,
    conv_bc_bias,
    dt_bias,
    a_log,
    d_skip,
    gnorm_gain,
    w_out,
    ln2_gain,
    w_shared_gu,
    w_shared_down,
    w_exp_gu,
    w_exp_down,
    cotangent,
):
    slots, width = x_in.shape
    n_dp = lax.axis_size("dp")
    n_t = lax.axis_size("tensor")
    my_t = lax.axis_index("tensor")
    my_dp = lax.axis_index("dp")
    piece = slots // n_t
    n_local = w_exp_gu.shape[0]
    n_experts = n_dp * n_local
    cap = slots * routes.shape[1] * 4 // (3 * n_experts)
    if cap > slots:
        cap = slots
    heads = dt_bias.shape[0]
    inner = conv_x.shape[1]
    head_size = inner // heads
    state = conv_bc.shape[1] // 2
    full_inner = inner * n_t
    rows = w_zx.shape[0]
    n_sh = w_shared_gu.shape[2]

    dt_at = 2 * inner + 2 * state
    first_width = dt_at + heads + -(dt_at + heads) % 128
    first = jnp.concatenate(
        [
            w_zx.reshape(rows, 2 * inner),
            w_bc,
            w_dt,
            jnp.zeros((rows, first_width - dt_at - heads), F32),
        ],
        axis=1,
    ).astype(BF)
    shared = jnp.concatenate([w_shared_gu.reshape(rows, 2 * n_sh), w_shared_down], axis=1)

    live = (jnp.arange(slots, dtype=jnp.int32) < lengths[0]).astype(F32)
    g2 = cotangent.astype(F32) * live[:, None]
    g2_low = g2.astype(BF)
    expert_range = jnp.arange(n_experts, dtype=jnp.int32)
    chosen = routes[:, :, None] == expert_range[None, None, :]
    weights = jnp.sum(jnp.where(chosen, route_w[:, :, None], 0.0), axis=1)
    high = weights.astype(BF)
    low = (weights - high.astype(F32)).astype(BF)
    table = jnp.concatenate([g2_low, high, low], axis=1)
    table = lax.dynamic_slice_in_dim(table, my_t * piece, piece, axis=0)
    g2_piece = lax.dynamic_slice_in_dim(g2_low, my_t * piece, piece, axis=0)

    first, proj_out, table = start([first, w_out.astype(BF)], table, n_dp, 1)
    shared, first = lax.optimization_barrier((shared.astype(BF), first))
    shared = lax.all_gather(shared, "dp", axis=0, tiled=True)
    shared_gu = shared[:, : 2 * n_sh]
    shared_down = shared[:, 2 * n_sh :]

    x_float = x_in.astype(F32)
    scale_one = rms_scale(x_float)
    normed_one = (x_float * scale_one * ln1_gain).astype(BF)
    firsts = dotf("td,df->tf", normed_one, first)
    zx = firsts[:, : 2 * inner]
    bc_proj = firsts[:, 2 * inner : dt_at]
    dt_proj = firsts[:, dt_at : dt_at + heads]

    gated_mix, mixer_back = mixer_forward(
        zx, bc_proj, dt_proj, conv_x, conv_x_bias, conv_bc, conv_bc_bias, dt_bias, a_log, d_skip
    )
    squares = lax.psum(jnp.sum(gated_mix * gated_mix, axis=-1), "tensor")
    scale_mix = lax.rsqrt(squares / full_inner + EPSILON)[:, None]
    normed_mix = (gated_mix * scale_mix * gnorm_gain).astype(BF)
    mixer_part = dotf("tc,dc->td", normed_mix, proj_out).astype(BF)
    x_piece = lax.dynamic_slice_in_dim(x_in, my_t * piece, piece, axis=0)
    all_rows, hidden_one = middle(mixer_part, x_piece, ln2_gain, n_dp, 2)
    mine = lax.dynamic_slice_in_dim(all_rows, my_dp * slots, slots, axis=0)

    shared_pre = dotf("td,df->tf", mine, shared_gu)
    s_gate, s_up = shared_pre[:, :n_sh], shared_pre[:, n_sh:]
    shared_silu, shared_slope = silu_parts(s_gate)
    shared_act = (shared_silu * s_up).astype(BF)
    grad_shared_act = dotf("td,df->tf", g2_low, shared_down)
    grad_shared_pre = jnp.concatenate(
        [grad_shared_act * s_up * shared_slope, grad_shared_act * shared_silu], axis=1
    ).astype(BF)
    grad_normed_shared = dotf("tf,df->td", grad_shared_pre, shared_gu)
    shared_part = dotf("tf,df->td", shared_act, shared_down)

    high = lax.dynamic_slice_in_dim(table, width + my_dp * n_local, n_local, axis=1)
    low = lax.dynamic_slice_in_dim(table, width + n_experts + my_dp * n_local, n_local, axis=1)
    weights = (high.astype(F32) + low.astype(F32)).reshape(n_dp, slots, n_local)
    member = (weights > 0.0).astype(BF)
    before = (
        jnp.arange(slots)[:, None] > jnp.arange(slots)[None, :]
    ).astype(BF)
    position = dotf("ut,ste->seu", before, member).astype(jnp.int32)
    weights = weights.transpose(0, 2, 1)
    position = jnp.where(weights > 0.0, position, -1)

    dxn_part, out_part, grad_exp_gu, grad_exp_down = experts(
        position, weights, all_rows, table, w_exp_gu, w_exp_down, cap
    )
    grad_exp_gu = grad_exp_gu.reshape(w_exp_gu.shape)

    def add_own(total, own):
        at = my_dp * slots
        own = own + lax.dynamic_slice_in_dim(total, at, slots, axis=0).astype(F32)
        return lax.dynamic_update_slice_in_dim(total, own.astype(BF), at, axis=0)

    dxn_part = add_own(dxn_part, grad_normed_shared)
    out_part = add_own(out_part, shared_part)
    ffn_out = scatter_rows(out_part, n_dp, 4)
    dxn_part, ffn_out = lax.optimization_barrier((dxn_part, ffn_out))
    grad_one, sum_ln2, dm = turn(
        dxn_part, hidden_one, g2_piece, ln2_gain, n_dp, 3
    )
    dm = dm.reshape(slots, width)

    layer_out = lax.all_gather(
        (hidden_one + ffn_out).astype(BF), "tensor", axis=0, tiled=True
    )
    grad_shared_down = dotf("td,tf->df", g2_low, shared_act)
    grad_shared_gu = dotf("td,tf->df", mine, grad_shared_pre)

    grad_shared_w = jnp.concatenate([grad_shared_gu, grad_shared_down], axis=1).astype(BF)
    grad_shared_w = lax.psum_scatter(grad_shared_w, "dp", scatter_dimension=0, tiled=True)
    grad_out_w = dotf("td,tc->dc", dm, normed_mix).astype(BF)
    grad_normed_mix = dotf("td,dc->tc", dm, proj_out)
    weighted_mix = gnorm_gain * grad_normed_mix
    grad_gnorm = jnp.sum(grad_normed_mix * gated_mix * scale_mix, axis=0)
    product_sum = lax.psum(jnp.sum(weighted_mix * gated_mix, axis=-1), "tensor")[:, None]
    grad_gated = scale_mix * weighted_mix - gated_mix * scale_mix**3 * product_sum / full_inner
    (
        grad_zx,
        grad_bc,
        grad_dt_low,
        grad_conv_x,
        grad_conv_x_bias,
        grad_conv_bc,
        grad_conv_bc_bias,
        grad_dt_bias,
        grad_a_log,
        grad_d_skip,
    ) = mixer_back(grad_gated)
    grad_first = jnp.concatenate(
        [
            grad_zx,
            grad_bc.astype(BF),
            grad_dt_low,
            jnp.zeros((slots, first_width - dt_at - heads), BF),
        ],
        axis=1,
    )
    grad_input_part = dotf("tf,df->td", grad_first, first).astype(BF)
    grad_first_w = dotf("td,tf->df", normed_one, grad_first).astype(BF)
    def lanes(*vectors):
        vector = jnp.concatenate([v.reshape(-1) for v in vectors])
        return jnp.pad(vector, (0, -vector.shape[0] % (8 * width))).reshape(-1, width)

    taps = conv_x.shape[0]
    wide = lanes(jnp.zeros((width,), F32), sum_ln2, grad_conv_bc, grad_conv_bc_bias)
    n_wide = wide.shape[0]
    narrow = lanes(
        grad_conv_x, grad_conv_x_bias, grad_gnorm, grad_dt_bias, grad_a_log, grad_d_skip
    )
    grad_first_w, grad_shared_w = lax.optimization_barrier((grad_first_w, grad_shared_w))
    grad_x, sums, (first_f, grad_out_w) = tail(
        [grad_first_w, grad_out_w],
        grad_input_part,
        grad_one,
        x_piece,
        ln1_gain,
        jnp.concatenate([wide, narrow], axis=0),
        n_wide,
        2 * inner,
        2 * state,
        n_dp,
        5,
    )
    grad_x = grad_x.reshape(slots, width).astype(F32)
    wide, narrow = sums[:n_wide].reshape(-1), sums[n_wide:].reshape(-1)
    at = [0]

    def take(vector, *shape):
        size = 1
        for s in shape:
            size *= s
        part = lax.slice_in_dim(vector, at[0], at[0] + size).reshape(shape)
        at[0] += size
        return part

    o_ln1 = take(wide, width)
    o_ln2 = take(wide, width)
    o_conv_bc = take(wide, taps, 2 * state)
    o_conv_bc_bias = take(wide, 2 * state)
    at[0] = 0
    o_conv_x = take(narrow, taps, inner)
    o_conv_x_bias = take(narrow, inner)
    o_gnorm = take(narrow, inner)
    o_dt_bias = take(narrow, heads)
    o_a_log = take(narrow, heads)
    o_d_skip = take(narrow, heads)
    shared_f = grad_shared_w.astype(F32)
    return (
        layer_out,
        grad_x,
        o_ln1,
        first_f[:, : 2 * inner].reshape(rows, 2, inner),
        first_f[:, 2 * inner : dt_at],
        first_f[:, dt_at : dt_at + heads],
        o_conv_x,
        o_conv_x_bias,
        o_conv_bc,
        o_conv_bc_bias,
        o_dt_bias,
        o_a_log,
        o_d_skip,
        o_gnorm,
        grad_out_w,
        o_ln2,
        shared_f[:, : 2 * n_sh].reshape(rows, 2, n_sh),
        shared_f[:, 2 * n_sh :],
        grad_exp_gu,
        grad_exp_down,
    )


def solution(mesh):
    return jax.shard_map(
        local,
        mesh=mesh,
        in_specs=(
            P("dp", None),
            P("dp"),
            P("dp", None),
            P("dp", None),
            P(),
            P("dp", None, "tensor"),
            P("dp", None),
            P("dp", "tensor"),
            P(None, "tensor"),
            P("tensor"),
            P(),
            P(),
            P("tensor"),
            P("tensor"),
            P("tensor"),
            P("tensor"),
            P("dp", "tensor"),
            P(),
            P("dp", None, "tensor"),
            P("dp", "tensor"),
            P("dp", None, None, "tensor"),
            P("dp", "tensor", None),
            P("dp", None),
        ),
        out_specs=(
            P("dp", None),
            P("dp", None),
            P(),
            P("dp", None, "tensor"),
            P("dp", None),
            P("dp", "tensor"),
            P(None, "tensor"),
            P("tensor"),
            P(),
            P(),
            P("tensor"),
            P("tensor"),
            P("tensor"),
            P("tensor"),
            P("dp", "tensor"),
            P(),
            P("dp", None, "tensor"),
            P("dp", "tensor"),
            P("dp", None, None, "tensor"),
            P("dp", "tensor", None),
        ),
        check_vma=False,
    )
```

```python
import functools

import jax
import jax.numpy as jnp
from jax import lax
from jax.experimental import pallas as pl
from jax.experimental.pallas import tpu as pltpu
from jax.sharding import PartitionSpec as P

BLOCK = 256


EPSILON = 1e-05
HIGHEST = lax.Precision.HIGHEST
BF = jnp.bfloat16
F32 = jnp.float32


def rms_scale(values):
    return lax.rsqrt(jnp.mean(values * values, axis=-1, keepdims=True) + EPSILON)


def silu_parts(values):
    sigmoid_val = jax.nn.sigmoid(values)
    return (values * sigmoid_val, sigmoid_val * (1.0 + values * (1.0 - sigmoid_val)))


def dotf(spec, a, b):
    return jnp.einsum(spec, a, b, preferred_element_type=F32)


MESH = pl.DeviceIdType.MESH
DMA = pltpu.SemaphoreType.DMA
VMEM_SPEC = pl.BlockSpec(memory_space=pltpu.VMEM)
ANY_SPEC = pl.BlockSpec(memory_space=pl.ANY)


def place():
    d = lax.axis_index("dp")
    t = lax.axis_index("tensor")
    return d // 2, d % 2, t // 2, t % 2


def device(hi, lo, th, tl):
    return (hi * 2 + lo, th * 2 + tl)


def peer(hi, k, n_hi):
    if n_hi & (n_hi - 1):
        return lax.rem(hi + k, n_hi)
    other, bit = hi, 1
    while bit <= k:
        if k & bit:
            other = other + bit * (1 - 2 * lax.rem(hi // bit, 2))
        bit *= 2
    return other


def back(k, n_hi):
    return n_hi - k if n_hi & (n_hi - 1) else k


def greet(n_hi, tensor=True):
    hi, lo, th, tl = place()
    barrier = pltpu.get_barrier_semaphore()
    others = [device(peer(hi, k, n_hi), lo, th, tl) for k in range(1, n_hi)]
    others += [device(hi, 1 - lo, th, tl)]
    if tensor:
        others += [device(hi, lo, 1 - th, tl), device(hi, lo, th, 1 - tl)]
    for other in others:
        pl.semaphore_signal(barrier, inc=1, device_id=other, device_id_type=MESH)
    pl.semaphore_wait(barrier, len(others))


def remote(src, dst, ssem, rsem, to):
    return pltpu.make_async_remote_copy(
        src_ref=src, dst_ref=dst, send_sem=ssem, recv_sem=rsem, device_id=to, device_id_type=MESH
    )


class Sends:
    def __init__(self):
        self.copies = []

    def push(self, src, dst, ssem, rsem, to):
        copy = remote(src, dst, ssem, rsem, to)
        copy.start()
        self.copies.append(copy)

    def finish(self):
        for copy in self.copies:
            copy.wait_send()


def arrive(dst, ssem, rsem, to):
    remote(dst, dst, ssem, rsem, to).wait_recv()


TENSOR_SUM_SCRATCH = lambda rows, width, dtype: [
    pltpu.VMEM((2, rows, width), dtype),
    pltpu.VMEM((rows, width), dtype),
    DMA((3,)),
    DMA((3,)),
]


def tensor_sum_start(sends, part_ref, got_c, ssem, rsem):
    hi, lo, th, tl = place()
    to_c = device(hi, lo, th, 1 - tl)
    for j, y in enumerate((1 - th, th)):
        sends.push(part_ref.at[y * 2 + 1 - tl], got_c.at[j], ssem.at[j], rsem.at[j], to_c)


def tensor_sum_middle(sends, part_ref, got_c, got_y, ssem, rsem):
    hi, lo, th, tl = place()
    arrive(got_c.at[0], ssem.at[0], rsem.at[0], device(hi, lo, th, 1 - tl))
    total = part_ref[(1 - th) * 2 + tl].astype(F32) + got_c[0].astype(F32)
    got_c[0] = total.astype(got_c.dtype)
    sends.push(got_c.at[0], got_y, ssem.at[2], rsem.at[2], device(hi, lo, 1 - th, tl))


def tensor_sum_end(part_ref, got_c, got_y, ssem, rsem):
    hi, lo, th, tl = place()
    arrive(got_c.at[1], ssem.at[1], rsem.at[1], device(hi, lo, th, 1 - tl))
    total = part_ref[th * 2 + tl].astype(F32) + got_c[1].astype(F32)
    arrive(got_y, ssem.at[2], rsem.at[2], device(hi, lo, 1 - th, tl))
    return total + got_y[...].astype(F32)


def tensor_spread_start(sends, o_ref, ssem, rsem):
    hi, lo, th, tl = place()
    own = o_ref.at[th * 2 + tl]
    sends.push(own, own, ssem.at[0], rsem.at[0], device(hi, lo, 1 - th, tl))
    sends.push(own, own, ssem.at[1], rsem.at[1], device(hi, lo, th, 1 - tl))


def tensor_spread_end(sends, o_ref, ssem, rsem):
    hi, lo, th, tl = place()
    other = o_ref.at[(1 - th) * 2 + tl]
    to_c = device(hi, lo, th, 1 - tl)
    arrive(other, ssem.at[0], rsem.at[0], device(hi, lo, 1 - th, tl))
    sends.push(other, other, ssem.at[2], rsem.at[2], to_c)
    arrive(o_ref.at[th * 2 + 1 - tl], ssem.at[1], rsem.at[1], to_c)
    arrive(o_ref.at[(1 - th) * 2 + 1 - tl], ssem.at[2], rsem.at[2], to_c)


def gather_steps(n_hi, x_ref, o_ref, own_sem, send_sem, recv_sem, lo_first=(True, False)):
    hi, lo, th, tl = place()
    rows = x_ref.shape[0]
    half = rows // 2
    own_block = (hi * 2 + lo) * 4 + th * 2 + tl
    own = pltpu.make_async_copy(x_ref, o_ref.at[pl.ds(own_block * rows, rows)], own_sem)
    own.start()
    sends = Sends()

    def slot(k, f, s, c):
        return ((c * 2 + s) * 2 + f) * n_hi + k

    def where(h, k, f, s, c):
        kk = peer(hi, k, n_hi)
        l = 1 - lo if (f if lo_first[h] else s) else lo
        y = 1 - th if (s if lo_first[h] else f) else th
        z = 1 - tl if c else tl
        return ((kk * 2 + l) * 4 + y * 2 + z) * rows + h * half

    def push(h, k, f, s, c, step):
        at = where(h, k, f, s, c)
        if k == 0 and not (f or s or c):
            src = x_ref.at[pl.ds(h * half, half)]
        else:
            src = o_ref.at[pl.ds(at, half)]
        if step == "c":
            to, r = device(hi, lo, th, 1 - tl), slot(k, f, s, 1)
        elif step == "s":
            to = device(hi, lo, 1 - th, tl) if lo_first[h] else device(hi, 1 - lo, th, tl)
            r = slot(k, f, 1, 0)
        elif step == "f":
            to = device(hi, 1 - lo, th, tl) if lo_first[h] else device(hi, lo, 1 - th, tl)
            r = slot(k, 1, 0, 0)
        else:
            to, r = device(peer(hi, step, n_hi), lo, th, tl), slot(back(step, n_hi), 0, 0, 0)
        sends.push(src, o_ref.at[pl.ds(at, half)], send_sem.at[h, r], recv_sem.at[h, r], to)

    def got(h, k, f, s, c):
        r = slot(k, f, s, c)
        arrive(
            o_ref.at[pl.ds(where(h, k, f, s, c), half)],
            send_sem.at[h, r], recv_sem.at[h, r], device(hi, lo, th, 1 - tl),
        )

    for k in range(n_hi):
        for h in range(2):
            if k:
                got(h, k, 0, 0, 0)
            if k < n_hi - 1:
                push(h, 0, 0, 0, 0, k + 1)
            for step in ("f", "s", "c"):
                push(h, k, 0, 0, 0, step)
        yield
        for h in range(2):
            got(h, k, 1, 0, 0)
            for step in ("s", "c"):
                push(h, k, 1, 0, 0, step)
        yield
    for k in range(n_hi):
        for f in range(2):
            for h in range(2):
                got(h, k, f, 1, 0)
                push(h, k, f, 1, 0, "c")
        yield
    for k in range(n_hi):
        for f in range(2):
            for s in range(2):
                for h in range(2):
                    got(h, k, f, s, 1)
    own.wait()
    sends.finish()


def in_turns(*streams):
    live = list(streams)
    while live:
        for stream in list(live):
            if next(stream, True) is True:
                live.remove(stream)


def middle_kernel(
    n_hi, part_ref, x_ref, gain_ref, o_ref, hidden_ref,
    normed, got_c, got_y, t_send, t_recv, *sems,
):
    greet(n_hi)
    sends = Sends()
    tensor_sum_start(sends, part_ref, got_c, t_send, t_recv)
    tensor_sum_middle(sends, part_ref, got_c, got_y, t_send, t_recv)
    hidden = x_ref[...].astype(F32) + tensor_sum_end(part_ref, got_c, got_y, t_send, t_recv)
    hidden_ref[...] = hidden
    normed[...] = (hidden * rms_scale(hidden) * gain_ref[...]).astype(normed.dtype)
    in_turns(gather_steps(n_hi, normed, o_ref, *sems))
    sends.finish()


def middle(part, x_piece, gain, n_dp, collective_id):
    rows, width = x_piece.shape
    n_hi = n_dp // 2
    return pl.pallas_call(
        functools.partial(middle_kernel, n_hi),
        out_shape=(
            jax.ShapeDtypeStruct((n_dp * 4 * rows, width), part.dtype),
            jax.ShapeDtypeStruct((rows, width), F32),
        ),
        in_specs=[VMEM_SPEC] * 3,
        out_specs=(ANY_SPEC, VMEM_SPEC),
        scratch_shapes=[pltpu.VMEM((rows, width), part.dtype)]
        + TENSOR_SUM_SCRATCH(rows, width, part.dtype)
        + [DMA, DMA((2, 8 * n_hi)), DMA((2, 8 * n_hi))],
        compiler_params=pltpu.CompilerParams(collective_id=collective_id, has_side_effects=True),
        name="middle",
    )(part.reshape(4, rows, width), x_piece, gain.reshape(1, width))


def weight_steps(n_hi, w_ref, o_ref, own_sem, send_b, recv_b, send_a, recv_a, send_f, recv_f):
    hi, lo, th, tl = place()
    to_f = device(hi, 1 - lo, th, tl)
    above = device(lax.rem(hi + 1, n_hi), lo, th, tl)
    below = device(lax.rem(hi + n_hi - 1, n_hi), lo, th, tl)
    sends = []

    def push(cond, src, at, h, ssem, rsem, to):
        copy = remote(src, o_ref.at[at, h], ssem, rsem, to)
        sends.append((cond, copy))
        if cond is None:
            copy.start()
        else:
            pl.when(cond)(copy.start)

    def block(j, l):
        return lax.rem(hi + j + n_hi, n_hi) * 2 + l

    for h in range(2):
        at = block(0, lo)
        push(hi < n_hi - 1, w_ref.at[h], at, h, send_b.at[h, 0], recv_b.at[h, 0], above)
        push(hi > 0, w_ref.at[h], at, h, send_a.at[h, 0], recv_a.at[h, 0], below)
        push(None, w_ref.at[h], at, h, send_f.at[h, 0], recv_f.at[h, 0], to_f)
    own = pltpu.make_async_copy(w_ref, o_ref.at[block(0, lo)], own_sem)
    own.start()
    yield
    for j in range(1, n_hi):
        for h in range(2):
            for down in (0, 1):
                valid = hi + j < n_hi if down else hi - j >= 0
                at = block(j if down else -j, lo)
                view = o_ref.at[at, h]
                sem = (send_a if down else send_b).at[h, j - 1], (recv_a if down else recv_b).at[h, j - 1]
                pl.when(valid)(remote(view, view, *sem, to_f).wait_recv)
                if j < n_hi - 1:
                    on = jnp.logical_and(valid, hi > 0 if down else hi < n_hi - 1)
                    push(
                        on, view, at, h, (send_a if down else send_b).at[h, j],
                        (recv_a if down else recv_b).at[h, j], below if down else above,
                    )
                f = 1 + down * (n_hi - 1) + j - 1
                push(valid, view, at, h, send_f.at[h, f], recv_f.at[h, f], to_f)
        yield
    for h in range(2):
        view = o_ref.at[block(0, 1 - lo), h]
        arrive(view, send_f.at[h, 0], recv_f.at[h, 0], to_f)
    for j in range(1, n_hi):
        for h in range(2):
            for down in (0, 1):
                valid = hi + j < n_hi if down else hi - j >= 0
                view = o_ref.at[block(j if down else -j, 1 - lo), h]
                f = 1 + down * (n_hi - 1) + j - 1
                pl.when(valid)(remote(view, view, send_f.at[h, f], recv_f.at[h, f], to_f).wait_recv)
    own.wait()
    for cond, copy in sends:
        if cond is None:
            copy.wait_send()
        else:
            pl.when(cond)(copy.wait_send)


def start_kernel(n_hi, n, *refs):
    ins, outs, sems = refs[: n + 1], refs[n + 1 : 2 * n + 2], refs[2 * n + 2 :]
    greet(n_hi)
    streams = [
        weight_steps(n_hi, ins[i], outs[i], *sems[7 * i : 7 * i + 7]) for i in range(n)
    ] + [gather_steps(n_hi, ins[n], outs[n], *sems[7 * n :], lo_first=(True, True))]
    in_turns(*streams)


def start(weights, table, n_dp, collective_id):
    n_hi = n_dp // 2
    n = len(weights)
    half = weights[0].shape[0] // 2
    outs = pl.pallas_call(
        functools.partial(start_kernel, n_hi, n),
        out_shape=[jax.ShapeDtypeStruct((n_dp, 2, half, w.shape[1]), w.dtype) for w in weights]
        + [jax.ShapeDtypeStruct((n_dp * 4 * table.shape[0], table.shape[1]), table.dtype)],
        in_specs=[ANY_SPEC] * (n + 1),
        out_specs=[ANY_SPEC] * (n + 1),
        scratch_shapes=[
            DMA,
            DMA((2, n_hi - 1)), DMA((2, n_hi - 1)),
            DMA((2, n_hi - 1)), DMA((2, n_hi - 1)),
            DMA((2, 2 * n_hi - 1)), DMA((2, 2 * n_hi - 1)),
        ] * n + [DMA, DMA((2, 8 * n_hi)), DMA((2, 8 * n_hi))],
        compiler_params=pltpu.CompilerParams(collective_id=collective_id, has_side_effects=True),
        name="start",
    )(*[w.reshape(2, half, w.shape[1]) for w in weights], table)
    return [o.reshape(n_dp * 2 * half, o.shape[3]) for o in outs[:n]] + [outs[n]]


def scatter_steps(n_hi, sends, p_ref, o_ref, bufs):
    (stage, from_c, from_f, from_s, from_h,
     stage_sem, send_c, recv_c, send_f, recv_f, send_s, recv_s, send_h, recv_h) = bufs
    depth = stage.shape[0]
    hi, lo, th, tl = place()
    to_c = device(hi, lo, th, 1 - tl)
    rows = o_ref.shape[0]
    half = rows // 2

    def where(h, k, f, s, c):
        kk = peer(hi, k, n_hi)
        l = 1 - lo if (f if h == 1 else s) else lo
        y = 1 - th if (s if h == 1 else f) else th
        z = 1 - tl if c else tl
        return ((kk * 2 + l) * 4 + y * 2 + z) * rows + h * half

    ks = list(range(1, n_hi)) + [0]
    order = []
    for i in range(n_hi + 2):
        for lag, groups in ((0, ((1, 1), (1, 0))), (1, ((0, 1),)), (2, ((0, 0),))):
            if 0 <= i - lag < n_hi:
                order += [(f, s, ks[i - lag], h) for f, s in groups for h in range(2)]

    def slot(f, s, k):
        return (f * 2 + s) * n_hi + k

    def first(h):
        return device(hi, lo, 1 - th, tl) if h == 0 else device(hi, 1 - lo, th, tl)

    def second(h):
        return device(hi, 1 - lo, th, tl) if h == 0 else device(hi, lo, 1 - th, tl)

    for f, s, k, h in order:
        n = slot(f, s, k)
        sends.push(
            p_ref.at[pl.ds(where(h, k, f, s, 1), half)], from_c.at[h, n], send_c.at[h, n],
            recv_c.at[h, n], to_c,
        )

    def load(i):
        f, s, k, h = order[i]
        return pltpu.make_async_copy(
            p_ref.at[pl.ds(where(h, k, f, s, 0), half)], stage.at[i % depth], stage_sem.at[i % depth]
        )

    for i in range(depth - 1):
        load(i).start()
    for i, (f, s, k, h) in enumerate(order):
        if i + depth - 1 < len(order):
            load(i + depth - 1).start()
        load(i).wait()
        n = slot(f, s, k)
        arrive(from_c.at[h, n], send_c.at[h, n], recv_c.at[h, n], to_c)
        total = stage[i % depth].astype(F32) + from_c[h, n].astype(F32)
        if f == 0:
            m = s * n_hi + k
            arrive(from_f.at[h, m], send_f.at[h, m], recv_f.at[h, m], to_c)
            total = total + from_f[h, m].astype(F32)
        if f == 0 and s == 0:
            arrive(from_s.at[h, k], send_s.at[h, k], recv_s.at[h, k], to_c)
            total = total + from_s[h, k].astype(F32)
        if f == 0 and s == 0 and k == 0:
            for j in range(n_hi - 1):
                arrive(from_h.at[h, j], send_h.at[h, j], recv_h.at[h, j], to_c)
                total = total + from_h[h, j].astype(F32)
            o_ref[pl.ds(h * half, half), :] = total
            continue
        from_c[h, n] = total.astype(from_c.dtype)
        src = from_c.at[h, n]
        if f == 1:
            m = s * n_hi + k
            sends.push(src, from_f.at[h, m], send_f.at[h, m], recv_f.at[h, m], first(h))
        elif s == 1:
            sends.push(src, from_s.at[h, k], send_s.at[h, k], recv_s.at[h, k], second(h))
        else:
            j = back(k, n_hi) - 1
            sends.push(
                src, from_h.at[h, j], send_h.at[h, j], recv_h.at[h, j],
                device(peer(hi, k, n_hi), lo, th, tl),
            )


def scatter_scratch(n_hi, half, width, dtype, depth=4):
    return [
        pltpu.VMEM((depth, half, width), dtype),
        pltpu.VMEM((2, 4 * n_hi, half, width), dtype),
        pltpu.VMEM((2, 2 * n_hi, half, width), dtype),
        pltpu.VMEM((2, n_hi, half, width), dtype),
        pltpu.VMEM((2, n_hi - 1, half, width), dtype),
        DMA((depth,)),
        DMA((2, 4 * n_hi)), DMA((2, 4 * n_hi)),
        DMA((2, 2 * n_hi)), DMA((2, 2 * n_hi)),
        DMA((2, n_hi)), DMA((2, n_hi)),
        DMA((2, n_hi - 1)), DMA((2, n_hi - 1)),
    ]


def scatter_kernel(n_hi, p_ref, o_ref, *bufs):
    greet(n_hi)
    sends = Sends()
    scatter_steps(n_hi, sends, p_ref, o_ref, bufs)
    sends.finish()


def scatter_rows(p, n_dp, collective_id):
    width = p.shape[1]
    rows = p.shape[0] // (n_dp * 4)
    n_hi = n_dp // 2
    return pl.pallas_call(
        functools.partial(scatter_kernel, n_hi),
        out_shape=jax.ShapeDtypeStruct((rows, width), F32),
        in_specs=[ANY_SPEC],
        out_specs=VMEM_SPEC,
        scratch_shapes=scatter_scratch(n_hi, rows // 2, width, p.dtype),
        compiler_params=pltpu.CompilerParams(
            collective_id=collective_id, has_side_effects=True, vmem_limit_bytes=60 << 20
        ),
        name="scatter_rows",
    )(p)


def turn_kernel(
    n_hi, p_ref, hidden_ref, g2_ref, gain_ref, grad_ref, sum_ref, dm_ref, total_ref, sp_send, sp_recv, *bufs
):
    hi, lo, th, tl = place()
    greet(n_hi)
    sends = Sends()
    scatter_steps(n_hi, sends, p_ref, total_ref, bufs)
    grad = total_ref[...]
    hidden = hidden_ref[...]
    scale = rms_scale(hidden)
    weighted = gain_ref[...] * grad
    sum_ref[...] = jnp.sum(grad * hidden * scale, axis=0, keepdims=True)
    mean = jnp.mean(weighted * hidden, axis=-1, keepdims=True)
    grad = g2_ref[...].astype(F32) + scale * weighted - hidden * (scale * scale * scale) * mean
    grad_ref[...] = grad
    dm_ref[th * 2 + tl] = grad.astype(dm_ref.dtype)
    tensor_spread_start(sends, dm_ref, sp_send, sp_recv)
    tensor_spread_end(sends, dm_ref, sp_send, sp_recv)
    sends.finish()


def turn(p, hidden, g2_piece, gain, n_dp, collective_id):
    rows, width = hidden.shape
    n_hi = n_dp // 2
    return pl.pallas_call(
        functools.partial(turn_kernel, n_hi),
        out_shape=(
            jax.ShapeDtypeStruct((rows, width), F32),
            jax.ShapeDtypeStruct((1, width), F32),
            jax.ShapeDtypeStruct((4, rows, width), p.dtype),
        ),
        in_specs=[ANY_SPEC] + [VMEM_SPEC] * 3,
        out_specs=(VMEM_SPEC,) * 3,
        scratch_shapes=[pltpu.VMEM((rows, width), F32), DMA((3,)), DMA((3,))]
        + scatter_scratch(n_hi, rows // 2, width, p.dtype),
        compiler_params=pltpu.CompilerParams(
            collective_id=collective_id, has_side_effects=True, vmem_limit_bytes=60 << 20
        ),
        name="turn",
    )(p, hidden, g2_piece, gain.reshape(1, width))


def tail_kernel(n_hi, wide, bc_at, n, *refs):
    part_ref, grad_ref, x_ref, gain_ref, small_ref = refs[:5]
    w_refs = refs[5 : 5 + n]
    ox_ref, os_ref = refs[5 + n : 7 + n]
    ow_refs = refs[7 + n : 7 + 2 * n]
    (got_c, got_y, t_send, t_recv, sp_send, sp_recv,
     small, small_f, small_h, small_t, sm_send, sm_recv, smh_send, smh_recv,
     bc_own, bc_got, bc_send, bc_recv) = refs[7 + 2 * n : 25 + 2 * n]
    rest = refs[25 + 2 * n :]
    bufs = [rest[8 * i : 8 * i + 8] for i in range(n)]
    hi, lo, th, tl = place()
    to_f, to_y, to_c = device(hi, 1 - lo, th, tl), device(hi, lo, 1 - th, tl), device(hi, lo, th, 1 - tl)
    greet(n_hi)
    sends = Sends()
    order = [(k, h) for k in reversed(range(n_hi)) for h in range(2)]
    events = [(w, k, h) for w in range(n) for k, h in order]
    events = [e for e in events if e[1]] + [e for e in events if not e[1]]

    def owner(k, l):
        return peer(hi, k, n_hi) * 2 + l

    def forward(i):
        if i < len(events):
            w, k, h = events[i]
            stage, from_f, from_h, stage_sem, send_f, recv_f, send_h, recv_h = bufs[w]
            sends.push(
                w_refs[w].at[owner(k, 1 - lo), h], from_f.at[h, k], send_f.at[h, k], recv_f.at[h, k], to_f
            )

    window = 4
    for i in range(window):
        forward(i)
    loads = []
    for w, k, h in events:
        copy = pltpu.make_async_copy(
            w_refs[w].at[owner(k, lo), h], bufs[w][0].at[h, k], bufs[w][3].at[h, k]
        )
        copy.start()
        loads.append(copy)
    tensor_sum_start(sends, part_ref, got_c, t_send, t_recv)
    tensor_sum_middle(sends, part_ref, got_c, got_y, t_send, t_recv)
    grad = tensor_sum_end(part_ref, got_c, got_y, t_send, t_recv)
    x = x_ref[...].astype(F32)
    scale = rms_scale(x)
    weighted = gain_ref[...] * grad
    mean = jnp.mean(weighted * x, axis=-1, keepdims=True)
    ox_ref[th * 2 + tl] = (
        grad_ref[...] + scale * weighted - x * (scale * scale * scale) * mean
    ).astype(ox_ref.dtype)
    tensor_spread_start(sends, ox_ref, sp_send, sp_recv)
    small[...] = small_ref[...]
    small[0:1, :] = jnp.sum(grad * x * scale, axis=0, keepdims=True)
    sends.push(small, small_f, sm_send.at[0], sm_recv.at[0], to_f)

    for i, (w, k, h) in enumerate(events):
        if k == 0:
            break
        stage, from_f, from_h, stage_sem, send_f, recv_f, send_h, recv_h = bufs[w]
        loads[i].wait()
        arrive(from_f.at[h, k], send_f.at[h, k], recv_f.at[h, k], to_c)
        forward(i + window)
        from_f[h, k] = (stage[h, k].astype(F32) + from_f[h, k].astype(F32)).astype(from_f.dtype)
        j = back(k, n_hi) - 1
        sends.push(
            from_f.at[h, k], from_h.at[h, j], send_h.at[h, j], recv_h.at[h, j],
            device(peer(hi, k, n_hi), lo, th, tl),
        )
        if i == 0:
            tensor_spread_end(sends, ox_ref, sp_send, sp_recv)
        if i == 1:
            arrive(small_f, sm_send.at[0], sm_recv.at[0], to_c)
            small_h[hi] = small[...] + small_f[...]
            for q in range(1, n_hi):
                sends.push(
                    small_h.at[hi], small_h.at[hi], smh_send.at[q - 1], smh_recv.at[back(q, n_hi) - 1],
                    device(peer(hi, q, n_hi), lo, th, tl),
                )
    for q in range(1, n_hi):
        arrive(small_h.at[peer(hi, q, n_hi)], smh_send.at[q - 1], smh_recv.at[q - 1], to_c)
    total = small_h[0]
    for q in range(1, n_hi):
        total = total + small_h[q]
    os_ref[...] = total
    sends.push(os_ref.at[pl.ds(0, wide)], small_t.at[0], sm_send.at[1], sm_recv.at[1], to_c)
    for i, (w, k, h) in enumerate(events):
        if k:
            continue
        forward(i + window)
        stage, from_f, from_h, stage_sem, send_f, recv_f, send_h, recv_h = bufs[w]
        loads[i].wait()
        arrive(from_f.at[h, 0], send_f.at[h, 0], recv_f.at[h, 0], to_c)
        total = stage[h, 0].astype(F32) + from_f[h, 0].astype(F32)
        for j in range(n_hi - 1):
            arrive(from_h.at[h, j], send_h.at[h, j], recv_h.at[h, j], to_c)
            total = total + from_h[h, j].astype(F32)
        ow_refs[w][h] = total
        if w == 0:
            bc_own[0, h] = total[:, bc_at : bc_at + bc_own.shape[3]].astype(bc_own.dtype)
            if h == 1:
                sends.push(bc_own.at[0], bc_got.at[0], bc_send.at[0], bc_recv.at[0], to_c)
                arrive(small_t.at[0], sm_send.at[1], sm_recv.at[1], to_c)
                small_t[2] = os_ref[pl.ds(0, wide), :] + small_t[0]
                sends.push(small_t.at[2], small_t.at[1], sm_send.at[2], sm_recv.at[2], to_y)
                arrive(bc_got.at[0], bc_send.at[0], bc_recv.at[0], to_c)
                bc_own[1] = (bc_own[0].astype(F32) + bc_got[0].astype(F32)).astype(bc_own.dtype)
                sends.push(bc_own.at[1], bc_got.at[1], bc_send.at[1], bc_recv.at[1], to_y)
    arrive(small_t.at[1], sm_send.at[2], sm_recv.at[2], to_c)
    arrive(bc_got.at[1], bc_send.at[1], bc_recv.at[1], to_c)
    for h in range(2):
        ow_refs[0][h, :, bc_at : bc_at + bc_own.shape[3]] = (
            bc_own[1, h].astype(F32) + bc_got[1, h].astype(F32)
        )
    sends.finish()
    os_ref[pl.ds(0, wide), :] = small_t[2] + small_t[1]


def tail(weights, part, grad_one, x_piece, gain, small, wide, bc_at, bc_width, n_dp, collective_id):
    rows, width = x_piece.shape
    n_hi = n_dp // 2
    n = len(weights)
    half = weights[0].shape[0] // (2 * n_dp)
    dt = weights[0].dtype
    scratch = TENSOR_SUM_SCRATCH(rows, width, part.dtype) + [
        DMA((3,)), DMA((3,)),
        pltpu.VMEM(small.shape, F32),
        pltpu.VMEM(small.shape, F32),
        pltpu.VMEM((n_hi,) + small.shape, F32),
        pltpu.VMEM((3, wide, small.shape[1]), F32),
        DMA((3,)), DMA((3,)),
        DMA((n_hi - 1,)), DMA((n_hi - 1,)),
        pltpu.VMEM((2, 2, half, bc_width), dt),
        pltpu.VMEM((2, 2, half, bc_width), dt),
        DMA((2,)), DMA((2,)),
    ]
    for w in weights:
        scratch += [
            pltpu.VMEM((2, n_hi, half, w.shape[1]), dt),
            pltpu.VMEM((2, n_hi, half, w.shape[1]), dt),
            pltpu.VMEM((2, n_hi - 1, half, w.shape[1]), dt),
            DMA((2, n_hi)),
            DMA((2, n_hi)), DMA((2, n_hi)),
            DMA((2, n_hi - 1)), DMA((2, n_hi - 1)),
        ]
    outs = pl.pallas_call(
        functools.partial(tail_kernel, n_hi, wide, bc_at, n),
        out_shape=[
            jax.ShapeDtypeStruct((4, rows, width), dt),
            jax.ShapeDtypeStruct(small.shape, F32),
        ] + [jax.ShapeDtypeStruct((2, half, w.shape[1]), F32) for w in weights],
        in_specs=[VMEM_SPEC] * 5 + [ANY_SPEC] * n,
        out_specs=[VMEM_SPEC] * (2 + n),
        scratch_shapes=scratch,
        compiler_params=pltpu.CompilerParams(
            collective_id=collective_id, has_side_effects=True, vmem_limit_bytes=60 << 20
        ),
        name="tail",
    )(
        part.reshape(4, rows, width), grad_one, x_piece, gain.reshape(1, width), small,
        *[w.reshape(n_dp, 2, half, w.shape[1]) for w in weights],
    )
    return outs[0], outs[1], [o.reshape(2 * half, o.shape[2]) for o in outs[2:]]


def dot_mm(a, b):
    return lax.dot_general(a, b, (((1,), (0,)), ((), ())), preferred_element_type=F32)


def dot_nt(a, b):
    return lax.dot_general(a, b, (((1,), (1,)), ((), ())), preferred_element_type=F32)


def dot_tn(a, b):
    return lax.dot_general(a, b, (((0,), (0,)), ((), ())), preferred_element_type=F32)


def experts_kernel(
    n_dp, n_local, cap, chunk, pos_ref, wt_ref, x_ref, g_ref, gu_ref, dn_ref,
    dxn_ref, out_ref, ggu_ref, gdn_ref, pick, xr, q, sw, gu,
):
    step = pl.program_id(0)
    width = x_ref.shape[1]
    hidden = dn_ref.shape[1]
    slots = x_ref.shape[0]
    columns = [pl.ds(c, chunk) for c in range(0, width, chunk)]

    @pl.when(step < n_dp)
    def _():
        s = step
        lane = lax.broadcasted_iota(jnp.int32, (cap, slots), 0)
        for e in range(n_local):
            hit = lane == pos_ref[0, e : e + 1, :]
            pick[s, e * cap : (e + 1) * cap, :] = jnp.where(hit, 1.0, 0.0).astype(BF)
            sw[e, s] = jnp.sum(jnp.where(hit, wt_ref[0, e : e + 1, :], 0.0), axis=1, keepdims=True)
        chosen = pick[s]
        for c in columns:
            rows = dot_mm(chosen, x_ref[:, c]).astype(BF)
            grads = dot_mm(chosen, g_ref[:, c])
            for e in range(n_local):
                xr[e, s, :, c] = rows[e * cap : (e + 1) * cap]
                q[e, s, :, c] = (grads[e * cap : (e + 1) * cap] * sw[e, s]).astype(BF)

    @pl.when(jnp.logical_and(step >= n_dp, step < n_dp + n_local))
    def _():
        e = step - n_dp
        gu[:, :hidden] = gu_ref[pl.ds(0, width, stride=2), :].astype(BF)
        gu[:, hidden:] = gu_ref[pl.ds(1, width, stride=2), :].astype(BF)
        down = dn_ref[0].astype(BF)
        x = xr[e].reshape(n_dp * cap, width)
        qe = q[e].reshape(n_dp * cap, width)
        pre = dot_mm(x, gu[...])
        grad_act = dot_nt(qe, down)
        gate, up = pre[:, :hidden], pre[:, hidden:]
        sig = 1.0 / (1.0 + jnp.exp(-gate))
        act_silu = gate * sig
        slope = sig * (1.0 + gate * (1.0 - sig))
        value = act_silu * up
        act = value.astype(BF)
        scaled = (value * sw[e].reshape(n_dp * cap, 1)).astype(BF)
        grad_pre = jnp.concatenate([grad_act * up * slope, grad_act * act_silu], axis=1).astype(BF)
        ggu = dot_tn(x, grad_pre)
        ggu_ref[pl.ds(0, width, stride=2), :] = ggu[:, :hidden]
        ggu_ref[pl.ds(1, width, stride=2), :] = ggu[:, hidden:]
        gdn_ref[0] = dot_tn(act, qe)
        for c in columns:
            xr[e, :, :, c] = dot_nt(grad_pre, gu[c, :]).astype(BF).reshape(n_dp, cap, chunk)
            q[e, :, :, c] = dot_mm(scaled, down[:, c.start : c.start + chunk]).astype(BF).reshape(n_dp, cap, chunk)

    @pl.when(step >= n_dp + n_local)
    def _():
        s = step - n_dp - n_local
        chosen = pick[s]
        for c in columns:
            dxn_ref[:, c] = dot_tn(chosen, xr[:, s, :, c].reshape(n_local * cap, chunk)).astype(BF)
            out_ref[:, c] = dot_tn(chosen, q[:, s, :, c].reshape(n_local * cap, chunk)).astype(BF)


def experts(position, weights, rows, table, w_gu, w_down, cap):
    n_dp, n_local, slots = position.shape
    width = rows.shape[1]
    hidden = w_down.shape[1]
    chunk = width // 3 if width % 384 == 0 else width
    by_source = lambda i: (jnp.clip(i, 0, n_dp - 1), 0, 0)
    rows_in = lambda i: (jnp.clip(i, 0, n_dp - 1), 0)
    rows_out = lambda i: (jnp.clip(i - n_dp - n_local, 0, n_dp - 1), 0)
    flat = lambda i: (jnp.clip(i - n_dp, 0, n_local - 1), 0)
    deep = lambda i: (jnp.clip(i - n_dp, 0, n_local - 1), 0, 0)
    total = n_dp * n_local * cap
    return pl.pallas_call(
        functools.partial(experts_kernel, n_dp, n_local, cap, chunk),
        grid=(2 * n_dp + n_local,),
        out_shape=(
            jax.ShapeDtypeStruct((n_dp * slots, width), BF),
            jax.ShapeDtypeStruct((n_dp * slots, width), BF),
            jax.ShapeDtypeStruct((n_local * width * 2, hidden), F32),
            jax.ShapeDtypeStruct((n_local, hidden, width), F32),
        ),
        in_specs=[
            pl.BlockSpec((1, n_local, slots), by_source),
            pl.BlockSpec((1, n_local, slots), by_source),
            pl.BlockSpec((slots, width), rows_in),
            pl.BlockSpec((slots, width), rows_in),
            pl.BlockSpec((width * 2, hidden), flat),
            pl.BlockSpec((1, hidden, width), deep),
        ],
        out_specs=(
            pl.BlockSpec((slots, width), rows_out),
            pl.BlockSpec((slots, width), rows_out),
            pl.BlockSpec((width * 2, hidden), flat),
            pl.BlockSpec((1, hidden, width), deep),
        ),
        scratch_shapes=[
            pltpu.VMEM((n_dp, n_local * cap, slots), BF),
            pltpu.VMEM((n_local, n_dp, cap, width), BF),
            pltpu.VMEM((n_local, n_dp, cap, width), BF),
            pltpu.VMEM((n_local, n_dp, cap, 1), F32),
            pltpu.VMEM((width, 2 * hidden), BF),
        ],
        compiler_params=pltpu.CompilerParams(
            dimension_semantics=("arbitrary",), vmem_limit_bytes=60 << 20
        ),
        cost_estimate=pl.CostEstimate(
            flops=8 * total * slots * width + 18 * total * width * hidden,
            bytes_accessed=8 * n_dp * slots * width + 24 * n_local * width * hidden,
            transcendentals=total * hidden,
        ),
        name="experts",
    )(
        position,
        weights,
        rows,
        table,
        w_gu.reshape(n_local * width * 2, hidden),
        w_down,
    )


def conv_pre(pad, values, taps, bias):
    n = values.shape[0]
    pad[pl.ds(8, n), :] = values
    count = taps.shape[0]
    total = bias + taps[count - 1 : count] * values
    for k in range(count - 1):
        total = total + taps[k : k + 1] * pad[pl.ds(8 - (count - 1) + k, n), :]
    return total


def sigmoid(v):
    return 1.0 / (1.0 + jnp.exp(-v))


def dot_exact(a, b):
    return lax.dot_general(
        a, b, (((1,), (0,)), ((), ())), precision=HIGHEST, preferred_element_type=F32
    )


def step_parts(first_ref, at, dtb_ref, alog_ref):
    raw = first_ref[:, at : at + 128] + dtb_ref[...]
    delta = jnp.maximum(raw, 0.0) + jnp.log(1.0 + jnp.exp(-jnp.abs(raw)))
    return raw, delta, -jnp.exp(alog_ref[...])


def lower_mask():
    t = lax.broadcasted_iota(jnp.int32, (BLOCK, BLOCK), 0)
    s = lax.broadcasted_iota(jnp.int32, (BLOCK, BLOCK), 1)
    return t >= s


def by_head(left, a, b):
    return jnp.where(left, a, b)


def mixer_forward_kernel(
    first_ref, cx_ref, cxb_ref, cbc_ref, cbcb_ref, dtb_ref, alog_ref, skip_ref,
    y_ref, gated_ref, square_ref, state_ref, pad,
):
    slots = first_ref.shape[0]
    inner = cx_ref.shape[1]
    n_blocks = slots // BLOCK
    bc_at = 2 * inner
    pad[0:8, :] = jnp.zeros((8, 128), F32)
    mask = lower_mask()
    tri = mask.astype(F32)
    left = lax.broadcasted_iota(jnp.int32, (BLOCK, 128), 1) < 64
    left_row = left[0:1]

    parts = []
    for c in (0, 128):
        pre = conv_pre(pad, first_ref[:, bc_at + c : bc_at + c + 128], cbc_ref[:, c : c + 128], cbcb_ref[:, c : c + 128])
        parts.append((pre * sigmoid(pre)).astype(BF))
    b_rows, c_rows = parts
    raw, delta, rate = step_parts(first_ref, bc_at + 256, dtb_ref, alog_ref)
    blocks = []
    for b in range(n_blocks):
        r = slice(b * BLOCK, (b + 1) * BLOCK)
        d = delta[r]
        cum = dot_exact(tri, rate * d)
        blocks.append((d, cum, d.T, cum.T, dot_nt(c_rows[r], b_rows[r])))
    squares = jnp.zeros((slots, 1), F32)
    for p in range(inner // 128):
        lanes = slice(p * 128, (p + 1) * 128)
        pre = conv_pre(pad, first_ref[:, inner + p * 128 : inner + (p + 1) * 128], cx_ref[:, lanes], cxb_ref[:, lanes])
        heads_in = (pre * sigmoid(pre)).astype(BF)
        state = None
        outs = []
        for b in range(n_blocks):
            d, cum, d_t, cum_t, inter = blocks[b]
            r = slice(b * BLOCK, (b + 1) * BLOCK)
            x = heads_in[r]
            ys = []
            for h in (2 * p, 2 * p + 1):
                decay = jnp.exp(jnp.where(mask, cum[:, h : h + 1] - cum_t[h : h + 1, :], -1e30))
                ys.append(dot_mm((inter * decay * d_t[h : h + 1, :]).astype(BF), x))
            y = by_head(left, ys[0], ys[1]) + skip_ref[:, lanes] * x.astype(F32)
            cum_p = by_head(left, cum[:, 2 * p : 2 * p + 1], cum[:, 2 * p + 1 : 2 * p + 2])
            d_p = by_head(left, d[:, 2 * p : 2 * p + 1], d[:, 2 * p + 1 : 2 * p + 2])
            if state is not None:
                state_ref[p, b - 1] = state
                y = y + jnp.exp(cum_p) * dot_mm(c_rows[r], state.astype(BF))
            if b + 1 < n_blocks:
                end = cum_p[BLOCK - 1 :]
                z_rows = x.astype(F32) * d_p * jnp.exp(end - cum_p)
                fresh = dot_tn(b_rows[r], z_rows.astype(BF))
                state = fresh if state is None else jnp.exp(end) * state + fresh
            outs.append(y)
        y = jnp.concatenate(outs, axis=0)
        z = first_ref[:, lanes]
        gated = y * (z * sigmoid(z))
        y_ref[:, lanes] = y
        gated_ref[:, lanes] = gated
        squares = squares + jnp.sum(gated * gated, axis=1, keepdims=True)
    square_ref[...] = squares


def mixer_backward_kernel(
    full_inner, first_ref, y_ref, gated_ref, dyn_ref, scale_ref, product_ref, gain_ref, state_ref,
    cx_ref, cxb_ref, cbc_ref, cbcb_ref, dtb_ref, alog_ref, skip_ref,
    grad_ref, small_ref, pad, after, cols, sums_t,
):
    slots = first_ref.shape[0]
    inner = cx_ref.shape[1]
    n_blocks = slots // BLOCK
    bc_at = 2 * inner
    taps = cx_ref.shape[0]
    pad[0:8, :] = jnp.zeros((8, 128), F32)
    after[pl.ds(slots, 8), :] = jnp.zeros((8, 128), F32)
    small_ref[...] = jnp.zeros_like(small_ref)
    cols[...] = jnp.zeros_like(cols)
    sums_t[...] = jnp.zeros_like(sums_t)
    mask = lower_mask()
    tri = mask.astype(F32)
    lane = lax.broadcasted_iota(jnp.int32, (BLOCK, 128), 1)
    left = lane < 64

    parts, bc_pre = [], []
    for c in (0, 128):
        pre = conv_pre(pad, first_ref[:, bc_at + c : bc_at + c + 128], cbc_ref[:, c : c + 128], cbcb_ref[:, c : c + 128])
        bc_pre.append(pre)
        parts.append((pre * sigmoid(pre)).astype(BF))
    b_rows, c_rows = parts
    raw, delta, rate = step_parts(first_ref, bc_at + 256, dtb_ref, alog_ref)
    scale = scale_ref[...]
    cube = scale * scale * scale * product_ref[...] * (1.0 / full_inner)
    blocks = []
    for b in range(n_blocks):
        r = slice(b * BLOCK, (b + 1) * BLOCK)
        d = delta[r]
        cum = dot_exact(tri, rate * d)
        blocks.append((d, cum, d.T, cum.T, dot_nt(c_rows[r], b_rows[r])))
    grad_inter = [jnp.zeros((BLOCK, BLOCK), F32) for _ in range(n_blocks)]
    grad_b = [jnp.zeros((BLOCK, 128), F32) for _ in range(n_blocks)]
    grad_c = [jnp.zeros((BLOCK, 128), F32) for _ in range(n_blocks)]

    def conv_back(grad_out, pre, values, taps_v, row, bias_row, lanes, at):
        sig = sigmoid(pre)
        a = grad_out * (sig * (1.0 + pre * (1.0 - sig)))
        after[pl.ds(0, slots), :] = a
        pad[pl.ds(8, slots), :] = values
        total = taps_v[taps - 1 : taps] * a
        small_ref[row + taps - 1 : row + taps, lanes] = jnp.sum(a * values, axis=0, keepdims=True)
        for k in range(taps - 1):
            total = total + taps_v[k : k + 1] * after[pl.ds(taps - 1 - k, slots), :]
            small_ref[row + k : row + k + 1, lanes] = jnp.sum(
                a * pad[pl.ds(8 - (taps - 1) + k, slots), :], axis=0, keepdims=True
            )
        small_ref[bias_row : bias_row + 1, lanes] = jnp.sum(a, axis=0, keepdims=True)
        grad_ref[:, at : at + 128] = total.astype(grad_ref.dtype)

    for p in range(inner // 128):
        lanes = slice(p * 128, (p + 1) * 128)
        values = first_ref[:, inner + p * 128 : inner + (p + 1) * 128]
        pre = conv_pre(pad, values, cx_ref[:, lanes], cxb_ref[:, lanes])
        heads_in = (pre * sigmoid(pre)).astype(BF)
        z = first_ref[:, lanes]
        sig = sigmoid(z)
        grad_gated = scale * gain_ref[:, lanes] * dyn_ref[:, lanes] - gated_ref[:, lanes] * cube
        grad_y = grad_gated * (z * sig)
        grad_ref[:, lanes] = (
            grad_gated * y_ref[:, lanes] * (sig * (1.0 + z * (1.0 - sig)))
        ).astype(grad_ref.dtype)
        skip = skip_ref[:, lanes]
        x_f = heads_in.astype(F32)
        small_ref[5:6, lanes] = jnp.sum(grad_y * x_f, axis=0, keepdims=True)
        grad_y_low = grad_y.astype(BF)
        grad_x = [None] * n_blocks
        grad_state = None
        for b in reversed(range(n_blocks)):
            d, cum, d_t, cum_t, inter = blocks[b]
            r = slice(b * BLOCK, (b + 1) * BLOCK)
            x, xf, dy, dyl = heads_in[r], x_f[r], grad_y[r], grad_y_low[r]
            cum_p = by_head(left, cum[:, 2 * p : 2 * p + 1], cum[:, 2 * p + 1 : 2 * p + 2])
            d_p = by_head(left, d[:, 2 * p : 2 * p + 1], d[:, 2 * p + 1 : 2 * p + 2])
            dxs = []
            for i, h in enumerate((2 * p, 2 * p + 1)):
                own = left if i == 0 else jnp.logical_not(left)
                q = dot_nt(jnp.where(own, dy, 0.0).astype(BF), x)
                decay = jnp.exp(jnp.where(mask, cum[:, h : h + 1] - cum_t[h : h + 1, :], -1e30))
                scaled = decay * d_t[h : h + 1, :]
                dxs.append(dot_tn((inter * scaled).astype(BF), dyl))
                grad_inter[b] = grad_inter[b] + scaled * q
                moved = inter * decay * q
                sums_t[b, h : h + 1, :] = jnp.sum(moved, axis=0, keepdims=True)
                rows = jnp.sum(moved * d_t[h : h + 1, :], axis=1, keepdims=True)
                cols[0, r, :] += jnp.where(lane == h, rows, 0.0)
            dx = by_head(left, dxs[0], dxs[1]) + skip * dy
            extra = None
            if b > 0:
                state = state_ref[p, b - 1]
                grown = dy * jnp.exp(cum_p)
                grown_low = grown.astype(BF)
                extra = grown * dot_mm(c_rows[r], state.astype(BF))
                grad_c[b] = grad_c[b] + dot_nt(grown_low, state.astype(BF))
                back_state = dot_tn(c_rows[r], grown_low)
            end = cum_p[BLOCK - 1 :]
            end_sum = None
            if grad_state is not None:
                weight = jnp.exp(end - cum_p)
                low_state = grad_state.astype(BF)
                dz_rows = dot_mm(b_rows[r], low_state)
                grad_b[b] = grad_b[b] + dot_nt((xf * d_p * weight).astype(BF), low_state)
                dx = dx + dz_rows * d_p * weight
                direct = dz_rows * xf * weight
                through = direct * d_p
                end_sum = jnp.sum(through, axis=0, keepdims=True)
                if b > 0:
                    end_sum = end_sum + jnp.exp(end) * jnp.sum(grad_state * state, axis=0, keepdims=True)
                extra = -through if extra is None else extra - through
            for i, h in enumerate((2 * p, 2 * p + 1)):
                own = left if i == 0 else jnp.logical_not(left)
                if extra is not None:
                    column = jnp.sum(jnp.where(own, extra, 0.0), axis=1, keepdims=True)
                    cols[0, r, :] += jnp.where(lane == h, column, 0.0)
                if end_sum is not None:
                    column = jnp.sum(jnp.where(own, direct, 0.0), axis=1, keepdims=True)
                    cols[1, r, :] += jnp.where(lane == h, column, 0.0)
                    last = jnp.sum(jnp.where(own[0:1], end_sum, 0.0), axis=1, keepdims=True)
                    at = slice((b + 1) * BLOCK - 1, (b + 1) * BLOCK)
                    cols[0, at, :] += jnp.where(lane[0:1] == h, last, 0.0)
            if b > 0:
                grad_state = back_state if grad_state is None else jnp.exp(end) * grad_state + back_state
            grad_x[b] = dx
        conv_back(
            jnp.concatenate(grad_x, axis=0), pre, values, cx_ref[:, lanes], 0, 4, lanes, inner + p * 128
        )
    upper = jnp.logical_not(mask).astype(F32) + (
        lax.broadcasted_iota(jnp.int32, (BLOCK, BLOCK), 0)
        == lax.broadcasted_iota(jnp.int32, (BLOCK, BLOCK), 1)
    ).astype(F32)
    ddts, logs = [], jnp.zeros((1, 128), F32)
    for b in range(n_blocks):
        d, cum, d_t, cum_t, inter = blocks[b]
        r = slice(b * BLOCK, (b + 1) * BLOCK)
        low = grad_inter[b].astype(BF)
        grad_c[b] = grad_c[b] + dot_mm(low, b_rows[r])
        grad_b[b] = grad_b[b] + dot_tn(low, c_rows[r])
        direct = sums_t[b].T
        reach = dot_exact(upper, cols[0, r, :] - direct * d)
        logs = logs + jnp.sum(rate * d * reach, axis=0, keepdims=True)
        ddts.append((direct + cols[1, r, :] + rate * reach) * sigmoid(raw[r]))
    ddt = jnp.concatenate(ddts, axis=0)
    grad_ref[:, bc_at + 256 : bc_at + 384] = ddt.astype(grad_ref.dtype)
    small_ref[11:12, 0:128] = logs
    small_ref[12:13, 0:128] = jnp.sum(ddt, axis=0, keepdims=True)
    for i, (c, grads) in enumerate(((0, grad_b), (128, grad_c))):
        conv_back(
            jnp.concatenate(grads, axis=0), bc_pre[i], first_ref[:, bc_at + c : bc_at + c + 128],
            cbc_ref[:, c : c + 128], 6, 10, slice(c, c + 128), bc_at + c,
        )


def pad_lanes(v):
    return jnp.pad(v, (0, -v.shape[0] % 128)).reshape(1, -1)


def mixer_params(conv_x, conv_x_bias, conv_bc, conv_bc_bias, dt_bias, a_log, d_skip):
    size = conv_x.shape[1] // d_skip.shape[0]
    return (
        conv_x, conv_x_bias.reshape(1, -1), conv_bc, conv_bc_bias.reshape(1, -1),
        pad_lanes(dt_bias), pad_lanes(a_log), jnp.repeat(d_skip, size).reshape(1, -1),
    )


def mixer_forward(firsts, params):
    slots = firsts.shape[0]
    inner = params[0].shape[1]
    pairs, n_blocks = inner // 128, slots // BLOCK
    shape = lambda *s: jax.ShapeDtypeStruct(s, F32)
    return pl.pallas_call(
        mixer_forward_kernel,
        out_shape=(
            shape(slots, inner), shape(slots, inner), shape(slots, 1),
            shape(pairs, n_blocks - 1, 128, 128),
        ),
        in_specs=[VMEM_SPEC] * 8,
        out_specs=(VMEM_SPEC,) * 4,
        scratch_shapes=[pltpu.VMEM((slots + 8, 128), F32)],
        compiler_params=pltpu.CompilerParams(vmem_limit_bytes=48 << 20),
        cost_estimate=pl.CostEstimate(
            flops=8 * slots * BLOCK * inner, bytes_accessed=24 * slots * inner,
            transcendentals=slots * BLOCK * inner // 32,
        ),
        name="mixer_forward",
    )(firsts, *params)


def mixer_backward(full_inner, firsts, y, gated, dyn, scale, product, gain, state, params):
    slots, width = firsts.shape
    inner = params[0].shape[1]
    return pl.pallas_call(
        functools.partial(mixer_backward_kernel, full_inner),
        out_shape=(
            jax.ShapeDtypeStruct((slots, width), BF),
            jax.ShapeDtypeStruct((16, inner), F32),
        ),
        in_specs=[VMEM_SPEC] * 15,
        out_specs=(VMEM_SPEC,) * 2,
        scratch_shapes=[
            pltpu.VMEM((slots + 8, 128), F32),
            pltpu.VMEM((slots + 8, 128), F32),
            pltpu.VMEM((2, slots, 128), F32),
            pltpu.VMEM((slots // BLOCK, 128, BLOCK), F32),
        ],
        compiler_params=pltpu.CompilerParams(vmem_limit_bytes=56 << 20),
        cost_estimate=pl.CostEstimate(
            flops=24 * slots * BLOCK * inner, bytes_accessed=40 * slots * inner,
            transcendentals=slots * BLOCK * inner // 32,
        ),
        name="mixer_backward",
    )(firsts, y, gated, dyn, scale, product, gain.reshape(1, -1), state, *params)


def local(
    x_in,
    lengths,
    routes,
    route_w,
    ln1_gain,
    w_zx,
    w_bc,
    w_dt,
    conv_x,
    conv_x_bias,
    conv_bc,
    conv_bc_bias,
    dt_bias,
    a_log,
    d_skip,
    gnorm_gain,
    w_out,
    ln2_gain,
    w_shared_gu,
    w_shared_down,
    w_exp_gu,
    w_exp_down,
    cotangent,
):
    slots, width = x_in.shape
    n_dp = lax.axis_size("dp")
    n_t = lax.axis_size("tensor")
    my_t = lax.axis_index("tensor")
    my_dp = lax.axis_index("dp")
    piece = slots // n_t
    n_local = w_exp_gu.shape[0]
    n_experts = n_dp * n_local
    cap = slots * routes.shape[1] * 4 // (3 * n_experts)
    if cap > slots:
        cap = slots
    heads = dt_bias.shape[0]
    inner = conv_x.shape[1]
    head_size = inner // heads
    state = conv_bc.shape[1] // 2
    full_inner = inner * n_t
    rows = w_zx.shape[0]
    n_sh = w_shared_gu.shape[2]

    dt_at = 2 * inner + 2 * state
    first_width = dt_at + heads + -(dt_at + heads) % 128
    first = jnp.concatenate(
        [
            w_zx.reshape(rows, 2 * inner),
            w_bc,
            w_dt,
            jnp.zeros((rows, first_width - dt_at - heads), F32),
        ],
        axis=1,
    ).astype(BF)
    shared = jnp.concatenate([w_shared_gu.reshape(rows, 2 * n_sh), w_shared_down], axis=1)

    live = (jnp.arange(slots, dtype=jnp.int32) < lengths[0]).astype(F32)
    g2 = cotangent.astype(F32) * live[:, None]
    g2_low = g2.astype(BF)
    expert_range = jnp.arange(n_experts, dtype=jnp.int32)
    chosen = routes[:, :, None] == expert_range[None, None, :]
    weights = jnp.sum(jnp.where(chosen, route_w[:, :, None], 0.0), axis=1)
    high = weights.astype(BF)
    low = (weights - high.astype(F32)).astype(BF)
    table = jnp.concatenate([g2_low, high, low], axis=1)
    table = lax.dynamic_slice_in_dim(table, my_t * piece, piece, axis=0)
    g2_piece = lax.dynamic_slice_in_dim(g2_low, my_t * piece, piece, axis=0)

    first, proj_out, table = start([first, w_out.astype(BF)], table, n_dp, 1)
    shared, first = lax.optimization_barrier((shared.astype(BF), first))
    shared = lax.all_gather(shared, "dp", axis=0, tiled=True)
    shared_gu = shared[:, : 2 * n_sh]
    shared_down = shared[:, 2 * n_sh :]

    x_float = x_in.astype(F32)
    scale_one = rms_scale(x_float)
    normed_one = (x_float * scale_one * ln1_gain).astype(BF)
    firsts = dotf("td,df->tf", normed_one, first)
    params = mixer_params(conv_x, conv_x_bias, conv_bc, conv_bc_bias, dt_bias, a_log, d_skip)
    y, gated_mix, squares, states = mixer_forward(firsts, params)
    squares = lax.psum(squares.reshape(slots), "tensor")[:, None]
    scale_mix = lax.rsqrt(squares / full_inner + EPSILON)
    normed_mix = (gated_mix * scale_mix * gnorm_gain).astype(BF)
    mixer_part = dotf("tc,dc->td", normed_mix, proj_out).astype(BF)
    x_piece = lax.dynamic_slice_in_dim(x_in, my_t * piece, piece, axis=0)
    all_rows, hidden_one = middle(mixer_part, x_piece, ln2_gain, n_dp, 2)
    mine = lax.dynamic_slice_in_dim(all_rows, my_dp * slots, slots, axis=0)

    shared_pre = dotf("td,df->tf", mine, shared_gu)
    s_gate, s_up = shared_pre[:, :n_sh], shared_pre[:, n_sh:]
    shared_silu, shared_slope = silu_parts(s_gate)
    shared_act = (shared_silu * s_up).astype(BF)
    grad_shared_act = dotf("td,df->tf", g2_low, shared_down)
    grad_shared_pre = jnp.concatenate(
        [grad_shared_act * s_up * shared_slope, grad_shared_act * shared_silu], axis=1
    ).astype(BF)
    grad_normed_shared = dotf("tf,df->td", grad_shared_pre, shared_gu)
    shared_part = dotf("tf,df->td", shared_act, shared_down)

    high = lax.dynamic_slice_in_dim(table, width + my_dp * n_local, n_local, axis=1)
    low = lax.dynamic_slice_in_dim(table, width + n_experts + my_dp * n_local, n_local, axis=1)
    weights = (high.astype(F32) + low.astype(F32)).reshape(n_dp, slots, n_local)
    member = (weights > 0.0).astype(BF)
    before = (
        jnp.arange(slots)[:, None] > jnp.arange(slots)[None, :]
    ).astype(BF)
    position = dotf("ut,ste->seu", before, member).astype(jnp.int32)
    weights = weights.transpose(0, 2, 1)
    position = jnp.where(weights > 0.0, position, -1)

    dxn_part, out_part, grad_exp_gu, grad_exp_down = experts(
        position, weights, all_rows, table, w_exp_gu, w_exp_down, cap
    )
    grad_exp_gu = grad_exp_gu.reshape(w_exp_gu.shape)

    def add_own(total, own):
        at = my_dp * slots
        own = own + lax.dynamic_slice_in_dim(total, at, slots, axis=0).astype(F32)
        return lax.dynamic_update_slice_in_dim(total, own.astype(BF), at, axis=0)

    dxn_part = add_own(dxn_part, grad_normed_shared)
    out_part = add_own(out_part, shared_part)
    ffn_out = scatter_rows(out_part, n_dp, 4)
    grad_shared_down = dotf("td,tf->df", g2_low, shared_act)
    grad_shared_gu = dotf("td,tf->df", mine, grad_shared_pre)
    grad_shared_w = jnp.concatenate([grad_shared_gu, grad_shared_down], axis=1).astype(BF)
    dxn_part, ffn_out, grad_shared_w = lax.optimization_barrier((dxn_part, ffn_out, grad_shared_w))
    grad_one, sum_ln2, dm = turn(
        dxn_part, hidden_one, g2_piece, ln2_gain, n_dp, 3
    )
    dm = dm.reshape(slots, width)

    layer_out = lax.all_gather(
        (hidden_one + ffn_out).astype(BF), "tensor", axis=0, tiled=True
    )
    grad_shared_w, dm = lax.optimization_barrier((grad_shared_w, dm))
    grad_shared_w = lax.psum_scatter(grad_shared_w, "dp", scatter_dimension=0, tiled=True)
    grad_out_w = dotf("td,tc->dc", dm, normed_mix).astype(BF)
    grad_normed_mix = dotf("td,dc->tc", dm, proj_out)
    weighted_mix = gnorm_gain * grad_normed_mix
    grad_gnorm = jnp.sum(grad_normed_mix * gated_mix * scale_mix, axis=0)
    product_sum = lax.psum(jnp.sum(weighted_mix * gated_mix, axis=-1), "tensor")[:, None]
    grad_first, mixer_sums = mixer_backward(
        full_inner, firsts, y, gated_mix, grad_normed_mix, scale_mix, product_sum, gnorm_gain,
        states, params,
    )
    taps = conv_x.shape[0]
    grad_conv_x, grad_conv_x_bias = mixer_sums[:taps], mixer_sums[4]
    grad_d_skip = jnp.sum(mixer_sums[5].reshape(heads, head_size), axis=1)
    grad_conv_bc, grad_conv_bc_bias = mixer_sums[6 : 6 + taps, : 2 * state], mixer_sums[10, : 2 * state]
    grad_a_log, grad_dt_bias = mixer_sums[11, :heads], mixer_sums[12, :heads]
    grad_input_part = dotf("tf,df->td", grad_first, first).astype(BF)
    grad_first_w = dotf("td,tf->df", normed_one, grad_first).astype(BF)
    def lanes(*vectors):
        vector = jnp.concatenate([v.reshape(-1) for v in vectors])
        return jnp.pad(vector, (0, -vector.shape[0] % (8 * width))).reshape(-1, width)

    wide = lanes(jnp.zeros((width,), F32), sum_ln2, grad_conv_bc, grad_conv_bc_bias)
    n_wide = wide.shape[0]
    narrow = lanes(
        grad_conv_x, grad_conv_x_bias, grad_gnorm, grad_dt_bias, grad_a_log, grad_d_skip
    )
    grad_first_w, grad_shared_w = lax.optimization_barrier((grad_first_w, grad_shared_w))
    grad_x, sums, (first_f, grad_out_w) = tail(
        [grad_first_w, grad_out_w],
        grad_input_part,
        grad_one,
        x_piece,
        ln1_gain,
        jnp.concatenate([wide, narrow], axis=0),
        n_wide,
        2 * inner,
        2 * state,
        n_dp,
        5,
    )
    grad_x = grad_x.reshape(slots, width).astype(F32)
    wide, narrow = sums[:n_wide].reshape(-1), sums[n_wide:].reshape(-1)
    at = [0]

    def take(vector, *shape):
        size = 1
        for s in shape:
            size *= s
        part = lax.slice_in_dim(vector, at[0], at[0] + size).reshape(shape)
        at[0] += size
        return part

    o_ln1 = take(wide, width)
    o_ln2 = take(wide, width)
    o_conv_bc = take(wide, taps, 2 * state)
    o_conv_bc_bias = take(wide, 2 * state)
    at[0] = 0
    o_conv_x = take(narrow, taps, inner)
    o_conv_x_bias = take(narrow, inner)
    o_gnorm = take(narrow, inner)
    o_dt_bias = take(narrow, heads)
    o_a_log = take(narrow, heads)
    o_d_skip = take(narrow, heads)
    shared_f = grad_shared_w.astype(F32)
    return (
        layer_out,
        grad_x,
        o_ln1,
        first_f[:, : 2 * inner].reshape(rows, 2, inner),
        first_f[:, 2 * inner : dt_at],
        first_f[:, dt_at : dt_at + heads],
        o_conv_x,
        o_conv_x_bias,
        o_conv_bc,
        o_conv_bc_bias,
        o_dt_bias,
        o_a_log,
        o_d_skip,
        o_gnorm,
        grad_out_w,
        o_ln2,
        shared_f[:, : 2 * n_sh].reshape(rows, 2, n_sh),
        shared_f[:, 2 * n_sh :],
        grad_exp_gu,
        grad_exp_down,
    )


def solution(mesh):
    return jax.shard_map(
        local,
        mesh=mesh,
        in_specs=(
            P("dp", None),
            P("dp"),
            P("dp", None),
            P("dp", None),
            P(),
            P("dp", None, "tensor"),
            P("dp", None),
            P("dp", "tensor"),
            P(None, "tensor"),
            P("tensor"),
            P(),
            P(),
            P("tensor"),
            P("tensor"),
            P("tensor"),
            P("tensor"),
            P("dp", "tensor"),
            P(),
            P("dp", None, "tensor"),
            P("dp", "tensor"),
            P("dp", None, None, "tensor"),
            P("dp", "tensor", None),
            P("dp", None),
        ),
        out_specs=(
            P("dp", None),
            P("dp", None),
            P(),
            P("dp", None, "tensor"),
            P("dp", None),
            P("dp", "tensor"),
            P(None, "tensor"),
            P("tensor"),
            P(),
            P(),
            P("tensor"),
            P("tensor"),
            P("tensor"),
            P("tensor"),
            P("dp", "tensor"),
            P(),
            P("dp", None, "tensor"),
            P("dp", "tensor"),
            P("dp", None, None, "tensor"),
            P("dp", "tensor", None),
        ),
        check_vma=False,
    )
```

```python
import functools

import jax
import jax.numpy as jnp
from jax import lax
from jax.experimental import pallas as pl
from jax.experimental.pallas import tpu as pltpu
from jax.sharding import PartitionSpec as P

BLOCK = 256


EPSILON = 1e-05
HIGHEST = lax.Precision.HIGHEST
BF = jnp.bfloat16
F32 = jnp.float32


def rms_scale(values):
    return lax.rsqrt(jnp.mean(values * values, axis=-1, keepdims=True) + EPSILON)


def silu_parts(values):
    sigmoid_val = jax.nn.sigmoid(values)
    return (values * sigmoid_val, sigmoid_val * (1.0 + values * (1.0 - sigmoid_val)))


def dotf(spec, a, b):
    return jnp.einsum(spec, a, b, preferred_element_type=F32)


MESH = pl.DeviceIdType.MESH
DMA = pltpu.SemaphoreType.DMA
VMEM_SPEC = pl.BlockSpec(memory_space=pltpu.VMEM)
ANY_SPEC = pl.BlockSpec(memory_space=pl.ANY)


def place():
    d = lax.axis_index("dp")
    t = lax.axis_index("tensor")
    return d // 2, d % 2, t // 2, t % 2


def device(hi, lo, th, tl):
    return (hi * 2 + lo, th * 2 + tl)


def peer(hi, k, n_hi):
    if n_hi & (n_hi - 1):
        return lax.rem(hi + k, n_hi)
    other, bit = hi, 1
    while bit <= k:
        if k & bit:
            other = other + bit * (1 - 2 * lax.rem(hi // bit, 2))
        bit *= 2
    return other


def back(k, n_hi):
    return n_hi - k if n_hi & (n_hi - 1) else k


def greet(n_hi, tensor=True):
    hi, lo, th, tl = place()
    barrier = pltpu.get_barrier_semaphore()
    others = [device(peer(hi, k, n_hi), lo, th, tl) for k in range(1, n_hi)]
    others += [device(hi, 1 - lo, th, tl)]
    if tensor:
        others += [device(hi, lo, 1 - th, tl), device(hi, lo, th, 1 - tl)]
    for other in others:
        pl.semaphore_signal(barrier, inc=1, device_id=other, device_id_type=MESH)
    pl.semaphore_wait(barrier, len(others))


def remote(src, dst, ssem, rsem, to):
    return pltpu.make_async_remote_copy(
        src_ref=src, dst_ref=dst, send_sem=ssem, recv_sem=rsem, device_id=to, device_id_type=MESH
    )


class Sends:
    def __init__(self):
        self.copies = []

    def push(self, src, dst, ssem, rsem, to):
        copy = remote(src, dst, ssem, rsem, to)
        copy.start()
        self.copies.append(copy)

    def finish(self):
        for copy in self.copies:
            copy.wait_send()


def arrive(dst, ssem, rsem, to):
    remote(dst, dst, ssem, rsem, to).wait_recv()


TENSOR_SUM_SCRATCH = lambda rows, width, dtype: [
    pltpu.VMEM((2, rows, width), dtype),
    pltpu.VMEM((rows, width), dtype),
    DMA((3,)),
    DMA((3,)),
]


def tensor_sum_start(sends, part_ref, got_c, ssem, rsem):
    hi, lo, th, tl = place()
    to_c = device(hi, lo, th, 1 - tl)
    for j, y in enumerate((1 - th, th)):
        sends.push(part_ref.at[y * 2 + 1 - tl], got_c.at[j], ssem.at[j], rsem.at[j], to_c)


def tensor_sum_middle(sends, part_ref, got_c, got_y, ssem, rsem):
    hi, lo, th, tl = place()
    arrive(got_c.at[0], ssem.at[0], rsem.at[0], device(hi, lo, th, 1 - tl))
    total = part_ref[(1 - th) * 2 + tl].astype(F32) + got_c[0].astype(F32)
    got_c[0] = total.astype(got_c.dtype)
    sends.push(got_c.at[0], got_y, ssem.at[2], rsem.at[2], device(hi, lo, 1 - th, tl))


def tensor_sum_end(part_ref, got_c, got_y, ssem, rsem):
    hi, lo, th, tl = place()
    arrive(got_c.at[1], ssem.at[1], rsem.at[1], device(hi, lo, th, 1 - tl))
    total = part_ref[th * 2 + tl].astype(F32) + got_c[1].astype(F32)
    arrive(got_y, ssem.at[2], rsem.at[2], device(hi, lo, 1 - th, tl))
    return total + got_y[...].astype(F32)


def tensor_spread_start(sends, o_ref, ssem, rsem):
    hi, lo, th, tl = place()
    own = o_ref.at[th * 2 + tl]
    sends.push(own, own, ssem.at[0], rsem.at[0], device(hi, lo, 1 - th, tl))
    sends.push(own, own, ssem.at[1], rsem.at[1], device(hi, lo, th, 1 - tl))


def tensor_spread_end(sends, o_ref, ssem, rsem):
    hi, lo, th, tl = place()
    other = o_ref.at[(1 - th) * 2 + tl]
    to_c = device(hi, lo, th, 1 - tl)
    arrive(other, ssem.at[0], rsem.at[0], device(hi, lo, 1 - th, tl))
    sends.push(other, other, ssem.at[2], rsem.at[2], to_c)
    arrive(o_ref.at[th * 2 + 1 - tl], ssem.at[1], rsem.at[1], to_c)
    arrive(o_ref.at[(1 - th) * 2 + 1 - tl], ssem.at[2], rsem.at[2], to_c)


def gather_steps(n_hi, x_ref, o_ref, own_sem, send_sem, recv_sem, lo_first=(True, False)):
    hi, lo, th, tl = place()
    rows = x_ref.shape[0]
    half = rows // 2
    own_block = (hi * 2 + lo) * 4 + th * 2 + tl
    own = pltpu.make_async_copy(x_ref, o_ref.at[pl.ds(own_block * rows, rows)], own_sem)
    own.start()
    sends = Sends()

    def slot(k, f, s, c):
        return ((c * 2 + s) * 2 + f) * n_hi + k

    def where(h, k, f, s, c):
        kk = peer(hi, k, n_hi)
        l = 1 - lo if (f if lo_first[h] else s) else lo
        y = 1 - th if (s if lo_first[h] else f) else th
        z = 1 - tl if c else tl
        return ((kk * 2 + l) * 4 + y * 2 + z) * rows + h * half

    def push(h, k, f, s, c, step):
        at = where(h, k, f, s, c)
        if k == 0 and not (f or s or c):
            src = x_ref.at[pl.ds(h * half, half)]
        else:
            src = o_ref.at[pl.ds(at, half)]
        if step == "c":
            to, r = device(hi, lo, th, 1 - tl), slot(k, f, s, 1)
        elif step == "s":
            to = device(hi, lo, 1 - th, tl) if lo_first[h] else device(hi, 1 - lo, th, tl)
            r = slot(k, f, 1, 0)
        elif step == "f":
            to = device(hi, 1 - lo, th, tl) if lo_first[h] else device(hi, lo, 1 - th, tl)
            r = slot(k, 1, 0, 0)
        else:
            to, r = device(peer(hi, step, n_hi), lo, th, tl), slot(back(step, n_hi), 0, 0, 0)
        sends.push(src, o_ref.at[pl.ds(at, half)], send_sem.at[h, r], recv_sem.at[h, r], to)

    def got(h, k, f, s, c):
        r = slot(k, f, s, c)
        arrive(
            o_ref.at[pl.ds(where(h, k, f, s, c), half)],
            send_sem.at[h, r], recv_sem.at[h, r], device(hi, lo, th, 1 - tl),
        )

    for k in range(n_hi):
        for h in range(2):
            if k:
                got(h, k, 0, 0, 0)
            if k < n_hi - 1:
                push(h, 0, 0, 0, 0, k + 1)
            for step in ("f", "s", "c"):
                push(h, k, 0, 0, 0, step)
        yield
        for h in range(2):
            got(h, k, 1, 0, 0)
            for step in ("s", "c"):
                push(h, k, 1, 0, 0, step)
        yield
    for k in range(n_hi):
        for f in range(2):
            for h in range(2):
                got(h, k, f, 1, 0)
                push(h, k, f, 1, 0, "c")
        yield
    for k in range(n_hi):
        for f in range(2):
            for s in range(2):
                for h in range(2):
                    got(h, k, f, s, 1)
    own.wait()
    sends.finish()


def in_turns(*streams):
    live = list(streams)
    while live:
        for stream in list(live):
            if next(stream, True) is True:
                live.remove(stream)


def middle_kernel(
    n_hi, part_ref, x_ref, gain_ref, o_ref, hidden_ref,
    normed, got_c, got_y, t_send, t_recv, *sems,
):
    greet(n_hi)
    sends = Sends()
    tensor_sum_start(sends, part_ref, got_c, t_send, t_recv)
    tensor_sum_middle(sends, part_ref, got_c, got_y, t_send, t_recv)
    hidden = x_ref[...].astype(F32) + tensor_sum_end(part_ref, got_c, got_y, t_send, t_recv)
    hidden_ref[...] = hidden
    normed[...] = (hidden * rms_scale(hidden) * gain_ref[...]).astype(normed.dtype)
    in_turns(gather_steps(n_hi, normed, o_ref, *sems))
    sends.finish()


def middle(part, x_piece, gain, n_dp, collective_id):
    rows, width = x_piece.shape
    n_hi = n_dp // 2
    return pl.pallas_call(
        functools.partial(middle_kernel, n_hi),
        out_shape=(
            jax.ShapeDtypeStruct((n_dp * 4 * rows, width), part.dtype),
            jax.ShapeDtypeStruct((rows, width), F32),
        ),
        in_specs=[VMEM_SPEC] * 3,
        out_specs=(ANY_SPEC, VMEM_SPEC),
        scratch_shapes=[pltpu.VMEM((rows, width), part.dtype)]
        + TENSOR_SUM_SCRATCH(rows, width, part.dtype)
        + [DMA, DMA((2, 8 * n_hi)), DMA((2, 8 * n_hi))],
        compiler_params=pltpu.CompilerParams(collective_id=collective_id, has_side_effects=True),
        name="middle",
    )(part.reshape(4, rows, width), x_piece, gain.reshape(1, width))


def weight_steps(n_hi, w_ref, o_ref, own_sem, send_b, recv_b, send_a, recv_a, send_f, recv_f):
    hi, lo, th, tl = place()
    to_f = device(hi, 1 - lo, th, tl)
    above = device(lax.rem(hi + 1, n_hi), lo, th, tl)
    below = device(lax.rem(hi + n_hi - 1, n_hi), lo, th, tl)
    sends = []

    def push(cond, src, at, h, ssem, rsem, to):
        copy = remote(src, o_ref.at[at, h], ssem, rsem, to)
        sends.append((cond, copy))
        if cond is None:
            copy.start()
        else:
            pl.when(cond)(copy.start)

    def block(j, l):
        return lax.rem(hi + j + n_hi, n_hi) * 2 + l

    for h in range(2):
        at = block(0, lo)
        push(hi < n_hi - 1, w_ref.at[h], at, h, send_b.at[h, 0], recv_b.at[h, 0], above)
        push(hi > 0, w_ref.at[h], at, h, send_a.at[h, 0], recv_a.at[h, 0], below)
        push(None, w_ref.at[h], at, h, send_f.at[h, 0], recv_f.at[h, 0], to_f)
    own = pltpu.make_async_copy(w_ref, o_ref.at[block(0, lo)], own_sem)
    own.start()
    yield
    for j in range(1, n_hi):
        for h in range(2):
            for down in (0, 1):
                valid = hi + j < n_hi if down else hi - j >= 0
                at = block(j if down else -j, lo)
                view = o_ref.at[at, h]
                sem = (send_a if down else send_b).at[h, j - 1], (recv_a if down else recv_b).at[h, j - 1]
                pl.when(valid)(remote(view, view, *sem, to_f).wait_recv)
                if j < n_hi - 1:
                    on = jnp.logical_and(valid, hi > 0 if down else hi < n_hi - 1)
                    push(
                        on, view, at, h, (send_a if down else send_b).at[h, j],
                        (recv_a if down else recv_b).at[h, j], below if down else above,
                    )
                f = 1 + down * (n_hi - 1) + j - 1
                push(valid, view, at, h, send_f.at[h, f], recv_f.at[h, f], to_f)
        yield
    for h in range(2):
        view = o_ref.at[block(0, 1 - lo), h]
        arrive(view, send_f.at[h, 0], recv_f.at[h, 0], to_f)
    for j in range(1, n_hi):
        for h in range(2):
            for down in (0, 1):
                valid = hi + j < n_hi if down else hi - j >= 0
                view = o_ref.at[block(j if down else -j, 1 - lo), h]
                f = 1 + down * (n_hi - 1) + j - 1
                pl.when(valid)(remote(view, view, send_f.at[h, f], recv_f.at[h, f], to_f).wait_recv)
    own.wait()
    for cond, copy in sends:
        if cond is None:
            copy.wait_send()
        else:
            pl.when(cond)(copy.wait_send)


def start_kernel(n_hi, n, *refs):
    ins, outs, sems = refs[: n + 1], refs[n + 1 : 2 * n + 2], refs[2 * n + 2 :]
    greet(n_hi)
    streams = [
        weight_steps(n_hi, ins[i], outs[i], *sems[7 * i : 7 * i + 7]) for i in range(n)
    ] + [gather_steps(n_hi, ins[n], outs[n], *sems[7 * n :], lo_first=(True, True))]
    in_turns(*streams)


def start(weights, table, n_dp, collective_id):
    n_hi = n_dp // 2
    n = len(weights)
    half = weights[0].shape[0] // 2
    outs = pl.pallas_call(
        functools.partial(start_kernel, n_hi, n),
        out_shape=[jax.ShapeDtypeStruct((n_dp, 2, half, w.shape[1]), w.dtype) for w in weights]
        + [jax.ShapeDtypeStruct((n_dp * 4 * table.shape[0], table.shape[1]), table.dtype)],
        in_specs=[ANY_SPEC] * (n + 1),
        out_specs=[ANY_SPEC] * (n + 1),
        scratch_shapes=[
            DMA,
            DMA((2, n_hi - 1)), DMA((2, n_hi - 1)),
            DMA((2, n_hi - 1)), DMA((2, n_hi - 1)),
            DMA((2, 2 * n_hi - 1)), DMA((2, 2 * n_hi - 1)),
        ] * n + [DMA, DMA((2, 8 * n_hi)), DMA((2, 8 * n_hi))],
        compiler_params=pltpu.CompilerParams(collective_id=collective_id, has_side_effects=True),
        name="start",
    )(*[w.reshape(2, half, w.shape[1]) for w in weights], table)
    return [o.reshape(n_dp * 2 * half, o.shape[3]) for o in outs[:n]] + [outs[n]]


def scatter_steps(n_hi, sends, p_ref, o_ref, bufs, lo_first=(False, True)):
    (stage, from_c, from_f, from_s, from_h,
     stage_sem, send_c, recv_c, send_f, recv_f, send_s, recv_s, send_h, recv_h) = bufs
    depth = stage.shape[0]
    hi, lo, th, tl = place()
    to_c = device(hi, lo, th, 1 - tl)
    rows = o_ref.shape[0]
    half = rows // 2

    def where(h, k, f, s, c):
        kk = peer(hi, k, n_hi)
        l = 1 - lo if (f if lo_first[h] else s) else lo
        y = 1 - th if (s if lo_first[h] else f) else th
        z = 1 - tl if c else tl
        return ((kk * 2 + l) * 4 + y * 2 + z) * rows + h * half

    ks = list(range(1, n_hi)) + [0]
    order = []
    for i in range(n_hi + 2):
        for lag, groups in ((0, ((1, 1), (1, 0))), (1, ((0, 1),)), (2, ((0, 0),))):
            if 0 <= i - lag < n_hi:
                order += [(f, s, ks[i - lag], h) for f, s in groups for h in range(2)]

    def slot(f, s, k):
        return (f * 2 + s) * n_hi + k

    def first(h):
        return device(hi, 1 - lo, th, tl) if lo_first[h] else device(hi, lo, 1 - th, tl)

    def second(h):
        return device(hi, lo, 1 - th, tl) if lo_first[h] else device(hi, 1 - lo, th, tl)

    for f, s, k, h in order:
        n = slot(f, s, k)
        sends.push(
            p_ref.at[pl.ds(where(h, k, f, s, 1), half)], from_c.at[h, n], send_c.at[h, n],
            recv_c.at[h, n], to_c,
        )

    def load(i):
        f, s, k, h = order[i]
        return pltpu.make_async_copy(
            p_ref.at[pl.ds(where(h, k, f, s, 0), half)], stage.at[i % depth], stage_sem.at[i % depth]
        )

    for i in range(depth - 1):
        load(i).start()
    for i, (f, s, k, h) in enumerate(order):
        if i + depth - 1 < len(order):
            load(i + depth - 1).start()
        if i % 4 == 0:
            yield
        load(i).wait()
        n = slot(f, s, k)
        arrive(from_c.at[h, n], send_c.at[h, n], recv_c.at[h, n], to_c)
        total = stage[i % depth].astype(F32) + from_c[h, n].astype(F32)
        if f == 0:
            m = s * n_hi + k
            arrive(from_f.at[h, m], send_f.at[h, m], recv_f.at[h, m], to_c)
            total = total + from_f[h, m].astype(F32)
        if f == 0 and s == 0:
            arrive(from_s.at[h, k], send_s.at[h, k], recv_s.at[h, k], to_c)
            total = total + from_s[h, k].astype(F32)
        if f == 0 and s == 0 and k == 0:
            for j in range(n_hi - 1):
                arrive(from_h.at[h, j], send_h.at[h, j], recv_h.at[h, j], to_c)
                total = total + from_h[h, j].astype(F32)
            o_ref[pl.ds(h * half, half), :] = total
            continue
        from_c[h, n] = total.astype(from_c.dtype)
        src = from_c.at[h, n]
        if f == 1:
            m = s * n_hi + k
            sends.push(src, from_f.at[h, m], send_f.at[h, m], recv_f.at[h, m], first(h))
        elif s == 1:
            sends.push(src, from_s.at[h, k], send_s.at[h, k], recv_s.at[h, k], second(h))
        else:
            j = back(k, n_hi) - 1
            sends.push(
                src, from_h.at[h, j], send_h.at[h, j], recv_h.at[h, j],
                device(peer(hi, k, n_hi), lo, th, tl),
            )


def scatter_scratch(n_hi, half, width, dtype, depth=4):
    return [
        pltpu.VMEM((depth, half, width), dtype),
        pltpu.VMEM((2, 4 * n_hi, half, width), dtype),
        pltpu.VMEM((2, 2 * n_hi, half, width), dtype),
        pltpu.VMEM((2, n_hi, half, width), dtype),
        pltpu.VMEM((2, n_hi - 1, half, width), dtype),
        DMA((depth,)),
        DMA((2, 4 * n_hi)), DMA((2, 4 * n_hi)),
        DMA((2, 2 * n_hi)), DMA((2, 2 * n_hi)),
        DMA((2, n_hi)), DMA((2, n_hi)),
        DMA((2, n_hi - 1)), DMA((2, n_hi - 1)),
    ]


def scatter_kernel(n_hi, p_ref, o_ref, *bufs):
    greet(n_hi)
    sends = Sends()
    in_turns(scatter_steps(n_hi, sends, p_ref, o_ref, bufs))
    sends.finish()


def scatter_rows(p, n_dp, collective_id):
    width = p.shape[1]
    rows = p.shape[0] // (n_dp * 4)
    n_hi = n_dp // 2
    return pl.pallas_call(
        functools.partial(scatter_kernel, n_hi),
        out_shape=jax.ShapeDtypeStruct((rows, width), F32),
        in_specs=[ANY_SPEC],
        out_specs=VMEM_SPEC,
        scratch_shapes=scatter_scratch(n_hi, rows // 2, width, p.dtype),
        compiler_params=pltpu.CompilerParams(
            collective_id=collective_id, has_side_effects=True, vmem_limit_bytes=60 << 20
        ),
        name="scatter_rows",
    )(p)


def turn_kernel(
    n_hi, p_ref, hidden_ref, g2_ref, gain_ref, grad_ref, sum_ref, dm_ref, total_ref, sp_send, sp_recv, *bufs
):
    hi, lo, th, tl = place()
    greet(n_hi)
    sends = Sends()
    in_turns(scatter_steps(n_hi, sends, p_ref, total_ref, bufs))
    grad = total_ref[...]
    hidden = hidden_ref[...]
    scale = rms_scale(hidden)
    weighted = gain_ref[...] * grad
    sum_ref[...] = jnp.sum(grad * hidden * scale, axis=0, keepdims=True)
    mean = jnp.mean(weighted * hidden, axis=-1, keepdims=True)
    grad = g2_ref[...].astype(F32) + scale * weighted - hidden * (scale * scale * scale) * mean
    grad_ref[...] = grad
    dm_ref[th * 2 + tl] = grad.astype(dm_ref.dtype)
    tensor_spread_start(sends, dm_ref, sp_send, sp_recv)
    tensor_spread_end(sends, dm_ref, sp_send, sp_recv)
    sends.finish()


def turn(p, hidden, g2_piece, gain, n_dp, collective_id):
    rows, width = hidden.shape
    n_hi = n_dp // 2
    return pl.pallas_call(
        functools.partial(turn_kernel, n_hi),
        out_shape=(
            jax.ShapeDtypeStruct((rows, width), F32),
            jax.ShapeDtypeStruct((1, width), F32),
            jax.ShapeDtypeStruct((4, rows, width), p.dtype),
        ),
        in_specs=[ANY_SPEC] + [VMEM_SPEC] * 3,
        out_specs=(VMEM_SPEC,) * 3,
        scratch_shapes=[pltpu.VMEM((rows, width), F32), DMA((3,)), DMA((3,))]
        + scatter_scratch(n_hi, rows // 2, width, p.dtype),
        compiler_params=pltpu.CompilerParams(
            collective_id=collective_id, has_side_effects=True, vmem_limit_bytes=60 << 20
        ),
        name="turn",
    )(p, hidden, g2_piece, gain.reshape(1, width))


def tail_kernel(n_hi, wide, bc_at, n, merged, *refs):
    if merged:
        p_ref, hidden_ref, refs = refs[0], refs[1], refs[2:]
    part_ref, grad_ref, x_ref, gain_ref, small_ref = refs[:5]
    w_refs = refs[5 : 5 + n]
    if merged:
        oy_ref, refs = refs[5 + n], refs[: 5 + n] + refs[6 + n :]
        o_total, y_send, y_recv = refs[-17:-14]
        p_bufs, refs = refs[-14:], refs[:-17]
    ox_ref, os_ref = refs[5 + n : 7 + n]
    ow_refs = refs[7 + n : 7 + 2 * n]
    (got_c, got_y, t_send, t_recv, sp_send, sp_recv,
     small, small_f, small_h, small_t, sm_send, sm_recv, smh_send, smh_recv,
     bc_own, bc_got, bc_send, bc_recv) = refs[7 + 2 * n : 25 + 2 * n]
    rest = refs[25 + 2 * n :]
    bufs = [rest[8 * i : 8 * i + 8] for i in range(n)]
    hi, lo, th, tl = place()
    to_f, to_y, to_c = device(hi, 1 - lo, th, tl), device(hi, lo, 1 - th, tl), device(hi, lo, th, 1 - tl)
    greet(n_hi)
    sends = Sends()
    order = [(k, h) for k in reversed(range(n_hi)) for h in range(2)]
    events = [(w, k, h) for w in range(n) for k, h in order]
    events = [e for e in events if e[1]] + [e for e in events if not e[1]]

    def owner(k, l):
        return peer(hi, k, n_hi) * 2 + l

    if merged:
        others = scatter_steps(n_hi, sends, p_ref, o_total, p_bufs, lo_first=(False, False))
    else:
        others = iter(())
    next(others, None)

    def forward(i):
        if i < len(events):
            w, k, h = events[i]
            stage, from_f, from_h, stage_sem, send_f, recv_f, send_h, recv_h = bufs[w]
            sends.push(
                w_refs[w].at[owner(k, 1 - lo), h], from_f.at[h, k], send_f.at[h, k], recv_f.at[h, k], to_f
            )

    window = 4
    for i in range(window):
        forward(i)
    loads = []
    for w, k, h in events:
        copy = pltpu.make_async_copy(
            w_refs[w].at[owner(k, lo), h], bufs[w][0].at[h, k], bufs[w][3].at[h, k]
        )
        copy.start()
        loads.append(copy)
    tensor_sum_start(sends, part_ref, got_c, t_send, t_recv)
    tensor_sum_middle(sends, part_ref, got_c, got_y, t_send, t_recv)
    grad = tensor_sum_end(part_ref, got_c, got_y, t_send, t_recv)
    x = x_ref[...].astype(F32)
    scale = rms_scale(x)
    weighted = gain_ref[...] * grad
    mean = jnp.mean(weighted * x, axis=-1, keepdims=True)
    ox_ref[th * 2 + tl] = (
        grad_ref[...] + scale * weighted - x * (scale * scale * scale) * mean
    ).astype(ox_ref.dtype)
    tensor_spread_start(sends, ox_ref, sp_send, sp_recv)
    small[...] = small_ref[...]
    small[0:1, :] = jnp.sum(grad * x * scale, axis=0, keepdims=True)
    sends.push(small, small_f, sm_send.at[0], sm_recv.at[0], to_f)

    for i, (w, k, h) in enumerate(events):
        if k == 0:
            break
        stage, from_f, from_h, stage_sem, send_f, recv_f, send_h, recv_h = bufs[w]
        next(others, None)
        loads[i].wait()
        arrive(from_f.at[h, k], send_f.at[h, k], recv_f.at[h, k], to_c)
        forward(i + window)
        from_f[h, k] = (stage[h, k].astype(F32) + from_f[h, k].astype(F32)).astype(from_f.dtype)
        j = back(k, n_hi) - 1
        sends.push(
            from_f.at[h, k], from_h.at[h, j], send_h.at[h, j], recv_h.at[h, j],
            device(peer(hi, k, n_hi), lo, th, tl),
        )
        if i == 0:
            tensor_spread_end(sends, ox_ref, sp_send, sp_recv)
        if i == 1:
            arrive(small_f, sm_send.at[0], sm_recv.at[0], to_c)
            small_h[hi] = small[...] + small_f[...]
            for q in range(1, n_hi):
                sends.push(
                    small_h.at[hi], small_h.at[hi], smh_send.at[q - 1], smh_recv.at[back(q, n_hi) - 1],
                    device(peer(hi, q, n_hi), lo, th, tl),
                )
    if merged:
        in_turns(others)
        oy_ref[th * 2 + tl] = (hidden_ref[...] + o_total[...]).astype(oy_ref.dtype)
        tensor_spread_start(sends, oy_ref, y_send, y_recv)
    for q in range(1, n_hi):
        arrive(small_h.at[peer(hi, q, n_hi)], smh_send.at[q - 1], smh_recv.at[q - 1], to_c)
    total = small_h[0]
    for q in range(1, n_hi):
        total = total + small_h[q]
    os_ref[...] = total
    sends.push(os_ref.at[pl.ds(0, wide)], small_t.at[0], sm_send.at[1], sm_recv.at[1], to_c)
    for i, (w, k, h) in enumerate(events):
        if k:
            continue
        forward(i + window)
        stage, from_f, from_h, stage_sem, send_f, recv_f, send_h, recv_h = bufs[w]
        loads[i].wait()
        arrive(from_f.at[h, 0], send_f.at[h, 0], recv_f.at[h, 0], to_c)
        total = stage[h, 0].astype(F32) + from_f[h, 0].astype(F32)
        for j in range(n_hi - 1):
            arrive(from_h.at[h, j], send_h.at[h, j], recv_h.at[h, j], to_c)
            total = total + from_h[h, j].astype(F32)
        ow_refs[w][h] = total
        if w == 0:
            bc_own[0, h] = total[:, bc_at : bc_at + bc_own.shape[3]].astype(bc_own.dtype)
            if h == 1:
                sends.push(bc_own.at[0], bc_got.at[0], bc_send.at[0], bc_recv.at[0], to_c)
                arrive(small_t.at[0], sm_send.at[1], sm_recv.at[1], to_c)
                small_t[2] = os_ref[pl.ds(0, wide), :] + small_t[0]
                sends.push(small_t.at[2], small_t.at[1], sm_send.at[2], sm_recv.at[2], to_y)
                arrive(bc_got.at[0], bc_send.at[0], bc_recv.at[0], to_c)
                bc_own[1] = (bc_own[0].astype(F32) + bc_got[0].astype(F32)).astype(bc_own.dtype)
                sends.push(bc_own.at[1], bc_got.at[1], bc_send.at[1], bc_recv.at[1], to_y)
    if merged:
        tensor_spread_end(sends, oy_ref, y_send, y_recv)
    arrive(small_t.at[1], sm_send.at[2], sm_recv.at[2], to_c)
    arrive(bc_got.at[1], bc_send.at[1], bc_recv.at[1], to_c)
    for h in range(2):
        ow_refs[0][h, :, bc_at : bc_at + bc_own.shape[3]] = (
            bc_own[1, h].astype(F32) + bc_got[1, h].astype(F32)
        )
    sends.finish()
    os_ref[pl.ds(0, wide), :] = small_t[2] + small_t[1]


def tail(
    weights, part, grad_one, x_piece, gain, small, wide, bc_at, bc_width, n_dp, collective_id,
    out_part=None, hidden=None,
):
    merged = out_part is not None
    rows, width = x_piece.shape
    n_hi = n_dp // 2
    n = len(weights)
    half = weights[0].shape[0] // (2 * n_dp)
    dt = weights[0].dtype
    scratch = TENSOR_SUM_SCRATCH(rows, width, part.dtype) + [
        DMA((3,)), DMA((3,)),
        pltpu.VMEM(small.shape, F32),
        pltpu.VMEM(small.shape, F32),
        pltpu.VMEM((n_hi,) + small.shape, F32),
        pltpu.VMEM((3, wide, small.shape[1]), F32),
        DMA((3,)), DMA((3,)),
        DMA((n_hi - 1,)), DMA((n_hi - 1,)),
        pltpu.VMEM((2, 2, half, bc_width), dt),
        pltpu.VMEM((2, 2, half, bc_width), dt),
        DMA((2,)), DMA((2,)),
    ]
    for w in weights:
        scratch += [
            pltpu.VMEM((2, n_hi, half, w.shape[1]), dt),
            pltpu.VMEM((2, n_hi, half, w.shape[1]), dt),
            pltpu.VMEM((2, n_hi - 1, half, w.shape[1]), dt),
            DMA((2, n_hi)),
            DMA((2, n_hi)), DMA((2, n_hi)),
            DMA((2, n_hi - 1)), DMA((2, n_hi - 1)),
        ]
    if merged:
        scratch += [pltpu.VMEM((rows, width), F32), DMA((3,)), DMA((3,))]
        scratch += scatter_scratch(n_hi, rows // 2, width, out_part.dtype)
    outs = pl.pallas_call(
        functools.partial(tail_kernel, n_hi, wide, bc_at, n, merged),
        out_shape=[jax.ShapeDtypeStruct((4, rows, width), dt)] * merged + [
            jax.ShapeDtypeStruct((4, rows, width), dt),
            jax.ShapeDtypeStruct(small.shape, F32),
        ] + [jax.ShapeDtypeStruct((2, half, w.shape[1]), F32) for w in weights],
        in_specs=[ANY_SPEC, VMEM_SPEC] * merged + [VMEM_SPEC] * 5 + [ANY_SPEC] * n,
        out_specs=[VMEM_SPEC] * (2 + n + merged),
        scratch_shapes=scratch,
        compiler_params=pltpu.CompilerParams(
            collective_id=collective_id, has_side_effects=True, vmem_limit_bytes=60 << 20
        ),
        name="tail",
    )(
        *([out_part, hidden] if merged else []), part.reshape(4, rows, width), grad_one, x_piece, gain.reshape(1, width), small,
        *[w.reshape(n_dp, 2, half, w.shape[1]) for w in weights],
    )
    out = outs[0].reshape(4 * rows, width) if merged else None
    outs = outs[merged:]
    return outs[0], outs[1], [o.reshape(2 * half, o.shape[2]) for o in outs[2:]], out


def dot_mm(a, b):
    return lax.dot_general(a, b, (((1,), (0,)), ((), ())), preferred_element_type=F32)


def dot_nt(a, b):
    return lax.dot_general(a, b, (((1,), (1,)), ((), ())), preferred_element_type=F32)


def dot_tn(a, b):
    return lax.dot_general(a, b, (((0,), (0,)), ((), ())), preferred_element_type=F32)


def experts_kernel(
    n_dp, n_local, cap, chunk, pos_ref, wt_ref, x_ref, g_ref, gu_ref, dn_ref,
    dxn_ref, out_ref, ggu_ref, gdn_ref, pick, xr, q, sw, gu,
):
    step = pl.program_id(0)
    width = x_ref.shape[1]
    hidden = dn_ref.shape[1]
    slots = x_ref.shape[0]
    columns = [pl.ds(c, chunk) for c in range(0, width, chunk)]

    @pl.when(step < n_dp)
    def _():
        s = step
        lane = lax.broadcasted_iota(jnp.int32, (cap, slots), 0)
        for e in range(n_local):
            hit = lane == pos_ref[0, e : e + 1, :]
            pick[s, e * cap : (e + 1) * cap, :] = jnp.where(hit, 1.0, 0.0).astype(BF)
            sw[e, s] = jnp.sum(jnp.where(hit, wt_ref[0, e : e + 1, :], 0.0), axis=1, keepdims=True)
        chosen = pick[s]
        for c in columns:
            rows = dot_mm(chosen, x_ref[:, c]).astype(BF)
            grads = dot_mm(chosen, g_ref[:, c])
            for e in range(n_local):
                xr[e, s, :, c] = rows[e * cap : (e + 1) * cap]
                q[e, s, :, c] = (grads[e * cap : (e + 1) * cap] * sw[e, s]).astype(BF)

    @pl.when(jnp.logical_and(step >= n_dp, step < n_dp + n_local))
    def _():
        e = step - n_dp
        gu[:, :hidden] = gu_ref[pl.ds(0, width, stride=2), :].astype(BF)
        gu[:, hidden:] = gu_ref[pl.ds(1, width, stride=2), :].astype(BF)
        down = dn_ref[0].astype(BF)
        x = xr[e].reshape(n_dp * cap, width)
        qe = q[e].reshape(n_dp * cap, width)
        pre = dot_mm(x, gu[...])
        grad_act = dot_nt(qe, down)
        gate, up = pre[:, :hidden], pre[:, hidden:]
        sig = 1.0 / (1.0 + jnp.exp(-gate))
        act_silu = gate * sig
        slope = sig * (1.0 + gate * (1.0 - sig))
        value = act_silu * up
        act = value.astype(BF)
        scaled = (value * sw[e].reshape(n_dp * cap, 1)).astype(BF)
        grad_pre = jnp.concatenate([grad_act * up * slope, grad_act * act_silu], axis=1).astype(BF)
        ggu = dot_tn(x, grad_pre)
        ggu_ref[pl.ds(0, width, stride=2), :] = ggu[:, :hidden]
        ggu_ref[pl.ds(1, width, stride=2), :] = ggu[:, hidden:]
        gdn_ref[0] = dot_tn(act, qe)
        for c in columns:
            xr[e, :, :, c] = dot_nt(grad_pre, gu[c, :]).astype(BF).reshape(n_dp, cap, chunk)
            q[e, :, :, c] = dot_mm(scaled, down[:, c.start : c.start + chunk]).astype(BF).reshape(n_dp, cap, chunk)

    @pl.when(step >= n_dp + n_local)
    def _():
        s = step - n_dp - n_local
        chosen = pick[s]
        for c in columns:
            dxn_ref[:, c] = dot_tn(chosen, xr[:, s, :, c].reshape(n_local * cap, chunk)).astype(BF)
            out_ref[:, c] = dot_tn(chosen, q[:, s, :, c].reshape(n_local * cap, chunk)).astype(BF)


def experts(position, weights, rows, table, w_gu, w_down, cap):
    n_dp, n_local, slots = position.shape
    width = rows.shape[1]
    hidden = w_down.shape[1]
    chunk = width // 3 if width % 384 == 0 else width
    by_source = lambda i: (jnp.clip(i, 0, n_dp - 1), 0, 0)
    rows_in = lambda i: (jnp.clip(i, 0, n_dp - 1), 0)
    rows_out = lambda i: (jnp.clip(i - n_dp - n_local, 0, n_dp - 1), 0)
    flat = lambda i: (jnp.clip(i - n_dp, 0, n_local - 1), 0)
    deep = lambda i: (jnp.clip(i - n_dp, 0, n_local - 1), 0, 0)
    total = n_dp * n_local * cap
    return pl.pallas_call(
        functools.partial(experts_kernel, n_dp, n_local, cap, chunk),
        grid=(2 * n_dp + n_local,),
        out_shape=(
            jax.ShapeDtypeStruct((n_dp * slots, width), BF),
            jax.ShapeDtypeStruct((n_dp * slots, width), BF),
            jax.ShapeDtypeStruct((n_local * width * 2, hidden), F32),
            jax.ShapeDtypeStruct((n_local, hidden, width), F32),
        ),
        in_specs=[
            pl.BlockSpec((1, n_local, slots), by_source),
            pl.BlockSpec((1, n_local, slots), by_source),
            pl.BlockSpec((slots, width), rows_in),
            pl.BlockSpec((slots, width), rows_in),
            pl.BlockSpec((width * 2, hidden), flat),
            pl.BlockSpec((1, hidden, width), deep),
        ],
        out_specs=(
            pl.BlockSpec((slots, width), rows_out),
            pl.BlockSpec((slots, width), rows_out),
            pl.BlockSpec((width * 2, hidden), flat),
            pl.BlockSpec((1, hidden, width), deep),
        ),
        scratch_shapes=[
            pltpu.VMEM((n_dp, n_local * cap, slots), BF),
            pltpu.VMEM((n_local, n_dp, cap, width), BF),
            pltpu.VMEM((n_local, n_dp, cap, width), BF),
            pltpu.VMEM((n_local, n_dp, cap, 1), F32),
            pltpu.VMEM((width, 2 * hidden), BF),
        ],
        compiler_params=pltpu.CompilerParams(
            dimension_semantics=("arbitrary",), vmem_limit_bytes=60 << 20
        ),
        cost_estimate=pl.CostEstimate(
            flops=8 * total * slots * width + 18 * total * width * hidden,
            bytes_accessed=8 * n_dp * slots * width + 24 * n_local * width * hidden,
            transcendentals=total * hidden,
        ),
        name="experts",
    )(
        position,
        weights,
        rows,
        table,
        w_gu.reshape(n_local * width * 2, hidden),
        w_down,
    )


def conv_pre(pad, values, taps, bias):
    n = values.shape[0]
    pad[pl.ds(8, n), :] = values
    count = taps.shape[0]
    total = bias + taps[count - 1 : count] * values
    for k in range(count - 1):
        total = total + taps[k : k + 1] * pad[pl.ds(8 - (count - 1) + k, n), :]
    return total


def sigmoid(v):
    return 1.0 / (1.0 + jnp.exp(-v))


def dot_exact(a, b):
    return lax.dot_general(
        a, b, (((1,), (0,)), ((), ())), precision=HIGHEST, preferred_element_type=F32
    )


def step_parts(first_ref, at, dtb_ref, alog_ref):
    raw = first_ref[:, at : at + 128] + dtb_ref[...]
    delta = jnp.maximum(raw, 0.0) + jnp.log(1.0 + jnp.exp(-jnp.abs(raw)))
    return raw, delta, -jnp.exp(alog_ref[...])


def lower_mask():
    t = lax.broadcasted_iota(jnp.int32, (BLOCK, BLOCK), 0)
    s = lax.broadcasted_iota(jnp.int32, (BLOCK, BLOCK), 1)
    return t >= s


def by_head(left, a, b):
    return jnp.where(left, a, b)


def mixer_forward_kernel(
    first_ref, cx_ref, cxb_ref, cbc_ref, cbcb_ref, dtb_ref, alog_ref, skip_ref,
    y_ref, gated_ref, square_ref, state_ref, pad,
):
    slots = first_ref.shape[0]
    inner = cx_ref.shape[1]
    n_blocks = slots // BLOCK
    bc_at = 2 * inner
    pad[0:8, :] = jnp.zeros((8, 128), F32)
    mask = lower_mask()
    tri = mask.astype(F32)
    left = lax.broadcasted_iota(jnp.int32, (BLOCK, 128), 1) < 64
    left_row = left[0:1]

    parts = []
    for c in (0, 128):
        pre = conv_pre(pad, first_ref[:, bc_at + c : bc_at + c + 128], cbc_ref[:, c : c + 128], cbcb_ref[:, c : c + 128])
        parts.append((pre * sigmoid(pre)).astype(BF))
    b_rows, c_rows = parts
    raw, delta, rate = step_parts(first_ref, bc_at + 256, dtb_ref, alog_ref)
    blocks = []
    for b in range(n_blocks):
        r = slice(b * BLOCK, (b + 1) * BLOCK)
        d = delta[r]
        cum = dot_exact(tri, rate * d)
        blocks.append((d, cum, d.T, cum.T, dot_nt(c_rows[r], b_rows[r])))
    squares = jnp.zeros((slots, 1), F32)
    for p in range(inner // 128):
        lanes = slice(p * 128, (p + 1) * 128)
        pre = conv_pre(pad, first_ref[:, inner + p * 128 : inner + (p + 1) * 128], cx_ref[:, lanes], cxb_ref[:, lanes])
        heads_in = (pre * sigmoid(pre)).astype(BF)
        state = None
        outs = []
        for b in range(n_blocks):
            d, cum, d_t, cum_t, inter = blocks[b]
            r = slice(b * BLOCK, (b + 1) * BLOCK)
            x = heads_in[r]
            ys = []
            for h in (2 * p, 2 * p + 1):
                decay = jnp.exp(jnp.where(mask, cum[:, h : h + 1] - cum_t[h : h + 1, :], -1e30))
                ys.append(dot_mm((inter * decay * d_t[h : h + 1, :]).astype(BF), x))
            y = by_head(left, ys[0], ys[1]) + skip_ref[:, lanes] * x.astype(F32)
            cum_p = by_head(left, cum[:, 2 * p : 2 * p + 1], cum[:, 2 * p + 1 : 2 * p + 2])
            d_p = by_head(left, d[:, 2 * p : 2 * p + 1], d[:, 2 * p + 1 : 2 * p + 2])
            if state is not None:
                state_ref[p, b - 1] = state
                y = y + jnp.exp(cum_p) * dot_mm(c_rows[r], state.astype(BF))
            if b + 1 < n_blocks:
                end = cum_p[BLOCK - 1 :]
                z_rows = x.astype(F32) * d_p * jnp.exp(end - cum_p)
                fresh = dot_tn(b_rows[r], z_rows.astype(BF))
                state = fresh if state is None else jnp.exp(end) * state + fresh
            outs.append(y)
        y = jnp.concatenate(outs, axis=0)
        z = first_ref[:, lanes]
        gated = y * (z * sigmoid(z))
        y_ref[:, lanes] = y
        gated_ref[:, lanes] = gated
        squares = squares + jnp.sum(gated * gated, axis=1, keepdims=True)
    square_ref[...] = squares


def mixer_backward_kernel(
    full_inner, first_ref, y_ref, gated_ref, dyn_ref, scale_ref, product_ref, gain_ref, state_ref,
    cx_ref, cxb_ref, cbc_ref, cbcb_ref, dtb_ref, alog_ref, skip_ref,
    grad_ref, small_ref, pad, after, cols, sums_t,
):
    slots = first_ref.shape[0]
    inner = cx_ref.shape[1]
    n_blocks = slots // BLOCK
    bc_at = 2 * inner
    taps = cx_ref.shape[0]
    pad[0:8, :] = jnp.zeros((8, 128), F32)
    after[pl.ds(slots, 8), :] = jnp.zeros((8, 128), F32)
    small_ref[...] = jnp.zeros_like(small_ref)
    cols[...] = jnp.zeros_like(cols)
    sums_t[...] = jnp.zeros_like(sums_t)
    mask = lower_mask()
    tri = mask.astype(F32)
    lane = lax.broadcasted_iota(jnp.int32, (BLOCK, 128), 1)
    left = lane < 64

    parts, bc_pre = [], []
    for c in (0, 128):
        pre = conv_pre(pad, first_ref[:, bc_at + c : bc_at + c + 128], cbc_ref[:, c : c + 128], cbcb_ref[:, c : c + 128])
        bc_pre.append(pre)
        parts.append((pre * sigmoid(pre)).astype(BF))
    b_rows, c_rows = parts
    raw, delta, rate = step_parts(first_ref, bc_at + 256, dtb_ref, alog_ref)
    scale = scale_ref[...]
    cube = scale * scale * scale * product_ref[...] * (1.0 / full_inner)
    blocks = []
    for b in range(n_blocks):
        r = slice(b * BLOCK, (b + 1) * BLOCK)
        d = delta[r]
        cum = dot_exact(tri, rate * d)
        blocks.append((d, cum, d.T, cum.T, dot_nt(c_rows[r], b_rows[r])))
    grad_inter = [jnp.zeros((BLOCK, BLOCK), F32) for _ in range(n_blocks)]
    grad_b = [jnp.zeros((BLOCK, 128), F32) for _ in range(n_blocks)]
    grad_c = [jnp.zeros((BLOCK, 128), F32) for _ in range(n_blocks)]

    def conv_back(grad_out, pre, values, taps_v, row, bias_row, lanes, at):
        sig = sigmoid(pre)
        a = grad_out * (sig * (1.0 + pre * (1.0 - sig)))
        after[pl.ds(0, slots), :] = a
        pad[pl.ds(8, slots), :] = values
        total = taps_v[taps - 1 : taps] * a
        small_ref[row + taps - 1 : row + taps, lanes] = jnp.sum(a * values, axis=0, keepdims=True)
        for k in range(taps - 1):
            total = total + taps_v[k : k + 1] * after[pl.ds(taps - 1 - k, slots), :]
            small_ref[row + k : row + k + 1, lanes] = jnp.sum(
                a * pad[pl.ds(8 - (taps - 1) + k, slots), :], axis=0, keepdims=True
            )
        small_ref[bias_row : bias_row + 1, lanes] = jnp.sum(a, axis=0, keepdims=True)
        grad_ref[:, at : at + 128] = total.astype(grad_ref.dtype)

    for p in range(inner // 128):
        lanes = slice(p * 128, (p + 1) * 128)
        values = first_ref[:, inner + p * 128 : inner + (p + 1) * 128]
        pre = conv_pre(pad, values, cx_ref[:, lanes], cxb_ref[:, lanes])
        heads_in = (pre * sigmoid(pre)).astype(BF)
        z = first_ref[:, lanes]
        sig = sigmoid(z)
        grad_gated = scale * gain_ref[:, lanes] * dyn_ref[:, lanes] - gated_ref[:, lanes] * cube
        grad_y = grad_gated * (z * sig)
        grad_ref[:, lanes] = (
            grad_gated * y_ref[:, lanes] * (sig * (1.0 + z * (1.0 - sig)))
        ).astype(grad_ref.dtype)
        skip = skip_ref[:, lanes]
        x_f = heads_in.astype(F32)
        small_ref[5:6, lanes] = jnp.sum(grad_y * x_f, axis=0, keepdims=True)
        grad_y_low = grad_y.astype(BF)
        grad_x = [None] * n_blocks
        grad_state = None
        for b in reversed(range(n_blocks)):
            d, cum, d_t, cum_t, inter = blocks[b]
            r = slice(b * BLOCK, (b + 1) * BLOCK)
            x, xf, dy, dyl = heads_in[r], x_f[r], grad_y[r], grad_y_low[r]
            cum_p = by_head(left, cum[:, 2 * p : 2 * p + 1], cum[:, 2 * p + 1 : 2 * p + 2])
            d_p = by_head(left, d[:, 2 * p : 2 * p + 1], d[:, 2 * p + 1 : 2 * p + 2])
            dxs = []
            for i, h in enumerate((2 * p, 2 * p + 1)):
                own = left if i == 0 else jnp.logical_not(left)
                q = dot_nt(jnp.where(own, dy, 0.0).astype(BF), x)
                decay = jnp.exp(jnp.where(mask, cum[:, h : h + 1] - cum_t[h : h + 1, :], -1e30))
                scaled = decay * d_t[h : h + 1, :]
                dxs.append(dot_tn((inter * scaled).astype(BF), dyl))
                grad_inter[b] = grad_inter[b] + scaled * q
                moved = inter * decay * q
                sums_t[b, h : h + 1, :] = jnp.sum(moved, axis=0, keepdims=True)
                rows = jnp.sum(moved * d_t[h : h + 1, :], axis=1, keepdims=True)
                cols[0, r, :] += jnp.where(lane == h, rows, 0.0)
            dx = by_head(left, dxs[0], dxs[1]) + skip * dy
            extra = None
            if b > 0:
                state = state_ref[p, b - 1]
                grown = dy * jnp.exp(cum_p)
                grown_low = grown.astype(BF)
                extra = grown * dot_mm(c_rows[r], state.astype(BF))
                grad_c[b] = grad_c[b] + dot_nt(grown_low, state.astype(BF))
                back_state = dot_tn(c_rows[r], grown_low)
            end = cum_p[BLOCK - 1 :]
            end_sum = None
            if grad_state is not None:
                weight = jnp.exp(end - cum_p)
                low_state = grad_state.astype(BF)
                dz_rows = dot_mm(b_rows[r], low_state)
                grad_b[b] = grad_b[b] + dot_nt((xf * d_p * weight).astype(BF), low_state)
                dx = dx + dz_rows * d_p * weight
                direct = dz_rows * xf * weight
                through = direct * d_p
                end_sum = jnp.sum(through, axis=0, keepdims=True)
                if b > 0:
                    end_sum = end_sum + jnp.exp(end) * jnp.sum(grad_state * state, axis=0, keepdims=True)
                extra = -through if extra is None else extra - through
            for i, h in enumerate((2 * p, 2 * p + 1)):
                own = left if i == 0 else jnp.logical_not(left)
                if extra is not None:
                    column = jnp.sum(jnp.where(own, extra, 0.0), axis=1, keepdims=True)
                    cols[0, r, :] += jnp.where(lane == h, column, 0.0)
                if end_sum is not None:
                    column = jnp.sum(jnp.where(own, direct, 0.0), axis=1, keepdims=True)
                    cols[1, r, :] += jnp.where(lane == h, column, 0.0)
                    last = jnp.sum(jnp.where(own[0:1], end_sum, 0.0), axis=1, keepdims=True)
                    at = slice((b + 1) * BLOCK - 1, (b + 1) * BLOCK)
                    cols[0, at, :] += jnp.where(lane[0:1] == h, last, 0.0)
            if b > 0:
                grad_state = back_state if grad_state is None else jnp.exp(end) * grad_state + back_state
            grad_x[b] = dx
        conv_back(
            jnp.concatenate(grad_x, axis=0), pre, values, cx_ref[:, lanes], 0, 4, lanes, inner + p * 128
        )
    upper = jnp.logical_not(mask).astype(F32) + (
        lax.broadcasted_iota(jnp.int32, (BLOCK, BLOCK), 0)
        == lax.broadcasted_iota(jnp.int32, (BLOCK, BLOCK), 1)
    ).astype(F32)
    ddts, logs = [], jnp.zeros((1, 128), F32)
    for b in range(n_blocks):
        d, cum, d_t, cum_t, inter = blocks[b]
        r = slice(b * BLOCK, (b + 1) * BLOCK)
        low = grad_inter[b].astype(BF)
        grad_c[b] = grad_c[b] + dot_mm(low, b_rows[r])
        grad_b[b] = grad_b[b] + dot_tn(low, c_rows[r])
        direct = sums_t[b].T
        reach = dot_exact(upper, cols[0, r, :] - direct * d)
        logs = logs + jnp.sum(rate * d * reach, axis=0, keepdims=True)
        ddts.append((direct + cols[1, r, :] + rate * reach) * sigmoid(raw[r]))
    ddt = jnp.concatenate(ddts, axis=0)
    grad_ref[:, bc_at + 256 : bc_at + 384] = ddt.astype(grad_ref.dtype)
    small_ref[11:12, 0:128] = logs
    small_ref[12:13, 0:128] = jnp.sum(ddt, axis=0, keepdims=True)
    for i, (c, grads) in enumerate(((0, grad_b), (128, grad_c))):
        conv_back(
            jnp.concatenate(grads, axis=0), bc_pre[i], first_ref[:, bc_at + c : bc_at + c + 128],
            cbc_ref[:, c : c + 128], 6, 10, slice(c, c + 128), bc_at + c,
        )


def pad_lanes(v):
    return jnp.pad(v, (0, -v.shape[0] % 128)).reshape(1, -1)


def mixer_params(conv_x, conv_x_bias, conv_bc, conv_bc_bias, dt_bias, a_log, d_skip):
    size = conv_x.shape[1] // d_skip.shape[0]
    return (
        conv_x, conv_x_bias.reshape(1, -1), conv_bc, conv_bc_bias.reshape(1, -1),
        pad_lanes(dt_bias), pad_lanes(a_log), jnp.repeat(d_skip, size).reshape(1, -1),
    )


def mixer_forward(firsts, params):
    slots = firsts.shape[0]
    inner = params[0].shape[1]
    pairs, n_blocks = inner // 128, slots // BLOCK
    shape = lambda *s: jax.ShapeDtypeStruct(s, F32)
    return pl.pallas_call(
        mixer_forward_kernel,
        out_shape=(
            shape(slots, inner), shape(slots, inner), shape(slots, 1),
            shape(pairs, n_blocks - 1, 128, 128),
        ),
        in_specs=[VMEM_SPEC] * 8,
        out_specs=(VMEM_SPEC,) * 4,
        scratch_shapes=[pltpu.VMEM((slots + 8, 128), F32)],
        compiler_params=pltpu.CompilerParams(vmem_limit_bytes=48 << 20),
        cost_estimate=pl.CostEstimate(
            flops=8 * slots * BLOCK * inner, bytes_accessed=24 * slots * inner,
            transcendentals=slots * BLOCK * inner // 32,
        ),
        name="mixer_forward",
    )(firsts, *params)


def mixer_backward(full_inner, firsts, y, gated, dyn, scale, product, gain, state, params):
    slots, width = firsts.shape
    inner = params[0].shape[1]
    return pl.pallas_call(
        functools.partial(mixer_backward_kernel, full_inner),
        out_shape=(
            jax.ShapeDtypeStruct((slots, width), BF),
            jax.ShapeDtypeStruct((16, inner), F32),
        ),
        in_specs=[VMEM_SPEC] * 15,
        out_specs=(VMEM_SPEC,) * 2,
        scratch_shapes=[
            pltpu.VMEM((slots + 8, 128), F32),
            pltpu.VMEM((slots + 8, 128), F32),
            pltpu.VMEM((2, slots, 128), F32),
            pltpu.VMEM((slots // BLOCK, 128, BLOCK), F32),
        ],
        compiler_params=pltpu.CompilerParams(vmem_limit_bytes=56 << 20),
        cost_estimate=pl.CostEstimate(
            flops=24 * slots * BLOCK * inner, bytes_accessed=40 * slots * inner,
            transcendentals=slots * BLOCK * inner // 32,
        ),
        name="mixer_backward",
    )(firsts, y, gated, dyn, scale, product, gain.reshape(1, -1), state, *params)


def local(
    x_in,
    lengths,
    routes,
    route_w,
    ln1_gain,
    w_zx,
    w_bc,
    w_dt,
    conv_x,
    conv_x_bias,
    conv_bc,
    conv_bc_bias,
    dt_bias,
    a_log,
    d_skip,
    gnorm_gain,
    w_out,
    ln2_gain,
    w_shared_gu,
    w_shared_down,
    w_exp_gu,
    w_exp_down,
    cotangent,
):
    slots, width = x_in.shape
    n_dp = lax.axis_size("dp")
    n_t = lax.axis_size("tensor")
    my_t = lax.axis_index("tensor")
    my_dp = lax.axis_index("dp")
    piece = slots // n_t
    n_local = w_exp_gu.shape[0]
    n_experts = n_dp * n_local
    cap = slots * routes.shape[1] * 4 // (3 * n_experts)
    if cap > slots:
        cap = slots
    heads = dt_bias.shape[0]
    inner = conv_x.shape[1]
    head_size = inner // heads
    state = conv_bc.shape[1] // 2
    full_inner = inner * n_t
    rows = w_zx.shape[0]
    n_sh = w_shared_gu.shape[2]

    dt_at = 2 * inner + 2 * state
    first_width = dt_at + heads + -(dt_at + heads) % 128
    first = jnp.concatenate(
        [
            w_zx.reshape(rows, 2 * inner),
            w_bc,
            w_dt,
            jnp.zeros((rows, first_width - dt_at - heads), F32),
        ],
        axis=1,
    ).astype(BF)
    shared = jnp.concatenate([w_shared_gu.reshape(rows, 2 * n_sh), w_shared_down], axis=1)

    live = (jnp.arange(slots, dtype=jnp.int32) < lengths[0]).astype(F32)
    g2 = cotangent.astype(F32) * live[:, None]
    g2_low = g2.astype(BF)
    expert_range = jnp.arange(n_experts, dtype=jnp.int32)
    chosen = routes[:, :, None] == expert_range[None, None, :]
    weights = jnp.sum(jnp.where(chosen, route_w[:, :, None], 0.0), axis=1)
    high = weights.astype(BF)
    low = (weights - high.astype(F32)).astype(BF)
    table = jnp.concatenate([g2_low, high, low], axis=1)
    table = lax.dynamic_slice_in_dim(table, my_t * piece, piece, axis=0)
    g2_piece = lax.dynamic_slice_in_dim(g2_low, my_t * piece, piece, axis=0)

    first, proj_out, table = start([first, w_out.astype(BF)], table, n_dp, 1)
    shared, first = lax.optimization_barrier((shared.astype(BF), first))
    shared = lax.all_gather(shared, "dp", axis=0, tiled=True)
    shared_gu = shared[:, : 2 * n_sh]
    shared_down = shared[:, 2 * n_sh :]

    x_float = x_in.astype(F32)
    scale_one = rms_scale(x_float)
    normed_one = (x_float * scale_one * ln1_gain).astype(BF)
    firsts = dotf("td,df->tf", normed_one, first)
    params = mixer_params(conv_x, conv_x_bias, conv_bc, conv_bc_bias, dt_bias, a_log, d_skip)
    y, gated_mix, squares, states = mixer_forward(firsts, params)
    squares = lax.psum(squares.reshape(slots), "tensor")[:, None]
    scale_mix = lax.rsqrt(squares / full_inner + EPSILON)
    normed_mix = (gated_mix * scale_mix * gnorm_gain).astype(BF)
    mixer_part = dotf("tc,dc->td", normed_mix, proj_out).astype(BF)
    x_piece = lax.dynamic_slice_in_dim(x_in, my_t * piece, piece, axis=0)
    all_rows, hidden_one = middle(mixer_part, x_piece, ln2_gain, n_dp, 2)
    mine = lax.dynamic_slice_in_dim(all_rows, my_dp * slots, slots, axis=0)

    shared_pre = dotf("td,df->tf", mine, shared_gu)
    s_gate, s_up = shared_pre[:, :n_sh], shared_pre[:, n_sh:]
    shared_silu, shared_slope = silu_parts(s_gate)
    shared_act = (shared_silu * s_up).astype(BF)
    grad_shared_act = dotf("td,df->tf", g2_low, shared_down)
    grad_shared_pre = jnp.concatenate(
        [grad_shared_act * s_up * shared_slope, grad_shared_act * shared_silu], axis=1
    ).astype(BF)
    grad_normed_shared = dotf("tf,df->td", grad_shared_pre, shared_gu)
    shared_part = dotf("tf,df->td", shared_act, shared_down)

    high = lax.dynamic_slice_in_dim(table, width + my_dp * n_local, n_local, axis=1)
    low = lax.dynamic_slice_in_dim(table, width + n_experts + my_dp * n_local, n_local, axis=1)
    weights = (high.astype(F32) + low.astype(F32)).reshape(n_dp, slots, n_local)
    member = (weights > 0.0).astype(BF)
    before = (
        jnp.arange(slots)[:, None] > jnp.arange(slots)[None, :]
    ).astype(BF)
    position = dotf("ut,ste->seu", before, member).astype(jnp.int32)
    weights = weights.transpose(0, 2, 1)
    position = jnp.where(weights > 0.0, position, -1)

    dxn_part, out_part, grad_exp_gu, grad_exp_down = experts(
        position, weights, all_rows, table, w_exp_gu, w_exp_down, cap
    )
    grad_exp_gu = grad_exp_gu.reshape(w_exp_gu.shape)

    def add_own(total, own):
        at = my_dp * slots
        own = own + lax.dynamic_slice_in_dim(total, at, slots, axis=0).astype(F32)
        return lax.dynamic_update_slice_in_dim(total, own.astype(BF), at, axis=0)

    dxn_part = add_own(dxn_part, grad_normed_shared)
    out_part = add_own(out_part, shared_part)
    grad_shared_down = dotf("td,tf->df", g2_low, shared_act)
    grad_shared_gu = dotf("td,tf->df", mine, grad_shared_pre)
    grad_shared_w = jnp.concatenate([grad_shared_gu, grad_shared_down], axis=1).astype(BF)
    dxn_part, grad_shared_w = lax.optimization_barrier((dxn_part, grad_shared_w))
    grad_one, sum_ln2, dm = turn(
        dxn_part, hidden_one, g2_piece, ln2_gain, n_dp, 3
    )
    dm = dm.reshape(slots, width)

    grad_shared_w = lax.psum_scatter(grad_shared_w, "dp", scatter_dimension=0, tiled=True)
    grad_out_w = dotf("td,tc->dc", dm, normed_mix).astype(BF)
    grad_normed_mix = dotf("td,dc->tc", dm, proj_out)
    weighted_mix = gnorm_gain * grad_normed_mix
    grad_gnorm = jnp.sum(grad_normed_mix * gated_mix * scale_mix, axis=0)
    product_sum = jnp.sum(weighted_mix * gated_mix, axis=-1).reshape(-1, 128)
    product_sum = lax.psum(product_sum, "tensor").reshape(slots, 1)
    grad_first, mixer_sums = mixer_backward(
        full_inner, firsts, y, gated_mix, grad_normed_mix, scale_mix, product_sum, gnorm_gain,
        states, params,
    )
    taps = conv_x.shape[0]
    grad_conv_x, grad_conv_x_bias = mixer_sums[:taps], mixer_sums[4]
    grad_d_skip = jnp.sum(mixer_sums[5].reshape(heads, head_size), axis=1)
    grad_conv_bc, grad_conv_bc_bias = mixer_sums[6 : 6 + taps, : 2 * state], mixer_sums[10, : 2 * state]
    grad_a_log, grad_dt_bias = mixer_sums[11, :heads], mixer_sums[12, :heads]
    grad_input_part = dotf("tf,df->td", grad_first, first).astype(BF)
    grad_first_w = dotf("td,tf->df", normed_one, grad_first).astype(BF)
    def lanes(*vectors):
        vector = jnp.concatenate([v.reshape(-1) for v in vectors])
        return jnp.pad(vector, (0, -vector.shape[0] % (8 * width))).reshape(-1, width)

    wide = lanes(jnp.zeros((width,), F32), sum_ln2, grad_conv_bc, grad_conv_bc_bias)
    n_wide = wide.shape[0]
    narrow = lanes(
        grad_conv_x, grad_conv_x_bias, grad_gnorm, grad_dt_bias, grad_a_log, grad_d_skip
    )
    grad_first_w, grad_shared_w = lax.optimization_barrier((grad_first_w, grad_shared_w))
    merged = n_dp <= 8
    grad_x, sums, (first_f, grad_out_w), layer_out = tail(
        [grad_first_w, grad_out_w],
        grad_input_part,
        grad_one,
        x_piece,
        ln1_gain,
        jnp.concatenate([wide, narrow], axis=0),
        n_wide,
        2 * inner,
        2 * state,
        n_dp,
        5,
        *((out_part, hidden_one) if merged else ()),
    )
    if not merged:
        ffn_out = scatter_rows(out_part, n_dp, 4)
        layer_out = lax.all_gather((hidden_one + ffn_out).astype(BF), "tensor", axis=0, tiled=True)
    grad_x = grad_x.reshape(slots, width).astype(F32)
    wide, narrow = sums[:n_wide].reshape(-1), sums[n_wide:].reshape(-1)
    at = [0]

    def take(vector, *shape):
        size = 1
        for s in shape:
            size *= s
        part = lax.slice_in_dim(vector, at[0], at[0] + size).reshape(shape)
        at[0] += size
        return part

    o_ln1 = take(wide, width)
    o_ln2 = take(wide, width)
    o_conv_bc = take(wide, taps, 2 * state)
    o_conv_bc_bias = take(wide, 2 * state)
    at[0] = 0
    o_conv_x = take(narrow, taps, inner)
    o_conv_x_bias = take(narrow, inner)
    o_gnorm = take(narrow, inner)
    o_dt_bias = take(narrow, heads)
    o_a_log = take(narrow, heads)
    o_d_skip = take(narrow, heads)
    shared_f = grad_shared_w.astype(F32)
    return (
        layer_out,
        grad_x,
        o_ln1,
        first_f[:, : 2 * inner].reshape(rows, 2, inner),
        first_f[:, 2 * inner : dt_at],
        first_f[:, dt_at : dt_at + heads],
        o_conv_x,
        o_conv_x_bias,
        o_conv_bc,
        o_conv_bc_bias,
        o_dt_bias,
        o_a_log,
        o_d_skip,
        o_gnorm,
        grad_out_w,
        o_ln2,
        shared_f[:, : 2 * n_sh].reshape(rows, 2, n_sh),
        shared_f[:, 2 * n_sh :],
        grad_exp_gu,
        grad_exp_down,
    )


def solution(mesh):
    return jax.shard_map(
        local,
        mesh=mesh,
        in_specs=(
            P("dp", None),
            P("dp"),
            P("dp", None),
            P("dp", None),
            P(),
            P("dp", None, "tensor"),
            P("dp", None),
            P("dp", "tensor"),
            P(None, "tensor"),
            P("tensor"),
            P(),
            P(),
            P("tensor"),
            P("tensor"),
            P("tensor"),
            P("tensor"),
            P("dp", "tensor"),
            P(),
            P("dp", None, "tensor"),
            P("dp", "tensor"),
            P("dp", None, None, "tensor"),
            P("dp", "tensor", None),
            P("dp", None),
        ),
        out_specs=(
            P("dp", None),
            P("dp", None),
            P(),
            P("dp", None, "tensor"),
            P("dp", None),
            P("dp", "tensor"),
            P(None, "tensor"),
            P("tensor"),
            P(),
            P(),
            P("tensor"),
            P("tensor"),
            P("tensor"),
            P("tensor"),
            P("dp", "tensor"),
            P(),
            P("dp", None, "tensor"),
            P("dp", "tensor"),
            P("dp", None, None, "tensor"),
            P("dp", "tensor", None),
        ),
        check_vma=False,
    )
```

```python
import functools

import jax
import jax.numpy as jnp
from jax import lax
from jax.experimental import pallas as pl
from jax.experimental.pallas import tpu as pltpu
from jax.sharding import PartitionSpec as P

BLOCK = 256


EPSILON = 1e-05
HIGHEST = lax.Precision.HIGHEST
BF = jnp.bfloat16
F32 = jnp.float32


def rms_scale(values):
    return lax.rsqrt(jnp.mean(values * values, axis=-1, keepdims=True) + EPSILON)


def silu_parts(values):
    sigmoid_val = jax.nn.sigmoid(values)
    return (values * sigmoid_val, sigmoid_val * (1.0 + values * (1.0 - sigmoid_val)))


def dotf(spec, a, b):
    return jnp.einsum(spec, a, b, preferred_element_type=F32)


MESH = pl.DeviceIdType.MESH
DMA = pltpu.SemaphoreType.DMA
VMEM_SPEC = pl.BlockSpec(memory_space=pltpu.VMEM)
ANY_SPEC = pl.BlockSpec(memory_space=pl.ANY)


def place():
    d = lax.axis_index("dp")
    t = lax.axis_index("tensor")
    return d // 2, d % 2, t // 2, t % 2


def device(hi, lo, th, tl):
    return (hi * 2 + lo, th * 2 + tl)


def peer(hi, k, n_hi):
    if n_hi & (n_hi - 1):
        return lax.rem(hi + k, n_hi)
    other, bit = hi, 1
    while bit <= k:
        if k & bit:
            other = other + bit * (1 - 2 * lax.rem(hi // bit, 2))
        bit *= 2
    return other


def back(k, n_hi):
    return n_hi - k if n_hi & (n_hi - 1) else k


def greet(n_hi, tensor=True):
    hi, lo, th, tl = place()
    barrier = pltpu.get_barrier_semaphore()
    others = [device(peer(hi, k, n_hi), lo, th, tl) for k in range(1, n_hi)]
    others += [device(hi, 1 - lo, th, tl)]
    if tensor:
        others += [device(hi, lo, 1 - th, tl), device(hi, lo, th, 1 - tl)]
    for other in others:
        pl.semaphore_signal(barrier, inc=1, device_id=other, device_id_type=MESH)
    pl.semaphore_wait(barrier, len(others))


def remote(src, dst, ssem, rsem, to):
    return pltpu.make_async_remote_copy(
        src_ref=src, dst_ref=dst, send_sem=ssem, recv_sem=rsem, device_id=to, device_id_type=MESH
    )


class Sends:
    def __init__(self):
        self.copies = []

    def push(self, src, dst, ssem, rsem, to):
        copy = remote(src, dst, ssem, rsem, to)
        copy.start()
        self.copies.append(copy)

    def finish(self):
        for copy in self.copies:
            copy.wait_send()


def arrive(dst, ssem, rsem, to):
    remote(dst, dst, ssem, rsem, to).wait_recv()


TENSOR_SUM_SCRATCH = lambda rows, width, dtype: [
    pltpu.VMEM((2, rows, width), dtype),
    pltpu.VMEM((rows, width), dtype),
    DMA((3,)),
    DMA((3,)),
]


def tensor_sum_start(sends, part_ref, got_c, ssem, rsem):
    hi, lo, th, tl = place()
    to_c = device(hi, lo, th, 1 - tl)
    for j, y in enumerate((1 - th, th)):
        sends.push(part_ref.at[y * 2 + 1 - tl], got_c.at[j], ssem.at[j], rsem.at[j], to_c)


def tensor_sum_middle(sends, part_ref, got_c, got_y, ssem, rsem):
    hi, lo, th, tl = place()
    arrive(got_c.at[0], ssem.at[0], rsem.at[0], device(hi, lo, th, 1 - tl))
    total = part_ref[(1 - th) * 2 + tl].astype(F32) + got_c[0].astype(F32)
    got_c[0] = total.astype(got_c.dtype)
    sends.push(got_c.at[0], got_y, ssem.at[2], rsem.at[2], device(hi, lo, 1 - th, tl))


def tensor_sum_end(part_ref, got_c, got_y, ssem, rsem):
    hi, lo, th, tl = place()
    arrive(got_c.at[1], ssem.at[1], rsem.at[1], device(hi, lo, th, 1 - tl))
    total = part_ref[th * 2 + tl].astype(F32) + got_c[1].astype(F32)
    arrive(got_y, ssem.at[2], rsem.at[2], device(hi, lo, 1 - th, tl))
    return total + got_y[...].astype(F32)


def tensor_spread_start(sends, o_ref, ssem, rsem):
    hi, lo, th, tl = place()
    own = o_ref.at[th * 2 + tl]
    sends.push(own, own, ssem.at[0], rsem.at[0], device(hi, lo, 1 - th, tl))
    sends.push(own, own, ssem.at[1], rsem.at[1], device(hi, lo, th, 1 - tl))


def tensor_spread_end(sends, o_ref, ssem, rsem):
    hi, lo, th, tl = place()
    other = o_ref.at[(1 - th) * 2 + tl]
    to_c = device(hi, lo, th, 1 - tl)
    arrive(other, ssem.at[0], rsem.at[0], device(hi, lo, 1 - th, tl))
    sends.push(other, other, ssem.at[2], rsem.at[2], to_c)
    arrive(o_ref.at[th * 2 + 1 - tl], ssem.at[1], rsem.at[1], to_c)
    arrive(o_ref.at[(1 - th) * 2 + 1 - tl], ssem.at[2], rsem.at[2], to_c)


def gather_steps(n_hi, x_ref, o_ref, own_sem, send_sem, recv_sem, lo_first=(True, False)):
    hi, lo, th, tl = place()
    rows = x_ref.shape[0]
    half = rows // 2
    own_block = (hi * 2 + lo) * 4 + th * 2 + tl
    own = pltpu.make_async_copy(x_ref, o_ref.at[pl.ds(own_block * rows, rows)], own_sem)
    own.start()
    sends = Sends()

    def slot(k, f, s, c):
        return ((c * 2 + s) * 2 + f) * n_hi + k

    def where(h, k, f, s, c):
        kk = peer(hi, k, n_hi)
        l = 1 - lo if (f if lo_first[h] else s) else lo
        y = 1 - th if (s if lo_first[h] else f) else th
        z = 1 - tl if c else tl
        return ((kk * 2 + l) * 4 + y * 2 + z) * rows + h * half

    def push(h, k, f, s, c, step):
        at = where(h, k, f, s, c)
        if k == 0 and not (f or s or c):
            src = x_ref.at[pl.ds(h * half, half)]
        else:
            src = o_ref.at[pl.ds(at, half)]
        if step == "c":
            to, r = device(hi, lo, th, 1 - tl), slot(k, f, s, 1)
        elif step == "s":
            to = device(hi, lo, 1 - th, tl) if lo_first[h] else device(hi, 1 - lo, th, tl)
            r = slot(k, f, 1, 0)
        elif step == "f":
            to = device(hi, 1 - lo, th, tl) if lo_first[h] else device(hi, lo, 1 - th, tl)
            r = slot(k, 1, 0, 0)
        else:
            to, r = device(peer(hi, step, n_hi), lo, th, tl), slot(back(step, n_hi), 0, 0, 0)
        sends.push(src, o_ref.at[pl.ds(at, half)], send_sem.at[h, r], recv_sem.at[h, r], to)

    def got(h, k, f, s, c):
        r = slot(k, f, s, c)
        arrive(
            o_ref.at[pl.ds(where(h, k, f, s, c), half)],
            send_sem.at[h, r], recv_sem.at[h, r], device(hi, lo, th, 1 - tl),
        )

    for k in range(n_hi):
        for h in range(2):
            if k:
                got(h, k, 0, 0, 0)
            if k < n_hi - 1:
                push(h, 0, 0, 0, 0, k + 1)
            for step in ("f", "s", "c"):
                push(h, k, 0, 0, 0, step)
        yield
        for h in range(2):
            got(h, k, 1, 0, 0)
            for step in ("s", "c"):
                push(h, k, 1, 0, 0, step)
        yield
    for k in range(n_hi):
        for f in range(2):
            for h in range(2):
                got(h, k, f, 1, 0)
                push(h, k, f, 1, 0, "c")
        yield
    for k in range(n_hi):
        for f in range(2):
            for s in range(2):
                for h in range(2):
                    got(h, k, f, s, 1)
    own.wait()
    sends.finish()


def in_turns(*streams):
    live = list(streams)
    while live:
        for stream in list(live):
            if next(stream, True) is True:
                live.remove(stream)


def middle_kernel(
    n_hi, part_ref, x_ref, gain_ref, o_ref, hidden_ref,
    normed, got_c, got_y, t_send, t_recv, *sems,
):
    greet(n_hi)
    sends = Sends()
    tensor_sum_start(sends, part_ref, got_c, t_send, t_recv)
    tensor_sum_middle(sends, part_ref, got_c, got_y, t_send, t_recv)
    hidden = x_ref[...].astype(F32) + tensor_sum_end(part_ref, got_c, got_y, t_send, t_recv)
    hidden_ref[...] = hidden
    normed[...] = (hidden * rms_scale(hidden) * gain_ref[...]).astype(normed.dtype)
    in_turns(gather_steps(n_hi, normed, o_ref, *sems))
    sends.finish()


def middle(part, x_piece, gain, n_dp, collective_id):
    rows, width = x_piece.shape
    n_hi = n_dp // 2
    return pl.pallas_call(
        functools.partial(middle_kernel, n_hi),
        out_shape=(
            jax.ShapeDtypeStruct((n_dp * 4 * rows, width), part.dtype),
            jax.ShapeDtypeStruct((rows, width), F32),
        ),
        in_specs=[VMEM_SPEC] * 3,
        out_specs=(ANY_SPEC, VMEM_SPEC),
        scratch_shapes=[pltpu.VMEM((rows, width), part.dtype)]
        + TENSOR_SUM_SCRATCH(rows, width, part.dtype)
        + [DMA, DMA((2, 8 * n_hi)), DMA((2, 8 * n_hi))],
        compiler_params=pltpu.CompilerParams(collective_id=collective_id, has_side_effects=True),
        name="middle",
    )(part.reshape(4, rows, width), x_piece, gain.reshape(1, width))


def weight_steps(n_hi, w_ref, o_ref, own_sem, send_b, recv_b, send_a, recv_a, send_f, recv_f):
    hi, lo, th, tl = place()
    to_f = device(hi, 1 - lo, th, tl)
    above = device(lax.rem(hi + 1, n_hi), lo, th, tl)
    below = device(lax.rem(hi + n_hi - 1, n_hi), lo, th, tl)
    sends = []

    def push(cond, src, at, h, ssem, rsem, to):
        copy = remote(src, o_ref.at[at, h], ssem, rsem, to)
        sends.append((cond, copy))
        if cond is None:
            copy.start()
        else:
            pl.when(cond)(copy.start)

    def block(j, l):
        return lax.rem(hi + j + n_hi, n_hi) * 2 + l

    for h in range(2):
        at = block(0, lo)
        push(hi < n_hi - 1, w_ref.at[h], at, h, send_b.at[h, 0], recv_b.at[h, 0], above)
        push(hi > 0, w_ref.at[h], at, h, send_a.at[h, 0], recv_a.at[h, 0], below)
        push(None, w_ref.at[h], at, h, send_f.at[h, 0], recv_f.at[h, 0], to_f)
    own = pltpu.make_async_copy(w_ref, o_ref.at[block(0, lo)], own_sem)
    own.start()
    yield
    for j in range(1, n_hi):
        for h in range(2):
            for down in (0, 1):
                valid = hi + j < n_hi if down else hi - j >= 0
                at = block(j if down else -j, lo)
                view = o_ref.at[at, h]
                sem = (send_a if down else send_b).at[h, j - 1], (recv_a if down else recv_b).at[h, j - 1]
                pl.when(valid)(remote(view, view, *sem, to_f).wait_recv)
                if j < n_hi - 1:
                    on = jnp.logical_and(valid, hi > 0 if down else hi < n_hi - 1)
                    push(
                        on, view, at, h, (send_a if down else send_b).at[h, j],
                        (recv_a if down else recv_b).at[h, j], below if down else above,
                    )
                f = 1 + down * (n_hi - 1) + j - 1
                push(valid, view, at, h, send_f.at[h, f], recv_f.at[h, f], to_f)
        yield
    for h in range(2):
        view = o_ref.at[block(0, 1 - lo), h]
        arrive(view, send_f.at[h, 0], recv_f.at[h, 0], to_f)
    for j in range(1, n_hi):
        for h in range(2):
            for down in (0, 1):
                valid = hi + j < n_hi if down else hi - j >= 0
                view = o_ref.at[block(j if down else -j, 1 - lo), h]
                f = 1 + down * (n_hi - 1) + j - 1
                pl.when(valid)(remote(view, view, send_f.at[h, f], recv_f.at[h, f], to_f).wait_recv)
    own.wait()
    for cond, copy in sends:
        if cond is None:
            copy.wait_send()
        else:
            pl.when(cond)(copy.wait_send)


def start_kernel(n_hi, n, *refs):
    ins, outs, sems = refs[: n + 1], refs[n + 1 : 2 * n + 2], refs[2 * n + 2 :]
    greet(n_hi)
    streams = [
        weight_steps(n_hi, ins[i], outs[i], *sems[7 * i : 7 * i + 7]) for i in range(n)
    ] + [gather_steps(n_hi, ins[n], outs[n], *sems[7 * n :], lo_first=(True, True))]
    in_turns(*streams)


def start(weights, table, n_dp, collective_id):
    n_hi = n_dp // 2
    n = len(weights)
    half = weights[0].shape[0] // 2
    outs = pl.pallas_call(
        functools.partial(start_kernel, n_hi, n),
        out_shape=[jax.ShapeDtypeStruct((n_dp, 2, half, w.shape[1]), w.dtype) for w in weights]
        + [jax.ShapeDtypeStruct((n_dp * 4 * table.shape[0], table.shape[1]), table.dtype)],
        in_specs=[ANY_SPEC] * (n + 1),
        out_specs=[ANY_SPEC] * (n + 1),
        scratch_shapes=[
            DMA,
            DMA((2, n_hi - 1)), DMA((2, n_hi - 1)),
            DMA((2, n_hi - 1)), DMA((2, n_hi - 1)),
            DMA((2, 2 * n_hi - 1)), DMA((2, 2 * n_hi - 1)),
        ] * n + [DMA, DMA((2, 8 * n_hi)), DMA((2, 8 * n_hi))],
        compiler_params=pltpu.CompilerParams(collective_id=collective_id, has_side_effects=True),
        name="start",
    )(*[w.reshape(2, half, w.shape[1]) for w in weights], table)
    return [o.reshape(n_dp * 2 * half, o.shape[3]) for o in outs[:n]] + [outs[n]]


def scatter_steps(n_hi, sends, p_ref, o_ref, bufs, lo_first=(False, True)):
    (stage, from_c, from_f, from_s, from_h,
     stage_sem, send_c, recv_c, send_f, recv_f, send_s, recv_s, send_h, recv_h) = bufs
    depth = stage.shape[0]
    hi, lo, th, tl = place()
    to_c = device(hi, lo, th, 1 - tl)
    rows = o_ref.shape[0]
    half = rows // 2

    def where(h, k, f, s, c):
        kk = peer(hi, k, n_hi)
        l = 1 - lo if (f if lo_first[h] else s) else lo
        y = 1 - th if (s if lo_first[h] else f) else th
        z = 1 - tl if c else tl
        return ((kk * 2 + l) * 4 + y * 2 + z) * rows + h * half

    ks = list(range(1, n_hi)) + [0]
    order = []
    for i in range(n_hi + 2):
        for lag, groups in ((0, ((1, 1), (1, 0))), (1, ((0, 1),)), (2, ((0, 0),))):
            if 0 <= i - lag < n_hi:
                order += [(f, s, ks[i - lag], h) for f, s in groups for h in range(2)]

    def slot(f, s, k):
        return (f * 2 + s) * n_hi + k

    def first(h):
        return device(hi, 1 - lo, th, tl) if lo_first[h] else device(hi, lo, 1 - th, tl)

    def second(h):
        return device(hi, lo, 1 - th, tl) if lo_first[h] else device(hi, 1 - lo, th, tl)

    for f, s, k, h in order:
        n = slot(f, s, k)
        sends.push(
            p_ref.at[pl.ds(where(h, k, f, s, 1), half)], from_c.at[h, n], send_c.at[h, n],
            recv_c.at[h, n], to_c,
        )

    def load(i):
        f, s, k, h = order[i]
        return pltpu.make_async_copy(
            p_ref.at[pl.ds(where(h, k, f, s, 0), half)], stage.at[i % depth], stage_sem.at[i % depth]
        )

    for i in range(depth - 1):
        load(i).start()
    for i, (f, s, k, h) in enumerate(order):
        if i + depth - 1 < len(order):
            load(i + depth - 1).start()
        if i % 4 == 0:
            yield
        load(i).wait()
        n = slot(f, s, k)
        arrive(from_c.at[h, n], send_c.at[h, n], recv_c.at[h, n], to_c)
        total = stage[i % depth].astype(F32) + from_c[h, n].astype(F32)
        if f == 0:
            m = s * n_hi + k
            arrive(from_f.at[h, m], send_f.at[h, m], recv_f.at[h, m], to_c)
            total = total + from_f[h, m].astype(F32)
        if f == 0 and s == 0:
            arrive(from_s.at[h, k], send_s.at[h, k], recv_s.at[h, k], to_c)
            total = total + from_s[h, k].astype(F32)
        if f == 0 and s == 0 and k == 0:
            for j in range(n_hi - 1):
                arrive(from_h.at[h, j], send_h.at[h, j], recv_h.at[h, j], to_c)
                total = total + from_h[h, j].astype(F32)
            o_ref[pl.ds(h * half, half), :] = total
            continue
        from_c[h, n] = total.astype(from_c.dtype)
        src = from_c.at[h, n]
        if f == 1:
            m = s * n_hi + k
            sends.push(src, from_f.at[h, m], send_f.at[h, m], recv_f.at[h, m], first(h))
        elif s == 1:
            sends.push(src, from_s.at[h, k], send_s.at[h, k], recv_s.at[h, k], second(h))
        else:
            j = back(k, n_hi) - 1
            sends.push(
                src, from_h.at[h, j], send_h.at[h, j], recv_h.at[h, j],
                device(peer(hi, k, n_hi), lo, th, tl),
            )


def scatter_scratch(n_hi, half, width, dtype, depth=4):
    return [
        pltpu.VMEM((depth, half, width), dtype),
        pltpu.VMEM((2, 4 * n_hi, half, width), dtype),
        pltpu.VMEM((2, 2 * n_hi, half, width), dtype),
        pltpu.VMEM((2, n_hi, half, width), dtype),
        pltpu.VMEM((2, n_hi - 1, half, width), dtype),
        DMA((depth,)),
        DMA((2, 4 * n_hi)), DMA((2, 4 * n_hi)),
        DMA((2, 2 * n_hi)), DMA((2, 2 * n_hi)),
        DMA((2, n_hi)), DMA((2, n_hi)),
        DMA((2, n_hi - 1)), DMA((2, n_hi - 1)),
    ]


def scatter_kernel(n_hi, p_ref, o_ref, *bufs):
    greet(n_hi)
    sends = Sends()
    in_turns(scatter_steps(n_hi, sends, p_ref, o_ref, bufs))
    sends.finish()


def scatter_rows(p, n_dp, collective_id):
    width = p.shape[1]
    rows = p.shape[0] // (n_dp * 4)
    n_hi = n_dp // 2
    return pl.pallas_call(
        functools.partial(scatter_kernel, n_hi),
        out_shape=jax.ShapeDtypeStruct((rows, width), F32),
        in_specs=[ANY_SPEC],
        out_specs=VMEM_SPEC,
        scratch_shapes=scatter_scratch(n_hi, rows // 2, width, p.dtype),
        compiler_params=pltpu.CompilerParams(
            collective_id=collective_id, has_side_effects=True, vmem_limit_bytes=60 << 20
        ),
        name="scatter_rows",
    )(p)


def turn_kernel(
    n_hi, p_ref, hidden_ref, g2_ref, gain_ref, grad_ref, sum_ref, dm_ref, total_ref, sp_send, sp_recv, *bufs
):
    hi, lo, th, tl = place()
    greet(n_hi)
    sends = Sends()
    in_turns(scatter_steps(n_hi, sends, p_ref, total_ref, bufs))
    grad = total_ref[...]
    hidden = hidden_ref[...]
    scale = rms_scale(hidden)
    weighted = gain_ref[...] * grad
    sum_ref[...] = jnp.sum(grad * hidden * scale, axis=0, keepdims=True)
    mean = jnp.mean(weighted * hidden, axis=-1, keepdims=True)
    grad = g2_ref[...].astype(F32) + scale * weighted - hidden * (scale * scale * scale) * mean
    grad_ref[...] = grad
    dm_ref[th * 2 + tl] = grad.astype(dm_ref.dtype)
    tensor_spread_start(sends, dm_ref, sp_send, sp_recv)
    tensor_spread_end(sends, dm_ref, sp_send, sp_recv)
    sends.finish()


def turn(p, hidden, g2_piece, gain, n_dp, collective_id):
    rows, width = hidden.shape
    n_hi = n_dp // 2
    return pl.pallas_call(
        functools.partial(turn_kernel, n_hi),
        out_shape=(
            jax.ShapeDtypeStruct((rows, width), F32),
            jax.ShapeDtypeStruct((1, width), F32),
            jax.ShapeDtypeStruct((4, rows, width), p.dtype),
        ),
        in_specs=[ANY_SPEC] + [VMEM_SPEC] * 3,
        out_specs=(VMEM_SPEC,) * 3,
        scratch_shapes=[pltpu.VMEM((rows, width), F32), DMA((3,)), DMA((3,))]
        + scatter_scratch(n_hi, rows // 2, width, p.dtype),
        compiler_params=pltpu.CompilerParams(
            collective_id=collective_id, has_side_effects=True, vmem_limit_bytes=60 << 20
        ),
        name="turn",
    )(p, hidden, g2_piece, gain.reshape(1, width))


def tail_kernel(n_hi, wide, bc_at, n, merged, *refs):
    if merged:
        p_ref, hidden_ref, refs = refs[0], refs[1], refs[2:]
    part_ref, grad_ref, x_ref, gain_ref, small_ref = refs[:5]
    w_refs = refs[5 : 5 + n]
    if merged:
        oy_ref, refs = refs[5 + n], refs[: 5 + n] + refs[6 + n :]
        o_total, y_send, y_recv = refs[-17:-14]
        p_bufs, refs = refs[-14:], refs[:-17]
    ox_ref, os_ref = refs[5 + n : 7 + n]
    ow_refs = refs[7 + n : 7 + 2 * n]
    (got_c, got_y, t_send, t_recv, sp_send, sp_recv,
     small, small_f, small_h, small_t, sm_send, sm_recv, smh_send, smh_recv,
     bc_own, bc_got, bc_send, bc_recv) = refs[7 + 2 * n : 25 + 2 * n]
    rest = refs[25 + 2 * n :]
    bufs = [rest[8 * i : 8 * i + 8] for i in range(n)]
    hi, lo, th, tl = place()
    to_f, to_y, to_c = device(hi, 1 - lo, th, tl), device(hi, lo, 1 - th, tl), device(hi, lo, th, 1 - tl)
    greet(n_hi)
    sends = Sends()
    order = [(k, h) for k in reversed(range(n_hi)) for h in range(2)]
    events = [(w, k, h) for w in range(n) for k, h in order]
    events = [e for e in events if e[1]] + [e for e in events if not e[1]]

    def owner(k, l):
        return peer(hi, k, n_hi) * 2 + l

    if merged:
        others = scatter_steps(n_hi, sends, p_ref, o_total, p_bufs, lo_first=(False, False))
    else:
        others = iter(())
    next(others, None)

    def forward(i):
        if i < len(events):
            w, k, h = events[i]
            stage, from_f, from_h, stage_sem, send_f, recv_f, send_h, recv_h = bufs[w]
            sends.push(
                w_refs[w].at[owner(k, 1 - lo), h], from_f.at[h, k], send_f.at[h, k], recv_f.at[h, k], to_f
            )

    window = 6
    for i in range(window):
        forward(i)
    loads = []
    for w, k, h in events:
        copy = pltpu.make_async_copy(
            w_refs[w].at[owner(k, lo), h], bufs[w][0].at[h, k], bufs[w][3].at[h, k]
        )
        copy.start()
        loads.append(copy)
    tensor_sum_start(sends, part_ref, got_c, t_send, t_recv)
    tensor_sum_middle(sends, part_ref, got_c, got_y, t_send, t_recv)
    grad = tensor_sum_end(part_ref, got_c, got_y, t_send, t_recv)
    x = x_ref[...].astype(F32)
    scale = rms_scale(x)
    weighted = gain_ref[...] * grad
    mean = jnp.mean(weighted * x, axis=-1, keepdims=True)
    ox_ref[th * 2 + tl] = (
        grad_ref[...] + scale * weighted - x * (scale * scale * scale) * mean
    ).astype(ox_ref.dtype)
    tensor_spread_start(sends, ox_ref, sp_send, sp_recv)
    small[...] = small_ref[...]
    small[0:1, :] = jnp.sum(grad * x * scale, axis=0, keepdims=True)
    sends.push(small, small_f, sm_send.at[0], sm_recv.at[0], to_f)

    for i, (w, k, h) in enumerate(events):
        if k == 0:
            break
        stage, from_f, from_h, stage_sem, send_f, recv_f, send_h, recv_h = bufs[w]
        next(others, None)
        loads[i].wait()
        arrive(from_f.at[h, k], send_f.at[h, k], recv_f.at[h, k], to_c)
        forward(i + window)
        from_f[h, k] = (stage[h, k].astype(F32) + from_f[h, k].astype(F32)).astype(from_f.dtype)
        j = back(k, n_hi) - 1
        sends.push(
            from_f.at[h, k], from_h.at[h, j], send_h.at[h, j], recv_h.at[h, j],
            device(peer(hi, k, n_hi), lo, th, tl),
        )
        if i == 0:
            tensor_spread_end(sends, ox_ref, sp_send, sp_recv)
        if i == 1:
            arrive(small_f, sm_send.at[0], sm_recv.at[0], to_c)
            small_h[hi] = small[...] + small_f[...]
            for q in range(1, n_hi):
                sends.push(
                    small_h.at[hi], small_h.at[hi], smh_send.at[q - 1], smh_recv.at[back(q, n_hi) - 1],
                    device(peer(hi, q, n_hi), lo, th, tl),
                )
    if merged:
        in_turns(others)
        oy_ref[th * 2 + tl] = (hidden_ref[...] + o_total[...]).astype(oy_ref.dtype)
        tensor_spread_start(sends, oy_ref, y_send, y_recv)
    for q in range(1, n_hi):
        arrive(small_h.at[peer(hi, q, n_hi)], smh_send.at[q - 1], smh_recv.at[q - 1], to_c)
    total = small_h[0]
    for q in range(1, n_hi):
        total = total + small_h[q]
    os_ref[...] = total
    sends.push(os_ref.at[pl.ds(0, wide)], small_t.at[0], sm_send.at[1], sm_recv.at[1], to_c)
    for i, (w, k, h) in enumerate(events):
        if k:
            continue
        forward(i + window)
        stage, from_f, from_h, stage_sem, send_f, recv_f, send_h, recv_h = bufs[w]
        loads[i].wait()
        arrive(from_f.at[h, 0], send_f.at[h, 0], recv_f.at[h, 0], to_c)
        total = stage[h, 0].astype(F32) + from_f[h, 0].astype(F32)
        for j in range(n_hi - 1):
            arrive(from_h.at[h, j], send_h.at[h, j], recv_h.at[h, j], to_c)
            total = total + from_h[h, j].astype(F32)
        ow_refs[w][h] = total
        if w == 0:
            bc_own[0, h] = total[:, bc_at : bc_at + bc_own.shape[3]].astype(bc_own.dtype)
            if h == 1:
                sends.push(bc_own.at[0], bc_got.at[0], bc_send.at[0], bc_recv.at[0], to_c)
                arrive(small_t.at[0], sm_send.at[1], sm_recv.at[1], to_c)
                small_t[2] = os_ref[pl.ds(0, wide), :] + small_t[0]
                sends.push(small_t.at[2], small_t.at[1], sm_send.at[2], sm_recv.at[2], to_y)
                arrive(bc_got.at[0], bc_send.at[0], bc_recv.at[0], to_c)
                bc_own[1] = (bc_own[0].astype(F32) + bc_got[0].astype(F32)).astype(bc_own.dtype)
                sends.push(bc_own.at[1], bc_got.at[1], bc_send.at[1], bc_recv.at[1], to_y)
    if merged:
        tensor_spread_end(sends, oy_ref, y_send, y_recv)
    arrive(small_t.at[1], sm_send.at[2], sm_recv.at[2], to_c)
    arrive(bc_got.at[1], bc_send.at[1], bc_recv.at[1], to_c)
    for h in range(2):
        ow_refs[0][h, :, bc_at : bc_at + bc_own.shape[3]] = (
            bc_own[1, h].astype(F32) + bc_got[1, h].astype(F32)
        )
    sends.finish()
    os_ref[pl.ds(0, wide), :] = small_t[2] + small_t[1]


def tail(
    weights, part, grad_one, x_piece, gain, small, wide, bc_at, bc_width, n_dp, collective_id,
    out_part=None, hidden=None,
):
    merged = out_part is not None
    rows, width = x_piece.shape
    n_hi = n_dp // 2
    n = len(weights)
    half = weights[0].shape[0] // (2 * n_dp)
    dt = weights[0].dtype
    scratch = TENSOR_SUM_SCRATCH(rows, width, part.dtype) + [
        DMA((3,)), DMA((3,)),
        pltpu.VMEM(small.shape, F32),
        pltpu.VMEM(small.shape, F32),
        pltpu.VMEM((n_hi,) + small.shape, F32),
        pltpu.VMEM((3, wide, small.shape[1]), F32),
        DMA((3,)), DMA((3,)),
        DMA((n_hi - 1,)), DMA((n_hi - 1,)),
        pltpu.VMEM((2, 2, half, bc_width), dt),
        pltpu.VMEM((2, 2, half, bc_width), dt),
        DMA((2,)), DMA((2,)),
    ]
    for w in weights:
        scratch += [
            pltpu.VMEM((2, n_hi, half, w.shape[1]), dt),
            pltpu.VMEM((2, n_hi, half, w.shape[1]), dt),
            pltpu.VMEM((2, n_hi - 1, half, w.shape[1]), dt),
            DMA((2, n_hi)),
            DMA((2, n_hi)), DMA((2, n_hi)),
            DMA((2, n_hi - 1)), DMA((2, n_hi - 1)),
        ]
    if merged:
        scratch += [pltpu.VMEM((rows, width), F32), DMA((3,)), DMA((3,))]
        scratch += scatter_scratch(n_hi, rows // 2, width, out_part.dtype)
    outs = pl.pallas_call(
        functools.partial(tail_kernel, n_hi, wide, bc_at, n, merged),
        out_shape=[jax.ShapeDtypeStruct((4, rows, width), dt)] * merged + [
            jax.ShapeDtypeStruct((4, rows, width), dt),
            jax.ShapeDtypeStruct(small.shape, F32),
        ] + [jax.ShapeDtypeStruct((2, half, w.shape[1]), F32) for w in weights],
        in_specs=[ANY_SPEC, VMEM_SPEC] * merged + [VMEM_SPEC] * 5 + [ANY_SPEC] * n,
        out_specs=[VMEM_SPEC] * (2 + n + merged),
        scratch_shapes=scratch,
        compiler_params=pltpu.CompilerParams(
            collective_id=collective_id, has_side_effects=True, vmem_limit_bytes=60 << 20
        ),
        name="tail",
    )(
        *([out_part, hidden] if merged else []), part.reshape(4, rows, width), grad_one, x_piece, gain.reshape(1, width), small,
        *[w.reshape(n_dp, 2, half, w.shape[1]) for w in weights],
    )
    out = outs[0].reshape(4 * rows, width) if merged else None
    outs = outs[merged:]
    return outs[0], outs[1], [o.reshape(2 * half, o.shape[2]) for o in outs[2:]], out


def dot_mm(a, b):
    return lax.dot_general(a, b, (((1,), (0,)), ((), ())), preferred_element_type=F32)


def dot_nt(a, b):
    return lax.dot_general(a, b, (((1,), (1,)), ((), ())), preferred_element_type=F32)


def dot_tn(a, b):
    return lax.dot_general(a, b, (((0,), (0,)), ((), ())), preferred_element_type=F32)


def experts_kernel(
    n_dp, n_local, cap, chunk, pos_ref, wt_ref, x_ref, g_ref, gu_ref, dn_ref,
    dxn_ref, out_ref, ggu_ref, gdn_ref, pick, xr, q, sw, gu,
):
    step = pl.program_id(0)
    width = x_ref.shape[1]
    hidden = dn_ref.shape[1]
    slots = x_ref.shape[0]
    columns = [pl.ds(c, chunk) for c in range(0, width, chunk)]

    @pl.when(step < n_dp)
    def _():
        s = step
        lane = lax.broadcasted_iota(jnp.int32, (cap, slots), 0)
        for e in range(n_local):
            hit = lane == pos_ref[0, e : e + 1, :]
            pick[s, e * cap : (e + 1) * cap, :] = jnp.where(hit, 1.0, 0.0).astype(BF)
            sw[e, s] = jnp.sum(jnp.where(hit, wt_ref[0, e : e + 1, :], 0.0), axis=1, keepdims=True)
        chosen = pick[s]
        for c in columns:
            rows = dot_mm(chosen, x_ref[:, c]).astype(BF)
            grads = dot_mm(chosen, g_ref[:, c])
            for e in range(n_local):
                xr[e, s, :, c] = rows[e * cap : (e + 1) * cap]
                q[e, s, :, c] = (grads[e * cap : (e + 1) * cap] * sw[e, s]).astype(BF)

    @pl.when(jnp.logical_and(step >= n_dp, step < n_dp + n_local))
    def _():
        e = step - n_dp
        gu[:, :hidden] = gu_ref[pl.ds(0, width, stride=2), :].astype(BF)
        gu[:, hidden:] = gu_ref[pl.ds(1, width, stride=2), :].astype(BF)
        down = dn_ref[0].astype(BF)
        x = xr[e].reshape(n_dp * cap, width)
        qe = q[e].reshape(n_dp * cap, width)
        pre = dot_mm(x, gu[...])
        grad_act = dot_nt(qe, down)
        gate, up = pre[:, :hidden], pre[:, hidden:]
        sig = 1.0 / (1.0 + jnp.exp(-gate))
        act_silu = gate * sig
        slope = sig * (1.0 + gate * (1.0 - sig))
        value = act_silu * up
        act = value.astype(BF)
        scaled = (value * sw[e].reshape(n_dp * cap, 1)).astype(BF)
        grad_pre = jnp.concatenate([grad_act * up * slope, grad_act * act_silu], axis=1).astype(BF)
        ggu = dot_tn(x, grad_pre)
        ggu_ref[pl.ds(0, width, stride=2), :] = ggu[:, :hidden]
        ggu_ref[pl.ds(1, width, stride=2), :] = ggu[:, hidden:]
        gdn_ref[0] = dot_tn(act, qe)
        for c in columns:
            xr[e, :, :, c] = dot_nt(grad_pre, gu[c, :]).astype(BF).reshape(n_dp, cap, chunk)
            q[e, :, :, c] = dot_mm(scaled, down[:, c.start : c.start + chunk]).astype(BF).reshape(n_dp, cap, chunk)

    @pl.when(step >= n_dp + n_local)
    def _():
        s = step - n_dp - n_local
        chosen = pick[s]
        for c in columns:
            dxn_ref[:, c] = dot_tn(chosen, xr[:, s, :, c].reshape(n_local * cap, chunk)).astype(BF)
            out_ref[:, c] = dot_tn(chosen, q[:, s, :, c].reshape(n_local * cap, chunk)).astype(BF)


def experts(position, weights, rows, table, w_gu, w_down, cap):
    n_dp, n_local, slots = position.shape
    width = rows.shape[1]
    hidden = w_down.shape[1]
    chunk = width // 3 if width % 384 == 0 else width
    by_source = lambda i: (jnp.clip(i, 0, n_dp - 1), 0, 0)
    rows_in = lambda i: (jnp.clip(i, 0, n_dp - 1), 0)
    rows_out = lambda i: (jnp.clip(i - n_dp - n_local, 0, n_dp - 1), 0)
    flat = lambda i: (jnp.clip(i - n_dp, 0, n_local - 1), 0)
    deep = lambda i: (jnp.clip(i - n_dp, 0, n_local - 1), 0, 0)
    total = n_dp * n_local * cap
    return pl.pallas_call(
        functools.partial(experts_kernel, n_dp, n_local, cap, chunk),
        grid=(2 * n_dp + n_local,),
        out_shape=(
            jax.ShapeDtypeStruct((n_dp * slots, width), BF),
            jax.ShapeDtypeStruct((n_dp * slots, width), BF),
            jax.ShapeDtypeStruct((n_local * width * 2, hidden), F32),
            jax.ShapeDtypeStruct((n_local, hidden, width), F32),
        ),
        in_specs=[
            pl.BlockSpec((1, n_local, slots), by_source),
            pl.BlockSpec((1, n_local, slots), by_source),
            pl.BlockSpec((slots, width), rows_in),
            pl.BlockSpec((slots, width), rows_in),
            pl.BlockSpec((width * 2, hidden), flat),
            pl.BlockSpec((1, hidden, width), deep),
        ],
        out_specs=(
            pl.BlockSpec((slots, width), rows_out),
            pl.BlockSpec((slots, width), rows_out),
            pl.BlockSpec((width * 2, hidden), flat),
            pl.BlockSpec((1, hidden, width), deep),
        ),
        scratch_shapes=[
            pltpu.VMEM((n_dp, n_local * cap, slots), BF),
            pltpu.VMEM((n_local, n_dp, cap, width), BF),
            pltpu.VMEM((n_local, n_dp, cap, width), BF),
            pltpu.VMEM((n_local, n_dp, cap, 1), F32),
            pltpu.VMEM((width, 2 * hidden), BF),
        ],
        compiler_params=pltpu.CompilerParams(
            dimension_semantics=("arbitrary",), vmem_limit_bytes=60 << 20
        ),
        cost_estimate=pl.CostEstimate(
            flops=8 * total * slots * width + 18 * total * width * hidden,
            bytes_accessed=8 * n_dp * slots * width + 24 * n_local * width * hidden,
            transcendentals=total * hidden,
        ),
        name="experts",
    )(
        position,
        weights,
        rows,
        table,
        w_gu.reshape(n_local * width * 2, hidden),
        w_down,
    )


def conv_pre(pad, values, taps, bias):
    n = values.shape[0]
    pad[pl.ds(8, n), :] = values
    count = taps.shape[0]
    total = bias + taps[count - 1 : count] * values
    for k in range(count - 1):
        total = total + taps[k : k + 1] * pad[pl.ds(8 - (count - 1) + k, n), :]
    return total


def sigmoid(v):
    return 1.0 / (1.0 + jnp.exp(-v))


def dot_exact(a, b):
    return lax.dot_general(
        a, b, (((1,), (0,)), ((), ())), precision=HIGHEST, preferred_element_type=F32
    )


def step_parts(first_ref, at, dtb_ref, alog_ref):
    raw = first_ref[:, at : at + 128] + dtb_ref[...]
    delta = jnp.maximum(raw, 0.0) + jnp.log(1.0 + jnp.exp(-jnp.abs(raw)))
    return raw, delta, -jnp.exp(alog_ref[...])


def lower_mask():
    t = lax.broadcasted_iota(jnp.int32, (BLOCK, BLOCK), 0)
    s = lax.broadcasted_iota(jnp.int32, (BLOCK, BLOCK), 1)
    return t >= s


def by_head(left, a, b):
    return jnp.where(left, a, b)


def mixer_forward_kernel(
    first_ref, cx_ref, cxb_ref, cbc_ref, cbcb_ref, dtb_ref, alog_ref, skip_ref,
    y_ref, gated_ref, square_ref, state_ref, pad,
):
    slots = first_ref.shape[0]
    inner = cx_ref.shape[1]
    n_blocks = slots // BLOCK
    bc_at = 2 * inner
    pad[0:8, :] = jnp.zeros((8, 128), F32)
    mask = lower_mask()
    tri = mask.astype(F32)
    left = lax.broadcasted_iota(jnp.int32, (BLOCK, 128), 1) < 64
    left_row = left[0:1]

    parts = []
    for c in (0, 128):
        pre = conv_pre(pad, first_ref[:, bc_at + c : bc_at + c + 128], cbc_ref[:, c : c + 128], cbcb_ref[:, c : c + 128])
        parts.append((pre * sigmoid(pre)).astype(BF))
    b_rows, c_rows = parts
    raw, delta, rate = step_parts(first_ref, bc_at + 256, dtb_ref, alog_ref)
    blocks = []
    for b in range(n_blocks):
        r = slice(b * BLOCK, (b + 1) * BLOCK)
        d = delta[r]
        cum = dot_exact(tri, rate * d)
        blocks.append((d, cum, d.T, cum.T, dot_nt(c_rows[r], b_rows[r])))
    squares = jnp.zeros((slots, 1), F32)
    for p in range(inner // 128):
        lanes = slice(p * 128, (p + 1) * 128)
        pre = conv_pre(pad, first_ref[:, inner + p * 128 : inner + (p + 1) * 128], cx_ref[:, lanes], cxb_ref[:, lanes])
        heads_in = (pre * sigmoid(pre)).astype(BF)
        state = None
        outs = []
        for b in range(n_blocks):
            d, cum, d_t, cum_t, inter = blocks[b]
            r = slice(b * BLOCK, (b + 1) * BLOCK)
            x = heads_in[r]
            ys = []
            for h in (2 * p, 2 * p + 1):
                decay = jnp.exp(jnp.where(mask, cum[:, h : h + 1] - cum_t[h : h + 1, :], -1e30))
                ys.append(dot_mm((inter * decay * d_t[h : h + 1, :]).astype(BF), x))
            y = by_head(left, ys[0], ys[1]) + skip_ref[:, lanes] * x.astype(F32)
            cum_p = by_head(left, cum[:, 2 * p : 2 * p + 1], cum[:, 2 * p + 1 : 2 * p + 2])
            d_p = by_head(left, d[:, 2 * p : 2 * p + 1], d[:, 2 * p + 1 : 2 * p + 2])
            if state is not None:
                state_ref[p, b - 1] = state
                y = y + jnp.exp(cum_p) * dot_mm(c_rows[r], state.astype(BF))
            if b + 1 < n_blocks:
                end = cum_p[BLOCK - 1 :]
                z_rows = x.astype(F32) * d_p * jnp.exp(end - cum_p)
                fresh = dot_tn(b_rows[r], z_rows.astype(BF))
                state = fresh if state is None else jnp.exp(end) * state + fresh
            outs.append(y)
        y = jnp.concatenate(outs, axis=0)
        z = first_ref[:, lanes]
        gated = y * (z * sigmoid(z))
        y_ref[:, lanes] = y
        gated_ref[:, lanes] = gated
        squares = squares + jnp.sum(gated * gated, axis=1, keepdims=True)
    square_ref[...] = squares


def mixer_backward_kernel(
    full_inner, first_ref, y_ref, gated_ref, dyn_ref, scale_ref, product_ref, gain_ref, state_ref,
    cx_ref, cxb_ref, cbc_ref, cbcb_ref, dtb_ref, alog_ref, skip_ref,
    grad_ref, small_ref, pad, after, cols, sums_t,
):
    slots = first_ref.shape[0]
    inner = cx_ref.shape[1]
    n_blocks = slots // BLOCK
    bc_at = 2 * inner
    taps = cx_ref.shape[0]
    pad[0:8, :] = jnp.zeros((8, 128), F32)
    after[pl.ds(slots, 8), :] = jnp.zeros((8, 128), F32)
    small_ref[...] = jnp.zeros_like(small_ref)
    cols[...] = jnp.zeros_like(cols)
    sums_t[...] = jnp.zeros_like(sums_t)
    mask = lower_mask()
    tri = mask.astype(F32)
    lane = lax.broadcasted_iota(jnp.int32, (BLOCK, 128), 1)
    left = lane < 64

    parts, bc_pre = [], []
    for c in (0, 128):
        pre = conv_pre(pad, first_ref[:, bc_at + c : bc_at + c + 128], cbc_ref[:, c : c + 128], cbcb_ref[:, c : c + 128])
        bc_pre.append(pre)
        parts.append((pre * sigmoid(pre)).astype(BF))
    b_rows, c_rows = parts
    raw, delta, rate = step_parts(first_ref, bc_at + 256, dtb_ref, alog_ref)
    scale = scale_ref[...]
    cube = scale * scale * scale * product_ref[...] * (1.0 / full_inner)
    blocks = []
    for b in range(n_blocks):
        r = slice(b * BLOCK, (b + 1) * BLOCK)
        d = delta[r]
        cum = dot_exact(tri, rate * d)
        blocks.append((d, cum, d.T, cum.T, dot_nt(c_rows[r], b_rows[r])))
    grad_inter = [jnp.zeros((BLOCK, BLOCK), F32) for _ in range(n_blocks)]
    grad_b = [jnp.zeros((BLOCK, 128), F32) for _ in range(n_blocks)]
    grad_c = [jnp.zeros((BLOCK, 128), F32) for _ in range(n_blocks)]

    def conv_back(grad_out, pre, values, taps_v, row, bias_row, lanes, at):
        sig = sigmoid(pre)
        a = grad_out * (sig * (1.0 + pre * (1.0 - sig)))
        after[pl.ds(0, slots), :] = a
        pad[pl.ds(8, slots), :] = values
        total = taps_v[taps - 1 : taps] * a
        small_ref[row + taps - 1 : row + taps, lanes] = jnp.sum(a * values, axis=0, keepdims=True)
        for k in range(taps - 1):
            total = total + taps_v[k : k + 1] * after[pl.ds(taps - 1 - k, slots), :]
            small_ref[row + k : row + k + 1, lanes] = jnp.sum(
                a * pad[pl.ds(8 - (taps - 1) + k, slots), :], axis=0, keepdims=True
            )
        small_ref[bias_row : bias_row + 1, lanes] = jnp.sum(a, axis=0, keepdims=True)
        grad_ref[:, at : at + 128] = total.astype(grad_ref.dtype)

    for p in range(inner // 128):
        lanes = slice(p * 128, (p + 1) * 128)
        values = first_ref[:, inner + p * 128 : inner + (p + 1) * 128]
        pre = conv_pre(pad, values, cx_ref[:, lanes], cxb_ref[:, lanes])
        heads_in = (pre * sigmoid(pre)).astype(BF)
        z = first_ref[:, lanes]
        sig = sigmoid(z)
        grad_gated = scale * gain_ref[:, lanes] * dyn_ref[:, lanes] - gated_ref[:, lanes] * cube
        grad_y = grad_gated * (z * sig)
        grad_ref[:, lanes] = (
            grad_gated * y_ref[:, lanes] * (sig * (1.0 + z * (1.0 - sig)))
        ).astype(grad_ref.dtype)
        skip = skip_ref[:, lanes]
        x_f = heads_in.astype(F32)
        small_ref[5:6, lanes] = jnp.sum(grad_y * x_f, axis=0, keepdims=True)
        grad_y_low = grad_y.astype(BF)
        grad_x = [None] * n_blocks
        grad_state = None
        for b in reversed(range(n_blocks)):
            d, cum, d_t, cum_t, inter = blocks[b]
            r = slice(b * BLOCK, (b + 1) * BLOCK)
            x, xf, dy, dyl = heads_in[r], x_f[r], grad_y[r], grad_y_low[r]
            cum_p = by_head(left, cum[:, 2 * p : 2 * p + 1], cum[:, 2 * p + 1 : 2 * p + 2])
            d_p = by_head(left, d[:, 2 * p : 2 * p + 1], d[:, 2 * p + 1 : 2 * p + 2])
            dxs = []
            for i, h in enumerate((2 * p, 2 * p + 1)):
                own = left if i == 0 else jnp.logical_not(left)
                q = dot_nt(jnp.where(own, dy, 0.0).astype(BF), x)
                decay = jnp.exp(jnp.where(mask, cum[:, h : h + 1] - cum_t[h : h + 1, :], -1e30))
                scaled = decay * d_t[h : h + 1, :]
                dxs.append(dot_tn((inter * scaled).astype(BF), dyl))
                grad_inter[b] = grad_inter[b] + scaled * q
                moved = inter * decay * q
                sums_t[b, h : h + 1, :] = jnp.sum(moved, axis=0, keepdims=True)
                rows = jnp.sum(moved * d_t[h : h + 1, :], axis=1, keepdims=True)
                cols[0, r, :] += jnp.where(lane == h, rows, 0.0)
            dx = by_head(left, dxs[0], dxs[1]) + skip * dy
            extra = None
            if b > 0:
                state = state_ref[p, b - 1]
                grown = dy * jnp.exp(cum_p)
                grown_low = grown.astype(BF)
                extra = grown * dot_mm(c_rows[r], state.astype(BF))
                grad_c[b] = grad_c[b] + dot_nt(grown_low, state.astype(BF))
                back_state = dot_tn(c_rows[r], grown_low)
            end = cum_p[BLOCK - 1 :]
            end_sum = None
            if grad_state is not None:
                weight = jnp.exp(end - cum_p)
                low_state = grad_state.astype(BF)
                dz_rows = dot_mm(b_rows[r], low_state)
                grad_b[b] = grad_b[b] + dot_nt((xf * d_p * weight).astype(BF), low_state)
                dx = dx + dz_rows * d_p * weight
                direct = dz_rows * xf * weight
                through = direct * d_p
                end_sum = jnp.sum(through, axis=0, keepdims=True)
                if b > 0:
                    end_sum = end_sum + jnp.exp(end) * jnp.sum(grad_state * state, axis=0, keepdims=True)
                extra = -through if extra is None else extra - through
            for i, h in enumerate((2 * p, 2 * p + 1)):
                own = left if i == 0 else jnp.logical_not(left)
                if extra is not None:
                    column = jnp.sum(jnp.where(own, extra, 0.0), axis=1, keepdims=True)
                    cols[0, r, :] += jnp.where(lane == h, column, 0.0)
                if end_sum is not None:
                    column = jnp.sum(jnp.where(own, direct, 0.0), axis=1, keepdims=True)
                    cols[1, r, :] += jnp.where(lane == h, column, 0.0)
                    last = jnp.sum(jnp.where(own[0:1], end_sum, 0.0), axis=1, keepdims=True)
                    at = slice((b + 1) * BLOCK - 1, (b + 1) * BLOCK)
                    cols[0, at, :] += jnp.where(lane[0:1] == h, last, 0.0)
            if b > 0:
                grad_state = back_state if grad_state is None else jnp.exp(end) * grad_state + back_state
            grad_x[b] = dx
        conv_back(
            jnp.concatenate(grad_x, axis=0), pre, values, cx_ref[:, lanes], 0, 4, lanes, inner + p * 128
        )
    upper = jnp.logical_not(mask).astype(F32) + (
        lax.broadcasted_iota(jnp.int32, (BLOCK, BLOCK), 0)
        == lax.broadcasted_iota(jnp.int32, (BLOCK, BLOCK), 1)
    ).astype(F32)
    ddts, logs = [], jnp.zeros((1, 128), F32)
    for b in range(n_blocks):
        d, cum, d_t, cum_t, inter = blocks[b]
        r = slice(b * BLOCK, (b + 1) * BLOCK)
        low = grad_inter[b].astype(BF)
        grad_c[b] = grad_c[b] + dot_mm(low, b_rows[r])
        grad_b[b] = grad_b[b] + dot_tn(low, c_rows[r])
        direct = sums_t[b].T
        reach = dot_exact(upper, cols[0, r, :] - direct * d)
        logs = logs + jnp.sum(rate * d * reach, axis=0, keepdims=True)
        ddts.append((direct + cols[1, r, :] + rate * reach) * sigmoid(raw[r]))
    ddt = jnp.concatenate(ddts, axis=0)
    grad_ref[:, bc_at + 256 : bc_at + 384] = ddt.astype(grad_ref.dtype)
    small_ref[11:12, 0:128] = logs
    small_ref[12:13, 0:128] = jnp.sum(ddt, axis=0, keepdims=True)
    for i, (c, grads) in enumerate(((0, grad_b), (128, grad_c))):
        conv_back(
            jnp.concatenate(grads, axis=0), bc_pre[i], first_ref[:, bc_at + c : bc_at + c + 128],
            cbc_ref[:, c : c + 128], 6, 10, slice(c, c + 128), bc_at + c,
        )


def pad_lanes(v):
    return jnp.pad(v, (0, -v.shape[0] % 128)).reshape(1, -1)


def mixer_params(conv_x, conv_x_bias, conv_bc, conv_bc_bias, dt_bias, a_log, d_skip):
    size = conv_x.shape[1] // d_skip.shape[0]
    return (
        conv_x, conv_x_bias.reshape(1, -1), conv_bc, conv_bc_bias.reshape(1, -1),
        pad_lanes(dt_bias), pad_lanes(a_log), jnp.repeat(d_skip, size).reshape(1, -1),
    )


def mixer_forward(firsts, params):
    slots = firsts.shape[0]
    inner = params[0].shape[1]
    pairs, n_blocks = inner // 128, slots // BLOCK
    shape = lambda *s: jax.ShapeDtypeStruct(s, F32)
    return pl.pallas_call(
        mixer_forward_kernel,
        out_shape=(
            shape(slots, inner), shape(slots, inner), shape(slots, 1),
            shape(pairs, n_blocks - 1, 128, 128),
        ),
        in_specs=[VMEM_SPEC] * 8,
        out_specs=(VMEM_SPEC,) * 4,
        scratch_shapes=[pltpu.VMEM((slots + 8, 128), F32)],
        compiler_params=pltpu.CompilerParams(vmem_limit_bytes=48 << 20),
        cost_estimate=pl.CostEstimate(
            flops=8 * slots * BLOCK * inner, bytes_accessed=24 * slots * inner,
            transcendentals=slots * BLOCK * inner // 32,
        ),
        name="mixer_forward",
    )(firsts, *params)


def mixer_backward(full_inner, firsts, y, gated, dyn, scale, product, gain, state, params):
    slots, width = firsts.shape
    inner = params[0].shape[1]
    return pl.pallas_call(
        functools.partial(mixer_backward_kernel, full_inner),
        out_shape=(
            jax.ShapeDtypeStruct((slots, width), BF),
            jax.ShapeDtypeStruct((16, inner), F32),
        ),
        in_specs=[VMEM_SPEC] * 15,
        out_specs=(VMEM_SPEC,) * 2,
        scratch_shapes=[
            pltpu.VMEM((slots + 8, 128), F32),
            pltpu.VMEM((slots + 8, 128), F32),
            pltpu.VMEM((2, slots, 128), F32),
            pltpu.VMEM((slots // BLOCK, 128, BLOCK), F32),
        ],
        compiler_params=pltpu.CompilerParams(vmem_limit_bytes=56 << 20),
        cost_estimate=pl.CostEstimate(
            flops=24 * slots * BLOCK * inner, bytes_accessed=40 * slots * inner,
            transcendentals=slots * BLOCK * inner // 32,
        ),
        name="mixer_backward",
    )(firsts, y, gated, dyn, scale, product, gain.reshape(1, -1), state, *params)


def local(
    x_in,
    lengths,
    routes,
    route_w,
    ln1_gain,
    w_zx,
    w_bc,
    w_dt,
    conv_x,
    conv_x_bias,
    conv_bc,
    conv_bc_bias,
    dt_bias,
    a_log,
    d_skip,
    gnorm_gain,
    w_out,
    ln2_gain,
    w_shared_gu,
    w_shared_down,
    w_exp_gu,
    w_exp_down,
    cotangent,
):
    slots, width = x_in.shape
    n_dp = lax.axis_size("dp")
    n_t = lax.axis_size("tensor")
    my_t = lax.axis_index("tensor")
    my_dp = lax.axis_index("dp")
    piece = slots // n_t
    n_local = w_exp_gu.shape[0]
    n_experts = n_dp * n_local
    cap = slots * routes.shape[1] * 4 // (3 * n_experts)
    if cap > slots:
        cap = slots
    heads = dt_bias.shape[0]
    inner = conv_x.shape[1]
    head_size = inner // heads
    state = conv_bc.shape[1] // 2
    full_inner = inner * n_t
    rows = w_zx.shape[0]
    n_sh = w_shared_gu.shape[2]

    dt_at = 2 * inner + 2 * state
    first_width = dt_at + heads + -(dt_at + heads) % 128
    first = jnp.concatenate(
        [
            w_zx.reshape(rows, 2 * inner),
            w_bc,
            w_dt,
            jnp.zeros((rows, first_width - dt_at - heads), F32),
        ],
        axis=1,
    ).astype(BF)
    shared = jnp.concatenate([w_shared_gu.reshape(rows, 2 * n_sh), w_shared_down], axis=1)

    live = (jnp.arange(slots, dtype=jnp.int32) < lengths[0]).astype(F32)
    g2 = cotangent.astype(F32) * live[:, None]
    g2_low = g2.astype(BF)
    expert_range = jnp.arange(n_experts, dtype=jnp.int32)
    chosen = routes[:, :, None] == expert_range[None, None, :]
    weights = jnp.sum(jnp.where(chosen, route_w[:, :, None], 0.0), axis=1)
    high = weights.astype(BF)
    low = (weights - high.astype(F32)).astype(BF)
    table = jnp.concatenate([g2_low, high, low], axis=1)
    table = lax.dynamic_slice_in_dim(table, my_t * piece, piece, axis=0)
    g2_piece = lax.dynamic_slice_in_dim(g2_low, my_t * piece, piece, axis=0)

    first, proj_out, table = start([first, w_out.astype(BF)], table, n_dp, 1)
    shared, first = lax.optimization_barrier((shared.astype(BF), first))
    shared = lax.all_gather(shared, "dp", axis=0, tiled=True)
    shared_gu = shared[:, : 2 * n_sh]
    shared_down = shared[:, 2 * n_sh :]

    x_float = x_in.astype(F32)
    scale_one = rms_scale(x_float)
    normed_one = (x_float * scale_one * ln1_gain).astype(BF)
    firsts = dotf("td,df->tf", normed_one, first)
    params = mixer_params(conv_x, conv_x_bias, conv_bc, conv_bc_bias, dt_bias, a_log, d_skip)
    y, gated_mix, squares, states = mixer_forward(firsts, params)
    squares = lax.psum(squares.reshape(slots), "tensor")[:, None]
    scale_mix = lax.rsqrt(squares / full_inner + EPSILON)
    normed_mix = (gated_mix * scale_mix * gnorm_gain).astype(BF)
    mixer_part = dotf("tc,dc->td", normed_mix, proj_out).astype(BF)
    x_piece = lax.dynamic_slice_in_dim(x_in, my_t * piece, piece, axis=0)
    all_rows, hidden_one = middle(mixer_part, x_piece, ln2_gain, n_dp, 2)
    mine = lax.dynamic_slice_in_dim(all_rows, my_dp * slots, slots, axis=0)

    shared_pre = dotf("td,df->tf", mine, shared_gu)
    s_gate, s_up = shared_pre[:, :n_sh], shared_pre[:, n_sh:]
    shared_silu, shared_slope = silu_parts(s_gate)
    shared_act = (shared_silu * s_up).astype(BF)
    grad_shared_act = dotf("td,df->tf", g2_low, shared_down)
    grad_shared_pre = jnp.concatenate(
        [grad_shared_act * s_up * shared_slope, grad_shared_act * shared_silu], axis=1
    ).astype(BF)
    grad_normed_shared = dotf("tf,df->td", grad_shared_pre, shared_gu)
    shared_part = dotf("tf,df->td", shared_act, shared_down)

    high = lax.dynamic_slice_in_dim(table, width + my_dp * n_local, n_local, axis=1)
    low = lax.dynamic_slice_in_dim(table, width + n_experts + my_dp * n_local, n_local, axis=1)
    weights = (high.astype(F32) + low.astype(F32)).reshape(n_dp, slots, n_local)
    member = (weights > 0.0).astype(BF)
    before = (
        jnp.arange(slots)[:, None] > jnp.arange(slots)[None, :]
    ).astype(BF)
    position = dotf("ut,ste->seu", before, member).astype(jnp.int32)
    weights = weights.transpose(0, 2, 1)
    position = jnp.where(weights > 0.0, position, -1)

    dxn_part, out_part, grad_exp_gu, grad_exp_down = experts(
        position, weights, all_rows, table, w_exp_gu, w_exp_down, cap
    )
    grad_exp_gu = grad_exp_gu.reshape(w_exp_gu.shape)

    def add_own(total, own):
        at = my_dp * slots
        own = own + lax.dynamic_slice_in_dim(total, at, slots, axis=0).astype(F32)
        return lax.dynamic_update_slice_in_dim(total, own.astype(BF), at, axis=0)

    dxn_part = add_own(dxn_part, grad_normed_shared)
    out_part = add_own(out_part, shared_part)
    grad_shared_down = dotf("td,tf->df", g2_low, shared_act)
    grad_shared_gu = dotf("td,tf->df", mine, grad_shared_pre)
    grad_shared_w = jnp.concatenate([grad_shared_gu, grad_shared_down], axis=1).astype(BF)
    dxn_part, grad_shared_w = lax.optimization_barrier((dxn_part, grad_shared_w))
    grad_one, sum_ln2, dm = turn(
        dxn_part, hidden_one, g2_piece, ln2_gain, n_dp, 3
    )
    dm = dm.reshape(slots, width)

    grad_shared_w = lax.psum_scatter(grad_shared_w, "dp", scatter_dimension=0, tiled=True)
    grad_out_w = dotf("td,tc->dc", dm, normed_mix).astype(BF)
    grad_normed_mix = dotf("td,dc->tc", dm, proj_out)
    weighted_mix = gnorm_gain * grad_normed_mix
    grad_gnorm = jnp.sum(grad_normed_mix * gated_mix * scale_mix, axis=0)
    product_sum = lax.optimization_barrier(jnp.sum(weighted_mix * gated_mix, axis=-1))
    product_sum = lax.optimization_barrier(lax.psum(product_sum, "tensor")).reshape(slots, 1)
    grad_first, mixer_sums = mixer_backward(
        full_inner, firsts, y, gated_mix, grad_normed_mix, scale_mix, product_sum, gnorm_gain,
        states, params,
    )
    taps = conv_x.shape[0]
    grad_conv_x, grad_conv_x_bias = mixer_sums[:taps], mixer_sums[4]
    grad_d_skip = jnp.sum(mixer_sums[5].reshape(heads, head_size), axis=1)
    grad_conv_bc, grad_conv_bc_bias = mixer_sums[6 : 6 + taps, : 2 * state], mixer_sums[10, : 2 * state]
    grad_a_log, grad_dt_bias = mixer_sums[11, :heads], mixer_sums[12, :heads]
    grad_input_part = dotf("tf,df->td", grad_first, first).astype(BF)
    grad_first_w = dotf("td,tf->df", normed_one, grad_first).astype(BF)
    def lanes(*vectors):
        vector = jnp.concatenate([v.reshape(-1) for v in vectors])
        return jnp.pad(vector, (0, -vector.shape[0] % (8 * width))).reshape(-1, width)

    wide = lanes(jnp.zeros((width,), F32), sum_ln2, grad_conv_bc, grad_conv_bc_bias)
    n_wide = wide.shape[0]
    narrow = lanes(
        grad_conv_x, grad_conv_x_bias, grad_gnorm, grad_dt_bias, grad_a_log, grad_d_skip
    )
    grad_first_w, grad_shared_w = lax.optimization_barrier((grad_first_w, grad_shared_w))
    merged = n_dp <= 8
    grad_x, sums, (first_f, grad_out_w), layer_out = tail(
        [grad_first_w, grad_out_w],
        grad_input_part,
        grad_one,
        x_piece,
        ln1_gain,
        jnp.concatenate([wide, narrow], axis=0),
        n_wide,
        2 * inner,
        2 * state,
        n_dp,
        5,
        *((out_part, hidden_one) if merged else ()),
    )
    if not merged:
        ffn_out = scatter_rows(out_part, n_dp, 4)
        layer_out = lax.all_gather((hidden_one + ffn_out).astype(BF), "tensor", axis=0, tiled=True)
    grad_x = grad_x.reshape(slots, width).astype(F32)
    wide, narrow = sums[:n_wide].reshape(-1), sums[n_wide:].reshape(-1)
    at = [0]

    def take(vector, *shape):
        size = 1
        for s in shape:
            size *= s
        part = lax.slice_in_dim(vector, at[0], at[0] + size).reshape(shape)
        at[0] += size
        return part

    o_ln1 = take(wide, width)
    o_ln2 = take(wide, width)
    o_conv_bc = take(wide, taps, 2 * state)
    o_conv_bc_bias = take(wide, 2 * state)
    at[0] = 0
    o_conv_x = take(narrow, taps, inner)
    o_conv_x_bias = take(narrow, inner)
    o_gnorm = take(narrow, inner)
    o_dt_bias = take(narrow, heads)
    o_a_log = take(narrow, heads)
    o_d_skip = take(narrow, heads)
    shared_f = grad_shared_w.astype(F32)
    return (
        layer_out,
        grad_x,
        o_ln1,
        first_f[:, : 2 * inner].reshape(rows, 2, inner),
        first_f[:, 2 * inner : dt_at],
        first_f[:, dt_at : dt_at + heads],
        o_conv_x,
        o_conv_x_bias,
        o_conv_bc,
        o_conv_bc_bias,
        o_dt_bias,
        o_a_log,
        o_d_skip,
        o_gnorm,
        grad_out_w,
        o_ln2,
        shared_f[:, : 2 * n_sh].reshape(rows, 2, n_sh),
        shared_f[:, 2 * n_sh :],
        grad_exp_gu,
        grad_exp_down,
    )


def solution(mesh):
    return jax.shard_map(
        local,
        mesh=mesh,
        in_specs=(
            P("dp", None),
            P("dp"),
            P("dp", None),
            P("dp", None),
            P(),
            P("dp", None, "tensor"),
            P("dp", None),
            P("dp", "tensor"),
            P(None, "tensor"),
            P("tensor"),
            P(),
            P(),
            P("tensor"),
            P("tensor"),
            P("tensor"),
            P("tensor"),
            P("dp", "tensor"),
            P(),
            P("dp", None, "tensor"),
            P("dp", "tensor"),
            P("dp", None, None, "tensor"),
            P("dp", "tensor", None),
            P("dp", None),
        ),
        out_specs=(
            P("dp", None),
            P("dp", None),
            P(),
            P("dp", None, "tensor"),
            P("dp", None),
            P("dp", "tensor"),
            P(None, "tensor"),
            P("tensor"),
            P(),
            P(),
            P("tensor"),
            P("tensor"),
            P("tensor"),
            P("tensor"),
            P("dp", "tensor"),
            P(),
            P("dp", None, "tensor"),
            P("dp", "tensor"),
            P("dp", None, None, "tensor"),
            P("dp", "tensor", None),
        ),
        check_vma=False,
    )
```

```python
import functools

import jax
import jax.numpy as jnp
from jax import lax
from jax.experimental import pallas as pl
from jax.experimental.pallas import tpu as pltpu
from jax.sharding import PartitionSpec as P

BLOCK = 256


EPSILON = 1e-05
HIGHEST = lax.Precision.HIGHEST
BF = jnp.bfloat16
F32 = jnp.float32


def rms_scale(values):
    return lax.rsqrt(jnp.mean(values * values, axis=-1, keepdims=True) + EPSILON)


def silu_parts(values):
    sigmoid_val = jax.nn.sigmoid(values)
    return (values * sigmoid_val, sigmoid_val * (1.0 + values * (1.0 - sigmoid_val)))


def dotf(spec, a, b):
    return jnp.einsum(spec, a, b, preferred_element_type=F32)


MESH = pl.DeviceIdType.MESH
DMA = pltpu.SemaphoreType.DMA
VMEM_SPEC = pl.BlockSpec(memory_space=pltpu.VMEM)
ANY_SPEC = pl.BlockSpec(memory_space=pl.ANY)


def place():
    d = lax.axis_index("dp")
    t = lax.axis_index("tensor")
    return d // 2, d % 2, t // 2, t % 2


def device(hi, lo, th, tl):
    return (hi * 2 + lo, th * 2 + tl)


def peer(hi, k, n_hi):
    if n_hi & (n_hi - 1):
        return lax.rem(hi + k, n_hi)
    other, bit = hi, 1
    while bit <= k:
        if k & bit:
            other = other + bit * (1 - 2 * lax.rem(hi // bit, 2))
        bit *= 2
    return other


def back(k, n_hi):
    return n_hi - k if n_hi & (n_hi - 1) else k


def greet(n_hi, tensor=True):
    hi, lo, th, tl = place()
    barrier = pltpu.get_barrier_semaphore()
    others = [device(peer(hi, k, n_hi), lo, th, tl) for k in range(1, n_hi)]
    others += [device(hi, 1 - lo, th, tl)]
    if tensor:
        others += [device(hi, lo, 1 - th, tl), device(hi, lo, th, 1 - tl)]
    for other in others:
        pl.semaphore_signal(barrier, inc=1, device_id=other, device_id_type=MESH)
    pl.semaphore_wait(barrier, len(others))


def remote(src, dst, ssem, rsem, to):
    return pltpu.make_async_remote_copy(
        src_ref=src, dst_ref=dst, send_sem=ssem, recv_sem=rsem, device_id=to, device_id_type=MESH
    )


class Sends:
    def __init__(self):
        self.copies = []

    def push(self, src, dst, ssem, rsem, to):
        copy = remote(src, dst, ssem, rsem, to)
        copy.start()
        self.copies.append(copy)

    def finish(self):
        for copy in self.copies:
            copy.wait_send()


def arrive(dst, ssem, rsem, to):
    remote(dst, dst, ssem, rsem, to).wait_recv()


TENSOR_SUM_SCRATCH = lambda rows, width, dtype: [
    pltpu.VMEM((2, rows, width), dtype),
    pltpu.VMEM((rows, width), dtype),
    DMA((3,)),
    DMA((3,)),
]


def tensor_sum_start(sends, part_ref, got_c, ssem, rsem):
    hi, lo, th, tl = place()
    to_c = device(hi, lo, th, 1 - tl)
    for j, y in enumerate((1 - th, th)):
        sends.push(part_ref.at[y * 2 + 1 - tl], got_c.at[j], ssem.at[j], rsem.at[j], to_c)


def tensor_sum_middle(sends, part_ref, got_c, got_y, ssem, rsem):
    hi, lo, th, tl = place()
    arrive(got_c.at[0], ssem.at[0], rsem.at[0], device(hi, lo, th, 1 - tl))
    total = part_ref[(1 - th) * 2 + tl].astype(F32) + got_c[0].astype(F32)
    got_c[0] = total.astype(got_c.dtype)
    sends.push(got_c.at[0], got_y, ssem.at[2], rsem.at[2], device(hi, lo, 1 - th, tl))


def tensor_sum_end(part_ref, got_c, got_y, ssem, rsem):
    hi, lo, th, tl = place()
    arrive(got_c.at[1], ssem.at[1], rsem.at[1], device(hi, lo, th, 1 - tl))
    total = part_ref[th * 2 + tl].astype(F32) + got_c[1].astype(F32)
    arrive(got_y, ssem.at[2], rsem.at[2], device(hi, lo, 1 - th, tl))
    return total + got_y[...].astype(F32)


def tensor_spread_start(sends, o_ref, ssem, rsem):
    hi, lo, th, tl = place()
    own = o_ref.at[th * 2 + tl]
    sends.push(own, own, ssem.at[0], rsem.at[0], device(hi, lo, 1 - th, tl))
    sends.push(own, own, ssem.at[1], rsem.at[1], device(hi, lo, th, 1 - tl))


def tensor_spread_end(sends, o_ref, ssem, rsem):
    hi, lo, th, tl = place()
    other = o_ref.at[(1 - th) * 2 + tl]
    to_c = device(hi, lo, th, 1 - tl)
    arrive(other, ssem.at[0], rsem.at[0], device(hi, lo, 1 - th, tl))
    sends.push(other, other, ssem.at[2], rsem.at[2], to_c)
    arrive(o_ref.at[th * 2 + 1 - tl], ssem.at[1], rsem.at[1], to_c)
    arrive(o_ref.at[(1 - th) * 2 + 1 - tl], ssem.at[2], rsem.at[2], to_c)


def gather_steps(n_hi, x_ref, o_ref, own_sem, send_sem, recv_sem, lo_first=(True, False)):
    hi, lo, th, tl = place()
    rows = x_ref.shape[0]
    half = rows // 2
    own_block = (hi * 2 + lo) * 4 + th * 2 + tl
    own = pltpu.make_async_copy(x_ref, o_ref.at[pl.ds(own_block * rows, rows)], own_sem)
    own.start()
    sends = Sends()

    def slot(k, f, s, c):
        return ((c * 2 + s) * 2 + f) * n_hi + k

    def where(h, k, f, s, c):
        kk = peer(hi, k, n_hi)
        l = 1 - lo if (f if lo_first[h] else s) else lo
        y = 1 - th if (s if lo_first[h] else f) else th
        z = 1 - tl if c else tl
        return ((kk * 2 + l) * 4 + y * 2 + z) * rows + h * half

    def push(h, k, f, s, c, step):
        at = where(h, k, f, s, c)
        if k == 0 and not (f or s or c):
            src = x_ref.at[pl.ds(h * half, half)]
        else:
            src = o_ref.at[pl.ds(at, half)]
        if step == "c":
            to, r = device(hi, lo, th, 1 - tl), slot(k, f, s, 1)
        elif step == "s":
            to = device(hi, lo, 1 - th, tl) if lo_first[h] else device(hi, 1 - lo, th, tl)
            r = slot(k, f, 1, 0)
        elif step == "f":
            to = device(hi, 1 - lo, th, tl) if lo_first[h] else device(hi, lo, 1 - th, tl)
            r = slot(k, 1, 0, 0)
        else:
            to, r = device(peer(hi, step, n_hi), lo, th, tl), slot(back(step, n_hi), 0, 0, 0)
        sends.push(src, o_ref.at[pl.ds(at, half)], send_sem.at[h, r], recv_sem.at[h, r], to)

    def got(h, k, f, s, c):
        r = slot(k, f, s, c)
        arrive(
            o_ref.at[pl.ds(where(h, k, f, s, c), half)],
            send_sem.at[h, r], recv_sem.at[h, r], device(hi, lo, th, 1 - tl),
        )

    for k in range(n_hi):
        for h in range(2):
            if k:
                got(h, k, 0, 0, 0)
            if k < n_hi - 1:
                push(h, 0, 0, 0, 0, k + 1)
            for step in ("f", "s", "c"):
                push(h, k, 0, 0, 0, step)
        yield
        for h in range(2):
            got(h, k, 1, 0, 0)
            for step in ("s", "c"):
                push(h, k, 1, 0, 0, step)
        yield
    for k in range(n_hi):
        for f in range(2):
            for h in range(2):
                got(h, k, f, 1, 0)
                push(h, k, f, 1, 0, "c")
        yield
    for k in range(n_hi):
        for f in range(2):
            for s in range(2):
                for h in range(2):
                    got(h, k, f, s, 1)
    own.wait()
    sends.finish()


def in_turns(*streams):
    live = list(streams)
    while live:
        for stream in list(live):
            if next(stream, True) is True:
                live.remove(stream)


def middle_kernel(
    n_hi, part_ref, x_ref, gain_ref, o_ref, hidden_ref,
    normed, got_c, got_y, t_send, t_recv, *sems,
):
    greet(n_hi)
    sends = Sends()
    tensor_sum_start(sends, part_ref, got_c, t_send, t_recv)
    tensor_sum_middle(sends, part_ref, got_c, got_y, t_send, t_recv)
    hidden = x_ref[...].astype(F32) + tensor_sum_end(part_ref, got_c, got_y, t_send, t_recv)
    hidden_ref[...] = hidden
    normed[...] = (hidden * rms_scale(hidden) * gain_ref[...]).astype(normed.dtype)
    in_turns(gather_steps(n_hi, normed, o_ref, *sems))
    sends.finish()


def middle(part, x_piece, gain, n_dp, collective_id):
    rows, width = x_piece.shape
    n_hi = n_dp // 2
    return pl.pallas_call(
        functools.partial(middle_kernel, n_hi),
        out_shape=(
            jax.ShapeDtypeStruct((n_dp * 4 * rows, width), part.dtype),
            jax.ShapeDtypeStruct((rows, width), F32),
        ),
        in_specs=[VMEM_SPEC] * 3,
        out_specs=(ANY_SPEC, VMEM_SPEC),
        scratch_shapes=[pltpu.VMEM((rows, width), part.dtype)]
        + TENSOR_SUM_SCRATCH(rows, width, part.dtype)
        + [DMA, DMA((2, 8 * n_hi)), DMA((2, 8 * n_hi))],
        compiler_params=pltpu.CompilerParams(collective_id=collective_id, has_side_effects=True),
        name="middle",
    )(part.reshape(4, rows, width), x_piece, gain.reshape(1, width))


def weight_steps(n_hi, w_ref, o_ref, own_sem, send_b, recv_b, send_a, recv_a, send_f, recv_f):
    hi, lo, th, tl = place()
    to_f = device(hi, 1 - lo, th, tl)
    above = device(lax.rem(hi + 1, n_hi), lo, th, tl)
    below = device(lax.rem(hi + n_hi - 1, n_hi), lo, th, tl)
    sends = []

    def push(cond, src, at, h, ssem, rsem, to):
        copy = remote(src, o_ref.at[at, h], ssem, rsem, to)
        sends.append((cond, copy))
        if cond is None:
            copy.start()
        else:
            pl.when(cond)(copy.start)

    def block(j, l):
        return lax.rem(hi + j + n_hi, n_hi) * 2 + l

    for h in range(2):
        at = block(0, lo)
        push(hi < n_hi - 1, w_ref.at[h], at, h, send_b.at[h, 0], recv_b.at[h, 0], above)
        push(hi > 0, w_ref.at[h], at, h, send_a.at[h, 0], recv_a.at[h, 0], below)
        push(None, w_ref.at[h], at, h, send_f.at[h, 0], recv_f.at[h, 0], to_f)
    own = pltpu.make_async_copy(w_ref, o_ref.at[block(0, lo)], own_sem)
    own.start()
    yield
    for j in range(1, n_hi):
        for h in range(2):
            for down in (0, 1):
                valid = hi + j < n_hi if down else hi - j >= 0
                at = block(j if down else -j, lo)
                view = o_ref.at[at, h]
                sem = (send_a if down else send_b).at[h, j - 1], (recv_a if down else recv_b).at[h, j - 1]
                pl.when(valid)(remote(view, view, *sem, to_f).wait_recv)
                if j < n_hi - 1:
                    on = jnp.logical_and(valid, hi > 0 if down else hi < n_hi - 1)
                    push(
                        on, view, at, h, (send_a if down else send_b).at[h, j],
                        (recv_a if down else recv_b).at[h, j], below if down else above,
                    )
                f = 1 + down * (n_hi - 1) + j - 1
                push(valid, view, at, h, send_f.at[h, f], recv_f.at[h, f], to_f)
        yield
    for h in range(2):
        view = o_ref.at[block(0, 1 - lo), h]
        arrive(view, send_f.at[h, 0], recv_f.at[h, 0], to_f)
    for j in range(1, n_hi):
        for h in range(2):
            for down in (0, 1):
                valid = hi + j < n_hi if down else hi - j >= 0
                view = o_ref.at[block(j if down else -j, 1 - lo), h]
                f = 1 + down * (n_hi - 1) + j - 1
                pl.when(valid)(remote(view, view, send_f.at[h, f], recv_f.at[h, f], to_f).wait_recv)
    own.wait()
    for cond, copy in sends:
        if cond is None:
            copy.wait_send()
        else:
            pl.when(cond)(copy.wait_send)


def start_kernel(n_hi, n, *refs):
    ins, outs, sems = refs[: n + 1], refs[n + 1 : 2 * n + 2], refs[2 * n + 2 :]
    greet(n_hi)
    streams = [
        weight_steps(n_hi, ins[i], outs[i], *sems[7 * i : 7 * i + 7]) for i in range(n)
    ] + [gather_steps(n_hi, ins[n], outs[n], *sems[7 * n :], lo_first=(True, False))]
    in_turns(*streams)


def start(weights, table, n_dp, collective_id):
    n_hi = n_dp // 2
    n = len(weights)
    half = weights[0].shape[0] // 2
    outs = pl.pallas_call(
        functools.partial(start_kernel, n_hi, n),
        out_shape=[jax.ShapeDtypeStruct((n_dp, 2, half, w.shape[1]), w.dtype) for w in weights]
        + [jax.ShapeDtypeStruct((n_dp * 4 * table.shape[0], table.shape[1]), table.dtype)],
        in_specs=[ANY_SPEC] * (n + 1),
        out_specs=[ANY_SPEC] * (n + 1),
        scratch_shapes=[
            DMA,
            DMA((2, n_hi - 1)), DMA((2, n_hi - 1)),
            DMA((2, n_hi - 1)), DMA((2, n_hi - 1)),
            DMA((2, 2 * n_hi - 1)), DMA((2, 2 * n_hi - 1)),
        ] * n + [DMA, DMA((2, 8 * n_hi)), DMA((2, 8 * n_hi))],
        compiler_params=pltpu.CompilerParams(collective_id=collective_id, has_side_effects=True),
        name="start",
    )(*[w.reshape(2, half, w.shape[1]) for w in weights], table)
    return [o.reshape(n_dp * 2 * half, o.shape[3]) for o in outs[:n]] + [outs[n]]


def scatter_steps(n_hi, sends, p_ref, o_ref, bufs, lo_first=(False, True)):
    (stage, from_c, from_f, from_s, from_h,
     stage_sem, send_c, recv_c, send_f, recv_f, send_s, recv_s, send_h, recv_h) = bufs
    depth = stage.shape[0]
    hi, lo, th, tl = place()
    to_c = device(hi, lo, th, 1 - tl)
    rows = o_ref.shape[0]
    half = rows // 2

    def where(h, k, f, s, c):
        kk = peer(hi, k, n_hi)
        l = 1 - lo if (f if lo_first[h] else s) else lo
        y = 1 - th if (s if lo_first[h] else f) else th
        z = 1 - tl if c else tl
        return ((kk * 2 + l) * 4 + y * 2 + z) * rows + h * half

    ks = list(range(1, n_hi)) + [0]
    order = []
    for i in range(n_hi + 2):
        for lag, groups in ((0, ((1, 1), (1, 0))), (1, ((0, 1),)), (2, ((0, 0),))):
            if 0 <= i - lag < n_hi:
                order += [(f, s, ks[i - lag], h) for f, s in groups for h in range(2)]

    def slot(f, s, k):
        return (f * 2 + s) * n_hi + k

    def first(h):
        return device(hi, 1 - lo, th, tl) if lo_first[h] else device(hi, lo, 1 - th, tl)

    def second(h):
        return device(hi, lo, 1 - th, tl) if lo_first[h] else device(hi, 1 - lo, th, tl)

    for f, s, k, h in order:
        n = slot(f, s, k)
        sends.push(
            p_ref.at[pl.ds(where(h, k, f, s, 1), half)], from_c.at[h, n], send_c.at[h, n],
            recv_c.at[h, n], to_c,
        )

    def load(i):
        f, s, k, h = order[i]
        return pltpu.make_async_copy(
            p_ref.at[pl.ds(where(h, k, f, s, 0), half)], stage.at[i % depth], stage_sem.at[i % depth]
        )

    for i in range(depth - 1):
        load(i).start()
    for i, (f, s, k, h) in enumerate(order):
        if i + depth - 1 < len(order):
            load(i + depth - 1).start()
        if i % 4 == 0:
            yield
        load(i).wait()
        n = slot(f, s, k)
        arrive(from_c.at[h, n], send_c.at[h, n], recv_c.at[h, n], to_c)
        total = stage[i % depth].astype(F32) + from_c[h, n].astype(F32)
        if f == 0:
            m = s * n_hi + k
            arrive(from_f.at[h, m], send_f.at[h, m], recv_f.at[h, m], to_c)
            total = total + from_f[h, m].astype(F32)
        if f == 0 and s == 0:
            arrive(from_s.at[h, k], send_s.at[h, k], recv_s.at[h, k], to_c)
            total = total + from_s[h, k].astype(F32)
        if f == 0 and s == 0 and k == 0:
            for j in range(n_hi - 1):
                arrive(from_h.at[h, j], send_h.at[h, j], recv_h.at[h, j], to_c)
                total = total + from_h[h, j].astype(F32)
            o_ref[pl.ds(h * half, half), :] = total
            continue
        from_c[h, n] = total.astype(from_c.dtype)
        src = from_c.at[h, n]
        if f == 1:
            m = s * n_hi + k
            sends.push(src, from_f.at[h, m], send_f.at[h, m], recv_f.at[h, m], first(h))
        elif s == 1:
            sends.push(src, from_s.at[h, k], send_s.at[h, k], recv_s.at[h, k], second(h))
        else:
            j = back(k, n_hi) - 1
            sends.push(
                src, from_h.at[h, j], send_h.at[h, j], recv_h.at[h, j],
                device(peer(hi, k, n_hi), lo, th, tl),
            )


def scatter_scratch(n_hi, half, width, dtype, depth=4):
    return [
        pltpu.VMEM((depth, half, width), dtype),
        pltpu.VMEM((2, 4 * n_hi, half, width), dtype),
        pltpu.VMEM((2, 2 * n_hi, half, width), dtype),
        pltpu.VMEM((2, n_hi, half, width), dtype),
        pltpu.VMEM((2, n_hi - 1, half, width), dtype),
        DMA((depth,)),
        DMA((2, 4 * n_hi)), DMA((2, 4 * n_hi)),
        DMA((2, 2 * n_hi)), DMA((2, 2 * n_hi)),
        DMA((2, n_hi)), DMA((2, n_hi)),
        DMA((2, n_hi - 1)), DMA((2, n_hi - 1)),
    ]


def scatter_kernel(n_hi, p_ref, o_ref, *bufs):
    greet(n_hi)
    sends = Sends()
    in_turns(scatter_steps(n_hi, sends, p_ref, o_ref, bufs))
    sends.finish()


def scatter_rows(p, n_dp, collective_id):
    width = p.shape[1]
    rows = p.shape[0] // (n_dp * 4)
    n_hi = n_dp // 2
    return pl.pallas_call(
        functools.partial(scatter_kernel, n_hi),
        out_shape=jax.ShapeDtypeStruct((rows, width), F32),
        in_specs=[ANY_SPEC],
        out_specs=VMEM_SPEC,
        scratch_shapes=scatter_scratch(n_hi, rows // 2, width, p.dtype),
        compiler_params=pltpu.CompilerParams(
            collective_id=collective_id, has_side_effects=True, vmem_limit_bytes=60 << 20
        ),
        name="scatter_rows",
    )(p)


def turn_kernel(
    n_hi, p_ref, hidden_ref, g2_ref, gain_ref, grad_ref, sum_ref, dm_ref, total_ref, sp_send, sp_recv, *bufs
):
    hi, lo, th, tl = place()
    greet(n_hi)
    sends = Sends()
    in_turns(scatter_steps(n_hi, sends, p_ref, total_ref, bufs))
    grad = total_ref[...]
    hidden = hidden_ref[...]
    scale = rms_scale(hidden)
    weighted = gain_ref[...] * grad
    sum_ref[...] = jnp.sum(grad * hidden * scale, axis=0, keepdims=True)
    mean = jnp.mean(weighted * hidden, axis=-1, keepdims=True)
    grad = g2_ref[...].astype(F32) + scale * weighted - hidden * (scale * scale * scale) * mean
    grad_ref[...] = grad
    dm_ref[th * 2 + tl] = grad.astype(dm_ref.dtype)
    tensor_spread_start(sends, dm_ref, sp_send, sp_recv)
    tensor_spread_end(sends, dm_ref, sp_send, sp_recv)
    sends.finish()


def turn(p, hidden, g2_piece, gain, n_dp, collective_id):
    rows, width = hidden.shape
    n_hi = n_dp // 2
    return pl.pallas_call(
        functools.partial(turn_kernel, n_hi),
        out_shape=(
            jax.ShapeDtypeStruct((rows, width), F32),
            jax.ShapeDtypeStruct((1, width), F32),
            jax.ShapeDtypeStruct((4, rows, width), p.dtype),
        ),
        in_specs=[ANY_SPEC] + [VMEM_SPEC] * 3,
        out_specs=(VMEM_SPEC,) * 3,
        scratch_shapes=[pltpu.VMEM((rows, width), F32), DMA((3,)), DMA((3,))]
        + scatter_scratch(n_hi, rows // 2, width, p.dtype),
        compiler_params=pltpu.CompilerParams(
            collective_id=collective_id, has_side_effects=True, vmem_limit_bytes=60 << 20
        ),
        name="turn",
    )(p, hidden, g2_piece, gain.reshape(1, width))


def tail_kernel(n_hi, wide, bc_at, n, merged, *refs):
    if merged:
        p_ref, hidden_ref, refs = refs[0], refs[1], refs[2:]
    part_ref, grad_ref, x_ref, gain_ref, small_ref = refs[:5]
    w_refs = refs[5 : 5 + n]
    if merged:
        oy_ref, refs = refs[5 + n], refs[: 5 + n] + refs[6 + n :]
        o_total, y_send, y_recv = refs[-17:-14]
        p_bufs, refs = refs[-14:], refs[:-17]
    ox_ref, os_ref = refs[5 + n : 7 + n]
    ow_refs = refs[7 + n : 7 + 2 * n]
    (got_c, got_y, t_send, t_recv, sp_send, sp_recv,
     small, small_f, small_h, small_t, sm_send, sm_recv, smh_send, smh_recv,
     bc_own, bc_got, bc_send, bc_recv) = refs[7 + 2 * n : 25 + 2 * n]
    rest = refs[25 + 2 * n :]
    bufs = [rest[8 * i : 8 * i + 8] for i in range(n)]
    hi, lo, th, tl = place()
    to_f, to_y, to_c = device(hi, 1 - lo, th, tl), device(hi, lo, 1 - th, tl), device(hi, lo, th, 1 - tl)
    greet(n_hi)
    sends = Sends()
    order = [(k, h) for k in reversed(range(n_hi)) for h in range(2)]
    events = [(w, k, h) for w in range(n) for k, h in order]
    events = [e for e in events if e[1]] + [e for e in events if not e[1]]

    def owner(k, l):
        return peer(hi, k, n_hi) * 2 + l

    if merged:
        others = scatter_steps(n_hi, sends, p_ref, o_total, p_bufs, lo_first=(False, True))
    else:
        others = iter(())
    next(others, None)

    def forward(i):
        if i < len(events):
            w, k, h = events[i]
            stage, from_f, from_h, stage_sem, send_f, recv_f, send_h, recv_h = bufs[w]
            sends.push(
                w_refs[w].at[owner(k, 1 - lo), h], from_f.at[h, k], send_f.at[h, k], recv_f.at[h, k], to_f
            )

    window = 6
    for i in range(window):
        forward(i)
    loads = []
    for w, k, h in events:
        copy = pltpu.make_async_copy(
            w_refs[w].at[owner(k, lo), h], bufs[w][0].at[h, k], bufs[w][3].at[h, k]
        )
        copy.start()
        loads.append(copy)
    tensor_sum_start(sends, part_ref, got_c, t_send, t_recv)
    tensor_sum_middle(sends, part_ref, got_c, got_y, t_send, t_recv)
    grad = tensor_sum_end(part_ref, got_c, got_y, t_send, t_recv)
    x = x_ref[...].astype(F32)
    scale = rms_scale(x)
    weighted = gain_ref[...] * grad
    mean = jnp.mean(weighted * x, axis=-1, keepdims=True)
    ox_ref[th * 2 + tl] = (
        grad_ref[...] + scale * weighted - x * (scale * scale * scale) * mean
    ).astype(ox_ref.dtype)
    tensor_spread_start(sends, ox_ref, sp_send, sp_recv)
    small[...] = small_ref[...]
    small[0:1, :] = jnp.sum(grad * x * scale, axis=0, keepdims=True)
    sends.push(small, small_f, sm_send.at[0], sm_recv.at[0], to_f)

    for i, (w, k, h) in enumerate(events):
        if k == 0:
            break
        stage, from_f, from_h, stage_sem, send_f, recv_f, send_h, recv_h = bufs[w]
        next(others, None)
        loads[i].wait()
        arrive(from_f.at[h, k], send_f.at[h, k], recv_f.at[h, k], to_c)
        forward(i + window)
        from_f[h, k] = (stage[h, k].astype(F32) + from_f[h, k].astype(F32)).astype(from_f.dtype)
        j = back(k, n_hi) - 1
        sends.push(
            from_f.at[h, k], from_h.at[h, j], send_h.at[h, j], recv_h.at[h, j],
            device(peer(hi, k, n_hi), lo, th, tl),
        )
        if i == 0:
            tensor_spread_end(sends, ox_ref, sp_send, sp_recv)
        if i == 1:
            arrive(small_f, sm_send.at[0], sm_recv.at[0], to_c)
            small_h[hi] = small[...] + small_f[...]
            for q in range(1, n_hi):
                sends.push(
                    small_h.at[hi], small_h.at[hi], smh_send.at[q - 1], smh_recv.at[back(q, n_hi) - 1],
                    device(peer(hi, q, n_hi), lo, th, tl),
                )
    if merged:
        in_turns(others)
        oy_ref[th * 2 + tl] = (hidden_ref[...] + o_total[...]).astype(oy_ref.dtype)
        tensor_spread_start(sends, oy_ref, y_send, y_recv)
    for q in range(1, n_hi):
        arrive(small_h.at[peer(hi, q, n_hi)], smh_send.at[q - 1], smh_recv.at[q - 1], to_c)
    total = small_h[0]
    for q in range(1, n_hi):
        total = total + small_h[q]
    os_ref[...] = total
    sends.push(os_ref.at[pl.ds(0, wide)], small_t.at[0], sm_send.at[1], sm_recv.at[1], to_c)
    for i, (w, k, h) in enumerate(events):
        if k:
            continue
        forward(i + window)
        stage, from_f, from_h, stage_sem, send_f, recv_f, send_h, recv_h = bufs[w]
        loads[i].wait()
        arrive(from_f.at[h, 0], send_f.at[h, 0], recv_f.at[h, 0], to_c)
        total = stage[h, 0].astype(F32) + from_f[h, 0].astype(F32)
        for j in range(n_hi - 1):
            arrive(from_h.at[h, j], send_h.at[h, j], recv_h.at[h, j], to_c)
            total = total + from_h[h, j].astype(F32)
        ow_refs[w][h] = total
        if w == 0:
            bc_own[0, h] = total[:, bc_at : bc_at + bc_own.shape[3]].astype(bc_own.dtype)
            if h == 1:
                sends.push(bc_own.at[0], bc_got.at[0], bc_send.at[0], bc_recv.at[0], to_c)
                arrive(small_t.at[0], sm_send.at[1], sm_recv.at[1], to_c)
                small_t[2] = os_ref[pl.ds(0, wide), :] + small_t[0]
                sends.push(small_t.at[2], small_t.at[1], sm_send.at[2], sm_recv.at[2], to_y)
                arrive(bc_got.at[0], bc_send.at[0], bc_recv.at[0], to_c)
                bc_own[1] = (bc_own[0].astype(F32) + bc_got[0].astype(F32)).astype(bc_own.dtype)
                sends.push(bc_own.at[1], bc_got.at[1], bc_send.at[1], bc_recv.at[1], to_y)
    if merged:
        tensor_spread_end(sends, oy_ref, y_send, y_recv)
    arrive(small_t.at[1], sm_send.at[2], sm_recv.at[2], to_c)
    arrive(bc_got.at[1], bc_send.at[1], bc_recv.at[1], to_c)
    for h in range(2):
        ow_refs[0][h, :, bc_at : bc_at + bc_own.shape[3]] = (
            bc_own[1, h].astype(F32) + bc_got[1, h].astype(F32)
        )
    sends.finish()
    os_ref[pl.ds(0, wide), :] = small_t[2] + small_t[1]


def tail(
    weights, part, grad_one, x_piece, gain, small, wide, bc_at, bc_width, n_dp, collective_id,
    out_part=None, hidden=None,
):
    merged = out_part is not None
    rows, width = x_piece.shape
    n_hi = n_dp // 2
    n = len(weights)
    half = weights[0].shape[0] // (2 * n_dp)
    dt = weights[0].dtype
    scratch = TENSOR_SUM_SCRATCH(rows, width, part.dtype) + [
        DMA((3,)), DMA((3,)),
        pltpu.VMEM(small.shape, F32),
        pltpu.VMEM(small.shape, F32),
        pltpu.VMEM((n_hi,) + small.shape, F32),
        pltpu.VMEM((3, wide, small.shape[1]), F32),
        DMA((3,)), DMA((3,)),
        DMA((n_hi - 1,)), DMA((n_hi - 1,)),
        pltpu.VMEM((2, 2, half, bc_width), dt),
        pltpu.VMEM((2, 2, half, bc_width), dt),
        DMA((2,)), DMA((2,)),
    ]
    for w in weights:
        scratch += [
            pltpu.VMEM((2, n_hi, half, w.shape[1]), dt),
            pltpu.VMEM((2, n_hi, half, w.shape[1]), dt),
            pltpu.VMEM((2, n_hi - 1, half, w.shape[1]), dt),
            DMA((2, n_hi)),
            DMA((2, n_hi)), DMA((2, n_hi)),
            DMA((2, n_hi - 1)), DMA((2, n_hi - 1)),
        ]
    if merged:
        scratch += [pltpu.VMEM((rows, width), F32), DMA((3,)), DMA((3,))]
        scratch += scatter_scratch(n_hi, rows // 2, width, out_part.dtype)
    outs = pl.pallas_call(
        functools.partial(tail_kernel, n_hi, wide, bc_at, n, merged),
        out_shape=[jax.ShapeDtypeStruct((4, rows, width), dt)] * merged + [
            jax.ShapeDtypeStruct((4, rows, width), dt),
            jax.ShapeDtypeStruct(small.shape, F32),
        ] + [jax.ShapeDtypeStruct((2, half, w.shape[1]), F32) for w in weights],
        in_specs=[ANY_SPEC, VMEM_SPEC] * merged + [VMEM_SPEC] * 5 + [ANY_SPEC] * n,
        out_specs=[VMEM_SPEC] * (2 + n + merged),
        scratch_shapes=scratch,
        compiler_params=pltpu.CompilerParams(
            collective_id=collective_id, has_side_effects=True, vmem_limit_bytes=60 << 20
        ),
        name="tail",
    )(
        *([out_part, hidden] if merged else []), part.reshape(4, rows, width), grad_one, x_piece, gain.reshape(1, width), small,
        *[w.reshape(n_dp, 2, half, w.shape[1]) for w in weights],
    )
    out = outs[0].reshape(4 * rows, width) if merged else None
    outs = outs[merged:]
    return outs[0], outs[1], [o.reshape(2 * half, o.shape[2]) for o in outs[2:]], out


def dot_mm(a, b):
    return lax.dot_general(a, b, (((1,), (0,)), ((), ())), preferred_element_type=F32)


def dot_nt(a, b):
    return lax.dot_general(a, b, (((1,), (1,)), ((), ())), preferred_element_type=F32)


def dot_tn(a, b):
    return lax.dot_general(a, b, (((0,), (0,)), ((), ())), preferred_element_type=F32)


def experts_kernel(
    n_dp, n_local, cap, chunk, pos_ref, wt_ref, x_ref, g_ref, gu_ref, dn_ref,
    dxn_ref, out_ref, ggu_ref, gdn_ref, pick, xr, q, sw, gu,
):
    step = pl.program_id(0)
    width = x_ref.shape[1]
    hidden = dn_ref.shape[1]
    slots = x_ref.shape[0]
    columns = [pl.ds(c, chunk) for c in range(0, width, chunk)]

    @pl.when(step < n_dp)
    def _():
        s = step
        lane = lax.broadcasted_iota(jnp.int32, (cap, slots), 0)
        for e in range(n_local):
            hit = lane == pos_ref[0, e : e + 1, :]
            pick[s, e * cap : (e + 1) * cap, :] = jnp.where(hit, 1.0, 0.0).astype(BF)
            sw[e, s] = jnp.sum(jnp.where(hit, wt_ref[0, e : e + 1, :], 0.0), axis=1, keepdims=True)
        chosen = pick[s]
        for c in columns:
            rows = dot_mm(chosen, x_ref[:, c]).astype(BF)
            grads = dot_mm(chosen, g_ref[:, c])
            for e in range(n_local):
                xr[e, s, :, c] = rows[e * cap : (e + 1) * cap]
                q[e, s, :, c] = (grads[e * cap : (e + 1) * cap] * sw[e, s]).astype(BF)

    @pl.when(jnp.logical_and(step >= n_dp, step < n_dp + n_local))
    def _():
        e = step - n_dp
        gu[:, :hidden] = gu_ref[pl.ds(0, width, stride=2), :].astype(BF)
        gu[:, hidden:] = gu_ref[pl.ds(1, width, stride=2), :].astype(BF)
        down = dn_ref[0].astype(BF)
        x = xr[e].reshape(n_dp * cap, width)
        qe = q[e].reshape(n_dp * cap, width)
        pre = dot_mm(x, gu[...])
        grad_act = dot_nt(qe, down)
        gate, up = pre[:, :hidden], pre[:, hidden:]
        sig = 1.0 / (1.0 + jnp.exp(-gate))
        act_silu = gate * sig
        slope = sig * (1.0 + gate * (1.0 - sig))
        value = act_silu * up
        act = value.astype(BF)
        scaled = (value * sw[e].reshape(n_dp * cap, 1)).astype(BF)
        grad_pre = jnp.concatenate([grad_act * up * slope, grad_act * act_silu], axis=1).astype(BF)
        ggu = dot_tn(x, grad_pre)
        ggu_ref[pl.ds(0, width, stride=2), :] = ggu[:, :hidden]
        ggu_ref[pl.ds(1, width, stride=2), :] = ggu[:, hidden:]
        gdn_ref[0] = dot_tn(act, qe)
        for c in columns:
            xr[e, :, :, c] = dot_nt(grad_pre, gu[c, :]).astype(BF).reshape(n_dp, cap, chunk)
            q[e, :, :, c] = dot_mm(scaled, down[:, c.start : c.start + chunk]).astype(BF).reshape(n_dp, cap, chunk)

    @pl.when(step >= n_dp + n_local)
    def _():
        s = step - n_dp - n_local
        chosen = pick[s]
        for c in columns:
            dxn_ref[:, c] = dot_tn(chosen, xr[:, s, :, c].reshape(n_local * cap, chunk)).astype(BF)
            out_ref[:, c] = dot_tn(chosen, q[:, s, :, c].reshape(n_local * cap, chunk)).astype(BF)


def experts(position, weights, rows, table, w_gu, w_down, cap):
    n_dp, n_local, slots = position.shape
    width = rows.shape[1]
    hidden = w_down.shape[1]
    chunk = width // 3 if width % 384 == 0 else width
    by_source = lambda i: (jnp.clip(i, 0, n_dp - 1), 0, 0)
    rows_in = lambda i: (jnp.clip(i, 0, n_dp - 1), 0)
    rows_out = lambda i: (jnp.clip(i - n_dp - n_local, 0, n_dp - 1), 0)
    flat = lambda i: (jnp.clip(i - n_dp, 0, n_local - 1), 0)
    deep = lambda i: (jnp.clip(i - n_dp, 0, n_local - 1), 0, 0)
    total = n_dp * n_local * cap
    return pl.pallas_call(
        functools.partial(experts_kernel, n_dp, n_local, cap, chunk),
        grid=(2 * n_dp + n_local,),
        out_shape=(
            jax.ShapeDtypeStruct((n_dp * slots, width), BF),
            jax.ShapeDtypeStruct((n_dp * slots, width), BF),
            jax.ShapeDtypeStruct((n_local * width * 2, hidden), F32),
            jax.ShapeDtypeStruct((n_local, hidden, width), F32),
        ),
        in_specs=[
            pl.BlockSpec((1, n_local, slots), by_source),
            pl.BlockSpec((1, n_local, slots), by_source),
            pl.BlockSpec((slots, width), rows_in),
            pl.BlockSpec((slots, width), rows_in),
            pl.BlockSpec((width * 2, hidden), flat),
            pl.BlockSpec((1, hidden, width), deep),
        ],
        out_specs=(
            pl.BlockSpec((slots, width), rows_out),
            pl.BlockSpec((slots, width), rows_out),
            pl.BlockSpec((width * 2, hidden), flat),
            pl.BlockSpec((1, hidden, width), deep),
        ),
        scratch_shapes=[
            pltpu.VMEM((n_dp, n_local * cap, slots), BF),
            pltpu.VMEM((n_local, n_dp, cap, width), BF),
            pltpu.VMEM((n_local, n_dp, cap, width), BF),
            pltpu.VMEM((n_local, n_dp, cap, 1), F32),
            pltpu.VMEM((width, 2 * hidden), BF),
        ],
        compiler_params=pltpu.CompilerParams(
            dimension_semantics=("arbitrary",), vmem_limit_bytes=60 << 20
        ),
        cost_estimate=pl.CostEstimate(
            flops=8 * total * slots * width + 18 * total * width * hidden,
            bytes_accessed=8 * n_dp * slots * width + 24 * n_local * width * hidden,
            transcendentals=total * hidden,
        ),
        name="experts",
    )(
        position,
        weights,
        rows,
        table,
        w_gu.reshape(n_local * width * 2, hidden),
        w_down,
    )


def conv_pre(pad, values, taps, bias):
    n = values.shape[0]
    pad[pl.ds(8, n), :] = values
    count = taps.shape[0]
    total = bias + taps[count - 1 : count] * values
    for k in range(count - 1):
        total = total + taps[k : k + 1] * pad[pl.ds(8 - (count - 1) + k, n), :]
    return total


def sigmoid(v):
    return 1.0 / (1.0 + jnp.exp(-v))


def dot_exact(a, b):
    return lax.dot_general(
        a, b, (((1,), (0,)), ((), ())), precision=HIGHEST, preferred_element_type=F32
    )


def step_parts(first_ref, at, dtb_ref, alog_ref):
    raw = first_ref[:, at : at + 128] + dtb_ref[...]
    delta = jnp.maximum(raw, 0.0) + jnp.log(1.0 + jnp.exp(-jnp.abs(raw)))
    return raw, delta, -jnp.exp(alog_ref[...])


def lower_mask():
    t = lax.broadcasted_iota(jnp.int32, (BLOCK, BLOCK), 0)
    s = lax.broadcasted_iota(jnp.int32, (BLOCK, BLOCK), 1)
    return t >= s


def by_head(left, a, b):
    return jnp.where(left, a, b)


def mixer_forward_kernel(
    first_ref, cx_ref, cxb_ref, cbc_ref, cbcb_ref, dtb_ref, alog_ref, skip_ref,
    y_ref, gated_ref, square_ref, state_ref, pad,
):
    slots = first_ref.shape[0]
    inner = cx_ref.shape[1]
    n_blocks = slots // BLOCK
    bc_at = 2 * inner
    pad[0:8, :] = jnp.zeros((8, 128), F32)
    mask = lower_mask()
    tri = mask.astype(F32)
    left = lax.broadcasted_iota(jnp.int32, (BLOCK, 128), 1) < 64
    left_row = left[0:1]

    parts = []
    for c in (0, 128):
        pre = conv_pre(pad, first_ref[:, bc_at + c : bc_at + c + 128], cbc_ref[:, c : c + 128], cbcb_ref[:, c : c + 128])
        parts.append((pre * sigmoid(pre)).astype(BF))
    b_rows, c_rows = parts
    raw, delta, rate = step_parts(first_ref, bc_at + 256, dtb_ref, alog_ref)
    blocks = []
    for b in range(n_blocks):
        r = slice(b * BLOCK, (b + 1) * BLOCK)
        d = delta[r]
        cum = dot_exact(tri, rate * d)
        blocks.append((d, cum, d.T, cum.T, dot_nt(c_rows[r], b_rows[r])))
    squares = jnp.zeros((slots, 1), F32)
    for p in range(inner // 128):
        lanes = slice(p * 128, (p + 1) * 128)
        pre = conv_pre(pad, first_ref[:, inner + p * 128 : inner + (p + 1) * 128], cx_ref[:, lanes], cxb_ref[:, lanes])
        heads_in = (pre * sigmoid(pre)).astype(BF)
        state = None
        outs = []
        for b in range(n_blocks):
            d, cum, d_t, cum_t, inter = blocks[b]
            r = slice(b * BLOCK, (b + 1) * BLOCK)
            x = heads_in[r]
            ys = []
            for h in (2 * p, 2 * p + 1):
                decay = jnp.exp(jnp.where(mask, cum[:, h : h + 1] - cum_t[h : h + 1, :], -1e30))
                ys.append(dot_mm((inter * decay * d_t[h : h + 1, :]).astype(BF), x))
            y = by_head(left, ys[0], ys[1]) + skip_ref[:, lanes] * x.astype(F32)
            cum_p = by_head(left, cum[:, 2 * p : 2 * p + 1], cum[:, 2 * p + 1 : 2 * p + 2])
            d_p = by_head(left, d[:, 2 * p : 2 * p + 1], d[:, 2 * p + 1 : 2 * p + 2])
            if state is not None:
                state_ref[p, b - 1] = state
                y = y + jnp.exp(cum_p) * dot_mm(c_rows[r], state.astype(BF))
            if b + 1 < n_blocks:
                end = cum_p[BLOCK - 1 :]
                z_rows = x.astype(F32) * d_p * jnp.exp(end - cum_p)
                fresh = dot_tn(b_rows[r], z_rows.astype(BF))
                state = fresh if state is None else jnp.exp(end) * state + fresh
            outs.append(y)
        y = jnp.concatenate(outs, axis=0)
        z = first_ref[:, lanes]
        gated = y * (z * sigmoid(z))
        y_ref[:, lanes] = y
        gated_ref[:, lanes] = gated
        squares = squares + jnp.sum(gated * gated, axis=1, keepdims=True)
    square_ref[...] = squares


def mixer_backward_kernel(
    full_inner, first_ref, y_ref, gated_ref, dyn_ref, scale_ref, product_ref, gain_ref, state_ref,
    cx_ref, cxb_ref, cbc_ref, cbcb_ref, dtb_ref, alog_ref, skip_ref,
    grad_ref, small_ref, pad, after, cols, sums_t,
):
    slots = first_ref.shape[0]
    inner = cx_ref.shape[1]
    n_blocks = slots // BLOCK
    bc_at = 2 * inner
    taps = cx_ref.shape[0]
    pad[0:8, :] = jnp.zeros((8, 128), F32)
    after[pl.ds(slots, 8), :] = jnp.zeros((8, 128), F32)
    small_ref[...] = jnp.zeros_like(small_ref)
    cols[...] = jnp.zeros_like(cols)
    sums_t[...] = jnp.zeros_like(sums_t)
    mask = lower_mask()
    tri = mask.astype(F32)
    lane = lax.broadcasted_iota(jnp.int32, (BLOCK, 128), 1)
    left = lane < 64

    parts, bc_pre = [], []
    for c in (0, 128):
        pre = conv_pre(pad, first_ref[:, bc_at + c : bc_at + c + 128], cbc_ref[:, c : c + 128], cbcb_ref[:, c : c + 128])
        bc_pre.append(pre)
        parts.append((pre * sigmoid(pre)).astype(BF))
    b_rows, c_rows = parts
    raw, delta, rate = step_parts(first_ref, bc_at + 256, dtb_ref, alog_ref)
    scale = scale_ref[...]
    cube = scale * scale * scale * product_ref[...] * (1.0 / full_inner)
    blocks = []
    for b in range(n_blocks):
        r = slice(b * BLOCK, (b + 1) * BLOCK)
        d = delta[r]
        cum = dot_exact(tri, rate * d)
        blocks.append((d, cum, d.T, cum.T, dot_nt(c_rows[r], b_rows[r])))
    grad_inter = [jnp.zeros((BLOCK, BLOCK), F32) for _ in range(n_blocks)]
    grad_b = [jnp.zeros((BLOCK, 128), F32) for _ in range(n_blocks)]
    grad_c = [jnp.zeros((BLOCK, 128), F32) for _ in range(n_blocks)]

    def conv_back(grad_out, pre, values, taps_v, row, bias_row, lanes, at):
        sig = sigmoid(pre)
        a = grad_out * (sig * (1.0 + pre * (1.0 - sig)))
        after[pl.ds(0, slots), :] = a
        pad[pl.ds(8, slots), :] = values
        total = taps_v[taps - 1 : taps] * a
        small_ref[row + taps - 1 : row + taps, lanes] = jnp.sum(a * values, axis=0, keepdims=True)
        for k in range(taps - 1):
            total = total + taps_v[k : k + 1] * after[pl.ds(taps - 1 - k, slots), :]
            small_ref[row + k : row + k + 1, lanes] = jnp.sum(
                a * pad[pl.ds(8 - (taps - 1) + k, slots), :], axis=0, keepdims=True
            )
        small_ref[bias_row : bias_row + 1, lanes] = jnp.sum(a, axis=0, keepdims=True)
        grad_ref[:, at : at + 128] = total.astype(grad_ref.dtype)

    for p in range(inner // 128):
        lanes = slice(p * 128, (p + 1) * 128)
        values = first_ref[:, inner + p * 128 : inner + (p + 1) * 128]
        pre = conv_pre(pad, values, cx_ref[:, lanes], cxb_ref[:, lanes])
        heads_in = (pre * sigmoid(pre)).astype(BF)
        z = first_ref[:, lanes]
        sig = sigmoid(z)
        grad_gated = scale * gain_ref[:, lanes] * dyn_ref[:, lanes] - gated_ref[:, lanes] * cube
        grad_y = grad_gated * (z * sig)
        grad_ref[:, lanes] = (
            grad_gated * y_ref[:, lanes] * (sig * (1.0 + z * (1.0 - sig)))
        ).astype(grad_ref.dtype)
        skip = skip_ref[:, lanes]
        x_f = heads_in.astype(F32)
        small_ref[5:6, lanes] = jnp.sum(grad_y * x_f, axis=0, keepdims=True)
        grad_y_low = grad_y.astype(BF)
        grad_x = [None] * n_blocks
        grad_state = None
        for b in reversed(range(n_blocks)):
            d, cum, d_t, cum_t, inter = blocks[b]
            r = slice(b * BLOCK, (b + 1) * BLOCK)
            x, xf, dy, dyl = heads_in[r], x_f[r], grad_y[r], grad_y_low[r]
            cum_p = by_head(left, cum[:, 2 * p : 2 * p + 1], cum[:, 2 * p + 1 : 2 * p + 2])
            d_p = by_head(left, d[:, 2 * p : 2 * p + 1], d[:, 2 * p + 1 : 2 * p + 2])
            dxs = []
            for i, h in enumerate((2 * p, 2 * p + 1)):
                own = left if i == 0 else jnp.logical_not(left)
                q = dot_nt(jnp.where(own, dy, 0.0).astype(BF), x)
                decay = jnp.exp(jnp.where(mask, cum[:, h : h + 1] - cum_t[h : h + 1, :], -1e30))
                scaled = decay * d_t[h : h + 1, :]
                dxs.append(dot_tn((inter * scaled).astype(BF), dyl))
                grad_inter[b] = grad_inter[b] + scaled * q
                moved = inter * decay * q
                sums_t[b, h : h + 1, :] = jnp.sum(moved, axis=0, keepdims=True)
                rows = jnp.sum(moved * d_t[h : h + 1, :], axis=1, keepdims=True)
                cols[0, r, :] += jnp.where(lane == h, rows, 0.0)
            dx = by_head(left, dxs[0], dxs[1]) + skip * dy
            extra = None
            if b > 0:
                state = state_ref[p, b - 1]
                grown = dy * jnp.exp(cum_p)
                grown_low = grown.astype(BF)
                extra = grown * dot_mm(c_rows[r], state.astype(BF))
                grad_c[b] = grad_c[b] + dot_nt(grown_low, state.astype(BF))
                back_state = dot_tn(c_rows[r], grown_low)
            end = cum_p[BLOCK - 1 :]
            end_sum = None
            if grad_state is not None:
                weight = jnp.exp(end - cum_p)
                low_state = grad_state.astype(BF)
                dz_rows = dot_mm(b_rows[r], low_state)
                grad_b[b] = grad_b[b] + dot_nt((xf * d_p * weight).astype(BF), low_state)
                dx = dx + dz_rows * d_p * weight
                direct = dz_rows * xf * weight
                through = direct * d_p
                end_sum = jnp.sum(through, axis=0, keepdims=True)
                if b > 0:
                    end_sum = end_sum + jnp.exp(end) * jnp.sum(grad_state * state, axis=0, keepdims=True)
                extra = -through if extra is None else extra - through
            for i, h in enumerate((2 * p, 2 * p + 1)):
                own = left if i == 0 else jnp.logical_not(left)
                if extra is not None:
                    column = jnp.sum(jnp.where(own, extra, 0.0), axis=1, keepdims=True)
                    cols[0, r, :] += jnp.where(lane == h, column, 0.0)
                if end_sum is not None:
                    column = jnp.sum(jnp.where(own, direct, 0.0), axis=1, keepdims=True)
                    cols[1, r, :] += jnp.where(lane == h, column, 0.0)
                    last = jnp.sum(jnp.where(own[0:1], end_sum, 0.0), axis=1, keepdims=True)
                    at = slice((b + 1) * BLOCK - 1, (b + 1) * BLOCK)
                    cols[0, at, :] += jnp.where(lane[0:1] == h, last, 0.0)
            if b > 0:
                grad_state = back_state if grad_state is None else jnp.exp(end) * grad_state + back_state
            grad_x[b] = dx
        conv_back(
            jnp.concatenate(grad_x, axis=0), pre, values, cx_ref[:, lanes], 0, 4, lanes, inner + p * 128
        )
    upper = jnp.logical_not(mask).astype(F32) + (
        lax.broadcasted_iota(jnp.int32, (BLOCK, BLOCK), 0)
        == lax.broadcasted_iota(jnp.int32, (BLOCK, BLOCK), 1)
    ).astype(F32)
    ddts, logs = [], jnp.zeros((1, 128), F32)
    for b in range(n_blocks):
        d, cum, d_t, cum_t, inter = blocks[b]
        r = slice(b * BLOCK, (b + 1) * BLOCK)
        low = grad_inter[b].astype(BF)
        grad_c[b] = grad_c[b] + dot_mm(low, b_rows[r])
        grad_b[b] = grad_b[b] + dot_tn(low, c_rows[r])
        direct = sums_t[b].T
        reach = dot_exact(upper, cols[0, r, :] - direct * d)
        logs = logs + jnp.sum(rate * d * reach, axis=0, keepdims=True)
        ddts.append((direct + cols[1, r, :] + rate * reach) * sigmoid(raw[r]))
    ddt = jnp.concatenate(ddts, axis=0)
    grad_ref[:, bc_at + 256 : bc_at + 384] = ddt.astype(grad_ref.dtype)
    small_ref[11:12, 0:128] = logs
    small_ref[12:13, 0:128] = jnp.sum(ddt, axis=0, keepdims=True)
    for i, (c, grads) in enumerate(((0, grad_b), (128, grad_c))):
        conv_back(
            jnp.concatenate(grads, axis=0), bc_pre[i], first_ref[:, bc_at + c : bc_at + c + 128],
            cbc_ref[:, c : c + 128], 6, 10, slice(c, c + 128), bc_at + c,
        )


def pad_lanes(v):
    return jnp.pad(v, (0, -v.shape[0] % 128)).reshape(1, -1)


def mixer_params(conv_x, conv_x_bias, conv_bc, conv_bc_bias, dt_bias, a_log, d_skip):
    size = conv_x.shape[1] // d_skip.shape[0]
    return (
        conv_x, conv_x_bias.reshape(1, -1), conv_bc, conv_bc_bias.reshape(1, -1),
        pad_lanes(dt_bias), pad_lanes(a_log), jnp.repeat(d_skip, size).reshape(1, -1),
    )


def mixer_forward(firsts, params):
    slots = firsts.shape[0]
    inner = params[0].shape[1]
    pairs, n_blocks = inner // 128, slots // BLOCK
    shape = lambda *s: jax.ShapeDtypeStruct(s, F32)
    return pl.pallas_call(
        mixer_forward_kernel,
        out_shape=(
            shape(slots, inner), shape(slots, inner), shape(slots, 1),
            shape(pairs, n_blocks - 1, 128, 128),
        ),
        in_specs=[VMEM_SPEC] * 8,
        out_specs=(VMEM_SPEC,) * 4,
        scratch_shapes=[pltpu.VMEM((slots + 8, 128), F32)],
        compiler_params=pltpu.CompilerParams(vmem_limit_bytes=48 << 20),
        cost_estimate=pl.CostEstimate(
            flops=8 * slots * BLOCK * inner, bytes_accessed=24 * slots * inner,
            transcendentals=slots * BLOCK * inner // 32,
        ),
        name="mixer_forward",
    )(firsts, *params)


def mixer_backward(full_inner, firsts, y, gated, dyn, scale, product, gain, state, params):
    slots, width = firsts.shape
    inner = params[0].shape[1]
    return pl.pallas_call(
        functools.partial(mixer_backward_kernel, full_inner),
        out_shape=(
            jax.ShapeDtypeStruct((slots, width), BF),
            jax.ShapeDtypeStruct((16, inner), F32),
        ),
        in_specs=[VMEM_SPEC] * 15,
        out_specs=(VMEM_SPEC,) * 2,
        scratch_shapes=[
            pltpu.VMEM((slots + 8, 128), F32),
            pltpu.VMEM((slots + 8, 128), F32),
            pltpu.VMEM((2, slots, 128), F32),
            pltpu.VMEM((slots // BLOCK, 128, BLOCK), F32),
        ],
        compiler_params=pltpu.CompilerParams(vmem_limit_bytes=56 << 20),
        cost_estimate=pl.CostEstimate(
            flops=24 * slots * BLOCK * inner, bytes_accessed=40 * slots * inner,
            transcendentals=slots * BLOCK * inner // 32,
        ),
        name="mixer_backward",
    )(firsts, y, gated, dyn, scale, product, gain.reshape(1, -1), state, *params)


def local(
    x_in,
    lengths,
    routes,
    route_w,
    ln1_gain,
    w_zx,
    w_bc,
    w_dt,
    conv_x,
    conv_x_bias,
    conv_bc,
    conv_bc_bias,
    dt_bias,
    a_log,
    d_skip,
    gnorm_gain,
    w_out,
    ln2_gain,
    w_shared_gu,
    w_shared_down,
    w_exp_gu,
    w_exp_down,
    cotangent,
):
    slots, width = x_in.shape
    n_dp = lax.axis_size("dp")
    n_t = lax.axis_size("tensor")
    my_t = lax.axis_index("tensor")
    my_dp = lax.axis_index("dp")
    piece = slots // n_t
    n_local = w_exp_gu.shape[0]
    n_experts = n_dp * n_local
    cap = slots * routes.shape[1] * 4 // (3 * n_experts)
    if cap > slots:
        cap = slots
    heads = dt_bias.shape[0]
    inner = conv_x.shape[1]
    head_size = inner // heads
    state = conv_bc.shape[1] // 2
    full_inner = inner * n_t
    rows = w_zx.shape[0]
    n_sh = w_shared_gu.shape[2]

    dt_at = 2 * inner + 2 * state
    first_width = dt_at + heads + -(dt_at + heads) % 128
    first = jnp.concatenate(
        [
            w_zx.reshape(rows, 2 * inner),
            w_bc,
            w_dt,
            jnp.zeros((rows, first_width - dt_at - heads), F32),
        ],
        axis=1,
    ).astype(BF)
    shared = jnp.concatenate([w_shared_gu.reshape(rows, 2 * n_sh), w_shared_down], axis=1)

    live = (jnp.arange(slots, dtype=jnp.int32) < lengths[0]).astype(F32)
    g2 = cotangent.astype(F32) * live[:, None]
    g2_low = g2.astype(BF)
    expert_range = jnp.arange(n_experts, dtype=jnp.int32)
    chosen = routes[:, :, None] == expert_range[None, None, :]
    weights = jnp.sum(jnp.where(chosen, route_w[:, :, None], 0.0), axis=1)
    high = weights.astype(BF)
    low = (weights - high.astype(F32)).astype(BF)
    table = jnp.concatenate([g2_low, high, low], axis=1)
    table = lax.dynamic_slice_in_dim(table, my_t * piece, piece, axis=0)
    g2_piece = lax.dynamic_slice_in_dim(g2_low, my_t * piece, piece, axis=0)

    first, proj_out, table = start([first, w_out.astype(BF)], table, n_dp, 1)
    shared, first = lax.optimization_barrier((shared.astype(BF), first))
    shared = lax.all_gather(shared, "dp", axis=0, tiled=True)
    shared_gu = shared[:, : 2 * n_sh]
    shared_down = shared[:, 2 * n_sh :]

    x_float = x_in.astype(F32)
    scale_one = rms_scale(x_float)
    normed_one = (x_float * scale_one * ln1_gain).astype(BF)
    firsts = dotf("td,df->tf", normed_one, first)
    params = mixer_params(conv_x, conv_x_bias, conv_bc, conv_bc_bias, dt_bias, a_log, d_skip)
    y, gated_mix, squares, states = mixer_forward(firsts, params)
    squares = lax.psum(squares.reshape(slots), "tensor")[:, None]
    scale_mix = lax.rsqrt(squares / full_inner + EPSILON)
    normed_mix = (gated_mix * scale_mix * gnorm_gain).astype(BF)
    mixer_part = dotf("tc,dc->td", normed_mix, proj_out).astype(BF)
    x_piece = lax.dynamic_slice_in_dim(x_in, my_t * piece, piece, axis=0)
    all_rows, hidden_one = middle(mixer_part, x_piece, ln2_gain, n_dp, 2)
    mine = lax.dynamic_slice_in_dim(all_rows, my_dp * slots, slots, axis=0)

    shared_pre = dotf("td,df->tf", mine, shared_gu)
    s_gate, s_up = shared_pre[:, :n_sh], shared_pre[:, n_sh:]
    shared_silu, shared_slope = silu_parts(s_gate)
    shared_act = (shared_silu * s_up).astype(BF)
    grad_shared_act = dotf("td,df->tf", g2_low, shared_down)
    grad_shared_pre = jnp.concatenate(
        [grad_shared_act * s_up * shared_slope, grad_shared_act * shared_silu], axis=1
    ).astype(BF)
    grad_normed_shared = dotf("tf,df->td", grad_shared_pre, shared_gu)
    shared_part = dotf("tf,df->td", shared_act, shared_down)

    high = lax.dynamic_slice_in_dim(table, width + my_dp * n_local, n_local, axis=1)
    low = lax.dynamic_slice_in_dim(table, width + n_experts + my_dp * n_local, n_local, axis=1)
    weights = (high.astype(F32) + low.astype(F32)).reshape(n_dp, slots, n_local)
    member = (weights > 0.0).astype(BF)
    before = (
        jnp.arange(slots)[:, None] > jnp.arange(slots)[None, :]
    ).astype(BF)
    position = dotf("ut,ste->seu", before, member).astype(jnp.int32)
    weights = weights.transpose(0, 2, 1)
    position = jnp.where(weights > 0.0, position, -1)

    dxn_part, out_part, grad_exp_gu, grad_exp_down = experts(
        position, weights, all_rows, table, w_exp_gu, w_exp_down, cap
    )
    grad_exp_gu = grad_exp_gu.reshape(w_exp_gu.shape)

    def add_own(total, own):
        at = my_dp * slots
        own = own + lax.dynamic_slice_in_dim(total, at, slots, axis=0).astype(F32)
        return lax.dynamic_update_slice_in_dim(total, own.astype(BF), at, axis=0)

    dxn_part = add_own(dxn_part, grad_normed_shared)
    out_part = add_own(out_part, shared_part)
    grad_shared_down = dotf("td,tf->df", g2_low, shared_act)
    grad_shared_gu = dotf("td,tf->df", mine, grad_shared_pre)
    grad_shared_w = jnp.concatenate([grad_shared_gu, grad_shared_down], axis=1).astype(BF)
    dxn_part, grad_shared_w = lax.optimization_barrier((dxn_part, grad_shared_w))
    grad_one, sum_ln2, dm = turn(
        dxn_part, hidden_one, g2_piece, ln2_gain, n_dp, 3
    )
    dm = dm.reshape(slots, width)

    grad_shared_w = lax.psum_scatter(grad_shared_w, "dp", scatter_dimension=0, tiled=True)
    grad_out_w = dotf("td,tc->dc", dm, normed_mix).astype(BF)
    grad_normed_mix = dotf("td,dc->tc", dm, proj_out)
    weighted_mix = gnorm_gain * grad_normed_mix
    grad_gnorm = jnp.sum(grad_normed_mix * gated_mix * scale_mix, axis=0)
    product_sum = lax.optimization_barrier(jnp.sum(weighted_mix * gated_mix, axis=-1))
    product_sum = lax.optimization_barrier(lax.psum(product_sum, "tensor")).reshape(slots, 1)
    grad_first, mixer_sums = mixer_backward(
        full_inner, firsts, y, gated_mix, grad_normed_mix, scale_mix, product_sum, gnorm_gain,
        states, params,
    )
    taps = conv_x.shape[0]
    grad_conv_x, grad_conv_x_bias = mixer_sums[:taps], mixer_sums[4]
    grad_d_skip = jnp.sum(mixer_sums[5].reshape(heads, head_size), axis=1)
    grad_conv_bc, grad_conv_bc_bias = mixer_sums[6 : 6 + taps, : 2 * state], mixer_sums[10, : 2 * state]
    grad_a_log, grad_dt_bias = mixer_sums[11, :heads], mixer_sums[12, :heads]
    grad_input_part = dotf("tf,df->td", grad_first, first).astype(BF)
    grad_first_w = dotf("td,tf->df", normed_one, grad_first).astype(BF)
    def lanes(*vectors):
        vector = jnp.concatenate([v.reshape(-1) for v in vectors])
        return jnp.pad(vector, (0, -vector.shape[0] % (8 * width))).reshape(-1, width)

    wide = lanes(jnp.zeros((width,), F32), sum_ln2, grad_conv_bc, grad_conv_bc_bias)
    n_wide = wide.shape[0]
    narrow = lanes(
        grad_conv_x, grad_conv_x_bias, grad_gnorm, grad_dt_bias, grad_a_log, grad_d_skip
    )
    grad_first_w, grad_shared_w = lax.optimization_barrier((grad_first_w, grad_shared_w))
    merged = n_dp <= 8
    grad_x, sums, (first_f, grad_out_w), layer_out = tail(
        [grad_first_w, grad_out_w],
        grad_input_part,
        grad_one,
        x_piece,
        ln1_gain,
        jnp.concatenate([wide, narrow], axis=0),
        n_wide,
        2 * inner,
        2 * state,
        n_dp,
        5,
        *((out_part, hidden_one) if merged else ()),
    )
    if not merged:
        ffn_out = scatter_rows(out_part, n_dp, 4)
        layer_out = lax.all_gather((hidden_one + ffn_out).astype(BF), "tensor", axis=0, tiled=True)
    grad_x = grad_x.reshape(slots, width).astype(F32)
    wide, narrow = sums[:n_wide].reshape(-1), sums[n_wide:].reshape(-1)
    at = [0]

    def take(vector, *shape):
        size = 1
        for s in shape:
            size *= s
        part = lax.slice_in_dim(vector, at[0], at[0] + size).reshape(shape)
        at[0] += size
        return part

    o_ln1 = take(wide, width)
    o_ln2 = take(wide, width)
    o_conv_bc = take(wide, taps, 2 * state)
    o_conv_bc_bias = take(wide, 2 * state)
    at[0] = 0
    o_conv_x = take(narrow, taps, inner)
    o_conv_x_bias = take(narrow, inner)
    o_gnorm = take(narrow, inner)
    o_dt_bias = take(narrow, heads)
    o_a_log = take(narrow, heads)
    o_d_skip = take(narrow, heads)
    shared_f = grad_shared_w.astype(F32)
    return (
        layer_out,
        grad_x,
        o_ln1,
        first_f[:, : 2 * inner].reshape(rows, 2, inner),
        first_f[:, 2 * inner : dt_at],
        first_f[:, dt_at : dt_at + heads],
        o_conv_x,
        o_conv_x_bias,
        o_conv_bc,
        o_conv_bc_bias,
        o_dt_bias,
        o_a_log,
        o_d_skip,
        o_gnorm,
        grad_out_w,
        o_ln2,
        shared_f[:, : 2 * n_sh].reshape(rows, 2, n_sh),
        shared_f[:, 2 * n_sh :],
        grad_exp_gu,
        grad_exp_down,
    )


def solution(mesh):
    return jax.shard_map(
        local,
        mesh=mesh,
        in_specs=(
            P("dp", None),
            P("dp"),
            P("dp", None),
            P("dp", None),
            P(),
            P("dp", None, "tensor"),
            P("dp", None),
            P("dp", "tensor"),
            P(None, "tensor"),
            P("tensor"),
            P(),
            P(),
            P("tensor"),
            P("tensor"),
            P("tensor"),
            P("tensor"),
            P("dp", "tensor"),
            P(),
            P("dp", None, "tensor"),
            P("dp", "tensor"),
            P("dp", None, None, "tensor"),
            P("dp", "tensor", None),
            P("dp", None),
        ),
        out_specs=(
            P("dp", None),
            P("dp", None),
            P(),
            P("dp", None, "tensor"),
            P("dp", None),
            P("dp", "tensor"),
            P(None, "tensor"),
            P("tensor"),
            P(),
            P(),
            P("tensor"),
            P("tensor"),
            P("tensor"),
            P("tensor"),
            P("dp", "tensor"),
            P(),
            P("dp", None, "tensor"),
            P("dp", "tensor"),
            P("dp", None, None, "tensor"),
            P("dp", "tensor", None),
        ),
        check_vma=False,
    )
```
